32 devices in a mesh: wide: 8 (over z, y), narrow: 4 (over x, core).
Axes of the slice: x: 2, y: 2, z: 4, core: 2. Of those that a mesh axis runs over, the one named last changes fastest.
Arguments:
- master: float32 [9728, 128], P(('wide', 'narrow')), may hold values from -4 to 4
- momentum: float32 [9728, 128], P(('wide', 'narrow')), may hold values from -164.60571 to 164.60571, as said below
- average: float32 [9728, 128], P(('wide', 'narrow')), may hold values from -4 to 4
- tokens: bfloat16 [75264, 320], P(('wide', 'narrow')), may hold values from -24 to 24
- clip_ids: int32 [75264], P(('wide', 'narrow')), may hold values from -1 to 31, as said below
- borders: int32 [75264], P(('wide', 'narrow')), may hold values from 0 to 63, as said below
- cotangent: bfloat16 [75264, 320], P(('wide', 'narrow')), may hold values from -5 to 5
Outputs:
- output: bfloat16 [75264, 320], P(('wide', 'narrow'))
- grad_tokens: bfloat16 [75264, 320], P(('wide', 'narrow'))
- gradient: float32 [9728, 128], P(('wide', 'narrow'))
- new_master: float32 [9728, 128], P(('wide', 'narrow'))
- new_momentum: float32 [9728, 128], P(('wide', 'narrow'))
- new_average: float32 [9728, 128], P(('wide', 'narrow'))
- new_copy: bfloat16 [9728, 128], P(('wide', 'narrow'))
The draws below stay inside these ranges and needn't reach their ends.
Inputs may be any that keep to these rules, and one draw needn't show every extreme that they name: `clip_ids`: each device's block of 2352 rows holds one whole clip from its first row on, with the clip's number on all its rows and -1 on the rows after it; every number is the clip of exactly one device. A clip has 3, 6 or 12 frames of 14 x 14 tokens in frame, row, column order; in every draw some clip fills its device's block and some has 3 frames. `borders`: bits 0 and 1 mark a clip's first and last frame, bits 2 and 3 the first and last token row of a frame, bits 4 and 5 the first and last column; rows with clip -1 have all six bits set. `momentum`: no entry is zero.
All inputs are finite; a program needn't handle non-finite values.
Results may differ from the reference program's by a relative error of at most 0.017.
Values may be sent and summed in bfloat16 or wider, within the bound.
No kernel may reach another device: no remote copies, remote signals or barrier semaphores. Data moves between devices by JAX's collectives and lax.ppermute only.
A program may use at most 320 MiB of HBM per device.

```python
import math
import jax
import jax.numpy as jnp
from jax import lax

HEADS = 5
HEAD_DIM = 64
DIM = 320
FFN = 1280
SIDE = 14
F_S = 3
TOK_DEV = 2352
CLIPS = 32
TOKENS = 75264
NPARAM = 1241600
PROWS = 9728


def clip_layout(key):
    selector = jax.random.randint(jax.random.fold_in(key, 11), (CLIPS,), 0, 100)
    frames = jnp.where(selector < 25, F_S, jnp.where(selector < 41, 2 * F_S, 4 * F_S))
    fullest = jax.random.randint(jax.random.fold_in(key, 12), (), 0, CLIPS)
    stride = jax.random.randint(jax.random.fold_in(key, 13), (), 1, CLIPS)
    shortest = (fullest + stride) % CLIPS
    device_index = jnp.arange(CLIPS)
    frames = jnp.where(device_index == fullest, 4 * F_S, jnp.where(device_index == shortest, F_S, frames))
    labels = jax.random.permutation(jax.random.fold_in(key, 14), CLIPS)
    position = jnp.arange(TOK_DEV)
    frame_cells = SIDE * SIDE
    inside = position[None, :] < (frames * frame_cells)[:, None]
    frame_index = (position // frame_cells)[None, :]
    remainder = position % frame_cells
    row_index = (remainder // SIDE)[None, :]
    column_index = (remainder % SIDE)[None, :]
    border_bits = (frame_index == 0).astype(jnp.int32) + 2 * (frame_index == frames[:, None] - 1).astype(jnp.int32) + 4 * (row_index == 0).astype(jnp.int32) + 8 * (row_index == SIDE - 1).astype(jnp.int32) + 16 * (column_index == 0).astype(jnp.int32) + 32 * (column_index == SIDE - 1).astype(jnp.int32)
    border_bits = jnp.where(inside, border_bits, 63)
    clip_label = jnp.where(inside, labels[:, None], -1)
    return (clip_label.reshape(-1).astype(jnp.int32), border_bits.reshape(-1).astype(jnp.int32))


def draw_clip_ids(key, part):
    return clip_layout(jax.random.fold_in(key, 5))[0]


def draw_borders(key, part):
    return clip_layout(jax.random.fold_in(key, 5))[1]


def weight_field(key):
    regions = [(27 * DIM, 0.0, 0.2), (DIM, 0.0, 0.1), (DIM, 1.0, 0.1), (DIM, 0.0, 0.1), (3 * DIM * DIM, 0.0, DIM ** (-0.5)), (2 * DIM, 0.0, 0.05), (DIM * DIM, 0.0, 10.0 * DIM ** (-0.5)), (DIM, 0.0, 0.1), (DIM, 1.0, 0.1), (DIM, 0.0, 0.1), (DIM * FFN, 0.0, DIM ** (-0.5)), (FFN, 0.0, 0.1), (FFN * DIM, 0.0, FFN ** (-0.5)), (DIM, 0.0, 0.1), (PROWS * 128 - NPARAM, 0.0, 0.02)]
    centre = jnp.concatenate([jnp.full((length,), centre_value, jnp.float32) for length, centre_value, spread in regions])
    spreads = jnp.concatenate([jnp.full((length,), spread, jnp.float32) for length, centre_value, spread in regions])
    normal_draw = jax.random.truncated_normal(key, -3.0, 3.0, (PROWS * 128,), jnp.float32)
    return (centre + spreads * normal_draw).reshape(PROWS, 128)


def draw_master(key, part):
    return weight_field(jax.random.fold_in(key, 21))


def draw_average(key, part):
    return weight_field(jax.random.fold_in(key, 22))


def draw_momentum(key, part):
    magnitude = jnp.exp(jax.random.uniform(jax.random.fold_in(key, 31), (PROWS, 128), jnp.float32, math.log(0.5), math.log(2.0)))
    signs = jax.random.rademacher(jax.random.fold_in(key, 32), (PROWS, 128)).astype(jnp.float32)
    return 0.3 * math.sqrt(TOKENS) * signs * magnitude


def draw_tokens(key, part):
    base_draw = jax.random.truncated_normal(jax.random.fold_in(key, 41), -4.0, 4.0, (TOKENS, DIM), jnp.float32)
    row_scale = jnp.exp(jax.random.uniform(jax.random.fold_in(key, 42), (TOKENS, 1), jnp.float32, math.log(0.4), math.log(4.0)))
    column_scale = jnp.exp(jax.random.uniform(jax.random.fold_in(key, 43), (1, DIM), jnp.float32, math.log(0.7), math.log(1.4)))
    return (base_draw * row_scale * column_scale).astype(jnp.bfloat16)


def block_scale(key, extent, cuts, smallest, largest):
    factor_of, own = 1.0, jax.random.fold_in(key, 6)
    for axis_at, parts in cuts:
        heights = jnp.exp(jax.random.uniform(jax.random.fold_in(own, axis_at), (parts,), jnp.float32, smallest / len(cuts), largest / len(cuts)))
        factor_of = factor_of * jnp.repeat(heights, extent[axis_at] // parts).reshape([-1 if axis == axis_at else 1 for axis in range(len(extent))])
    return factor_of


def noise(own_key, dims, scale, reach, split=(), kind=jnp.bfloat16):
    entries = scale * jax.random.normal(own_key, dims, jnp.float32)
    if split:
        entries = entries * block_scale(own_key, dims, split, -0.22, 0.18)
    return jnp.clip(entries, -reach, reach).astype(kind)


def setup_inputs(seed: int = 0) -> dict:
    seeds = jax.random.split(jax.random.key(seed), 8)
    master = draw_master(jax.random.fold_in(seeds[7], 71), 0)
    momentum = draw_momentum(jax.random.fold_in(seeds[7], 71), 0)
    average = draw_average(jax.random.fold_in(seeds[7], 71), 0)
    tokens = draw_tokens(jax.random.fold_in(seeds[7], 71), 0)
    clip_ids = draw_clip_ids(jax.random.fold_in(seeds[7], 71), 0)
    borders = draw_borders(jax.random.fold_in(seeds[7], 71), 0)
    cotangent = noise(seeds[6], (TOKENS, DIM), 1.0, 5.0, ((0, 32),))
    return {"master": master, "momentum": momentum, "average": average, "tokens": tokens, "clip_ids": clip_ids, "borders": borders, "cotangent": cotangent}


@jax.custom_vjp
def low(v):
    return lax.optimization_barrier(v.astype(jnp.bfloat16)).astype(jnp.float32)

@jax.custom_vjp
def low_back(v):
    return v

def low_keep(v):
    return (low(v), None)

def low_pass(kept, grad):
    return (grad,)

def back_keep(v):
    return (v, None)

def back_low(kept, grad):
    return (low(grad),)
low.defvjp(low_keep, low_pass)
low_back.defvjp(back_keep, back_low)
EPSILON = 1e-06
MOMENTUM = 0.9
DECAY_RATE = 0.0001
AVERAGE_KEEP = 0.8
RATE_FACTOR = 0.03
NEGATIVE = -1000000000.0
TAP_STEPS = [(frame_step, row_step, column_step) for frame_step in (-1, 0, 1) for row_step in (-1, 0, 1) for column_step in (-1, 0, 1)]

def split_params(rounded):
    lengths = [27 * DIM, DIM, DIM, DIM, 3 * DIM * DIM, 2 * DIM, DIM * DIM, DIM, DIM, DIM, DIM * FFN, FFN, FFN * DIM, DIM]
    pieces = []
    offset = 0
    for length in lengths:
        pieces.append(rounded[offset:offset + length])
        offset = offset + length
    return (pieces[0].reshape(27, DIM), pieces[1], pieces[2], pieces[3], pieces[4].reshape(DIM, 3 * DIM), pieces[5], pieces[6].reshape(DIM, DIM), pieces[7], pieces[8], pieces[9], pieces[10].reshape(DIM, FFN), pieces[11], pieces[12].reshape(FFN, DIM), pieces[13])

def tap_masks(borders):
    bit_flags = [borders >> shift_bit & 1 for shift_bit in range(6)]
    validity = []
    for frame_step, row_step, column_step in TAP_STEPS:
        allowed = jnp.ones(borders.shape, jnp.float32)
        for step_value, low_bit, high_bit in ((frame_step, 0, 1), (row_step, 2, 3), (column_step, 4, 5)):
            if step_value == -1:
                allowed = allowed * (1 - bit_flags[low_bit]).astype(jnp.float32)
            if step_value == 1:
                allowed = allowed * (1 - bit_flags[high_bit]).astype(jnp.float32)
        validity.append(allowed)
    return jnp.stack(validity)

def position_mix(values, conv_weight, validity):
    margin = SIDE * SIDE + SIDE + 1
    row_count = values.shape[0]
    padded = jnp.pad(values, ((margin, margin), (0, 0)))
    summed = jnp.zeros_like(values)
    for tap_index, (frame_step, row_step, column_step) in enumerate(TAP_STEPS):
        offset = frame_step * SIDE * SIDE + row_step * SIDE + column_step
        shifted = padded[margin + offset:margin + offset + row_count]
        summed = summed + validity[tap_index][:, None] * shifted * conv_weight[tap_index]
    return summed

def layer_norm(values):
    centered = values - lax.optimization_barrier(jnp.mean(values, axis=-1, keepdims=True))
    variance = lax.optimization_barrier(jnp.mean(centered * centered, axis=-1, keepdims=True))
    return centered * lax.rsqrt(variance + EPSILON)

def forward(rounded, values, block_ids, validity):
    conv_weight, conv_bias, gain_one, shift_one, qkv_weight, qv_bias, proj_weight, proj_bias, gain_two, shift_two, fc1_weight, fc1_bias, fc2_weight, fc2_bias = split_params(rounded)
    highest = lax.Precision.HIGHEST
    mixed_rows = values + position_mix(values, conv_weight, validity) + conv_bias
    normed = low(layer_norm(mixed_rows) * gain_one + shift_one)
    bias_full = jnp.concatenate([qv_bias[:DIM], jnp.zeros((DIM,), qv_bias.dtype), qv_bias[DIM:]])
    projected = low_back(jnp.dot(normed, qkv_weight, precision=highest) + bias_full)
    queries = low(HEAD_DIM ** (-0.5) * projected[:, :DIM]).reshape(-1, HEADS, HEAD_DIM)
    key_rows = low(projected[:, DIM:2 * DIM]).reshape(-1, HEADS, HEAD_DIM)
    value_rows = low(projected[:, 2 * DIM:]).reshape(-1, HEADS, HEAD_DIM)
    scores = low_back(jnp.einsum('qhd,khd->hqk', queries, key_rows, precision=highest))
    same_clip = block_ids[:, None] == block_ids[None, :]
    scores = jnp.where(same_clip[None], scores, NEGATIVE)
    attention_weights = low(jax.nn.softmax(scores, axis=-1))
    attended = jnp.einsum('hqk,khd->qhd', attention_weights, value_rows, precision=highest).reshape(-1, DIM)
    attended = low(low_back(attended))
    branch = low_back(jnp.dot(attended, proj_weight, precision=highest) + proj_bias)
    middle = mixed_rows + branch
    normed_two = low(layer_norm(middle) * gain_two + shift_two)
    inner_value = low_back(jnp.dot(normed_two, fc1_weight, precision=highest) + fc1_bias)
    activated = low(jax.nn.gelu(inner_value, approximate=False))
    outer_value = low_back(jnp.dot(activated, fc2_weight, precision=highest) + fc2_bias)
    return middle + outer_value

def reference(master, momentum, average, tokens, clip_ids, borders, cotangent):
    rounded = low(master.reshape(-1))
    token_blocks = tokens.reshape(CLIPS, TOK_DEV, DIM)
    id_blocks = clip_ids.reshape(CLIPS, TOK_DEV)
    border_blocks = borders.reshape(CLIPS, TOK_DEV)
    cotangent_blocks = cotangent.reshape(CLIPS, TOK_DEV, DIM)

    def per_device(grad_sum, inputs):
        block_tokens, block_ids, block_borders, block_cotangent = inputs
        validity = tap_masks(block_borders)
        present = (block_ids >= 0).astype(jnp.float32)

        def apply_block(params, values):
            return forward(params, values, block_ids, validity)
        result, pullback = jax.vjp(apply_block, rounded, block_tokens.astype(jnp.float32))
        grad_params, grad_values = pullback(block_cotangent.astype(jnp.float32) * present[:, None])
        return (grad_sum + grad_params, (result.astype(jnp.bfloat16), grad_values.astype(jnp.bfloat16)))
    grad_flat, (results, grad_rows) = lax.scan(per_device, jnp.zeros(rounded.shape, jnp.float32), (token_blocks, id_blocks, border_blocks, cotangent_blocks))
    gradient = grad_flat.reshape(PROWS, 128)
    step_rate = RATE_FACTOR / math.sqrt(TOKENS)
    decayed = gradient + DECAY_RATE * master
    new_momentum = MOMENTUM * momentum + decayed
    new_master = master - step_rate * (decayed + MOMENTUM * new_momentum)
    new_average = AVERAGE_KEEP * average + (1.0 - AVERAGE_KEEP) * new_master
    return (results.reshape(TOKENS, DIM), grad_rows.reshape(TOKENS, DIM), gradient, new_master, new_momentum, new_average, new_master.astype(jnp.bfloat16))
```

```python
import functools
import math

import jax
import jax.numpy as jnp
from jax import lax
from jax.experimental import pallas as pl
from jax.experimental.pallas import tpu as pltpu
from jax.sharding import PartitionSpec as P

HEADS = 5
HEAD_DIM = 64
DIM = 320
FFN = 1280
SIDE = 14
FRAME = SIDE * SIDE
LANES = 128
WIDE_HEADS = HEADS * LANES

EPSILON = 1e-06
MOMENTUM = 0.9
DECAY_RATE = 0.0001
AVERAGE_KEEP = 0.8
RATE_FACTOR = 0.03
LOG2E = 1.0 / math.log(2.0)
LN2 = math.log(2.0)
INVERSE_ROOT_TWO_PI = 1.0 / math.sqrt(2.0 * math.pi)
BLOCKED = -(2.0**30)
SAFE_BOUND = 80.0

bf16 = jnp.bfloat16
f32 = jnp.float32

AT_CONV = 0
AT_QKV = 150
AT_QV = 4950
AT_PROJ = 4960
AT_VEC = 6560
AT_FC1 = 6575
AT_FC1B = 12975
AT_FC2 = 12995
AT_FC2B = 19395
HALF_END = 19400


def dot(a, b):
    return lax.dot_general(a, b, (((1,), (0,)), ((), ())), preferred_element_type=f32)


def dot_nt(a, b):
    return lax.dot_general(a, b, (((1,), (1,)), ((), ())), preferred_element_type=f32)


def dot_tn(a, b):
    return lax.dot_general(a, b, (((0,), (0,)), ((), ())), preferred_element_type=f32)


def params(limit=58):
    return pltpu.CompilerParams(vmem_limit_bytes=limit << 20)


def lane_of(shape):
    return lax.broadcasted_iota(jnp.int32, shape, len(shape) - 1)


def row_of(shape):
    return lax.broadcasted_iota(jnp.int32, shape, 0)


def low_half(value, side):
    return value if side == 0 else pltpu.roll(value, 64, axis=1)


def high_half(value, side):
    return value if side == 1 else pltpu.roll(value, 64, axis=1)


def split3(value):
    first = value.astype(bf16).astype(f32)
    rest = value - first
    second = rest.astype(bf16).astype(f32)
    return first, second, rest - second


def read_half(flat, at, length, step, count, parity, j):
    index = at + parity * length + j
    return flat[pl.ds(index // 2, count, stride=step), :], index % 2


def read_vector(flat, at, length):
    tiles = []
    lane = lane_of((1, LANES))
    for j in range(0, length, 2):
        row, side = divmod(at + j, 2)
        low = low_half(flat[row : row + 1, :], side)
        if j + 1 < length:
            row, side = divmod(at + j + 1, 2)
            tiles.append(jnp.where(lane < 64, low, high_half(flat[row : row + 1, :], side)))
        else:
            tiles.append(low[:, :64])
    return jnp.concatenate(tiles, axis=1)


def odd_matrix(flat, out, at, length, rows):
    pairs = rows // 2
    for parity in range(2):
        for tile in range((length + 1) // 2):
            low, side = read_half(flat, at, length, length, pairs, parity, 2 * tile)
            low = low_half(low, side)
            place = pl.ds(parity, pairs, stride=2)
            if 2 * tile + 1 < length:
                high, side = read_half(flat, at, length, length, pairs, parity, 2 * tile + 1)
                merged = jnp.where(lane_of(low.shape) < 64, low, high_half(high, side))
            else:
                merged = low
            out[tile, place, :] = merged


def unpack_kernel(first, rest, wqkv, wproj, fc1, fc2, bqkv, vecs, fc1b, flat, wide, tall):
    quarter = first.shape[0]
    flat[:quarter, :] = first[...].astype(f32)
    flat[quarter:, :] = rest[...].astype(f32)
    for parity in range(2):
        for j in range(15):
            value, side = read_half(flat, AT_QKV, 15, 15, 160, parity, j)
            value = jnp.where(lane_of(value.shape) < 64, low_half(value, side), 0.0)
            wide[j, pl.ds(parity, 160, stride=2), :] = value
    for j in range(15):
        wqkv[:, j * LANES : (j + 1) * LANES] = wide[j].astype(bf16)
    lane = lane_of((1, LANES))
    for j in range(15):
        if 5 <= j < 10:
            bqkv[:, j * LANES : (j + 1) * LANES] = jnp.zeros((1, LANES), f32)
        else:
            row, side = divmod(AT_QV + (j if j < 5 else j - 5), 2)
            value = low_half(flat[row : row + 1, :], side)
            bqkv[:, j * LANES : (j + 1) * LANES] = jnp.where(lane < 64, value, 0.0)
    odd_matrix(flat, wide, AT_PROJ, 5, DIM)
    for head in range(HEADS):
        for tile in range(3):
            width = LANES if tile < 2 else 64
            columns = slice(tile * LANES, tile * LANES + width)
            part = wide[tile, head * 64 : head * 64 + 64, :width].astype(bf16)
            wproj[head * LANES : head * LANES + 64, columns] = part
        wproj[head * LANES + 64 : (head + 1) * LANES, :] = jnp.zeros((64, DIM), bf16)
    for row in range(3):
        vecs[row : row + 1, :] = read_vector(flat, AT_VEC + 5 * row, 5)
    vecs[3:4, :] = read_vector(flat, AT_FC2B, 5)
    vecs[4:8, :] = jnp.zeros((4, DIM), f32)
    fc1b[...] = read_vector(flat, AT_FC1B, 20)
    for tile in range(10):
        low, side = read_half(flat, AT_FC1, 20, 10, DIM, 0, 2 * tile)
        high, side_high = read_half(flat, AT_FC1, 20, 10, DIM, 0, 2 * tile + 1)
        merged = jnp.where(lane_of(low.shape) < 64, low_half(low, side), high_half(high, side_high))
        fc1[:, tile * LANES : (tile + 1) * LANES] = merged.astype(bf16)
    odd_matrix(flat, tall, AT_FC2, 5, FFN)
    for tile in range(3):
        width = LANES if tile < 2 else 64
        fc2[:, tile * LANES : tile * LANES + width] = tall[tile, :, :width].astype(bf16)


def unpack(first, rest):
    rows = first.shape[0] + rest.shape[0]
    return pl.pallas_call(
        unpack_kernel,
        name="unpack",
        out_shape=[
            jax.ShapeDtypeStruct((DIM, 3 * WIDE_HEADS), bf16),
            jax.ShapeDtypeStruct((WIDE_HEADS, DIM), bf16),
            jax.ShapeDtypeStruct((DIM, FFN), bf16),
            jax.ShapeDtypeStruct((FFN, DIM), bf16),
            jax.ShapeDtypeStruct((1, 3 * WIDE_HEADS), f32),
            jax.ShapeDtypeStruct((8, DIM), f32),
            jax.ShapeDtypeStruct((1, FFN), f32),
        ],
        scratch_shapes=[
            pltpu.VMEM((rows, LANES), f32),
            pltpu.VMEM((15, DIM, LANES), f32),
            pltpu.VMEM((3, FFN, LANES), f32),
        ],
        compiler_params=params(),
    )(first, rest)


PAD_ROWS = 16 * 16
BODY = SIDE * 16


def spread_matrix(shift):
    cell = lax.broadcasted_iota(jnp.int32, (PAD_ROWS, 208), 0)
    source = lax.broadcasted_iota(jnp.int32, (PAD_ROWS, 208), 1)
    row, column = cell >> 4, cell & 15
    inside = (row >= 1) & (row <= SIDE) & (column < SIDE)
    wanted = (row - 1) * SIDE + column + shift
    return jnp.where(inside & (source == wanted), 1.0, 0.0).astype(bf16)


def gather_matrix(shift):
    target = lax.broadcasted_iota(jnp.int32, (208, BODY), 0)
    cell = lax.broadcasted_iota(jnp.int32, (208, BODY), 1)
    row, column = cell >> 4, cell & 15
    wanted = row * SIDE + column + shift
    return jnp.where((column < SIDE) & (target == wanted), 1.0, 0.0).astype(bf16)


def window(group, member):
    start = group * (4 * FRAME) + member * FRAME - 4 * member
    return pl.ds(pl.multiple_of(start, 16), 208)


TILES = ((0, 128), (128, 256), (256, 320))


def pieces(value):
    first = value.astype(bf16)
    return first, (value - first.astype(f32)).astype(bf16)


def pad_frames(padded, frames, rows_at, exact, shifts):
    zero = jnp.zeros((PAD_ROWS, DIM), f32)
    for copy in range(len(shifts)):
        padded[copy, 0] = zero
        padded[copy, 13] = zero
    for member in range(4):
        spread = spread_matrix(4 * member)

        def fill(group, carry, member=member, spread=spread):
            frame = group * 4 + member

            @pl.when(frame < frames)
            def _():
                part = rows_at(window(group, member))
                if exact:
                    cells = dot(spread, part)
                else:
                    first, second = pieces(part)
                    cells = dot(spread, first) + dot(spread, second)
                for copy, shift in enumerate(shifts):
                    moved = pltpu.roll(cells, shift % PAD_ROWS, axis=0) if shift else cells
                    padded[copy, frame + 1] = moved

            @pl.when(frame >= frames)
            def _():
                for copy in range(len(shifts)):
                    padded[copy, frame + 1] = zero

            return carry

        lax.fori_loop(0, 3, fill, 0)


def mix_frame(padded, weights, frame, sign, low, high):
    total = None
    for a in (-1, 0, 1):
        for b in (-1, 0, 1):
            for c in (-1, 0, 1):
                tap = 9 * (a + 1) + 3 * (b + 1) + (c + 1)
                begin = 16 + sign * b * 16
                cells = padded[c + 1, frame + 1 + sign * a, begin : begin + BODY, low:high]
                term = cells * weights[tap : tap + 1, low:high]
                total = term if total is None else total + term
    return total


def conv_params(head, flat, weights):
    flat[...] = head[...].astype(f32)
    for parity in range(2):
        for tile in range(3):
            low, side = read_half(flat, AT_CONV, 5, 5, 15, parity, 2 * tile)
            low = low_half(low, side)
            place = pl.ds(parity, 15, stride=2)
            if tile < 2:
                high, side = read_half(flat, AT_CONV, 5, 5, 15, parity, 2 * tile + 1)
                low = jnp.where(lane_of(low.shape) < 64, low, high_half(high, side))
            weights[tile, place, :] = low


def conv_kernel(frames_ref, tokens, head, mixed, convp, flat, weights, padded, comp):
    frames = frames_ref[0]
    conv_params(head, flat, weights)
    for tile, (low, high) in enumerate(TILES):
        convp[:, low:high] = weights[tile, :, : high - low]
    pad_frames(padded, frames, lambda place: tokens[place, :], True, (1, 0, -1))
    mixed[...] = jnp.zeros(mixed.shape, f32)
    for member in range(4):
        spread = spread_matrix(4 * member)
        back = gather_matrix(4 * member)

        def each(group, carry, member=member, spread=spread, back=back):
            frame = group * 4 + member
            place = window(group, member)

            @pl.when(frame < frames)
            def _():
                for low, high in TILES:
                    own = padded[1, frame + 1, 16 : 16 + BODY, low:high]
                    comp[:, low:high] = own + mix_frame(padded, convp, frame, 1, low, high)

            @pl.when(frame >= frames)
            def _():
                own = dot(spread, tokens[place, :])[16 : 16 + BODY, :]
                comp[...] = own + own * convp[13:14, :]

            first, second = pieces(comp[...] + convp[27:28, :])
            mixed[place, :] += dot(back, first) + dot(back, second)
            return carry

        lax.fori_loop(0, 3, each, 0)


SMEM_SPEC = pl.BlockSpec(memory_space=pltpu.SMEM)
VMEM_SPEC = pl.BlockSpec(memory_space=pltpu.VMEM)


def conv_forward(frames, tokens, head):
    rows = tokens.shape[0]
    return pl.pallas_call(
        conv_kernel,
        name="conv_forward",
        in_specs=[SMEM_SPEC, VMEM_SPEC, VMEM_SPEC],
        out_shape=[jax.ShapeDtypeStruct((rows, DIM), f32), jax.ShapeDtypeStruct((32, DIM), f32)],
        scratch_shapes=[
            pltpu.VMEM(head.shape, f32),
            pltpu.VMEM((3, 32, LANES), f32),
            pltpu.VMEM((3, 14, PAD_ROWS, DIM), f32),
            pltpu.VMEM((BODY, DIM), f32),
        ],
        compiler_params=params(),
    )(frames, tokens, head)


def normalize(values):
    centered = values - jnp.mean(values, axis=-1, keepdims=True)
    variance = jnp.mean(centered * centered, axis=-1, keepdims=True)
    inverse = lax.rsqrt(variance + EPSILON)
    return centered * inverse, inverse


def qkv_kernel(frames_ref, mixed, convp, wqkv, bqkv, normed_out, q_out, k_out, v_out, size):
    block = pl.program_id(0)
    rows = mixed.shape[0]
    frames = frames_ref[0]
    normal, unused_inverse = normalize(mixed[...])
    normed = (normal * convp[28:29, :] + convp[29:30, :]).astype(bf16)
    normed_out[...] = normed
    lane = lane_of((rows, LANES))
    inside = row_of((rows, LANES)) + block * rows < frames * FRAME
    q_mask = jnp.where(
        ((lane == 64) & ~inside) | ((lane == 65) & inside), BLOCKED, 0.0
    )
    k_mask = jnp.where(
        ((lane == 64) & inside) | ((lane == 65) & ~inside) | ((lane >= 66) & (lane < 69)), 1.0, 0.0
    )
    v_mask = jnp.where((lane >= 64) & (lane < 67), 1.0, 0.0)
    scale = HEAD_DIM ** (-0.5) * LOG2E

    @pl.when(block == 0)
    def _():
        size[...] = jnp.zeros(size.shape, f32)

    for head in range(HEADS):
        def columns(kind, head=head):
            place = slice((kind * HEADS + head) * LANES, (kind * HEADS + head + 1) * LANES)
            return dot(normed, wqkv[:, place]) + bqkv[:, place]

        query = (columns(0) * scale).astype(bf16)
        key = columns(1).astype(bf16)
        query_size = jnp.max(jnp.sum(query.astype(f32) ** 2, axis=-1, keepdims=True), axis=0, keepdims=True)
        key_size = jnp.max(jnp.sum(key.astype(f32) ** 2, axis=-1, keepdims=True), axis=0, keepdims=True)
        q_out[head] = (query.astype(f32) + q_mask).astype(bf16)
        k_out[head] = (key.astype(f32) + k_mask).astype(bf16)
        v_out[head] = (columns(2) + v_mask).astype(bf16)
        size[head : head + 1, :] = jnp.maximum(size[head : head + 1, :], query_size)
        size[head + 8 : head + 9, :] = jnp.maximum(size[head + 8 : head + 9, :], key_size)


def project(frames, mixed, convp, wqkv, bqkv, block=784):
    rows = mixed.shape[0]
    heads_spec = pl.BlockSpec((HEADS, block, LANES), lambda i: (0, i, 0))
    rows_spec = pl.BlockSpec((block, DIM), lambda i: (i, 0))
    heads_shape = jax.ShapeDtypeStruct((HEADS, rows, LANES), bf16)
    return pl.pallas_call(
        qkv_kernel,
        name="qkv_forward",
        grid=(rows // block,),
        in_specs=[
            SMEM_SPEC,
            rows_spec,
            pl.BlockSpec((32, DIM), lambda i: (0, 0)),
            pl.BlockSpec((DIM, 3 * WIDE_HEADS), lambda i: (0, 0)),
            pl.BlockSpec((1, 3 * WIDE_HEADS), lambda i: (0, 0)),
        ],
        out_specs=[rows_spec, heads_spec, heads_spec, heads_spec, pl.BlockSpec((16, LANES), lambda i: (0, 0))],
        out_shape=[
            jax.ShapeDtypeStruct((rows, DIM), bf16),
            heads_shape,
            heads_shape,
            heads_shape,
            jax.ShapeDtypeStruct((16, LANES), f32),
        ],
        compiler_params=params(),
    )(frames, mixed, convp, wqkv, bqkv)


def attend_kernel(chunk, q, k, v, size, o_out, q_back, query, shift):
    head = pl.program_id(0)
    keys = k.shape[1]
    tall = q.shape[1]
    bound = jnp.max(size[pl.ds(head, 1), :] * size[pl.ds(head + 8, 1), :])
    query[...] = q[0]
    shift[...] = jnp.zeros(shift.shape, f32)

    @pl.when(bound > SAFE_BOUND * SAFE_BOUND)
    def _():
        shift[...] = jnp.full(shift.shape, -jnp.inf, f32)

        def peak(step, carry):
            scores = dot_nt(k[0, pl.ds(pl.multiple_of(step * 112, 16), 112), :], q[0])
            shift[...] = jnp.maximum(shift[...], jnp.max(scores, axis=0, keepdims=True))
            return carry

        lax.fori_loop(0, keys // 112, peak, 0)
        first, second, third = split3(-shift[...])
        row = row_of((LANES, tall))
        tail = jnp.where(row == 66, first, jnp.where(row == 67, second, jnp.where(row == 68, third, 0.0)))
        query[...] = (q[0].astype(f32) + tail.T).astype(bf16)

    total = None
    for start in range(0, keys, chunk):
        place = slice(start, min(start + chunk, keys))
        weights = jnp.exp2(dot_nt(k[0, place, :], query[...])).astype(bf16)
        part = dot_tn(v[0, place, :], weights)
        total = part if total is None else total + part
    sums = total[64:65, :]
    first, second, third = split3(-(shift[...] + jnp.log2(sums)))
    row = row_of((8, tall))
    tail = jnp.where(row == 2, first, jnp.where(row == 3, second, jnp.where(row == 4, third, 0.0)))
    stacked = jnp.concatenate([total[:64, :] / sums, tail, jnp.zeros((56, tall), f32)], axis=0).T
    lane = lane_of((tall, LANES))
    o_out[0] = jnp.where(lane < 64, stacked, 0.0).astype(bf16)
    q_back[0] = jnp.where((lane >= 66) & (lane < 69), stacked, q[0].astype(f32)).astype(bf16)


def attend(q, k, v, size, chunk=512):
    rows = q.shape[1]
    whole = pl.BlockSpec((1, rows, LANES), lambda h: (h, 0, 0))
    shape = jax.ShapeDtypeStruct((HEADS, rows, LANES), bf16)
    return pl.pallas_call(
        functools.partial(attend_kernel, chunk),
        name="attend",
        grid=(HEADS,),
        in_specs=[whole, whole, whole, pl.BlockSpec((16, LANES), lambda h: (0, 0))],
        out_specs=[whole, whole],
        out_shape=[shape, shape],
        scratch_shapes=[pltpu.VMEM((rows, LANES), bf16), pltpu.VMEM((1, rows), f32)],
        compiler_params=params(),
    )(q, k, v, size)


def attend_back_kernel(rows, q, do, k, v, dq_out, dk_out, dv_out, dq):
    step = pl.program_id(1)
    wide = k.shape[1]
    inside = row_of((wide, LANES)) + step * wide < rows
    key = jnp.where(inside, k[0], jnp.zeros((), bf16))
    value = jnp.where(inside, v[0], jnp.zeros((), bf16))
    weights = jnp.exp2(dot_nt(q[0], key))
    grad_scores = (weights * dot_nt(do[0], value)).astype(bf16)
    weights = weights.astype(bf16)
    dv_out[0] = dot_tn(do[0], weights).T.astype(bf16)
    dk_out[0] = (dot_tn(q[0], grad_scores) * LN2).T.astype(bf16)
    part = dot(grad_scores, key)

    @pl.when(step == 0)
    def _():
        dq[...] = part

    @pl.when(step > 0)
    def _():
        dq[...] += part

    @pl.when(step == pl.num_programs(1) - 1)
    def _():
        dq_out[0] = (dq[...] * HEAD_DIM ** (-0.5)).astype(bf16)


def attend_back(q, do, k, v, wide=1280):
    heads, rows = q.shape[:2]
    block = pl.BlockSpec((1, wide, LANES), lambda h, i: (h, i, 0))
    whole = pl.BlockSpec((1, rows, LANES), lambda h, i: (h, 0, 0))
    shape = jax.ShapeDtypeStruct((heads, rows, LANES), bf16)
    return pl.pallas_call(
        functools.partial(attend_back_kernel, rows),
        name="attend_back",
        grid=(heads, pl.cdiv(rows, wide)),
        in_specs=[whole, whole, block, block],
        out_specs=[whole, block, block],
        out_shape=[shape, shape, shape],
        scratch_shapes=[pltpu.VMEM((rows, LANES), f32)],
        compiler_params=params(),
    )(q, do, k, v)


def erf_parts(value):
    bell = jnp.exp(-0.5 * value * value)
    return bell, 0.5 * (1.0 + lax.erf(value * (1.0 / math.sqrt(2.0))))


def add_tiles(ref, place, value):
    for tile, (low, high) in enumerate(TILES):
        ref[tile, place, : high - low] += value[:, low:high]


def middle_kernel(
    frames_ref, o, mixed, cot, wproj, fc1, fc2, vecs, fc1b,
    output, gmid_out, do_out, gproj, gfc1, gfc2, gvec, gfc1b, chunk,
):
    block = pl.program_id(0)
    rows = mixed.shape[0]
    inside = row_of((rows, DIM)) + block * rows < frames_ref[0] * FRAME

    @pl.when(block == 0)
    def _():
        for ref in (gproj, gfc1, gfc2, gvec, gfc1b):
            ref[...] = jnp.zeros(ref.shape, f32)

    attended = jnp.concatenate([o[head] for head in range(HEADS)], axis=1)
    middle = mixed[...] + (dot(attended, wproj[...]) + vecs[0:1, :])
    normal, inverse = normalize(middle)
    normed = (normal * vecs[1:2, :] + vecs[2:3, :]).astype(bf16)
    grad_output = jnp.where(inside, cot[...].astype(f32), 0.0)
    grad_outer = grad_output.astype(bf16)
    total = middle + vecs[3:4, :]
    grad_normed = jnp.zeros((rows, DIM), f32)
    for start in range(0, FFN, chunk):
        place = slice(start, start + chunk)
        inner = dot(normed, fc1[:, place]) + fc1b[:, place]
        bell, gate = erf_parts(inner)
        activated = (inner * gate).astype(bf16)
        total += dot(activated, fc2[place, :])
        slope = gate + inner * bell * INVERSE_ROOT_TWO_PI
        grad_inner = (dot_nt(grad_outer, fc2[place, :]) * slope)
        gfc1b[:, place] += jnp.sum(grad_inner, axis=0, keepdims=True)
        grad_inner = grad_inner.astype(bf16)
        add_tiles(gfc2, place, dot_tn(activated, grad_outer))
        gfc1[:, place] += dot_tn(normed, grad_inner)
        grad_normed += dot_nt(grad_inner, fc1[:, place])
    output[...] = total.astype(bf16)
    scaled = grad_normed * vecs[1:2, :]
    grad_middle = grad_output + inverse * (
        scaled
        - jnp.mean(scaled, axis=-1, keepdims=True)
        - normal * jnp.mean(scaled * normal, axis=-1, keepdims=True)
    )
    gmid_out[...] = grad_middle
    grad_branch = grad_middle.astype(bf16)
    add_tiles(gproj, slice(None), dot_tn(attended, grad_branch))
    gvec[0:1, :] += jnp.sum(grad_branch.astype(f32), axis=0, keepdims=True)
    gvec[1:2, :] += jnp.sum(grad_normed * normal, axis=0, keepdims=True)
    gvec[2:3, :] += jnp.sum(grad_normed, axis=0, keepdims=True)
    gvec[3:4, :] += jnp.sum(grad_output, axis=0, keepdims=True)
    lane = lane_of((rows, LANES))
    for head in range(HEADS):
        grad_head = dot_nt(grad_branch, wproj[head * LANES : (head + 1) * LANES, :])
        delta = jnp.sum(grad_head * o[head].astype(f32), axis=-1, keepdims=True)
        first, second, third = split3(-delta)
        tail = jnp.where(lane == 64, first, jnp.where(lane == 65, second, third))
        do_out[head] = jnp.where((lane >= 64) & (lane < 67), tail, grad_head).astype(bf16)


def feed_forward(frames, o, mixed, cot, wproj, fc1, fc2, vecs, fc1b, block=784, chunk=256):
    rows = mixed.shape[0]
    heads_spec = pl.BlockSpec((HEADS, block, LANES), lambda i: (0, i, 0))
    rows_spec = pl.BlockSpec((block, DIM), lambda i: (i, 0))

    def full(*shape):
        return pl.BlockSpec(shape, lambda i: (0,) * len(shape))

    return pl.pallas_call(
        functools.partial(middle_kernel, chunk=chunk),
        name="feed_forward",
        grid=(rows // block,),
        in_specs=[
            SMEM_SPEC, heads_spec, rows_spec, rows_spec,
            full(WIDE_HEADS, DIM), full(DIM, FFN), full(FFN, DIM), full(8, DIM), full(1, FFN),
        ],
        out_specs=[
            rows_spec, rows_spec, heads_spec,
            full(3, WIDE_HEADS, LANES), full(DIM, FFN), full(3, FFN, LANES), full(8, DIM), full(1, FFN),
        ],
        out_shape=[
            jax.ShapeDtypeStruct((rows, DIM), bf16),
            jax.ShapeDtypeStruct((rows, DIM), f32),
            jax.ShapeDtypeStruct((HEADS, rows, LANES), bf16),
            jax.ShapeDtypeStruct((3, WIDE_HEADS, LANES), f32),
            jax.ShapeDtypeStruct((DIM, FFN), f32),
            jax.ShapeDtypeStruct((3, FFN, LANES), f32),
            jax.ShapeDtypeStruct((8, DIM), f32),
            jax.ShapeDtypeStruct((1, FFN), f32),
        ],
        compiler_params=params(),
    )(frames, o, mixed, cot, wproj, fc1, fc2, vecs, fc1b)


def qkv_back_kernel(dq, dk, dv, normed, mixed, gmid, wqkv, convp, gmix_out, gqkv, gbias, gvec):
    block = pl.program_id(0)

    @pl.when(block == 0)
    def _():
        for ref in (gqkv, gbias, gvec):
            ref[...] = jnp.zeros(ref.shape, f32)

    normal, inverse = normalize(mixed[...])
    grads = jnp.concatenate([part[head] for part in (dq, dk, dv) for head in range(HEADS)], axis=1)
    grad_qkv = dot_tn(normed[...], grads)
    for tile in range(15):
        gqkv[tile] += grad_qkv[:, tile * LANES : (tile + 1) * LANES]
    gbias[...] += jnp.sum(grads.astype(f32), axis=0, keepdims=True)
    grad_normed = dot_nt(grads, wqkv[...])
    gvec[1:2, :] += jnp.sum(grad_normed * normal, axis=0, keepdims=True)
    gvec[2:3, :] += jnp.sum(grad_normed, axis=0, keepdims=True)
    scaled = grad_normed * convp[28:29, :]
    grad_mixed = gmid[...] + inverse * (
        scaled
        - jnp.mean(scaled, axis=-1, keepdims=True)
        - normal * jnp.mean(scaled * normal, axis=-1, keepdims=True)
    )
    gvec[0:1, :] += jnp.sum(grad_mixed, axis=0, keepdims=True)
    gmix_out[...] = grad_mixed


def project_back(dq, dk, dv, normed, mixed, gmid, wqkv, convp, block=784):
    rows = mixed.shape[0]
    heads_spec = pl.BlockSpec((HEADS, block, LANES), lambda i: (0, i, 0))
    rows_spec = pl.BlockSpec((block, DIM), lambda i: (i, 0))

    def full(*shape):
        return pl.BlockSpec(shape, lambda i: (0,) * len(shape))

    return pl.pallas_call(
        qkv_back_kernel,
        name="qkv_back",
        grid=(rows // block,),
        in_specs=[heads_spec, heads_spec, heads_spec, rows_spec, rows_spec, rows_spec,
                  full(DIM, 3 * WIDE_HEADS), full(32, DIM)],
        out_specs=[rows_spec, full(15, DIM, LANES), full(1, 3 * WIDE_HEADS), full(8, DIM)],
        out_shape=[
            jax.ShapeDtypeStruct((rows, DIM), f32),
            jax.ShapeDtypeStruct((15, DIM, LANES), f32),
            jax.ShapeDtypeStruct((1, 3 * WIDE_HEADS), f32),
            jax.ShapeDtypeStruct((8, DIM), f32),
        ],
        compiler_params=params(),
    )(dq, dk, dv, normed, mixed, gmid, wqkv, convp)


def conv_weight_kernel(frames_ref, tokens, gmix, gvec, out, xpad, gpad, sums, tiles, flat):
    frames = frames_ref[0]
    pad_frames(xpad, frames, lambda place: tokens[place, :], True, (0,))
    pad_frames(gpad, frames, lambda place: gmix[place, :], False, (-1, 0, 1))
    sums[...] = jnp.zeros(sums.shape, f32)

    def weight_frame(frame, carry):
        for low, high in TILES:
            for c in (-1, 0, 1):
                body = gpad[c + 1, frame + 1, 16 : 16 + BODY, low:high]
                for a in (-1, 0, 1):
                    for b in (-1, 0, 1):
                        tap = 9 * (a + 1) + 3 * (b + 1) + (c + 1)
                        begin = 16 + b * 16
                        cells = xpad[0, frame + 1 + a, begin : begin + BODY, low:high]
                        product = (body * cells).reshape(BODY // 8, 8, high - low)
                        sums[tap, :, low:high] += jnp.sum(product, axis=0)
        return carry

    lax.fori_loop(0, frames, weight_frame, 0)
    tiles[...] = jnp.zeros(tiles.shape, f32)
    flat[...] = jnp.zeros(flat.shape, f32)
    for tile, (low, high) in enumerate(TILES):
        tiles[tile, 0:27, : high - low] = jnp.sum(sums[:, :, low:high], axis=1)
        tiles[tile, 27:30, : high - low] = gvec[0:3, low:high]
    for parity in range(2):
        for j in range(5):
            value = tiles[j // 2, pl.ds(parity, 15, stride=2), :]
            put_half(flat, AT_CONV + parity * 5 + j, value, j % 2, 5, 15)
    out[...] = flat[...].astype(bf16)


def conv_weight_grads(frames, tokens, gmix, gvec):
    return pl.pallas_call(
        conv_weight_kernel,
        name="conv_weight_grads",
        in_specs=[SMEM_SPEC, VMEM_SPEC, VMEM_SPEC, VMEM_SPEC],
        out_shape=jax.ShapeDtypeStruct((80, LANES), bf16),
        scratch_shapes=[
            pltpu.VMEM((1, 14, PAD_ROWS, DIM), f32),
            pltpu.VMEM((3, 14, PAD_ROWS, DIM), f32),
            pltpu.VMEM((27, 8, DIM), f32),
            pltpu.VMEM((3, 32, LANES), f32),
            pltpu.VMEM((80, LANES), f32),
        ],
        compiler_params=params(),
    )(frames, tokens, gmix, gvec)


def conv_token_kernel(frames_ref, gmix, convp, gtok, gpad, comp):
    frames = frames_ref[0]
    pad_frames(gpad, frames, lambda place: gmix[place, :], False, (-1, 0, 1))
    gtok[...] = jnp.zeros(gtok.shape, bf16)
    for member in range(4):
        back = gather_matrix(4 * member)

        def each(group, carry, member=member, back=back):
            frame = group * 4 + member

            @pl.when(frame < frames)
            def _():
                for low, high in TILES:
                    own = gpad[1, frame + 1, 16 : 16 + BODY, low:high]
                    comp[:, low:high] = own + mix_frame(gpad, convp, frame, -1, low, high)
                place = window(group, member)
                moved = dot(back, comp[...].astype(bf16))
                gtok[place, :] = (gtok[place, :].astype(f32) + moved).astype(bf16)

            return carry

        lax.fori_loop(0, 3, each, 0)


def conv_token_grads(frames, gmix, convp):
    rows = gmix.shape[0]
    return pl.pallas_call(
        conv_token_kernel,
        name="conv_token_grads",
        in_specs=[SMEM_SPEC, VMEM_SPEC, VMEM_SPEC],
        out_shape=jax.ShapeDtypeStruct((rows, DIM), bf16),
        scratch_shapes=[pltpu.VMEM((3, 14, PAD_ROWS, DIM), f32), pltpu.VMEM((BODY, DIM), f32)],
        compiler_params=params(),
    )(frames, gmix, convp)


def put_half(flat, index, value, side, step=1, count=1):
    row, wanted = divmod(index, 2)
    place = pl.ds(row, count, stride=step) if step > 1 else pl.ds(row, count)
    lane = lane_of(value.shape)
    if wanted == 0:
        flat[place, :] += jnp.where(lane < 64, low_half(value, side), 0.0)
    else:
        flat[place, :] += jnp.where(lane >= 64, high_half(value, side), 0.0)


def put_vector(flat, index, value):
    width = value.shape[1]
    for j in range(width // 64):
        low = (j // 2) * LANES
        part = value[:, low : min(low + LANES, width)]
        if part.shape[1] < LANES:
            part = jnp.concatenate([part, jnp.zeros((1, 64), f32)], axis=1)
        put_half(flat, index + j, part, j % 2)


PACK_BASE = 2432


def pack_main_kernel(gproj, gfc1, gfc2, gvec, gfc1b, out, flat):
    flat[...] = jnp.zeros(flat.shape, f32)
    base = 2 * PACK_BASE
    for parity in range(2):
        for j in range(5):
            for head in range(HEADS):
                value = gproj[j // 2, pl.ds(head * LANES + parity, 32, stride=2), :]
                put_half(flat, AT_PROJ - base + (64 * head + parity) * 5 + j, value, j % 2, 5, 32)
            value = gfc2[j // 2, pl.ds(parity, FFN // 2, stride=2), :]
            put_half(flat, AT_FC2 - base + parity * 5 + j, value, j % 2, 5, FFN // 2)
    for j in range(20):
        value = gfc1[:, (j // 2) * LANES : (j // 2 + 1) * LANES]
        put_half(flat, AT_FC1 - base + j, value, j % 2, 10, DIM)
    for row in range(3):
        put_vector(flat, AT_VEC - base + 5 * row, gvec[row : row + 1, :])
    put_vector(flat, AT_FC2B - base, gvec[3:4, :])
    put_vector(flat, AT_FC1B - base, gfc1b[...])
    out[...] = flat[...].astype(bf16)


def pack_main(gproj, gfc1, gfc2, gvec, gfc1b, rows):
    return pl.pallas_call(
        pack_main_kernel,
        name="pack_main",
        out_shape=jax.ShapeDtypeStruct((rows - PACK_BASE, LANES), bf16),
        scratch_shapes=[pltpu.VMEM((rows - PACK_BASE, LANES), f32)],
        compiler_params=params(),
    )(gproj, gfc1, gfc2, gvec, gfc1b)


QKV_ROWS = 2480


def pack_qkv_kernel(gqkv, gbias, out, end, flat):
    flat[...] = jnp.zeros(flat.shape, f32)
    for parity in range(2):
        for j in range(15):
            value = gqkv[j, pl.ds(parity, DIM // 2, stride=2), :]
            put_half(flat, AT_QKV + parity * 15 + j, value, 0, 15, DIM // 2)
    for j in range(10):
        tile = j if j < 5 else j + 5
        put_half(flat, AT_QV + j, gbias[:, tile * LANES : (tile + 1) * LANES], 0)
    out[...] = flat[:PACK_BASE, :].astype(bf16)
    end[...] = flat[PACK_BASE:, :].astype(bf16)


def pack_qkv(gqkv, gbias):
    return pl.pallas_call(
        pack_qkv_kernel,
        name="pack_qkv",
        out_shape=[
            jax.ShapeDtypeStruct((PACK_BASE, LANES), bf16),
            jax.ShapeDtypeStruct((QKV_ROWS - PACK_BASE, LANES), bf16),
        ],
        scratch_shapes=[pltpu.VMEM((QKV_ROWS, LANES), f32)],
        compiler_params=params(),
    )(gqkv, gbias)


AXES = ("wide", "narrow")


def exchange(value, bit):
    count = lax.axis_size(AXES)
    return lax.ppermute(value, AXES, [(i, i ^ (1 << bit)) for i in range(count)])


def my_bit(bit):
    return (lax.axis_index(AXES) >> bit) & 1


def join(value, bit, axis):
    other = exchange(value, bit)
    upper = my_bit(bit) == 1
    pair = jnp.stack([jnp.where(upper, other, value), jnp.where(upper, value, other)], axis=axis)
    return pair.reshape(pair.shape[: axis - 1] + (2 * pair.shape[axis - 1],) + pair.shape[axis + 1 :])


def gather_params(block, bits):
    quarters = block[None]
    for bit in (bits - 1, bits - 2):
        quarters = join(quarters, bit, 1)
    first, rest = quarters[:1, None], quarters[1:, None]
    for bit in range(bits - 3, -1, -1):
        first = join(first, bit, 2)
        rest = join(rest, bit, 2)
    return first.reshape(-1, LANES), rest.reshape(-1, LANES)


def reduce_first(value, bits):
    count = 1 << (bits - 2)
    value = value.reshape(count, -1, LANES)
    for bit in range(bits - 2):
        value = value.reshape(value.shape[0] // 2, 2, -1, LANES)
        mine = my_bit(bit)
        keep = lax.dynamic_index_in_dim(value, mine, 1, keepdims=False)
        give = lax.dynamic_index_in_dim(value, 1 - mine, 1, keepdims=False)
        value = keep + exchange(give, bit)
    value = value[0]
    for bit in (bits - 2, bits - 1):
        value = value + exchange(value, bit)
    return value


def on_device(master, momentum, average, tokens, clip_ids, borders, cotangent):
    wide_count, narrow_count = lax.axis_size("wide"), lax.axis_size("narrow")
    count = wide_count * narrow_count
    bits = count.bit_length() - 1
    own_rows = master.shape[0]
    first, rest = gather_params(master.astype(bf16), bits)
    frames = (jnp.sum((clip_ids >= 0).astype(jnp.int32)) // FRAME).reshape(1)
    mixed, convp = conv_forward(frames, tokens, first[:80])
    wqkv, wproj, fc1, fc2, bqkv, vecs, fc1b = unpack(first, rest)
    normed, q, k, v, size = project(frames, mixed, convp, wqkv, bqkv)
    o, q_back = attend(q, k, v, size)
    output, gmid, do, gproj, gfc1, gfc2, gvec, gfc1b = feed_forward(
        frames, o, mixed, cotangent, wproj, fc1, fc2, vecs, fc1b
    )
    main = pack_main(gproj, gfc1, gfc2, gvec, gfc1b, count * own_rows)
    main = main.reshape(-1, narrow_count, own_rows, LANES)
    main = lax.psum_scatter(main, "narrow", scatter_dimension=1, tiled=True)
    main = jnp.concatenate([jnp.zeros((wide_count // 4,) + main.shape[1:], bf16), main], axis=0)
    main = lax.psum_scatter(main, "wide", scatter_dimension=0, tiled=True).reshape(own_rows, LANES)
    dq, dk, dv = attend_back(q_back, do, k, v)
    gmix, gqkv, gbias, gvec_one = project_back(dq, dk, dv, normed, mixed, gmid, wqkv, convp)
    qkv, qkv_end = pack_qkv(gqkv, gbias)
    qkv = reduce_first(qkv, bits)
    conv = conv_weight_grads(frames, tokens, gmix, gvec_one)
    late = jnp.concatenate([conv, qkv_end], axis=0)
    for bit in range(bits):
        late = late + exchange(late, bit)
    gtok = conv_token_grads(frames, gmix, convp)
    me = lax.axis_index(AXES)
    early = jnp.where(me < count // 4, qkv.astype(f32), main.astype(f32))
    conv, qkv_end = late[:80].astype(f32), late[80:].astype(f32)
    if own_rows < 80:
        conv = conv[:own_rows]
    conv = jnp.pad(conv, ((0, own_rows - conv.shape[0]), (0, 0)))
    qkv_end = jnp.pad(qkv_end, ((0, own_rows - qkv_end.shape[0]), (0, 0)))
    owned = early + jnp.where(me == 0, conv, jnp.where(me == count // 4, qkv_end, 0.0))
    rate = RATE_FACTOR / math.sqrt(tokens.shape[0] * count)
    decayed = owned + DECAY_RATE * master
    new_momentum = MOMENTUM * momentum + decayed
    new_master = master - rate * (decayed + MOMENTUM * new_momentum)
    new_average = AVERAGE_KEEP * average + (1.0 - AVERAGE_KEEP) * new_master
    return (output, gtok, owned, new_master, new_momentum, new_average, new_master.astype(bf16))


def solution(mesh):
    rows = P(("wide", "narrow"), None)
    return jax.shard_map(
        on_device,
        mesh=mesh,
        in_specs=(rows, rows, rows, rows, P(("wide", "narrow")), P(("wide", "narrow")), rows),
        out_specs=(rows,) * 7,
        check_vma=False,
    )
```

```python
import functools
import math

import jax
import jax.numpy as jnp
from jax import lax
from jax.experimental import pallas as pl
from jax.experimental.pallas import tpu as pltpu
from jax.sharding import PartitionSpec as P

HEADS = 5
HEAD_DIM = 64
DIM = 320
FFN = 1280
SIDE = 14
FRAME = SIDE * SIDE
LANES = 128
WIDE_HEADS = HEADS * LANES

EPSILON = 1e-06
MOMENTUM = 0.9
DECAY_RATE = 0.0001
AVERAGE_KEEP = 0.8
RATE_FACTOR = 0.03
LOG2E = 1.0 / math.log(2.0)
LN2 = math.log(2.0)
INVERSE_ROOT_TWO_PI = 1.0 / math.sqrt(2.0 * math.pi)
BLOCKED = -(2.0**30)
SAFE_BOUND = 80.0

bf16 = jnp.bfloat16
f32 = jnp.float32

AT_CONV = 0
AT_QKV = 150
AT_QV = 4950
AT_PROJ = 4960
AT_VEC = 6560
AT_FC1 = 6575
AT_FC1B = 12975
AT_FC2 = 12995
AT_FC2B = 19395
HALF_END = 19400


SMEM_SPEC = pl.BlockSpec(memory_space=pltpu.SMEM)
VMEM_SPEC = pl.BlockSpec(memory_space=pltpu.VMEM)
ANY_SPEC = pl.BlockSpec(memory_space=pl.ANY)


def dot(a, b):
    return lax.dot_general(a, b, (((1,), (0,)), ((), ())), preferred_element_type=f32)


def dot_nt(a, b):
    return lax.dot_general(a, b, (((1,), (1,)), ((), ())), preferred_element_type=f32)


def dot_tn(a, b):
    return lax.dot_general(a, b, (((0,), (0,)), ((), ())), preferred_element_type=f32)


def params(limit=58):
    return pltpu.CompilerParams(vmem_limit_bytes=limit << 20)


def lane_of(shape):
    return lax.broadcasted_iota(jnp.int32, shape, len(shape) - 1)


def row_of(shape):
    return lax.broadcasted_iota(jnp.int32, shape, 0)


def low_half(value, side):
    return value if side == 0 else pltpu.roll(value, 64, axis=1)


def high_half(value, side):
    return value if side == 1 else pltpu.roll(value, 64, axis=1)


def split3(value):
    first = value.astype(bf16).astype(f32)
    rest = value - first
    second = rest.astype(bf16).astype(f32)
    return first, second, rest - second


def read_half(flat, at, length, step, count, parity, j):
    index = at + parity * length + j
    return flat[pl.ds(index // 2, count, stride=step), :], index % 2


def read_vector(flat, at, length):
    tiles = []
    lane = lane_of((1, LANES))
    for j in range(0, length, 2):
        row, side = divmod(at + j, 2)
        low = low_half(flat[row : row + 1, :], side)
        if j + 1 < length:
            row, side = divmod(at + j + 1, 2)
            tiles.append(jnp.where(lane < 64, low, high_half(flat[row : row + 1, :], side)))
        else:
            tiles.append(low[:, :64])
    return jnp.concatenate(tiles, axis=1)


def odd_matrix(flat, out, at, length, rows):
    pairs = rows // 2
    for parity in range(2):
        for tile in range((length + 1) // 2):
            low, side = read_half(flat, at, length, length, pairs, parity, 2 * tile)
            low = low_half(low, side)
            place = pl.ds(parity, pairs, stride=2)
            if 2 * tile + 1 < length:
                high, side = read_half(flat, at, length, length, pairs, parity, 2 * tile + 1)
                merged = jnp.where(lane_of(low.shape) < 64, low, high_half(high, side))
            else:
                merged = low
            out[tile, place, :] = merged


def unpack_kernel(order, first, rest, wqkv, wproj, fc1, fc2, bqkv, vecs, fc1b, flat, wide, tall):
    blocks, rows = first.shape[:2]
    for block in range(blocks):
        place = order[block]
        for quarter in range(4):
            start = (quarter * blocks + block) * rows
            value = first[place] if quarter == 0 else rest[place, quarter - 1]
            flat[start : start + rows, :] = value.astype(f32)
    for parity in range(2):
        for j in range(15):
            value, side = read_half(flat, AT_QKV, 15, 15, 160, parity, j)
            value = jnp.where(lane_of(value.shape) < 64, low_half(value, side), 0.0)
            wide[j, pl.ds(parity, 160, stride=2), :] = value
    for j in range(15):
        wqkv[:, j * LANES : (j + 1) * LANES] = wide[j].astype(bf16)
    lane = lane_of((1, LANES))
    for j in range(15):
        if 5 <= j < 10:
            bqkv[:, j * LANES : (j + 1) * LANES] = jnp.zeros((1, LANES), f32)
        else:
            row, side = divmod(AT_QV + (j if j < 5 else j - 5), 2)
            value = low_half(flat[row : row + 1, :], side)
            bqkv[:, j * LANES : (j + 1) * LANES] = jnp.where(lane < 64, value, 0.0)
    odd_matrix(flat, wide, AT_PROJ, 5, DIM)
    for head in range(HEADS):
        for tile in range(3):
            width = LANES if tile < 2 else 64
            columns = slice(tile * LANES, tile * LANES + width)
            part = wide[tile, head * 64 : head * 64 + 64, :width].astype(bf16)
            wproj[head * LANES : head * LANES + 64, columns] = part
        wproj[head * LANES + 64 : (head + 1) * LANES, :] = jnp.zeros((64, DIM), bf16)
    for row in range(3):
        vecs[row : row + 1, :] = read_vector(flat, AT_VEC + 5 * row, 5)
    vecs[3:4, :] = read_vector(flat, AT_FC2B, 5)
    vecs[4:8, :] = jnp.zeros((4, DIM), f32)
    fc1b[...] = read_vector(flat, AT_FC1B, 20)
    for tile in range(10):
        low, side = read_half(flat, AT_FC1, 20, 10, DIM, 0, 2 * tile)
        high, side_high = read_half(flat, AT_FC1, 20, 10, DIM, 0, 2 * tile + 1)
        merged = jnp.where(lane_of(low.shape) < 64, low_half(low, side), high_half(high, side_high))
        fc1[:, tile * LANES : (tile + 1) * LANES] = merged.astype(bf16)
    odd_matrix(flat, tall, AT_FC2, 5, FFN)
    for tile in range(3):
        width = LANES if tile < 2 else 64
        fc2[:, tile * LANES : tile * LANES + width] = tall[tile, :, :width].astype(bf16)


def unpack(order, first, rest):
    rows = 4 * first.shape[0] * first.shape[1]
    return pl.pallas_call(
        unpack_kernel,
        name="unpack",
        in_specs=[SMEM_SPEC, VMEM_SPEC, VMEM_SPEC],
        out_shape=[
            jax.ShapeDtypeStruct((DIM, 3 * WIDE_HEADS), bf16),
            jax.ShapeDtypeStruct((WIDE_HEADS, DIM), bf16),
            jax.ShapeDtypeStruct((DIM, FFN), bf16),
            jax.ShapeDtypeStruct((FFN, DIM), bf16),
            jax.ShapeDtypeStruct((1, 3 * WIDE_HEADS), f32),
            jax.ShapeDtypeStruct((8, DIM), f32),
            jax.ShapeDtypeStruct((1, FFN), f32),
        ],
        scratch_shapes=[
            pltpu.VMEM((rows, LANES), f32),
            pltpu.VMEM((15, DIM, LANES), f32),
            pltpu.VMEM((3, FFN, LANES), f32),
        ],
        compiler_params=params(),
    )(order, first, rest)


PAD_ROWS = 16 * 16
BODY = SIDE * 16


def spread_matrix(shift):
    cell = lax.broadcasted_iota(jnp.int32, (PAD_ROWS, 208), 0)
    source = lax.broadcasted_iota(jnp.int32, (PAD_ROWS, 208), 1)
    row, column = cell >> 4, cell & 15
    inside = (row >= 1) & (row <= SIDE) & (column < SIDE)
    wanted = (row - 1) * SIDE + column + shift
    return jnp.where(inside & (source == wanted), 1.0, 0.0).astype(bf16)


def gather_matrix(shift):
    target = lax.broadcasted_iota(jnp.int32, (208, BODY), 0)
    cell = lax.broadcasted_iota(jnp.int32, (208, BODY), 1)
    row, column = cell >> 4, cell & 15
    wanted = row * SIDE + column + shift
    return jnp.where((column < SIDE) & (target == wanted), 1.0, 0.0).astype(bf16)


TILES = ((0, 128), (128, 256), (256, 320))


def pieces(value):
    first = value.astype(bf16)
    return first, (value - first.astype(f32)).astype(bf16)


def one_hot_tables(spread, back):
    for member in range(4):
        spread[member] = spread_matrix(4 * member)
        if back is not None:
            back[member] = gather_matrix(4 * member)


def pad_frames(padded, spread, source, frames, first, count, exact, shifts):
    zero = jnp.zeros((PAD_ROWS, DIM), f32)

    def fill(index, carry):
        frame = index + first

        @pl.when((frame >= 0) & (frame < frames))
        def _():
            member = frame & 3
            part = source[pl.ds(pl.multiple_of(frame * FRAME - 4 * member, 16), 208), :]
            if exact:
                cells = dot(spread[member], part)
            else:
                high, low = pieces(part)
                cells = dot(spread[member], high) + dot(spread[member], low)
            for copy, shift in enumerate(shifts):
                padded[copy, index] = pltpu.roll(cells, shift % PAD_ROWS, axis=0) if shift else cells

        @pl.when((frame < 0) | (frame >= frames))
        def _():
            for copy in range(len(shifts)):
                padded[copy, index] = zero

        return carry

    lax.fori_loop(0, count, fill, 0)


def mix_frame(padded, weights, index, sign, low, high):
    total = None
    for a in (-1, 0, 1):
        for b in (-1, 0, 1):
            for c in (-1, 0, 1):
                tap = 9 * (a + 1) + 3 * (b + 1) + (c + 1)
                begin = 16 + sign * b * 16
                cells = padded[c + 1, index + sign * a, begin : begin + BODY, low:high]
                term = cells * weights[tap : tap + 1, low:high]
                total = term if total is None else total + term
    return total


def conv_params(head, flat, weights):
    flat[...] = head[...].astype(f32)
    for parity in range(2):
        for tile in range(3):
            low, side = read_half(flat, AT_CONV, 5, 5, 15, parity, 2 * tile)
            low = low_half(low, side)
            place = pl.ds(parity, 15, stride=2)
            if tile < 2:
                high, side = read_half(flat, AT_CONV, 5, 5, 15, parity, 2 * tile + 1)
                low = jnp.where(lane_of(low.shape) < 64, low, high_half(high, side))
            weights[tile, place, :] = low


def turn_kernel(source, out):
    out[...] = source[...].T


def turn(value):
    rows, columns = value.shape
    return pl.pallas_call(
        turn_kernel,
        name="turn",
        in_specs=[VMEM_SPEC],
        out_specs=VMEM_SPEC,
        out_shape=jax.ShapeDtypeStruct((columns, rows), value.dtype),
        compiler_params=params(32),
        cost_estimate=pl.CostEstimate(flops=0, bytes_accessed=4 * rows * columns, transcendentals=0),
    )(value)


def tables_kernel(spread, back):
    one_hot_tables(spread, back)


def tables():
    return pl.pallas_call(
        tables_kernel,
        name="tables",
        out_shape=[
            jax.ShapeDtypeStruct((4, PAD_ROWS, 208), bf16),
            jax.ShapeDtypeStruct((4, 208, BODY), bf16),
        ],
    )()


PIECE = 4 * FRAME


def conv_piece_kernel(piece, frames_ref, tokens, head, spread, back, *refs):
    if piece > 0:
        refs = refs[1:]
    mixed, convp, flat, weights, padded, comp = refs
    frames = frames_ref[0]
    conv_params(head, flat, weights)
    for tile, (low, high) in enumerate(TILES):
        convp[:, low:high] = weights[tile, :, : high - low]
    pad_frames(padded, spread, tokens, frames, 4 * piece - 1, 6, True, (1, 0, -1))
    mixed[...] = jnp.zeros(mixed.shape, f32)

    def each(member, carry):
        frame = 4 * piece + member

        @pl.when(frame < frames)
        def _():
            for low, high in TILES:
                own = padded[1, member + 1, 16 : 16 + BODY, low:high]
                comp[:, low:high] = own + mix_frame(padded, convp, member + 1, 1, low, high)

        @pl.when(frame >= frames)
        def _():
            rows = tokens[pl.ds(pl.multiple_of(PIECE * piece + 192 * member, 16), 208), :]
            own = dot(spread[member], rows)[16 : 16 + BODY, :]
            comp[...] = own + own * convp[13:14, :]

        high, low = pieces(comp[...] + convp[27:28, :])
        place = pl.ds(pl.multiple_of(192 * member, 16), 208)
        mixed[place, :] += dot(back[member], high) + dot(back[member], low)
        return carry

    lax.fori_loop(0, 4, each, 0)


def conv_piece(piece, frames, tokens, head, spread, back, mixed):
    rows = tokens.shape[0]
    operands = [frames, tokens, head, spread, back] + ([] if piece == 0 else [mixed])
    return pl.pallas_call(
        functools.partial(conv_piece_kernel, piece),
        name=f"conv_piece{piece}",
        grid=(1,),
        in_specs=[SMEM_SPEC] + [VMEM_SPEC] * 4 + [ANY_SPEC] * (piece > 0),
        out_specs=[
            pl.BlockSpec((PIECE, DIM), lambda i: (piece, 0)),
            pl.BlockSpec((32, DIM), lambda i: (0, 0)),
        ],
        out_shape=[jax.ShapeDtypeStruct((rows, DIM), f32), jax.ShapeDtypeStruct((32, DIM), f32)],
        input_output_aliases={5: 0} if piece else {},
        scratch_shapes=[
            pltpu.VMEM(head.shape, f32),
            pltpu.VMEM((3, 32, LANES), f32),
            pltpu.VMEM((3, 6, PAD_ROWS, DIM), f32),
            pltpu.VMEM((BODY, DIM), f32),
        ],
        compiler_params=params(),
    )(*operands)


def normalize(values):
    centered = values - jnp.mean(values, axis=-1, keepdims=True)
    variance = jnp.mean(centered * centered, axis=-1, keepdims=True)
    inverse = lax.rsqrt(variance + EPSILON)
    return centered * inverse, inverse


def qkv_kernel(frames_ref, mixed, convp, wqkv, bqkv, normed_out, q_out, k_out, v_out, size):
    block = pl.program_id(0)
    rows = mixed.shape[0]
    frames = frames_ref[0]
    normal, unused_inverse = normalize(mixed[...])
    normed = (normal * convp[28:29, :] + convp[29:30, :]).astype(bf16)
    normed_out[...] = normed
    lane = lane_of((rows, LANES))
    inside = row_of((rows, LANES)) + block * rows < frames * FRAME
    q_mask = jnp.where(
        ((lane == 64) & ~inside) | ((lane == 65) & inside), BLOCKED, 0.0
    )
    k_mask = jnp.where(
        ((lane == 64) & inside) | ((lane == 65) & ~inside) | ((lane >= 66) & (lane < 69)), 1.0, 0.0
    )
    v_mask = jnp.where((lane >= 64) & (lane < 67), 1.0, 0.0)
    scale = HEAD_DIM ** (-0.5) * LOG2E

    @pl.when(block == 0)
    def _():
        size[...] = jnp.zeros(size.shape, f32)

    for head in range(HEADS):
        def columns(kind, head=head):
            place = slice((kind * HEADS + head) * LANES, (kind * HEADS + head + 1) * LANES)
            return dot(normed, wqkv[:, place]) + bqkv[:, place]

        query = (columns(0) * scale).astype(bf16)
        key = columns(1).astype(bf16)
        query_size = jnp.max(jnp.sum(query.astype(f32) ** 2, axis=-1, keepdims=True), axis=0, keepdims=True)
        key_size = jnp.max(jnp.sum(key.astype(f32) ** 2, axis=-1, keepdims=True), axis=0, keepdims=True)
        q_out[head] = (query.astype(f32) + q_mask).astype(bf16)
        k_out[head] = (key.astype(f32) + k_mask).astype(bf16)
        v_out[head] = (columns(2) + v_mask).astype(bf16)
        size[head : head + 1, :] = jnp.maximum(size[head : head + 1, :], query_size)
        size[head + 8 : head + 9, :] = jnp.maximum(size[head + 8 : head + 9, :], key_size)


def project(frames, mixed, convp, wqkv, bqkv, block=784):
    rows = mixed.shape[0]
    heads_spec = pl.BlockSpec((HEADS, block, LANES), lambda i: (0, i, 0))
    rows_spec = pl.BlockSpec((block, DIM), lambda i: (i, 0))
    heads_shape = jax.ShapeDtypeStruct((HEADS, rows, LANES), bf16)
    return pl.pallas_call(
        qkv_kernel,
        name="qkv_forward",
        grid=(rows // block,),
        in_specs=[
            SMEM_SPEC,
            rows_spec,
            pl.BlockSpec((32, DIM), lambda i: (0, 0)),
            pl.BlockSpec((DIM, 3 * WIDE_HEADS), lambda i: (0, 0)),
            pl.BlockSpec((1, 3 * WIDE_HEADS), lambda i: (0, 0)),
        ],
        out_specs=[rows_spec, heads_spec, heads_spec, heads_spec, pl.BlockSpec((16, LANES), lambda i: (0, 0))],
        out_shape=[
            jax.ShapeDtypeStruct((rows, DIM), bf16),
            heads_shape,
            heads_shape,
            heads_shape,
            jax.ShapeDtypeStruct((16, LANES), f32),
        ],
        compiler_params=params(),
    )(frames, mixed, convp, wqkv, bqkv)


def attend_kernel(chunk, q, k, v, size, o_out, q_back, query, shift):
    head = pl.program_id(0)
    keys = k.shape[1]
    tall = q.shape[1]
    bound = jnp.max(size[pl.ds(head, 1), :] * size[pl.ds(head + 8, 1), :])
    query[...] = q[0]
    shift[...] = jnp.zeros(shift.shape, f32)

    @pl.when(bound > SAFE_BOUND * SAFE_BOUND)
    def _():
        shift[...] = jnp.full(shift.shape, -jnp.inf, f32)

        def peak(step, carry):
            scores = dot_nt(k[0, pl.ds(pl.multiple_of(step * 112, 16), 112), :], q[0])
            shift[...] = jnp.maximum(shift[...], jnp.max(scores, axis=0, keepdims=True))
            return carry

        lax.fori_loop(0, keys // 112, peak, 0)
        first, second, third = split3(-shift[...])
        row = row_of((LANES, tall))
        tail = jnp.where(row == 66, first, jnp.where(row == 67, second, jnp.where(row == 68, third, 0.0)))
        query[...] = (q[0].astype(f32) + tail.T).astype(bf16)

    total = None
    for start in range(0, keys, chunk):
        place = slice(start, min(start + chunk, keys))
        weights = jnp.exp2(dot_nt(k[0, place, :], query[...])).astype(bf16)
        part = dot_tn(v[0, place, :], weights)
        total = part if total is None else total + part
    sums = total[64:65, :]
    first, second, third = split3(-(shift[...] + jnp.log2(sums)))
    row = row_of((8, tall))
    tail = jnp.where(row == 2, first, jnp.where(row == 3, second, jnp.where(row == 4, third, 0.0)))
    stacked = jnp.concatenate([total[:64, :] / sums, tail, jnp.zeros((56, tall), f32)], axis=0).T
    lane = lane_of((tall, LANES))
    o_out[0] = jnp.where(lane < 64, stacked, 0.0).astype(bf16)
    q_back[0] = jnp.where((lane >= 66) & (lane < 69), stacked, q[0].astype(f32)).astype(bf16)


def attend(q, k, v, size, chunk=512):
    rows = q.shape[1]
    whole = pl.BlockSpec((1, rows, LANES), lambda h: (h, 0, 0))
    shape = jax.ShapeDtypeStruct((HEADS, rows, LANES), bf16)
    return pl.pallas_call(
        functools.partial(attend_kernel, chunk),
        name="attend",
        grid=(HEADS,),
        in_specs=[whole, whole, whole, pl.BlockSpec((16, LANES), lambda h: (0, 0))],
        out_specs=[whole, whole],
        out_shape=[shape, shape],
        scratch_shapes=[pltpu.VMEM((rows, LANES), bf16), pltpu.VMEM((1, rows), f32)],
        compiler_params=params(),
    )(q, k, v, size)


def attend_back_kernel(rows, q, do, k, v, dq_out, dk_out, dv_out, dq):
    step = pl.program_id(1)
    wide = k.shape[1]
    inside = row_of((wide, LANES)) + step * wide < rows
    key = jnp.where(inside, k[0], jnp.zeros((), bf16))
    value = jnp.where(inside, v[0], jnp.zeros((), bf16))
    weights = jnp.exp2(dot_nt(q[0], key))
    grad_scores = (weights * dot_nt(do[0], value)).astype(bf16)
    weights = weights.astype(bf16)
    dv_out[0] = dot_tn(do[0], weights).T.astype(bf16)
    dk_out[0] = (dot_tn(q[0], grad_scores) * LN2).T.astype(bf16)
    part = dot(grad_scores, key)

    @pl.when(step == 0)
    def _():
        dq[...] = part

    @pl.when(step > 0)
    def _():
        dq[...] += part

    @pl.when(step == pl.num_programs(1) - 1)
    def _():
        dq_out[0] = (dq[...] * HEAD_DIM ** (-0.5)).astype(bf16)


def attend_back(q, do, k, v, wide=1280):
    heads, rows = q.shape[:2]
    block = pl.BlockSpec((1, wide, LANES), lambda h, i: (h, i, 0))
    whole = pl.BlockSpec((1, rows, LANES), lambda h, i: (h, 0, 0))
    shape = jax.ShapeDtypeStruct((heads, rows, LANES), bf16)
    return pl.pallas_call(
        functools.partial(attend_back_kernel, rows),
        name="attend_back",
        grid=(heads, pl.cdiv(rows, wide)),
        in_specs=[whole, whole, block, block],
        out_specs=[whole, block, block],
        out_shape=[shape, shape, shape],
        scratch_shapes=[pltpu.VMEM((rows, LANES), f32)],
        compiler_params=params(),
    )(q, do, k, v)


def erf_parts(value):
    bell = jnp.exp(-0.5 * value * value)
    return bell, 0.5 * (1.0 + lax.erf(value * (1.0 / math.sqrt(2.0))))


def add_tiles(ref, place, value):
    for tile, (low, high) in enumerate(TILES):
        ref[tile, place, : high - low] += value[:, low:high]


def middle_kernel(
    frames_ref, o, mixed, cot, wproj, fc1, fc2, vecs, fc1b,
    output, gmid_out, do_out, gproj, gfc1, gfc2, gvec, gfc1b, chunk,
):
    block = pl.program_id(0)
    rows = mixed.shape[0]
    inside = row_of((rows, DIM)) + block * rows < frames_ref[0] * FRAME

    @pl.when(block == 0)
    def _():
        for ref in (gproj, gfc1, gfc2, gvec, gfc1b):
            ref[...] = jnp.zeros(ref.shape, f32)

    attended = jnp.concatenate([o[head] for head in range(HEADS)], axis=1)
    middle = mixed[...] + (dot(attended, wproj[...]) + vecs[0:1, :])
    normal, inverse = normalize(middle)
    normed = (normal * vecs[1:2, :] + vecs[2:3, :]).astype(bf16)
    grad_output = jnp.where(inside, cot[...].astype(f32), 0.0)
    grad_outer = grad_output.astype(bf16)
    total = middle + vecs[3:4, :]
    grad_normed = jnp.zeros((rows, DIM), f32)
    for start in range(0, FFN, chunk):
        place = slice(start, start + chunk)
        inner = dot(normed, fc1[:, place]) + fc1b[:, place]
        bell, gate = erf_parts(inner)
        activated = (inner * gate).astype(bf16)
        total += dot(activated, fc2[place, :])
        slope = gate + inner * bell * INVERSE_ROOT_TWO_PI
        grad_inner = (dot_nt(grad_outer, fc2[place, :]) * slope)
        gfc1b[:, place] += jnp.sum(grad_inner, axis=0, keepdims=True)
        grad_inner = grad_inner.astype(bf16)
        add_tiles(gfc2, place, dot_tn(activated, grad_outer))
        gfc1[:, place] += dot_tn(normed, grad_inner)
        grad_normed += dot_nt(grad_inner, fc1[:, place])
    output[...] = total.astype(bf16)
    scaled = grad_normed * vecs[1:2, :]
    grad_middle = grad_output + inverse * (
        scaled
        - jnp.mean(scaled, axis=-1, keepdims=True)
        - normal * jnp.mean(scaled * normal, axis=-1, keepdims=True)
    )
    gmid_out[...] = grad_middle
    grad_branch = grad_middle.astype(bf16)
    add_tiles(gproj, slice(None), dot_tn(attended, grad_branch))
    gvec[0:1, :] += jnp.sum(grad_branch.astype(f32), axis=0, keepdims=True)
    gvec[1:2, :] += jnp.sum(grad_normed * normal, axis=0, keepdims=True)
    gvec[2:3, :] += jnp.sum(grad_normed, axis=0, keepdims=True)
    gvec[3:4, :] += jnp.sum(grad_output, axis=0, keepdims=True)
    lane = lane_of((rows, LANES))
    for head in range(HEADS):
        grad_head = dot_nt(grad_branch, wproj[head * LANES : (head + 1) * LANES, :])
        delta = jnp.sum(grad_head * o[head].astype(f32), axis=-1, keepdims=True)
        first, second, third = split3(-delta)
        tail = jnp.where(lane == 64, first, jnp.where(lane == 65, second, third))
        do_out[head] = jnp.where((lane >= 64) & (lane < 67), tail, grad_head).astype(bf16)


def feed_forward(frames, o, mixed, cot, wproj, fc1, fc2, vecs, fc1b, block=784, chunk=256):
    rows = mixed.shape[0]
    heads_spec = pl.BlockSpec((HEADS, block, LANES), lambda i: (0, i, 0))
    rows_spec = pl.BlockSpec((block, DIM), lambda i: (i, 0))

    def full(*shape):
        return pl.BlockSpec(shape, lambda i: (0,) * len(shape))

    return pl.pallas_call(
        functools.partial(middle_kernel, chunk=chunk),
        name="feed_forward",
        grid=(rows // block,),
        in_specs=[
            SMEM_SPEC, heads_spec, rows_spec, rows_spec,
            full(WIDE_HEADS, DIM), full(DIM, FFN), full(FFN, DIM), full(8, DIM), full(1, FFN),
        ],
        out_specs=[
            rows_spec, rows_spec, heads_spec,
            full(3, WIDE_HEADS, LANES), full(DIM, FFN), full(3, FFN, LANES), full(8, DIM), full(1, FFN),
        ],
        out_shape=[
            jax.ShapeDtypeStruct((rows, DIM), bf16),
            jax.ShapeDtypeStruct((rows, DIM), f32),
            jax.ShapeDtypeStruct((HEADS, rows, LANES), bf16),
            jax.ShapeDtypeStruct((3, WIDE_HEADS, LANES), f32),
            jax.ShapeDtypeStruct((DIM, FFN), f32),
            jax.ShapeDtypeStruct((3, FFN, LANES), f32),
            jax.ShapeDtypeStruct((8, DIM), f32),
            jax.ShapeDtypeStruct((1, FFN), f32),
        ],
        compiler_params=params(),
    )(frames, o, mixed, cot, wproj, fc1, fc2, vecs, fc1b)


def qkv_back_kernel(dq, dk, dv, normed, mixed, gmid, wqkv, convp, gmix_out, gqkv, gbias, gvec):
    block = pl.program_id(0)

    @pl.when(block == 0)
    def _():
        for ref in (gqkv, gbias, gvec):
            ref[...] = jnp.zeros(ref.shape, f32)

    normal, inverse = normalize(mixed[...])
    grads = jnp.concatenate([part[head] for part in (dq, dk, dv) for head in range(HEADS)], axis=1)
    grad_qkv = dot_tn(normed[...], grads)
    for tile in range(15):
        gqkv[tile] += grad_qkv[:, tile * LANES : (tile + 1) * LANES]
    gbias[...] += jnp.sum(grads.astype(f32), axis=0, keepdims=True)
    grad_normed = dot_nt(grads, wqkv[...])
    gvec[1:2, :] += jnp.sum(grad_normed * normal, axis=0, keepdims=True)
    gvec[2:3, :] += jnp.sum(grad_normed, axis=0, keepdims=True)
    scaled = grad_normed * convp[28:29, :]
    grad_mixed = gmid[...] + inverse * (
        scaled
        - jnp.mean(scaled, axis=-1, keepdims=True)
        - normal * jnp.mean(scaled * normal, axis=-1, keepdims=True)
    )
    gvec[0:1, :] += jnp.sum(grad_mixed, axis=0, keepdims=True)
    gmix_out[...] = grad_mixed


def project_back(dq, dk, dv, normed, mixed, gmid, wqkv, convp, block=784):
    rows = mixed.shape[0]
    heads_spec = pl.BlockSpec((HEADS, block, LANES), lambda i: (0, i, 0))
    rows_spec = pl.BlockSpec((block, DIM), lambda i: (i, 0))

    def full(*shape):
        return pl.BlockSpec(shape, lambda i: (0,) * len(shape))

    return pl.pallas_call(
        qkv_back_kernel,
        name="qkv_back",
        grid=(rows // block,),
        in_specs=[heads_spec, heads_spec, heads_spec, rows_spec, rows_spec, rows_spec,
                  full(DIM, 3 * WIDE_HEADS), full(32, DIM)],
        out_specs=[rows_spec, full(15, DIM, LANES), full(1, 3 * WIDE_HEADS), full(8, DIM)],
        out_shape=[
            jax.ShapeDtypeStruct((rows, DIM), f32),
            jax.ShapeDtypeStruct((15, DIM, LANES), f32),
            jax.ShapeDtypeStruct((1, 3 * WIDE_HEADS), f32),
            jax.ShapeDtypeStruct((8, DIM), f32),
        ],
        compiler_params=params(),
    )(dq, dk, dv, normed, mixed, gmid, wqkv, convp)


def conv_weight_kernel(frames_ref, tokens, gmix, gvec, spread, out, xpad, gpad, sums, tiles, flat):
    frames = frames_ref[0]
    pad_frames(xpad, spread, tokens, frames, -1, 14, True, (0,))
    pad_frames(gpad, spread, gmix, frames, 0, 12, False, (-1, 0, 1))
    sums[...] = jnp.zeros(sums.shape, f32)

    def weight_frame(frame, carry):
        for low, high in TILES:
            for c in (-1, 0, 1):
                body = gpad[c + 1, frame, 16 : 16 + BODY, low:high]
                for a in (-1, 0, 1):
                    for b in (-1, 0, 1):
                        tap = 9 * (a + 1) + 3 * (b + 1) + (c + 1)
                        begin = 16 + b * 16
                        cells = xpad[0, frame + 1 + a, begin : begin + BODY, low:high]
                        product = (body * cells).reshape(BODY // 8, 8, high - low)
                        sums[tap, :, low:high] += jnp.sum(product, axis=0)
        return carry

    lax.fori_loop(0, frames, weight_frame, 0)
    tiles[...] = jnp.zeros(tiles.shape, f32)
    flat[...] = jnp.zeros(flat.shape, f32)
    for tile, (low, high) in enumerate(TILES):
        tiles[tile, 0:27, : high - low] = jnp.sum(sums[:, :, low:high], axis=1)
        tiles[tile, 27:30, : high - low] = gvec[0:3, low:high]
    for parity in range(2):
        for j in range(5):
            value = tiles[j // 2, pl.ds(parity, 15, stride=2), :]
            put_half(flat, AT_CONV + parity * 5 + j, value, j % 2, 5, 15)
    out[...] = flat[...].astype(bf16)


def conv_weight_grads(frames, tokens, gmix, gvec, spread):
    return pl.pallas_call(
        conv_weight_kernel,
        name="conv_weight_grads",
        in_specs=[SMEM_SPEC] + [VMEM_SPEC] * 4,
        out_shape=jax.ShapeDtypeStruct((80, LANES), bf16),
        scratch_shapes=[
            pltpu.VMEM((1, 14, PAD_ROWS, DIM), f32),
            pltpu.VMEM((3, 12, PAD_ROWS, DIM), f32),
            pltpu.VMEM((27, 8, DIM), f32),
            pltpu.VMEM((3, 32, LANES), f32),
            pltpu.VMEM((80, LANES), f32),
        ],
        compiler_params=params(),
    )(frames, tokens, gmix, gvec, spread)


def token_piece_kernel(piece, frames_ref, gmix, convp, spread, back, *refs):
    if piece > 0:
        refs = refs[1:]
    gtok, gpad, comp, rows = refs
    frames = frames_ref[0]
    pad_frames(gpad, spread, gmix, frames, 4 * piece - 1, 6, False, (-1, 0, 1))
    rows[...] = jnp.zeros(rows.shape, f32)

    def each(member, carry):
        @pl.when(4 * piece + member < frames)
        def _():
            for low, high in TILES:
                own = gpad[1, member + 1, 16 : 16 + BODY, low:high]
                comp[:, low:high] = own + mix_frame(gpad, convp, member + 1, -1, low, high)
            place = pl.ds(pl.multiple_of(192 * member, 16), 208)
            rows[place, :] += dot(back[member], comp[...].astype(bf16))

        return carry

    lax.fori_loop(0, 4, each, 0)
    gtok[...] = rows[...].astype(bf16)


def token_piece(piece, frames, gmix, convp, spread, back, gtok):
    rows = gmix.shape[0]
    operands = [frames, gmix, convp, spread, back] + ([] if piece == 0 else [gtok])
    return pl.pallas_call(
        functools.partial(token_piece_kernel, piece),
        name=f"token_piece{piece}",
        grid=(1,),
        in_specs=[SMEM_SPEC] + [VMEM_SPEC] * 4 + [ANY_SPEC] * (piece > 0),
        out_specs=pl.BlockSpec((PIECE, DIM), lambda i: (piece, 0)),
        out_shape=jax.ShapeDtypeStruct((rows, DIM), bf16),
        input_output_aliases={5: 0} if piece else {},
        scratch_shapes=[
            pltpu.VMEM((3, 6, PAD_ROWS, DIM), f32),
            pltpu.VMEM((BODY, DIM), f32),
            pltpu.VMEM((PIECE, DIM), f32),
        ],
        compiler_params=params(),
    )(*operands)


def put_half(flat, index, value, side, step=1, count=1):
    row, wanted = divmod(index, 2)
    place = pl.ds(row, count, stride=step) if step > 1 else pl.ds(row, count)
    lane = lane_of(value.shape)
    if wanted == 0:
        flat[place, :] += jnp.where(lane < 64, low_half(value, side), 0.0)
    else:
        flat[place, :] += jnp.where(lane >= 64, high_half(value, side), 0.0)


def put_vector(flat, index, value):
    width = value.shape[1]
    for j in range(width // 64):
        low = (j // 2) * LANES
        part = value[:, low : min(low + LANES, width)]
        if part.shape[1] < LANES:
            part = jnp.concatenate([part, jnp.zeros((1, 64), f32)], axis=1)
        put_half(flat, index + j, part, j % 2)


PACK_BASE = 2432


def pack_main_kernel(gproj, gfc1, gfc2, gvec, gfc1b, out, flat):
    flat[...] = jnp.zeros(flat.shape, f32)
    for parity in range(2):
        for j in range(5):
            for head in range(HEADS):
                value = gproj[j // 2, pl.ds(head * LANES + parity, 32, stride=2), :]
                put_half(flat, AT_PROJ + (64 * head + parity) * 5 + j, value, j % 2, 5, 32)
            value = gfc2[j // 2, pl.ds(parity, FFN // 2, stride=2), :]
            put_half(flat, AT_FC2 + parity * 5 + j, value, j % 2, 5, FFN // 2)
    for j in range(20):
        value = gfc1[:, (j // 2) * LANES : (j // 2 + 1) * LANES]
        put_half(flat, AT_FC1 + j, value, j % 2, 10, DIM)
    for row in range(3):
        put_vector(flat, AT_VEC + 5 * row, gvec[row : row + 1, :])
    put_vector(flat, AT_FC2B, gvec[3:4, :])
    put_vector(flat, AT_FC1B, gfc1b[...])
    out[...] = flat[...].astype(bf16)


def pack_main(gproj, gfc1, gfc2, gvec, gfc1b, rows):
    return pl.pallas_call(
        pack_main_kernel,
        name="pack_main",
        out_shape=jax.ShapeDtypeStruct((rows, LANES), bf16),
        scratch_shapes=[pltpu.VMEM((rows, LANES), f32)],
        compiler_params=params(),
    )(gproj, gfc1, gfc2, gvec, gfc1b)


QKV_ROWS = 2480


def pack_qkv_kernel(gqkv, gbias, out, end, flat):
    flat[...] = jnp.zeros(flat.shape, f32)
    for parity in range(2):
        for j in range(15):
            value = gqkv[j, pl.ds(parity, DIM // 2, stride=2), :]
            put_half(flat, AT_QKV + parity * 15 + j, value, 0, 15, DIM // 2)
    for j in range(10):
        tile = j if j < 5 else j + 5
        put_half(flat, AT_QV + j, gbias[:, tile * LANES : (tile + 1) * LANES], 0)
    out[...] = flat[:PACK_BASE, :].astype(bf16)
    end[...] = flat[PACK_BASE:, :].astype(bf16)


def pack_qkv(gqkv, gbias):
    return pl.pallas_call(
        pack_qkv_kernel,
        name="pack_qkv",
        out_shape=[
            jax.ShapeDtypeStruct((PACK_BASE, LANES), bf16),
            jax.ShapeDtypeStruct((QKV_ROWS - PACK_BASE, LANES), bf16),
        ],
        scratch_shapes=[pltpu.VMEM((QKV_ROWS, LANES), f32)],
        compiler_params=params(),
    )(gqkv, gbias)


AXES = ("wide", "narrow")


def exchange(value, bit):
    count = lax.axis_size(AXES)
    return lax.ppermute(value, AXES, [(i, i ^ (1 << bit)) for i in range(count)])


def my_bit(bit):
    return (lax.axis_index(AXES) >> bit) & 1


def tie(*values):
    return lax.optimization_barrier(values)


def halve(value, bits):
    for bit in range(bits):
        value = value.reshape(value.shape[0] // 2, 2, -1, LANES)
        mine = my_bit(bit)
        keep = lax.dynamic_index_in_dim(value, mine, 1, keepdims=False)
        give = lax.dynamic_index_in_dim(value, 1 - mine, 1, keepdims=False)
        value = keep + exchange(give, bit)
    return value[0]


def on_device(master, momentum, average, tokens, clip_ids, borders, cotangent):
    wide_count, narrow_count = lax.axis_size("wide"), lax.axis_size("narrow")
    count = wide_count * narrow_count
    bits = count.bit_length() - 1
    own_rows = master.shape[0]
    frames = (jnp.sum((clip_ids >= 0).astype(jnp.int32)) // FRAME).reshape(1)
    me = lax.axis_index(AXES)
    quarter = me >> (bits - 2)
    blocks = master.astype(bf16)[None]
    other = exchange(blocks, bits - 2)
    tokens = turn(tokens.T)
    other, tokens = tie(other, tokens)
    blocks = jnp.concatenate([blocks, other], axis=0)
    other, cotangent, tokens = tie(exchange(blocks, bits - 1), turn(tie(blocks, cotangent.T)[1]), tokens)
    spread, back = tables()
    blocks = jnp.concatenate([blocks, other], axis=0)
    first = lax.dynamic_index_in_dim(blocks, quarter, 0)
    rest = [lax.dynamic_index_in_dim(blocks, quarter ^ index, 0) for index in (1, 2, 3)]
    rest = jnp.concatenate(rest, axis=0)[None]
    low_bits = list(range(bits - 3, -1, -1))
    for step, bit in enumerate(low_bits):
        first = jnp.concatenate([first, exchange(first, bit)], axis=0)
        if step == 0:
            first, rest, frames, spread, back = tie(first, rest, frames, spread, back)
            rest = jnp.concatenate([rest, exchange(rest, bit)], axis=0)
    order = [0] * (count // 4)
    for step, bit in enumerate(low_bits):
        order = [place | (((index >> bit) & 1) << step) for index, place in enumerate(order)]
    mine = sum((((me >> bit) & 1) << step) for step, bit in enumerate(low_bits))
    order = jnp.array(order, jnp.int32) ^ mine
    head = lax.dynamic_index_in_dim(first, mine, 0, keepdims=False)
    head = jnp.concatenate([head, jnp.zeros((4, LANES), bf16)], axis=0)[:80] if own_rows < 80 else head[:80]
    mixed, convp = None, None
    for step, bit in enumerate(low_bits[1:]):
        if step < 2:
            rest, head = tie(rest, head)
        other = exchange(rest, bit)
        if step == 0:
            mixed, convp = conv_piece(0, frames, tokens, head, spread, back, None)
            other, mixed = tie(other, mixed)
        elif step == 1:
            mixed, convp = conv_piece(1, frames, tokens, head, spread, back, mixed)
            mixed, convp = conv_piece(2, frames, tokens, head, spread, back, mixed)
            other, mixed = tie(other, mixed)
        rest = jnp.concatenate([rest, other], axis=0)
    wqkv, wproj, fc1, fc2, bqkv, vecs, fc1b = unpack(order, first, rest)
    normed, q, k, v, size = project(frames, mixed, convp, wqkv, bqkv)
    o, q_back = attend(q, k, v, size)
    output, gmid, do, gproj, gfc1, gfc2, gvec, gfc1b = feed_forward(
        frames, o, mixed, cotangent, wproj, fc1, fc2, vecs, fc1b
    )
    main = pack_main(gproj, gfc1, gfc2, gvec, gfc1b, count * own_rows)
    main = main.reshape(wide_count, narrow_count, own_rows, LANES)
    main = lax.psum_scatter(main, "wide", scatter_dimension=0, tiled=True)[0]
    dq, dk, dv = attend_back(q_back, do, k, v)
    gmix, gqkv, gbias, gvec_one = project_back(dq, dk, dv, normed, mixed, gmid, wqkv, convp)
    qkv, qkv_end = pack_qkv(gqkv, gbias)
    qkv = halve(qkv.reshape(count // 4, own_rows, LANES), bits - 2)
    for bit in (bits - 2, bits - 1):
        qkv = qkv + exchange(qkv, bit)
    conv = conv_weight_grads(frames, tokens, gmix, gvec_one, spread)
    late = jnp.concatenate([conv, qkv_end], axis=0)
    main, late = tie(main, late)
    main = halve(main, narrow_count.bit_length() - 1)
    gtok = None
    for bit in range(bits):
        if bit < 3:
            late, gmix = tie(late, gmix)
        elif bit == 3:
            late, output = tie(late, output)
        elif bit == 4:
            late, gtok = tie(late, gtok)
        other = exchange(late, bit)
        if bit < 3:
            gtok = token_piece(bit, frames, gmix, convp, spread, back, gtok)
            other, gtok = tie(other, gtok)
        elif bit == 3:
            other, output = tie(other, turn(output))
        elif bit == 4:
            other, gtok = tie(other, turn(gtok))
        late = late + other
    early = jnp.where(me < count // 4, qkv.astype(f32), main.astype(f32))
    conv, qkv_end = late[:80].astype(f32), late[80:].astype(f32)
    if own_rows < 80:
        conv = conv[:own_rows]
    conv = jnp.pad(conv, ((0, own_rows - conv.shape[0]), (0, 0)))
    qkv_end = jnp.pad(qkv_end, ((0, own_rows - qkv_end.shape[0]), (0, 0)))
    owned = early + jnp.where(me == 0, conv, jnp.where(me == count // 4, qkv_end, 0.0))
    rate = RATE_FACTOR / math.sqrt(tokens.shape[0] * count)
    decayed = owned + DECAY_RATE * master
    new_momentum = MOMENTUM * momentum + decayed
    new_master = master - rate * (decayed + MOMENTUM * new_momentum)
    new_average = AVERAGE_KEEP * average + (1.0 - AVERAGE_KEEP) * new_master
    return (output.T, gtok.T, owned, new_master, new_momentum, new_average, new_master.astype(bf16))


def solution(mesh):
    rows = P(("wide", "narrow"), None)
    return jax.shard_map(
        on_device,
        mesh=mesh,
        in_specs=(rows, rows, rows, rows, P(("wide", "narrow")), P(("wide", "narrow")), rows),
        out_specs=(rows,) * 7,
        check_vma=False,
    )
```

```python
import functools
import math

import jax
import jax.numpy as jnp
from jax import lax
from jax.experimental import pallas as pl
from jax.experimental.pallas import tpu as pltpu
from jax.sharding import PartitionSpec as P

HEADS = 5
HEAD_DIM = 64
DIM = 320
FFN = 1280
SIDE = 14
FRAME = SIDE * SIDE
LANES = 128
WIDE_HEADS = HEADS * LANES

EPSILON = 1e-06
MOMENTUM = 0.9
DECAY_RATE = 0.0001
AVERAGE_KEEP = 0.8
RATE_FACTOR = 0.03
LOG2E = 1.0 / math.log(2.0)
LN2 = math.log(2.0)
INVERSE_ROOT_TWO_PI = 1.0 / math.sqrt(2.0 * math.pi)
BLOCKED = -(2.0**30)
SAFE_BOUND = 80.0

bf16 = jnp.bfloat16
f32 = jnp.float32

AT_CONV = 0
AT_QKV = 150
AT_QV = 4950
AT_PROJ = 4960
AT_VEC = 6560
AT_FC1 = 6575
AT_FC1B = 12975
AT_FC2 = 12995
AT_FC2B = 19395
HALF_END = 19400


SMEM_SPEC = pl.BlockSpec(memory_space=pltpu.SMEM)
VMEM_SPEC = pl.BlockSpec(memory_space=pltpu.VMEM)
ANY_SPEC = pl.BlockSpec(memory_space=pl.ANY)


def dot(a, b):
    return lax.dot_general(a, b, (((1,), (0,)), ((), ())), preferred_element_type=f32)


def dot_nt(a, b):
    return lax.dot_general(a, b, (((1,), (1,)), ((), ())), preferred_element_type=f32)


def dot_tn(a, b):
    return lax.dot_general(a, b, (((0,), (0,)), ((), ())), preferred_element_type=f32)


def params(limit=58):
    return pltpu.CompilerParams(vmem_limit_bytes=limit << 20)


def lane_of(shape):
    return lax.broadcasted_iota(jnp.int32, shape, len(shape) - 1)


def row_of(shape):
    return lax.broadcasted_iota(jnp.int32, shape, 0)


def low_half(value, side):
    return value if side == 0 else pltpu.roll(value, 64, axis=1)


def high_half(value, side):
    return value if side == 1 else pltpu.roll(value, 64, axis=1)


def split3(value):
    first = value.astype(bf16).astype(f32)
    rest = value - first
    second = rest.astype(bf16).astype(f32)
    return first, second, rest - second


def read_half(flat, at, length, step, count, parity, j):
    index = at + parity * length + j
    return flat[pl.ds(index // 2, count, stride=step), :], index % 2


def read_vector(flat, at, length):
    tiles = []
    lane = lane_of((1, LANES))
    for j in range(0, length, 2):
        row, side = divmod(at + j, 2)
        low = low_half(flat[row : row + 1, :], side)
        if j + 1 < length:
            row, side = divmod(at + j + 1, 2)
            tiles.append(jnp.where(lane < 64, low, high_half(flat[row : row + 1, :], side)))
        else:
            tiles.append(low[:, :64])
    return jnp.concatenate(tiles, axis=1)


def odd_matrix(flat, out, at, length, rows):
    pairs = rows // 2
    for parity in range(2):
        for tile in range((length + 1) // 2):
            low, side = read_half(flat, at, length, length, pairs, parity, 2 * tile)
            low = low_half(low, side)
            place = pl.ds(parity, pairs, stride=2)
            if 2 * tile + 1 < length:
                high, side = read_half(flat, at, length, length, pairs, parity, 2 * tile + 1)
                merged = jnp.where(lane_of(low.shape) < 64, low, high_half(high, side))
            else:
                merged = low
            out[tile, place, :] = merged


def unpack_kernel(order, first, rest, wqkv, wproj, fc1, fc2, bqkv, vecs, fc1b, flat, wide, tall):
    blocks, rows = first.shape[:2]
    for block in range(blocks):
        place = order[block]
        for quarter in range(4):
            start = (quarter * blocks + block) * rows
            value = first[place] if quarter == 0 else rest[place, quarter - 1]
            flat[start : start + rows, :] = value.astype(f32)
    for parity in range(2):
        for j in range(15):
            value, side = read_half(flat, AT_QKV, 15, 15, 160, parity, j)
            value = jnp.where(lane_of(value.shape) < 64, low_half(value, side), 0.0)
            wide[j, pl.ds(parity, 160, stride=2), :] = value
    for j in range(15):
        wqkv[:, j * LANES : (j + 1) * LANES] = wide[j].astype(bf16)
    lane = lane_of((1, LANES))
    for j in range(15):
        if 5 <= j < 10:
            bqkv[:, j * LANES : (j + 1) * LANES] = jnp.zeros((1, LANES), f32)
        else:
            row, side = divmod(AT_QV + (j if j < 5 else j - 5), 2)
            value = low_half(flat[row : row + 1, :], side)
            bqkv[:, j * LANES : (j + 1) * LANES] = jnp.where(lane < 64, value, 0.0)
    odd_matrix(flat, wide, AT_PROJ, 5, DIM)
    for head in range(HEADS):
        for tile in range(3):
            width = LANES if tile < 2 else 64
            columns = slice(tile * LANES, tile * LANES + width)
            part = wide[tile, head * 64 : head * 64 + 64, :width].astype(bf16)
            wproj[head * LANES : head * LANES + 64, columns] = part
        wproj[head * LANES + 64 : (head + 1) * LANES, :] = jnp.zeros((64, DIM), bf16)
    for row in range(3):
        vecs[row : row + 1, :] = read_vector(flat, AT_VEC + 5 * row, 5)
    vecs[3:4, :] = read_vector(flat, AT_FC2B, 5)
    vecs[4:8, :] = jnp.zeros((4, DIM), f32)
    fc1b[...] = read_vector(flat, AT_FC1B, 20)
    for tile in range(10):
        low, side = read_half(flat, AT_FC1, 20, 10, DIM, 0, 2 * tile)
        high, side_high = read_half(flat, AT_FC1, 20, 10, DIM, 0, 2 * tile + 1)
        merged = jnp.where(lane_of(low.shape) < 64, low_half(low, side), high_half(high, side_high))
        fc1[:, tile * LANES : (tile + 1) * LANES] = merged.astype(bf16)
    odd_matrix(flat, tall, AT_FC2, 5, FFN)
    for tile in range(3):
        width = LANES if tile < 2 else 64
        fc2[:, tile * LANES : tile * LANES + width] = tall[tile, :, :width].astype(bf16)


def unpack(order, first, rest):
    rows = 4 * first.shape[0] * first.shape[1]
    return pl.pallas_call(
        unpack_kernel,
        name="unpack",
        in_specs=[SMEM_SPEC, VMEM_SPEC, VMEM_SPEC],
        out_shape=[
            jax.ShapeDtypeStruct((DIM, 3 * WIDE_HEADS), bf16),
            jax.ShapeDtypeStruct((WIDE_HEADS, DIM), bf16),
            jax.ShapeDtypeStruct((DIM, FFN), bf16),
            jax.ShapeDtypeStruct((FFN, DIM), bf16),
            jax.ShapeDtypeStruct((1, 3 * WIDE_HEADS), f32),
            jax.ShapeDtypeStruct((8, DIM), f32),
            jax.ShapeDtypeStruct((1, FFN), f32),
        ],
        scratch_shapes=[
            pltpu.VMEM((rows, LANES), f32),
            pltpu.VMEM((15, DIM, LANES), f32),
            pltpu.VMEM((3, FFN, LANES), f32),
        ],
        compiler_params=params(),
    )(order, first, rest)


PAD_ROWS = 16 * 16
BODY = SIDE * 16


def spread_matrix(shift):
    cell = lax.broadcasted_iota(jnp.int32, (PAD_ROWS, 208), 0)
    source = lax.broadcasted_iota(jnp.int32, (PAD_ROWS, 208), 1)
    row, column = cell >> 4, cell & 15
    inside = (row >= 1) & (row <= SIDE) & (column < SIDE)
    wanted = (row - 1) * SIDE + column + shift
    return jnp.where(inside & (source == wanted), 1.0, 0.0).astype(bf16)


def gather_matrix(shift):
    target = lax.broadcasted_iota(jnp.int32, (208, BODY), 0)
    cell = lax.broadcasted_iota(jnp.int32, (208, BODY), 1)
    row, column = cell >> 4, cell & 15
    wanted = row * SIDE + column + shift
    return jnp.where((column < SIDE) & (target == wanted), 1.0, 0.0).astype(bf16)


TILES = ((0, 128), (128, 256), (256, 320))


def pieces(value):
    first = value.astype(bf16)
    return first, (value - first.astype(f32)).astype(bf16)


def prepare_kernel(turned, padded, spread, back, tokens):
    for member in range(4):
        spread[member] = spread_matrix(4 * member)
        back[member] = gather_matrix(4 * member)
    tokens[...] = turned[...].T

    def fill(frame, carry):
        member = frame & 3
        place = pl.ds(pl.multiple_of(frame * FRAME - 4 * member, 16), 208)
        padded[frame] = dot(spread[member], tokens[place, :])
        return carry

    lax.fori_loop(0, padded.shape[0], fill, 0)


def prepare(turned):
    rows = turned.shape[1]
    return pl.pallas_call(
        prepare_kernel,
        name="prepare",
        in_specs=[VMEM_SPEC],
        out_shape=[
            jax.ShapeDtypeStruct((rows // FRAME, PAD_ROWS, DIM), f32),
            jax.ShapeDtypeStruct((4, PAD_ROWS, 208), bf16),
            jax.ShapeDtypeStruct((4, 208, BODY), bf16),
        ],
        scratch_shapes=[pltpu.VMEM((rows, DIM), bf16)],
        compiler_params=params(),
    )(turned)


PIECE = 4 * FRAME


def fetch_frames(source, slots, sem, piece):
    first, last = max(4 * piece - 1, 0), min(4 * piece + 5, source.shape[0])
    start = first - (4 * piece - 1)
    return pltpu.make_async_copy(
        source.at[pl.ds(first, last - first)], slots.at[pl.ds(start, last - first)], sem
    )


def mix_frame(slots, at, weights, sums, out, sign):
    for low, high in TILES:
        for start in range(0, BODY, 56):
            parts = [None, None, None]
            for a in (-1, 0, 1):
                for b in (-1, 0, 1):
                    begin = 16 + sign * b * 16 + start
                    cells = slots[at[1 + sign * a], begin : begin + 56, low:high]
                    for c in range(3):
                        tap = 9 * (a + 1) + 3 * (b + 1) + c
                        term = cells * weights[tap : tap + 1, low:high]
                        parts[c] = term if parts[c] is None else parts[c] + term
            parts[1] = parts[1] + slots[at[1], 16 + start : 16 + start + 56, low:high]
            for c in range(3):
                sums[c, start : start + 56, low:high] = parts[c]
    before, after = (0, 2) if sign == 1 else (2, 0)
    for low, high in TILES:
        out[:, low:high] = (
            sums[1, :, low:high]
            + pltpu.roll(sums[before, :, low:high], 1, axis=0)
            + pltpu.roll(sums[after, :, low:high], BODY - 1, axis=0)
        )


def mask_weights(weights, masked, first, middle, last):
    for tap in range(27):
        keep = (first, middle, last)[tap // 9]
        scale = 1.0 if tap == 13 else jnp.where(keep, 1.0, 0.0)
        masked[tap : tap + 1, :] = weights[tap : tap + 1, :] * scale


def conv_params(head, flat, weights):
    flat[...] = head[...].astype(f32)
    for parity in range(2):
        for tile in range(3):
            low, side = read_half(flat, AT_CONV, 5, 5, 15, parity, 2 * tile)
            low = low_half(low, side)
            place = pl.ds(parity, 15, stride=2)
            if tile < 2:
                high, side = read_half(flat, AT_CONV, 5, 5, 15, parity, 2 * tile + 1)
                low = jnp.where(lane_of(low.shape) < 64, low, high_half(high, side))
            weights[tile, place, :] = low


def turn_kernel(source, out):
    out[...] = source[...].T


def turn(value):
    rows, columns = value.shape
    return pl.pallas_call(
        turn_kernel,
        name="turn",
        in_specs=[VMEM_SPEC],
        out_specs=VMEM_SPEC,
        out_shape=jax.ShapeDtypeStruct((columns, rows), value.dtype),
        compiler_params=params(32),
        cost_estimate=pl.CostEstimate(flops=0, bytes_accessed=4 * rows * columns, transcendentals=0),
    )(value)


def conv_piece_kernel(piece, frames_ref, head, padded, back, *refs):
    if piece > 0:
        refs = refs[1:]
    mixed, convp, flat, weights, masked, slots, sums, comp, sem = refs
    copy = fetch_frames(padded, slots, sem, piece)
    copy.start()
    frames = frames_ref[0]
    conv_params(head, flat, weights)
    for tile, (low, high) in enumerate(TILES):
        convp[:, low:high] = weights[tile, :, : high - low]
    mixed[...] = jnp.zeros(mixed.shape, f32)
    copy.wait()

    def each(member, carry):
        frame = 4 * piece + member
        there = frame < frames
        before = there & (frame > 0)
        after = frame + 1 < frames
        mask_weights(convp, masked, before, there, after)
        at = (member + jnp.where(before, 0, 1), member + 1, member + jnp.where(after, 2, 1))
        mix_frame(slots, at, masked, sums, comp, 1)
        high, low = pieces(comp[...] + convp[27:28, :])
        place = pl.ds(pl.multiple_of(192 * member, 16), 208)
        mixed[place, :] += dot(back[member], high) + dot(back[member], low)
        return carry

    lax.fori_loop(0, 4, each, 0)


def conv_piece(piece, frames, head, padded, back, mixed):
    rows = padded.shape[0] * FRAME
    operands = [frames, head, padded, back] + ([] if piece == 0 else [mixed])
    return pl.pallas_call(
        functools.partial(conv_piece_kernel, piece),
        name=f"conv_piece{piece}",
        grid=(1,),
        in_specs=[SMEM_SPEC, VMEM_SPEC, ANY_SPEC, VMEM_SPEC] + [ANY_SPEC] * (piece > 0),
        out_specs=[
            pl.BlockSpec((PIECE, DIM), lambda i: (piece, 0)),
            pl.BlockSpec((32, DIM), lambda i: (0, 0)),
        ],
        out_shape=[jax.ShapeDtypeStruct((rows, DIM), f32), jax.ShapeDtypeStruct((32, DIM), f32)],
        input_output_aliases={4: 0} if piece else {},
        scratch_shapes=[
            pltpu.VMEM(head.shape, f32),
            pltpu.VMEM((3, 32, LANES), f32),
            pltpu.VMEM((32, DIM), f32),
            pltpu.VMEM((6, PAD_ROWS, DIM), f32),
            pltpu.VMEM((3, BODY, DIM), f32),
            pltpu.VMEM((BODY, DIM), f32),
            pltpu.SemaphoreType.DMA(()),
        ],
        compiler_params=params(),
    )(*operands)


def normalize(values):
    centered = values - jnp.mean(values, axis=-1, keepdims=True)
    variance = jnp.mean(centered * centered, axis=-1, keepdims=True)
    inverse = lax.rsqrt(variance + EPSILON)
    return centered * inverse, inverse


def row_size(value):
    part = jnp.where(lane_of(value.shape) < HEAD_DIM, value.astype(f32), 0.0)
    return jnp.sum(part * part, axis=-1, keepdims=True)


def qkv_kernel(frames_ref, mixed, convp, wqkv, bqkv, normed_out, q_out, k_out, v_out, size):
    block = pl.program_id(0)
    rows = mixed.shape[0]
    frames = frames_ref[0]
    normal, unused_inverse = normalize(mixed[...])
    normed = (normal * convp[28:29, :] + convp[29:30, :]).astype(bf16)
    normed_out[...] = normed
    lane = lane_of((rows, LANES))
    inside = row_of((rows, LANES)) + block * rows < frames * FRAME
    q_mask = jnp.where(
        ((lane == 64) & ~inside) | ((lane == 65) & inside), BLOCKED, 0.0
    )
    k_mask = jnp.where(
        ((lane == 64) & inside) | ((lane == 65) & ~inside) | ((lane >= 66) & (lane < 69)), 1.0, 0.0
    )
    v_mask = jnp.where((lane >= 64) & (lane < 67), 1.0, 0.0)
    scale = HEAD_DIM ** (-0.5) * LOG2E

    @pl.when(block == 0)
    def _():
        size[...] = jnp.zeros(size.shape, f32)

    projected = dot(normed, wqkv[...])
    for head in range(HEADS):

        def columns(kind, head=head):
            place = slice((kind * HEADS + head) * LANES, (kind * HEADS + head + 1) * LANES)
            return projected[:, place] + bqkv[:, place]

        query = (columns(0) * scale + q_mask).astype(bf16)
        key = (columns(1) + k_mask).astype(bf16)
        query_size = jnp.max(row_size(query), axis=0, keepdims=True)
        key_size = jnp.max(row_size(key), axis=0, keepdims=True)
        q_out[head] = query
        k_out[head] = key
        v_out[head] = (columns(2) + v_mask).astype(bf16)
        size[head : head + 1, :] = jnp.maximum(size[head : head + 1, :], query_size)
        size[head + 8 : head + 9, :] = jnp.maximum(size[head + 8 : head + 9, :], key_size)


def project(frames, mixed, convp, wqkv, bqkv, block=784):
    rows = mixed.shape[0]
    heads_spec = pl.BlockSpec((HEADS, block, LANES), lambda i: (0, i, 0))
    rows_spec = pl.BlockSpec((block, DIM), lambda i: (i, 0))
    heads_shape = jax.ShapeDtypeStruct((HEADS, rows, LANES), bf16)
    return pl.pallas_call(
        qkv_kernel,
        name="qkv_forward",
        grid=(rows // block,),
        in_specs=[
            SMEM_SPEC,
            rows_spec,
            pl.BlockSpec((32, DIM), lambda i: (0, 0)),
            pl.BlockSpec((DIM, 3 * WIDE_HEADS), lambda i: (0, 0)),
            pl.BlockSpec((1, 3 * WIDE_HEADS), lambda i: (0, 0)),
        ],
        out_specs=[rows_spec, heads_spec, heads_spec, heads_spec, pl.BlockSpec((16, LANES), lambda i: (0, 0))],
        out_shape=[
            jax.ShapeDtypeStruct((rows, DIM), bf16),
            heads_shape,
            heads_shape,
            heads_shape,
            jax.ShapeDtypeStruct((16, LANES), f32),
        ],
        compiler_params=params(),
    )(frames, mixed, convp, wqkv, bqkv)


def attend_kernel(chunk, q, k, v, size, o_out, q_back, query, shift):
    head = pl.program_id(0)
    keys = k.shape[1]
    tall = q.shape[1]
    bound = jnp.max(size[pl.ds(head, 1), :] * size[pl.ds(head + 8, 1), :])
    query[...] = q[0]
    shift[...] = jnp.zeros(shift.shape, f32)

    @pl.when(bound > SAFE_BOUND * SAFE_BOUND)
    def _():
        shift[...] = jnp.full(shift.shape, -jnp.inf, f32)

        def peak(step, carry):
            scores = dot_nt(k[0, pl.ds(pl.multiple_of(step * 112, 16), 112), :], q[0])
            shift[...] = jnp.maximum(shift[...], jnp.max(scores, axis=0, keepdims=True))
            return carry

        lax.fori_loop(0, keys // 112, peak, 0)
        first, second, third = split3(-shift[...])
        row = row_of((LANES, tall))
        tail = jnp.where(row == 66, first, jnp.where(row == 67, second, jnp.where(row == 68, third, 0.0)))
        query[...] = (q[0].astype(f32) + tail.T).astype(bf16)

    total = None
    for start in range(0, keys, chunk):
        place = slice(start, min(start + chunk, keys))
        weights = jnp.exp2(dot_nt(k[0, place, :], query[...])).astype(bf16)
        part = dot_tn(v[0, place, :], weights)
        total = part if total is None else total + part
    sums = total[64:65, :]
    first, second, third = split3(-(shift[...] + jnp.log2(sums)))
    row = row_of((8, tall))
    tail = jnp.where(row == 2, first, jnp.where(row == 3, second, jnp.where(row == 4, third, 0.0)))
    stacked = jnp.concatenate([total[:64, :] / sums, tail, jnp.zeros((56, tall), f32)], axis=0).T
    lane = lane_of((tall, LANES))
    o_out[0] = jnp.where(lane < 64, stacked, 0.0).astype(bf16)
    q_back[0] = jnp.where((lane >= 66) & (lane < 69), stacked, q[0].astype(f32)).astype(bf16)


def attend(q, k, v, size, chunk=512):
    rows = q.shape[1]
    whole = pl.BlockSpec((1, rows, LANES), lambda h: (h, 0, 0))
    shape = jax.ShapeDtypeStruct((HEADS, rows, LANES), bf16)
    return pl.pallas_call(
        functools.partial(attend_kernel, chunk),
        name="attend",
        grid=(HEADS,),
        in_specs=[whole, whole, whole, pl.BlockSpec((16, LANES), lambda h: (0, 0))],
        out_specs=[whole, whole],
        out_shape=[shape, shape],
        scratch_shapes=[pltpu.VMEM((rows, LANES), bf16), pltpu.VMEM((1, rows), f32)],
        compiler_params=params(),
    )(q, k, v, size)


def attend_back_kernel(rows, q, do, k, v, dq_out, dk_out, dv_out, dq):
    step = pl.program_id(1)
    wide = k.shape[1]
    inside = row_of((wide, LANES)) + step * wide < rows
    key = jnp.where(inside, k[0], jnp.zeros((), bf16))
    value = jnp.where(inside, v[0], jnp.zeros((), bf16))
    weights = jnp.exp2(dot_nt(q[0], key))
    grad_scores = (weights * dot_nt(do[0], value)).astype(bf16)
    weights = weights.astype(bf16)
    dv_out[0] = dot_tn(do[0], weights).T.astype(bf16)
    dk_out[0] = (dot_tn(q[0], grad_scores) * LN2).T.astype(bf16)
    part = dot(grad_scores, key)

    @pl.when(step == 0)
    def _():
        dq[...] = part

    @pl.when(step > 0)
    def _():
        dq[...] += part

    @pl.when(step == pl.num_programs(1) - 1)
    def _():
        dq_out[0] = (dq[...] * HEAD_DIM ** (-0.5)).astype(bf16)


def attend_back(q, do, k, v, wide=1280):
    heads, rows = q.shape[:2]
    block = pl.BlockSpec((1, wide, LANES), lambda h, i: (h, i, 0))
    whole = pl.BlockSpec((1, rows, LANES), lambda h, i: (h, 0, 0))
    shape = jax.ShapeDtypeStruct((heads, rows, LANES), bf16)
    return pl.pallas_call(
        functools.partial(attend_back_kernel, rows),
        name="attend_back",
        grid=(heads, pl.cdiv(rows, wide)),
        in_specs=[whole, whole, block, block],
        out_specs=[whole, block, block],
        out_shape=[shape, shape, shape],
        scratch_shapes=[pltpu.VMEM((rows, LANES), f32)],
        compiler_params=params(),
    )(q, do, k, v)


def erf_parts(value):
    bell = jnp.exp(-0.5 * value * value)
    return bell, 0.5 * (1.0 + lax.erf(value * (1.0 / math.sqrt(2.0))))


def add_tiles(ref, place, value):
    for tile, (low, high) in enumerate(TILES):
        ref[tile, place, : high - low] += value[:, low:high]


def middle_kernel(
    frames_ref, o, mixed, cot, wproj, fc1, fc2, vecs, fc1b,
    output, gmid_out, do_out, gproj, gfc1, gfc2, gvec, gfc1b, chunk,
):
    block = pl.program_id(0)
    rows = mixed.shape[0]
    inside = row_of((rows, DIM)) + block * rows < frames_ref[0] * FRAME

    @pl.when(block == 0)
    def _():
        for ref in (gproj, gfc1, gfc2, gvec, gfc1b):
            ref[...] = jnp.zeros(ref.shape, f32)

    attended = jnp.concatenate([o[head] for head in range(HEADS)], axis=1)
    middle = mixed[...] + (dot(attended, wproj[...]) + vecs[0:1, :])
    normal, inverse = normalize(middle)
    normed = (normal * vecs[1:2, :] + vecs[2:3, :]).astype(bf16)
    grad_output = jnp.where(inside, cot[...].astype(f32), 0.0)
    grad_outer = grad_output.astype(bf16)
    total = middle + vecs[3:4, :]
    grad_normed = jnp.zeros((rows, DIM), f32)
    for start in range(0, FFN, chunk):
        place = slice(start, start + chunk)
        inner = dot(normed, fc1[:, place]) + fc1b[:, place]
        bell, gate = erf_parts(inner)
        activated = (inner * gate).astype(bf16)
        total += dot(activated, fc2[place, :])
        slope = gate + inner * bell * INVERSE_ROOT_TWO_PI
        grad_inner = (dot_nt(grad_outer, fc2[place, :]) * slope)
        gfc1b[:, place] += jnp.sum(grad_inner, axis=0, keepdims=True)
        grad_inner = grad_inner.astype(bf16)
        add_tiles(gfc2, place, dot_tn(activated, grad_outer))
        gfc1[:, place] += dot_tn(normed, grad_inner)
        grad_normed += dot_nt(grad_inner, fc1[:, place])
    output[...] = total.astype(bf16)
    scaled = grad_normed * vecs[1:2, :]
    grad_middle = grad_output + inverse * (
        scaled
        - jnp.mean(scaled, axis=-1, keepdims=True)
        - normal * jnp.mean(scaled * normal, axis=-1, keepdims=True)
    )
    gmid_out[...] = grad_middle
    grad_branch = grad_middle.astype(bf16)
    add_tiles(gproj, slice(None), dot_tn(attended, grad_branch))
    gvec[0:1, :] += jnp.sum(grad_branch.astype(f32), axis=0, keepdims=True)
    gvec[1:2, :] += jnp.sum(grad_normed * normal, axis=0, keepdims=True)
    gvec[2:3, :] += jnp.sum(grad_normed, axis=0, keepdims=True)
    gvec[3:4, :] += jnp.sum(grad_output, axis=0, keepdims=True)
    lane = lane_of((rows, LANES))
    grad_attended = dot_nt(grad_branch, wproj[...])
    for head in range(HEADS):
        grad_head = grad_attended[:, head * LANES : (head + 1) * LANES]
        delta = jnp.sum(grad_head * o[head].astype(f32), axis=-1, keepdims=True)
        first, second, third = split3(-delta)
        tail = jnp.where(lane == 64, first, jnp.where(lane == 65, second, third))
        do_out[head] = jnp.where((lane >= 64) & (lane < 67), tail, grad_head).astype(bf16)


def feed_forward(frames, o, mixed, cot, wproj, fc1, fc2, vecs, fc1b, block=784, chunk=256):
    rows = mixed.shape[0]
    heads_spec = pl.BlockSpec((HEADS, block, LANES), lambda i: (0, i, 0))
    rows_spec = pl.BlockSpec((block, DIM), lambda i: (i, 0))

    def full(*shape):
        return pl.BlockSpec(shape, lambda i: (0,) * len(shape))

    return pl.pallas_call(
        functools.partial(middle_kernel, chunk=chunk),
        name="feed_forward",
        grid=(rows // block,),
        in_specs=[
            SMEM_SPEC, heads_spec, rows_spec, rows_spec,
            full(WIDE_HEADS, DIM), full(DIM, FFN), full(FFN, DIM), full(8, DIM), full(1, FFN),
        ],
        out_specs=[
            rows_spec, rows_spec, heads_spec,
            full(3, WIDE_HEADS, LANES), full(DIM, FFN), full(3, FFN, LANES), full(8, DIM), full(1, FFN),
        ],
        out_shape=[
            jax.ShapeDtypeStruct((rows, DIM), bf16),
            jax.ShapeDtypeStruct((rows, DIM), f32),
            jax.ShapeDtypeStruct((HEADS, rows, LANES), bf16),
            jax.ShapeDtypeStruct((3, WIDE_HEADS, LANES), f32),
            jax.ShapeDtypeStruct((DIM, FFN), f32),
            jax.ShapeDtypeStruct((3, FFN, LANES), f32),
            jax.ShapeDtypeStruct((8, DIM), f32),
            jax.ShapeDtypeStruct((1, FFN), f32),
        ],
        compiler_params=params(),
    )(frames, o, mixed, cot, wproj, fc1, fc2, vecs, fc1b)


def qkv_back_kernel(dq, dk, dv, normed, mixed, gmid, wqkv, convp, spread, padded, gqkv, gbias, gvec, gmix):
    block = pl.program_id(0)

    @pl.when(block == 0)
    def _():
        for ref in (gqkv, gbias, gvec):
            ref[...] = jnp.zeros(ref.shape, f32)

    normal, inverse = normalize(mixed[...])
    grads = jnp.concatenate([part[head] for part in (dq, dk, dv) for head in range(HEADS)], axis=1)
    grad_qkv = dot_tn(normed[...], grads)
    for tile in range(15):
        gqkv[tile] += grad_qkv[:, tile * LANES : (tile + 1) * LANES]
    gbias[...] += jnp.sum(grads.astype(f32), axis=0, keepdims=True)
    grad_normed = dot_nt(grads, wqkv[...])
    gvec[1:2, :] += jnp.sum(grad_normed * normal, axis=0, keepdims=True)
    gvec[2:3, :] += jnp.sum(grad_normed, axis=0, keepdims=True)
    scaled = grad_normed * convp[28:29, :]
    grad_mixed = gmid[...] + inverse * (
        scaled
        - jnp.mean(scaled, axis=-1, keepdims=True)
        - normal * jnp.mean(scaled * normal, axis=-1, keepdims=True)
    )
    gvec[0:1, :] += jnp.sum(grad_mixed, axis=0, keepdims=True)
    gmix[...] = grad_mixed
    for member in range(mixed.shape[0] // FRAME):
        high, low = pieces(gmix[192 * member : 192 * member + 208, :])
        padded[member] = dot(spread[member], high) + dot(spread[member], low)


def project_back(dq, dk, dv, normed, mixed, gmid, wqkv, convp, spread, block=PIECE):
    rows = mixed.shape[0]
    heads_spec = pl.BlockSpec((HEADS, block, LANES), lambda i: (0, i, 0))
    rows_spec = pl.BlockSpec((block, DIM), lambda i: (i, 0))

    def full(*shape):
        return pl.BlockSpec(shape, lambda i: (0,) * len(shape))

    return pl.pallas_call(
        qkv_back_kernel,
        name="qkv_back",
        grid=(rows // block,),
        in_specs=[heads_spec, heads_spec, heads_spec, rows_spec, rows_spec, rows_spec,
                  full(DIM, 3 * WIDE_HEADS), full(32, DIM), full(4, PAD_ROWS, 208)],
        out_specs=[pl.BlockSpec((4, PAD_ROWS, DIM), lambda i: (i, 0, 0)), full(15, DIM, LANES), full(1, 3 * WIDE_HEADS), full(8, DIM)],
        out_shape=[
            jax.ShapeDtypeStruct((rows // FRAME, PAD_ROWS, DIM), f32),
            jax.ShapeDtypeStruct((15, DIM, LANES), f32),
            jax.ShapeDtypeStruct((1, 3 * WIDE_HEADS), f32),
            jax.ShapeDtypeStruct((8, DIM), f32),
        ],
        scratch_shapes=[pltpu.VMEM((block, DIM), f32)],
        compiler_params=params(),
    )(dq, dk, dv, normed, mixed, gmid, wqkv, convp, spread)


def conv_weight_kernel(frames_ref, xsource, gsource, gvec, out, xpad, gpad, moved, sums, tiles, flat, xsem, gsem):
    frames = frames_ref[0]
    count = xpad.shape[0]
    copies = []
    for group in range(count // 4):
        place = pl.ds(4 * group, 4)
        copies.append(pltpu.make_async_copy(xsource.at[place], xpad.at[place], xsem.at[group]))
        copies.append(pltpu.make_async_copy(gsource.at[place], gpad.at[place], gsem.at[group]))
    for copy in copies:
        copy.start()
    sums[...] = jnp.zeros(sums.shape, f32)

    def weight_frame(frame, carry):
        for low, high in TILES:
            body = gpad[frame, 16 : 16 + BODY, low:high]
            moved[0, :, low:high] = pltpu.roll(body, BODY - 1, axis=0)
            moved[1, :, low:high] = pltpu.roll(body, 1, axis=0)
        for a in (-1, 0, 1):
            at = frame + a

            @pl.when((at >= 0) & (at < frames))
            def _():
                for low, high in TILES:
                    for b in (-1, 0, 1):
                        cells = xpad[at, 16 + b * 16 : 16 + b * 16 + BODY, low:high]
                        for c in range(3):
                            body = (
                                gpad[frame, 16 : 16 + BODY, low:high]
                                if c == 1
                                else moved[c // 2, :, low:high]
                            )
                            product = (body * cells).reshape(BODY // 8, 8, high - low)
                            tap = 9 * (a + 1) + 3 * (b + 1) + c
                            sums[tap, :, low:high] += jnp.sum(product, axis=0)

        return carry

    for group in range(count // 4):
        copies[2 * group].wait()
        copies[2 * group + 1].wait()
        start = max(4 * group - 1, 0)
        stop = 4 * group + 3 if group < count // 4 - 1 else count
        lax.fori_loop(jnp.minimum(start, frames), jnp.minimum(stop, frames), weight_frame, 0)
    tiles[...] = jnp.zeros(tiles.shape, f32)
    flat[...] = jnp.zeros(flat.shape, f32)
    for tile, (low, high) in enumerate(TILES):
        tiles[tile, 0:27, : high - low] = jnp.sum(sums[:, :, low:high], axis=1)
        tiles[tile, 27:30, : high - low] = gvec[0:3, low:high]
    for parity in range(2):
        for j in range(5):
            value = tiles[j // 2, pl.ds(parity, 15, stride=2), :]
            put_half(flat, AT_CONV + parity * 5 + j, value, j % 2, 5, 15)
    out[...] = flat[...].astype(bf16)


def conv_weight_grads(frames, xpad, gpad, gvec):
    return pl.pallas_call(
        conv_weight_kernel,
        name="conv_weight_grads",
        in_specs=[SMEM_SPEC, ANY_SPEC, ANY_SPEC, VMEM_SPEC],
        out_shape=jax.ShapeDtypeStruct((80, LANES), bf16),
        scratch_shapes=[
            pltpu.VMEM(xpad.shape, f32),
            pltpu.VMEM(gpad.shape, f32),
            pltpu.VMEM((2, BODY, DIM), f32),
            pltpu.VMEM((27, 8, DIM), f32),
            pltpu.VMEM((3, 32, LANES), f32),
            pltpu.VMEM((80, LANES), f32),
            pltpu.SemaphoreType.DMA((xpad.shape[0] // 4,)),
            pltpu.SemaphoreType.DMA((xpad.shape[0] // 4,)),
        ],
        compiler_params=params(),
    )(frames, xpad, gpad, gvec)


def token_piece_kernel(piece, frames_ref, convp, gsource, back, *refs):
    if piece > 0:
        refs = refs[1:]
    gtok, masked, slots, sums, comp, rows, sem = refs
    frames = frames_ref[0]
    copy = fetch_frames(gsource, slots, sem, piece)
    copy.start()
    rows[...] = jnp.zeros(rows.shape, f32)
    copy.wait()

    def each(member, carry):
        frame = 4 * piece + member
        there = frame < frames
        before = there & (frame > 0)
        after = frame + 1 < frames
        mask_weights(convp, masked, after, there, before)
        at = (member + jnp.where(before, 0, 1), member + 1, member + jnp.where(after, 2, 1))
        mix_frame(slots, at, masked, sums, comp, -1)
        place = pl.ds(pl.multiple_of(192 * member, 16), 208)
        rows[place, :] += dot(back[member], comp[...].astype(bf16))
        return carry

    lax.fori_loop(0, 4, each, 0)
    gtok[...] = rows[...].astype(bf16)


def token_piece(piece, frames, convp, gpad, back, gtok):
    count = gpad.shape[0]
    operands = [frames, convp, gpad, back] + ([] if piece == 0 else [gtok])
    return pl.pallas_call(
        functools.partial(token_piece_kernel, piece),
        name=f"token_piece{piece}",
        grid=(1,),
        in_specs=[SMEM_SPEC, VMEM_SPEC, ANY_SPEC, VMEM_SPEC] + [ANY_SPEC] * (piece > 0),
        out_specs=pl.BlockSpec((PIECE, DIM), lambda i: (piece, 0)),
        out_shape=jax.ShapeDtypeStruct((count * FRAME, DIM), bf16),
        input_output_aliases={4: 0} if piece else {},
        scratch_shapes=[
            pltpu.VMEM((32, DIM), f32),
            pltpu.VMEM((6, PAD_ROWS, DIM), f32),
            pltpu.VMEM((3, BODY, DIM), f32),
            pltpu.VMEM((BODY, DIM), f32),
            pltpu.VMEM((PIECE, DIM), f32),
            pltpu.SemaphoreType.DMA(()),
        ],
        compiler_params=params(),
    )(*operands)


def put_half(flat, index, value, side, step=1, count=1):
    row, wanted = divmod(index, 2)
    place = pl.ds(row, count, stride=step) if step > 1 else pl.ds(row, count)
    lane = lane_of(value.shape)
    if wanted == 0:
        flat[place, :] += jnp.where(lane < 64, low_half(value, side), 0.0)
    else:
        flat[place, :] += jnp.where(lane >= 64, high_half(value, side), 0.0)


def put_vector(flat, index, value):
    width = value.shape[1]
    for j in range(width // 64):
        low = (j // 2) * LANES
        part = value[:, low : min(low + LANES, width)]
        if part.shape[1] < LANES:
            part = jnp.concatenate([part, jnp.zeros((1, 64), f32)], axis=1)
        put_half(flat, index + j, part, j % 2)


PACK_BASE = 2432


def pack_main_kernel(gproj, gfc1, gfc2, gvec, gfc1b, out, flat):
    flat[...] = jnp.zeros(flat.shape, f32)
    for parity in range(2):
        for j in range(5):
            for head in range(HEADS):
                value = gproj[j // 2, pl.ds(head * LANES + parity, 32, stride=2), :]
                put_half(flat, AT_PROJ + (64 * head + parity) * 5 + j, value, j % 2, 5, 32)
            value = gfc2[j // 2, pl.ds(parity, FFN // 2, stride=2), :]
            put_half(flat, AT_FC2 + parity * 5 + j, value, j % 2, 5, FFN // 2)
    for j in range(20):
        value = gfc1[:, (j // 2) * LANES : (j // 2 + 1) * LANES]
        put_half(flat, AT_FC1 + j, value, j % 2, 10, DIM)
    for row in range(3):
        put_vector(flat, AT_VEC + 5 * row, gvec[row : row + 1, :])
    put_vector(flat, AT_FC2B, gvec[3:4, :])
    put_vector(flat, AT_FC1B, gfc1b[...])
    out[...] = flat[...].astype(bf16)


def pack_main(gproj, gfc1, gfc2, gvec, gfc1b, rows):
    return pl.pallas_call(
        pack_main_kernel,
        name="pack_main",
        out_shape=jax.ShapeDtypeStruct((rows, LANES), bf16),
        scratch_shapes=[pltpu.VMEM((rows, LANES), f32)],
        compiler_params=params(),
    )(gproj, gfc1, gfc2, gvec, gfc1b)


QKV_ROWS = 2480


def pack_qkv_kernel(gqkv, gbias, out, end, flat):
    flat[...] = jnp.zeros(flat.shape, f32)
    for parity in range(2):
        for j in range(15):
            value = gqkv[j, pl.ds(parity, DIM // 2, stride=2), :]
            put_half(flat, AT_QKV + parity * 15 + j, value, 0, 15, DIM // 2)
    for j in range(10):
        tile = j if j < 5 else j + 5
        put_half(flat, AT_QV + j, gbias[:, tile * LANES : (tile + 1) * LANES], 0)
    out[...] = flat[:PACK_BASE, :].astype(bf16)
    end[...] = flat[PACK_BASE:, :].astype(bf16)


def pack_qkv(gqkv, gbias):
    return pl.pallas_call(
        pack_qkv_kernel,
        name="pack_qkv",
        out_shape=[
            jax.ShapeDtypeStruct((PACK_BASE, LANES), bf16),
            jax.ShapeDtypeStruct((QKV_ROWS - PACK_BASE, LANES), bf16),
        ],
        scratch_shapes=[pltpu.VMEM((QKV_ROWS, LANES), f32)],
        compiler_params=params(),
    )(gqkv, gbias)


AXES = ("wide", "narrow")


def exchange(value, bit):
    count = lax.axis_size(AXES)
    return lax.ppermute(value, AXES, [(i, i ^ (1 << bit)) for i in range(count)])


def my_bit(bit):
    return (lax.axis_index(AXES) >> bit) & 1


def tie(*values):
    return lax.optimization_barrier(values)


def halve(value, bits):
    for bit in range(bits):
        value = value.reshape(value.shape[0] // 2, 2, -1, LANES)
        mine = my_bit(bit)
        keep = lax.dynamic_index_in_dim(value, mine, 1, keepdims=False)
        give = lax.dynamic_index_in_dim(value, 1 - mine, 1, keepdims=False)
        value = keep + exchange(give, bit)
    return value[0]


def on_device(master, momentum, average, tokens, clip_ids, borders, cotangent):
    wide_count, narrow_count = lax.axis_size("wide"), lax.axis_size("narrow")
    count = wide_count * narrow_count
    bits = count.bit_length() - 1
    own_rows = master.shape[0]
    frames = (jnp.sum((clip_ids >= 0).astype(jnp.int32)) // FRAME).reshape(1)
    me = lax.axis_index(AXES)
    quarter = me >> (bits - 2)
    blocks = master.astype(bf16)[None]
    other = exchange(blocks, bits - 2)
    xpad, spread, back = prepare(tokens.T)
    other, xpad = tie(other, xpad)
    blocks = jnp.concatenate([blocks, other], axis=0)
    other, cotangent = tie(exchange(blocks, bits - 1), turn(tie(blocks, cotangent.T)[1]))
    blocks = jnp.concatenate([blocks, other], axis=0)
    first = lax.dynamic_index_in_dim(blocks, quarter, 0)
    rest = [lax.dynamic_index_in_dim(blocks, quarter ^ index, 0) for index in (1, 2, 3)]
    rest = jnp.concatenate(rest, axis=0)[None]
    low_bits = list(range(bits - 3, -1, -1))
    for step, bit in enumerate(low_bits):
        first = jnp.concatenate([first, exchange(first, bit)], axis=0)
        if step == 0:
            first, rest, frames = tie(first, rest, frames)
            rest = jnp.concatenate([rest, exchange(rest, bit)], axis=0)
    order = [0] * (count // 4)
    for step, bit in enumerate(low_bits):
        order = [place | (((index >> bit) & 1) << step) for index, place in enumerate(order)]
    mine = sum((((me >> bit) & 1) << step) for step, bit in enumerate(low_bits))
    order = jnp.array(order, jnp.int32) ^ mine
    head = lax.dynamic_index_in_dim(first, mine, 0, keepdims=False)
    head = jnp.concatenate([head, jnp.zeros((4, LANES), bf16)], axis=0)[:80] if own_rows < 80 else head[:80]
    mixed, convp = None, None
    for step, bit in enumerate(low_bits[1:]):
        if step < 2:
            rest, head = tie(rest, head)
        other = exchange(rest, bit)
        if step == 0:
            mixed, convp = conv_piece(0, frames, head, xpad, back, None)
            other, mixed = tie(other, mixed)
        elif step == 1:
            mixed, convp = conv_piece(1, frames, head, xpad, back, mixed)
            mixed, convp = conv_piece(2, frames, head, xpad, back, mixed)
            other, mixed = tie(other, mixed)
        rest = jnp.concatenate([rest, other], axis=0)
    wqkv, wproj, fc1, fc2, bqkv, vecs, fc1b = unpack(order, first, rest)
    normed, q, k, v, size = project(frames, mixed, convp, wqkv, bqkv)
    o, q_back = attend(q, k, v, size)
    output, gmid, do, gproj, gfc1, gfc2, gvec, gfc1b = feed_forward(
        frames, o, mixed, cotangent, wproj, fc1, fc2, vecs, fc1b
    )
    main = pack_main(gproj, gfc1, gfc2, gvec, gfc1b, count * own_rows)
    main = main.reshape(wide_count, narrow_count, own_rows, LANES)
    main = lax.psum_scatter(main, "wide", scatter_dimension=0, tiled=True)[0]
    dq, dk, dv = attend_back(q_back, do, k, v)
    gpad, gqkv, gbias, gvec_one = project_back(dq, dk, dv, normed, mixed, gmid, wqkv, convp, spread)
    qkv, qkv_end = pack_qkv(gqkv, gbias)
    qkv = halve(qkv.reshape(count // 4, own_rows, LANES), bits - 2)
    for bit in (bits - 2, bits - 1):
        qkv = qkv + exchange(qkv, bit)
    conv = conv_weight_grads(frames, xpad, gpad, gvec_one)
    late = jnp.concatenate([conv, qkv_end], axis=0)
    main, late = tie(main, late)
    main = halve(main, narrow_count.bit_length() - 1)
    gtok = None
    for bit in range(bits):
        if bit < 3:
            late, gpad = tie(late, gpad)
        elif bit == 3:
            late, output = tie(late, output)
        elif bit == 4:
            late, gtok = tie(late, gtok)
        other = exchange(late, bit)
        if bit < 3:
            gtok = token_piece(bit, frames, convp, gpad, back, gtok)
            other, gtok = tie(other, gtok)
        elif bit == 3:
            other, output = tie(other, turn(output))
        elif bit == 4:
            other, gtok = tie(other, turn(gtok))
        late = late + other
    early = jnp.where(me < count // 4, qkv.astype(f32), main.astype(f32))
    conv, qkv_end = late[:80].astype(f32), late[80:].astype(f32)
    if own_rows < 80:
        conv = conv[:own_rows]
    conv = jnp.pad(conv, ((0, own_rows - conv.shape[0]), (0, 0)))
    qkv_end = jnp.pad(qkv_end, ((0, own_rows - qkv_end.shape[0]), (0, 0)))
    owned = early + jnp.where(me == 0, conv, jnp.where(me == count // 4, qkv_end, 0.0))
    rate = RATE_FACTOR / math.sqrt(tokens.shape[0] * count)
    decayed = owned + DECAY_RATE * master
    new_momentum = MOMENTUM * momentum + decayed
    new_master = master - rate * (decayed + MOMENTUM * new_momentum)
    new_average = AVERAGE_KEEP * average + (1.0 - AVERAGE_KEEP) * new_master
    return (output.T, gtok.T, owned, new_master, new_momentum, new_average, new_master.astype(bf16))


def solution(mesh):
    rows = P(("wide", "narrow"), None)
    return jax.shard_map(
        on_device,
        mesh=mesh,
        in_specs=(rows, rows, rows, rows, P(("wide", "narrow")), P(("wide", "narrow")), rows),
        out_specs=(rows,) * 7,
        check_vma=False,
    )
```

```python
import functools
import math

import jax
import jax.numpy as jnp
from jax import lax
from jax.experimental import pallas as pl
from jax.experimental.pallas import tpu as pltpu
from jax.sharding import PartitionSpec as P

HEADS = 5
HEAD_DIM = 64
DIM = 320
FFN = 1280
SIDE = 14
FRAME = SIDE * SIDE
LANES = 128
WIDE_HEADS = HEADS * LANES

EPSILON = 1e-06
MOMENTUM = 0.9
DECAY_RATE = 0.0001
AVERAGE_KEEP = 0.8
RATE_FACTOR = 0.03
LOG2E = 1.0 / math.log(2.0)
LN2 = math.log(2.0)
INVERSE_ROOT_TWO_PI = 1.0 / math.sqrt(2.0 * math.pi)
BLOCKED = -(2.0**30)
SAFE_BOUND = 80.0

bf16 = jnp.bfloat16
f32 = jnp.float32

AT_CONV = 0
AT_QKV = 150
AT_QV = 4950
AT_PROJ = 4960
AT_VEC = 6560
AT_FC1 = 6575
AT_FC1B = 12975
AT_FC2 = 12995
AT_FC2B = 19395
HALF_END = 19400


SMEM_SPEC = pl.BlockSpec(memory_space=pltpu.SMEM)
VMEM_SPEC = pl.BlockSpec(memory_space=pltpu.VMEM)
ANY_SPEC = pl.BlockSpec(memory_space=pl.ANY)
HBM_SPEC = pl.BlockSpec(memory_space=pltpu.HBM)


def in_hbm(value):
    return pltpu.with_memory_space_constraint(value, pltpu.HBM)


def dot(a, b):
    return lax.dot_general(a, b, (((1,), (0,)), ((), ())), preferred_element_type=f32)


def dot_nt(a, b):
    return lax.dot_general(a, b, (((1,), (1,)), ((), ())), preferred_element_type=f32)


def dot_tn(a, b):
    return lax.dot_general(a, b, (((0,), (0,)), ((), ())), preferred_element_type=f32)


def params(limit=58):
    return pltpu.CompilerParams(vmem_limit_bytes=limit << 20)


def lane_of(shape):
    return lax.broadcasted_iota(jnp.int32, shape, len(shape) - 1)


def row_of(shape):
    return lax.broadcasted_iota(jnp.int32, shape, 0)


def low_half(value, side):
    return value if side == 0 else pltpu.roll(value, 64, axis=1)


def high_half(value, side):
    return value if side == 1 else pltpu.roll(value, 64, axis=1)


def split3(value):
    first = value.astype(bf16).astype(f32)
    rest = value - first
    second = rest.astype(bf16).astype(f32)
    return first, second, rest - second


def read_half(flat, at, length, step, count, parity, j):
    index = at + parity * length + j
    return flat[pl.ds(index // 2, count, stride=step), :], index % 2


def read_vector(flat, at, length):
    tiles = []
    lane = lane_of((1, LANES))
    for j in range(0, length, 2):
        row, side = divmod(at + j, 2)
        low = low_half(flat[row : row + 1, :], side)
        if j + 1 < length:
            row, side = divmod(at + j + 1, 2)
            tiles.append(jnp.where(lane < 64, low, high_half(flat[row : row + 1, :], side)))
        else:
            tiles.append(low[:, :64])
    return jnp.concatenate(tiles, axis=1)


def odd_matrix(flat, out, at, length, rows):
    pairs = rows // 2
    for parity in range(2):
        for tile in range((length + 1) // 2):
            low, side = read_half(flat, at, length, length, pairs, parity, 2 * tile)
            low = low_half(low, side)
            place = pl.ds(parity, pairs, stride=2)
            if 2 * tile + 1 < length:
                high, side = read_half(flat, at, length, length, pairs, parity, 2 * tile + 1)
                merged = jnp.where(lane_of(low.shape) < 64, low, high_half(high, side))
            else:
                merged = low
            out[tile, place, :] = merged


def unpack_kernel(order, first, rest, wqkv, wproj, fc1, fc2, bqkv, vecs, fc1b, flat, wide, tall):
    blocks, rows = first.shape[:2]
    for block in range(blocks):
        place = order[block]
        for quarter in range(4):
            start = (quarter * blocks + block) * rows
            value = first[place] if quarter == 0 else rest[place, quarter - 1]
            flat[start : start + rows, :] = value.astype(f32)
    for parity in range(2):
        for j in range(15):
            value, side = read_half(flat, AT_QKV, 15, 15, 160, parity, j)
            value = jnp.where(lane_of(value.shape) < 64, low_half(value, side), 0.0)
            wide[j, pl.ds(parity, 160, stride=2), :] = value
    for j in range(15):
        wqkv[:, j * LANES : (j + 1) * LANES] = wide[j].astype(bf16)
    lane = lane_of((1, LANES))
    for j in range(15):
        if 5 <= j < 10:
            bqkv[:, j * LANES : (j + 1) * LANES] = jnp.zeros((1, LANES), f32)
        else:
            row, side = divmod(AT_QV + (j if j < 5 else j - 5), 2)
            value = low_half(flat[row : row + 1, :], side)
            bqkv[:, j * LANES : (j + 1) * LANES] = jnp.where(lane < 64, value, 0.0)
    odd_matrix(flat, wide, AT_PROJ, 5, DIM)
    for head in range(HEADS):
        for tile in range(3):
            width = LANES if tile < 2 else 64
            columns = slice(tile * LANES, tile * LANES + width)
            part = wide[tile, head * 64 : head * 64 + 64, :width].astype(bf16)
            wproj[head * LANES : head * LANES + 64, columns] = part
        wproj[head * LANES + 64 : (head + 1) * LANES, :] = jnp.zeros((64, DIM), bf16)
    for row in range(3):
        vecs[row : row + 1, :] = read_vector(flat, AT_VEC + 5 * row, 5)
    vecs[3:4, :] = read_vector(flat, AT_FC2B, 5)
    vecs[4:8, :] = jnp.zeros((4, DIM), f32)
    fc1b[...] = read_vector(flat, AT_FC1B, 20)
    for tile in range(10):
        low, side = read_half(flat, AT_FC1, 20, 10, DIM, 0, 2 * tile)
        high, side_high = read_half(flat, AT_FC1, 20, 10, DIM, 0, 2 * tile + 1)
        merged = jnp.where(lane_of(low.shape) < 64, low_half(low, side), high_half(high, side_high))
        fc1[:, tile * LANES : (tile + 1) * LANES] = merged.astype(bf16)
    odd_matrix(flat, tall, AT_FC2, 5, FFN)
    for tile in range(3):
        width = LANES if tile < 2 else 64
        fc2[:, tile * LANES : tile * LANES + width] = tall[tile, :, :width].astype(bf16)


def unpack(order, first, rest):
    rows = 4 * first.shape[0] * first.shape[1]
    return pl.pallas_call(
        unpack_kernel,
        name="unpack",
        in_specs=[SMEM_SPEC, VMEM_SPEC, VMEM_SPEC],
        out_shape=[
            jax.ShapeDtypeStruct((DIM, 3 * WIDE_HEADS), bf16),
            jax.ShapeDtypeStruct((WIDE_HEADS, DIM), bf16),
            jax.ShapeDtypeStruct((DIM, FFN), bf16),
            jax.ShapeDtypeStruct((FFN, DIM), bf16),
            jax.ShapeDtypeStruct((1, 3 * WIDE_HEADS), f32),
            jax.ShapeDtypeStruct((8, DIM), f32),
            jax.ShapeDtypeStruct((1, FFN), f32),
        ],
        scratch_shapes=[
            pltpu.VMEM((rows, LANES), f32),
            pltpu.VMEM((15, DIM, LANES), f32),
            pltpu.VMEM((3, FFN, LANES), f32),
        ],
        compiler_params=params(16),
    )(order, first, rest)


PAD_ROWS = 16 * 16
BODY = SIDE * 16


def spread_matrix(shift):
    cell = lax.broadcasted_iota(jnp.int32, (PAD_ROWS, 208), 0)
    source = lax.broadcasted_iota(jnp.int32, (PAD_ROWS, 208), 1)
    row, column = cell >> 4, cell & 15
    inside = (row >= 1) & (row <= SIDE) & (column < SIDE)
    wanted = (row - 1) * SIDE + column + shift
    return jnp.where(inside & (source == wanted), 1.0, 0.0).astype(bf16)


def gather_matrix(shift):
    target = lax.broadcasted_iota(jnp.int32, (208, BODY), 0)
    cell = lax.broadcasted_iota(jnp.int32, (208, BODY), 1)
    row, column = cell >> 4, cell & 15
    wanted = row * SIDE + column + shift
    return jnp.where((column < SIDE) & (target == wanted), 1.0, 0.0).astype(bf16)


TILES = ((0, 128), (128, 256), (256, 320))


def pieces(value):
    first = value.astype(bf16)
    return first, (value - first.astype(f32)).astype(bf16)


def prepare_kernel(frames, turned, padded, spread, back, passed, tokens):
    for member in range(4):
        spread[member] = spread_matrix(4 * member)
        back[member] = gather_matrix(4 * member)
    passed[0] = frames[0]
    tokens[...] = turned[...].T

    def fill(frame, carry):
        member = frame & 3
        place = pl.ds(pl.multiple_of(frame * FRAME - 4 * member, 16), 208)
        padded[frame] = dot(spread[member], tokens[place, :])
        return carry

    lax.fori_loop(0, padded.shape[0], fill, 0)


def prepare(frames, turned):
    rows = turned.shape[1]
    return pl.pallas_call(
        prepare_kernel,
        name="prepare",
        in_specs=[SMEM_SPEC, VMEM_SPEC],
        out_specs=[VMEM_SPEC, VMEM_SPEC, VMEM_SPEC, SMEM_SPEC],
        out_shape=[
            jax.ShapeDtypeStruct((rows // FRAME, PAD_ROWS, DIM), f32),
            jax.ShapeDtypeStruct((4, PAD_ROWS, 208), bf16),
            jax.ShapeDtypeStruct((4, 208, BODY), bf16),
            jax.ShapeDtypeStruct((1,), jnp.int32),
        ],
        scratch_shapes=[pltpu.VMEM((rows, DIM), bf16)],
        compiler_params=params(10),
    )(frames, turned)


PIECE = 4 * FRAME


def fetch_frames(source, slots, sems, piece):
    first, last = max(4 * piece - 1, 0), min(4 * piece + 5, source.shape[0])
    middle = 4 * piece + 2
    copies = []
    for index, (start, stop) in enumerate(((first, middle), (middle, last))):
        slot = start - (4 * piece - 1)
        copies.append(
            pltpu.make_async_copy(
                source.at[pl.ds(start, stop - start)], slots.at[pl.ds(slot, stop - start)], sems.at[index]
            )
        )
    return copies


def mix_frame(slots, at, weights, sums, out, sign):
    for low, high in TILES:
        for start in range(0, BODY, 56):
            parts = [None, None, None]
            for a in (-1, 0, 1):
                for b in (-1, 0, 1):
                    begin = 16 + sign * b * 16 + start
                    cells = slots[at[1 + sign * a], begin : begin + 56, low:high]
                    for c in range(3):
                        tap = 9 * (a + 1) + 3 * (b + 1) + c
                        term = cells * weights[tap : tap + 1, low:high]
                        parts[c] = term if parts[c] is None else parts[c] + term
            parts[1] = parts[1] + slots[at[1], 16 + start : 16 + start + 56, low:high]
            for c in range(3):
                sums[c, start : start + 56, low:high] = parts[c]
    before, after = (0, 2) if sign == 1 else (2, 0)
    for low, high in TILES:
        out[:, low:high] = (
            sums[1, :, low:high]
            + pltpu.roll(sums[before, :, low:high], 1, axis=0)
            + pltpu.roll(sums[after, :, low:high], BODY - 1, axis=0)
        )


def mask_weights(weights, masked, first, middle, last):
    for tap in range(27):
        keep = (first, middle, last)[tap // 9]
        scale = 1.0 if tap == 13 else jnp.where(keep, 1.0, 0.0)
        masked[tap : tap + 1, :] = weights[tap : tap + 1, :] * scale


def conv_params(head, flat, weights):
    flat[...] = head[...].astype(f32)
    for parity in range(2):
        for tile in range(3):
            low, side = read_half(flat, AT_CONV, 5, 5, 15, parity, 2 * tile)
            low = low_half(low, side)
            place = pl.ds(parity, 15, stride=2)
            if tile < 2:
                high, side = read_half(flat, AT_CONV, 5, 5, 15, parity, 2 * tile + 1)
                low = jnp.where(lane_of(low.shape) < 64, low, high_half(high, side))
            weights[tile, place, :] = low


def turn_kernel(frames, source, out, passed):
    passed[0] = frames[0]
    out[...] = source[...].T


def turn(frames, value):
    rows, columns = value.shape
    return pl.pallas_call(
        turn_kernel,
        name="turn",
        in_specs=[SMEM_SPEC, VMEM_SPEC],
        out_specs=[VMEM_SPEC, SMEM_SPEC],
        out_shape=[
            jax.ShapeDtypeStruct((columns, rows), value.dtype),
            jax.ShapeDtypeStruct((1,), jnp.int32),
        ],
        compiler_params=params(10),
        cost_estimate=pl.CostEstimate(flops=0, bytes_accessed=4 * rows * columns, transcendentals=0),
    )(frames, value)


def conv_piece_kernel(piece, frames_ref, head, padded, back, *refs):
    if piece > 0:
        refs = refs[1:]
    mixed, convp, passed, flat, weights, masked, slots, sums, comp, sem = refs
    passed[0] = frames_ref[0]
    copies = fetch_frames(padded, slots, sem, piece)
    for copy in copies:
        copy.start()
    frames = frames_ref[0]
    conv_params(head, flat, weights)
    for tile, (low, high) in enumerate(TILES):
        convp[:, low:high] = weights[tile, :, : high - low]
    mixed[...] = jnp.zeros(mixed.shape, f32)
    copies[0].wait()

    def each(member, carry):
        @pl.when(member == 1)
        def _():
            copies[1].wait()

        frame = 4 * piece + member
        there = frame < frames
        before = there & (frame > 0)
        after = frame + 1 < frames
        mask_weights(convp, masked, before, there, after)
        at = (member + jnp.where(before, 0, 1), member + 1, member + jnp.where(after, 2, 1))
        mix_frame(slots, at, masked, sums, comp, 1)
        high, low = pieces(comp[...] + convp[27:28, :])
        place = pl.ds(pl.multiple_of(192 * member, 16), 208)
        mixed[place, :] += dot(back[member], high) + dot(back[member], low)
        return carry

    lax.fori_loop(0, 4, each, 0)


def conv_piece(piece, frames, head, padded, back, mixed):
    rows = padded.shape[0] * FRAME
    operands = [frames, head, in_hbm(padded), back] + ([] if piece == 0 else [mixed])
    return pl.pallas_call(
        functools.partial(conv_piece_kernel, piece),
        name=f"conv_piece{piece}",
        grid=(1,),
        in_specs=[SMEM_SPEC, VMEM_SPEC, HBM_SPEC, VMEM_SPEC] + [ANY_SPEC] * (piece > 0),
        out_specs=[
            pl.BlockSpec((PIECE, DIM), lambda i: (piece, 0)),
            pl.BlockSpec((32, DIM), lambda i: (0, 0)),
            SMEM_SPEC,
        ],
        out_shape=[
            jax.ShapeDtypeStruct((rows, DIM), f32),
            jax.ShapeDtypeStruct((32, DIM), f32),
            jax.ShapeDtypeStruct((1,), jnp.int32),
        ],
        input_output_aliases={4: 0} if piece else {},
        scratch_shapes=[
            pltpu.VMEM(head.shape, f32),
            pltpu.VMEM((3, 32, LANES), f32),
            pltpu.VMEM((32, DIM), f32),
            pltpu.VMEM((6, PAD_ROWS, DIM), f32),
            pltpu.VMEM((3, BODY, DIM), f32),
            pltpu.VMEM((BODY, DIM), f32),
            pltpu.SemaphoreType.DMA((2,)),
        ],
        compiler_params=params(10),
    )(*operands)


def normalize(values):
    centered = values - jnp.mean(values, axis=-1, keepdims=True)
    variance = jnp.mean(centered * centered, axis=-1, keepdims=True)
    inverse = lax.rsqrt(variance + EPSILON)
    return centered * inverse, inverse


def row_size(value):
    part = jnp.where(lane_of(value.shape) < HEAD_DIM, value.astype(f32), 0.0)
    return jnp.sum(part * part, axis=-1, keepdims=True)


def qkv_kernel(frames_ref, mixed, convp, wqkv, bqkv, normed_out, q_out, k_out, v_out, size):
    block = pl.program_id(0)
    rows = mixed.shape[0]
    frames = frames_ref[0]
    normal, unused_inverse = normalize(mixed[...])
    normed = (normal * convp[28:29, :] + convp[29:30, :]).astype(bf16)
    normed_out[...] = normed
    lane = lane_of((rows, LANES))
    inside = row_of((rows, LANES)) + block * rows < frames * FRAME
    q_mask = jnp.where(
        ((lane == 64) & ~inside) | ((lane == 65) & inside), BLOCKED, 0.0
    )
    k_mask = jnp.where(
        ((lane == 64) & inside) | ((lane == 65) & ~inside) | ((lane >= 66) & (lane < 69)), 1.0, 0.0
    )
    v_mask = jnp.where((lane >= 64) & (lane < 67), 1.0, 0.0)
    scale = HEAD_DIM ** (-0.5) * LOG2E

    @pl.when(block == 0)
    def _():
        size[...] = jnp.zeros(size.shape, f32)

    projected = dot(normed, wqkv[...])
    for head in range(HEADS):

        def columns(kind, head=head):
            place = slice((kind * HEADS + head) * LANES, (kind * HEADS + head + 1) * LANES)
            return projected[:, place] + bqkv[:, place]

        query = (columns(0) * scale + q_mask).astype(bf16)
        key = (columns(1) + k_mask).astype(bf16)
        query_size = jnp.max(row_size(query), axis=0, keepdims=True)
        key_size = jnp.max(row_size(key), axis=0, keepdims=True)
        q_out[head] = query
        k_out[head] = key
        v_out[head] = (columns(2) + v_mask).astype(bf16)
        size[head : head + 1, :] = jnp.maximum(size[head : head + 1, :], query_size)
        size[head + 8 : head + 9, :] = jnp.maximum(size[head + 8 : head + 9, :], key_size)


def project(frames, mixed, convp, wqkv, bqkv, block=784):
    rows = mixed.shape[0]
    heads_spec = pl.BlockSpec((HEADS, block, LANES), lambda i: (0, i, 0))
    rows_spec = pl.BlockSpec((block, DIM), lambda i: (i, 0))
    heads_shape = jax.ShapeDtypeStruct((HEADS, rows, LANES), bf16)
    return pl.pallas_call(
        qkv_kernel,
        name="qkv_forward",
        grid=(rows // block,),
        in_specs=[
            SMEM_SPEC,
            rows_spec,
            pl.BlockSpec((32, DIM), lambda i: (0, 0)),
            pl.BlockSpec((DIM, 3 * WIDE_HEADS), lambda i: (0, 0)),
            pl.BlockSpec((1, 3 * WIDE_HEADS), lambda i: (0, 0)),
        ],
        out_specs=[rows_spec, heads_spec, heads_spec, heads_spec, pl.BlockSpec((16, LANES), lambda i: (0, 0))],
        out_shape=[
            pltpu.HBM((rows, DIM), bf16),
            heads_shape,
            heads_shape,
            heads_shape,
            jax.ShapeDtypeStruct((16, LANES), f32),
        ],
        compiler_params=params(14),
    )(frames, mixed, convp, wqkv, bqkv)


def attend_kernel(chunk, q, k, v, size, o_out, q_back, query, shift):
    head = pl.program_id(0)
    keys = k.shape[1]
    tall = q.shape[1]
    bound = jnp.max(size[pl.ds(head, 1), :] * size[pl.ds(head + 8, 1), :])
    query[...] = q[0]
    shift[...] = jnp.zeros(shift.shape, f32)

    @pl.when(bound > SAFE_BOUND * SAFE_BOUND)
    def _():
        shift[...] = jnp.full(shift.shape, -jnp.inf, f32)

        def peak(step, carry):
            scores = dot_nt(k[0, pl.ds(pl.multiple_of(step * 112, 16), 112), :], q[0])
            shift[...] = jnp.maximum(shift[...], jnp.max(scores, axis=0, keepdims=True))
            return carry

        lax.fori_loop(0, keys // 112, peak, 0)
        first, second, third = split3(-shift[...])
        row = row_of((LANES, tall))
        tail = jnp.where(row == 66, first, jnp.where(row == 67, second, jnp.where(row == 68, third, 0.0)))
        query[...] = (q[0].astype(f32) + tail.T).astype(bf16)

    total = None
    for start in range(0, keys, chunk):
        place = slice(start, min(start + chunk, keys))
        weights = jnp.exp2(dot_nt(k[0, place, :], query[...])).astype(bf16)
        part = dot_tn(v[0, place, :], weights)
        total = part if total is None else total + part
    sums = total[64:65, :]
    first, second, third = split3(-(shift[...] + jnp.log2(sums)))
    row = row_of((8, tall))
    tail = jnp.where(row == 2, first, jnp.where(row == 3, second, jnp.where(row == 4, third, 0.0)))
    stacked = jnp.concatenate([total[:64, :] / sums, tail, jnp.zeros((56, tall), f32)], axis=0).T
    lane = lane_of((tall, LANES))
    o_out[0] = jnp.where(lane < 64, stacked, 0.0).astype(bf16)
    q_back[0] = jnp.where((lane >= 66) & (lane < 69), stacked, q[0].astype(f32)).astype(bf16)


def attend(q, k, v, size, chunk=512):
    rows = q.shape[1]
    whole = pl.BlockSpec((1, rows, LANES), lambda h: (h, 0, 0))
    shape = jax.ShapeDtypeStruct((HEADS, rows, LANES), bf16)
    return pl.pallas_call(
        functools.partial(attend_kernel, chunk),
        name="attend",
        grid=(HEADS,),
        in_specs=[whole, whole, whole, pl.BlockSpec((16, LANES), lambda h: (0, 0))],
        out_specs=[whole, whole],
        out_shape=[shape, pltpu.HBM(shape.shape, bf16)],
        scratch_shapes=[pltpu.VMEM((rows, LANES), bf16), pltpu.VMEM((1, rows), f32)],
        compiler_params=params(18),
    )(q, k, v, size)


def attend_back_kernel(rows, q, do, k, v, dq_out, dk_out, dv_out, dq):
    step = pl.program_id(1)
    wide = k.shape[1]
    inside = row_of((wide, LANES)) + step * wide < rows
    key = jnp.where(inside, k[0], jnp.zeros((), bf16))
    value = jnp.where(inside, v[0], jnp.zeros((), bf16))
    weights = jnp.exp2(dot_nt(q[0], key))
    grad_scores = (weights * dot_nt(do[0], value)).astype(bf16)
    weights = weights.astype(bf16)
    dv_out[0] = dot_tn(do[0], weights).T.astype(bf16)
    dk_out[0] = (dot_tn(q[0], grad_scores) * LN2).T.astype(bf16)
    part = dot(grad_scores, key)

    @pl.when(step == 0)
    def _():
        dq[...] = part

    @pl.when(step > 0)
    def _():
        dq[...] += part

    @pl.when(step == pl.num_programs(1) - 1)
    def _():
        dq_out[0] = (dq[...] * HEAD_DIM ** (-0.5)).astype(bf16)


def attend_back(q, do, k, v, wide=1280):
    heads, rows = q.shape[:2]
    block = pl.BlockSpec((1, wide, LANES), lambda h, i: (h, i, 0))
    whole = pl.BlockSpec((1, rows, LANES), lambda h, i: (h, 0, 0))
    shape = jax.ShapeDtypeStruct((heads, rows, LANES), bf16)
    return pl.pallas_call(
        functools.partial(attend_back_kernel, rows),
        name="attend_back",
        grid=(heads, pl.cdiv(rows, wide)),
        in_specs=[whole, whole, block, block],
        out_specs=[whole, block, block],
        out_shape=[shape, shape, shape],
        scratch_shapes=[pltpu.VMEM((rows, LANES), f32)],
        compiler_params=params(26),
    )(q, do, k, v)


def erf_parts(value):
    bell = jnp.exp(-0.5 * value * value)
    return bell, 0.5 * (1.0 + lax.erf(value * (1.0 / math.sqrt(2.0))))


def add_tiles(ref, place, value):
    for tile, (low, high) in enumerate(TILES):
        ref[tile, place, : high - low] += value[:, low:high]


def middle_kernel(
    frames_ref, o, mixed, cot, wproj, fc1, fc2, vecs, fc1b,
    output, gmid_out, do_out, gproj, gfc1, gfc2, gvec, gfc1b, chunk,
):
    block = pl.program_id(0)
    rows = mixed.shape[0]
    inside = row_of((rows, DIM)) + block * rows < frames_ref[0] * FRAME

    @pl.when(block == 0)
    def _():
        for ref in (gproj, gfc1, gfc2, gvec, gfc1b):
            ref[...] = jnp.zeros(ref.shape, f32)

    attended = jnp.concatenate([o[head] for head in range(HEADS)], axis=1)
    middle = mixed[...] + (dot(attended, wproj[...]) + vecs[0:1, :])
    normal, inverse = normalize(middle)
    normed = (normal * vecs[1:2, :] + vecs[2:3, :]).astype(bf16)
    grad_output = jnp.where(inside, cot[...].astype(f32), 0.0)
    grad_outer = grad_output.astype(bf16)
    total = middle + vecs[3:4, :]
    grad_normed = jnp.zeros((rows, DIM), f32)
    for start in range(0, FFN, chunk):
        place = slice(start, start + chunk)
        inner = dot(normed, fc1[:, place]) + fc1b[:, place]
        bell, gate = erf_parts(inner)
        activated = (inner * gate).astype(bf16)
        total += dot(activated, fc2[place, :])
        slope = gate + inner * bell * INVERSE_ROOT_TWO_PI
        grad_inner = (dot_nt(grad_outer, fc2[place, :]) * slope)
        gfc1b[:, place] += jnp.sum(grad_inner, axis=0, keepdims=True)
        grad_inner = grad_inner.astype(bf16)
        add_tiles(gfc2, place, dot_tn(activated, grad_outer))
        gfc1[:, place] += dot_tn(normed, grad_inner)
        grad_normed += dot_nt(grad_inner, fc1[:, place])
    output[...] = total.astype(bf16)
    scaled = grad_normed * vecs[1:2, :]
    grad_middle = grad_output + inverse * (
        scaled
        - jnp.mean(scaled, axis=-1, keepdims=True)
        - normal * jnp.mean(scaled * normal, axis=-1, keepdims=True)
    )
    gmid_out[...] = grad_middle
    grad_branch = grad_middle.astype(bf16)
    add_tiles(gproj, slice(None), dot_tn(attended, grad_branch))
    gvec[0:1, :] += jnp.sum(grad_branch.astype(f32), axis=0, keepdims=True)
    gvec[1:2, :] += jnp.sum(grad_normed * normal, axis=0, keepdims=True)
    gvec[2:3, :] += jnp.sum(grad_normed, axis=0, keepdims=True)
    gvec[3:4, :] += jnp.sum(grad_output, axis=0, keepdims=True)
    lane = lane_of((rows, LANES))
    grad_attended = dot_nt(grad_branch, wproj[...])
    for head in range(HEADS):
        grad_head = grad_attended[:, head * LANES : (head + 1) * LANES]
        delta = jnp.sum(grad_head * o[head].astype(f32), axis=-1, keepdims=True)
        first, second, third = split3(-delta)
        tail = jnp.where(lane == 64, first, jnp.where(lane == 65, second, third))
        do_out[head] = jnp.where((lane >= 64) & (lane < 67), tail, grad_head).astype(bf16)


def feed_forward(frames, o, mixed, cot, wproj, fc1, fc2, vecs, fc1b, block=784, chunk=256):
    rows = mixed.shape[0]
    heads_spec = pl.BlockSpec((HEADS, block, LANES), lambda i: (0, i, 0))
    rows_spec = pl.BlockSpec((block, DIM), lambda i: (i, 0))

    def full(*shape):
        return pl.BlockSpec(shape, lambda i: (0,) * len(shape))

    return pl.pallas_call(
        functools.partial(middle_kernel, chunk=chunk),
        name="feed_forward",
        grid=(rows // block,),
        in_specs=[
            SMEM_SPEC, heads_spec, rows_spec, rows_spec,
            full(WIDE_HEADS, DIM), full(DIM, FFN), full(FFN, DIM), full(8, DIM), full(1, FFN),
        ],
        out_specs=[
            rows_spec, rows_spec, heads_spec,
            full(3, WIDE_HEADS, LANES), full(DIM, FFN), full(3, FFN, LANES), full(8, DIM), full(1, FFN),
        ],
        out_shape=[
            pltpu.HBM((rows, DIM), bf16),
            pltpu.HBM((rows, DIM), f32),
            pltpu.HBM((HEADS, rows, LANES), bf16),
            jax.ShapeDtypeStruct((3, WIDE_HEADS, LANES), f32),
            jax.ShapeDtypeStruct((DIM, FFN), f32),
            jax.ShapeDtypeStruct((3, FFN, LANES), f32),
            jax.ShapeDtypeStruct((8, DIM), f32),
            jax.ShapeDtypeStruct((1, FFN), f32),
        ],
        compiler_params=params(22),
    )(frames, o, mixed, cot, wproj, fc1, fc2, vecs, fc1b)


def qkv_back_kernel(dq, dk, dv, normed, mixed, gmid, wqkv, convp, spread, padded, gqkv, gbias, gvec, gmix):
    block = pl.program_id(0)

    @pl.when(block == 0)
    def _():
        for ref in (gqkv, gbias, gvec):
            ref[...] = jnp.zeros(ref.shape, f32)

    normal, inverse = normalize(mixed[...])
    grads = jnp.concatenate([part[head] for part in (dq, dk, dv) for head in range(HEADS)], axis=1)
    grad_qkv = dot_tn(normed[...], grads)
    for tile in range(15):
        gqkv[tile] += grad_qkv[:, tile * LANES : (tile + 1) * LANES]
    gbias[...] += jnp.sum(grads.astype(f32), axis=0, keepdims=True)
    grad_normed = dot_nt(grads, wqkv[...])
    gvec[1:2, :] += jnp.sum(grad_normed * normal, axis=0, keepdims=True)
    gvec[2:3, :] += jnp.sum(grad_normed, axis=0, keepdims=True)
    scaled = grad_normed * convp[28:29, :]
    grad_mixed = gmid[...] + inverse * (
        scaled
        - jnp.mean(scaled, axis=-1, keepdims=True)
        - normal * jnp.mean(scaled * normal, axis=-1, keepdims=True)
    )
    gvec[0:1, :] += jnp.sum(grad_mixed, axis=0, keepdims=True)
    gmix[...] = grad_mixed
    for member in range(mixed.shape[0] // FRAME):
        high, low = pieces(gmix[192 * member : 192 * member + 208, :])
        padded[member] = dot(spread[member], high) + dot(spread[member], low)


def project_back(dq, dk, dv, normed, mixed, gmid, wqkv, convp, spread, block=PIECE):
    rows = mixed.shape[0]
    heads_spec = pl.BlockSpec((HEADS, block, LANES), lambda i: (0, i, 0))
    rows_spec = pl.BlockSpec((block, DIM), lambda i: (i, 0))

    def full(*shape):
        return pl.BlockSpec(shape, lambda i: (0,) * len(shape))

    return pl.pallas_call(
        qkv_back_kernel,
        name="qkv_back",
        grid=(rows // block,),
        in_specs=[heads_spec, heads_spec, heads_spec, rows_spec, rows_spec, rows_spec,
                  full(DIM, 3 * WIDE_HEADS), full(32, DIM), full(4, PAD_ROWS, 208)],
        out_specs=[pl.BlockSpec((4, PAD_ROWS, DIM), lambda i: (i, 0, 0)), full(15, DIM, LANES), full(1, 3 * WIDE_HEADS), full(8, DIM)],
        out_shape=[
            pltpu.HBM((rows // FRAME, PAD_ROWS, DIM), f32),
            jax.ShapeDtypeStruct((15, DIM, LANES), f32),
            jax.ShapeDtypeStruct((1, 3 * WIDE_HEADS), f32),
            jax.ShapeDtypeStruct((8, DIM), f32),
        ],
        scratch_shapes=[pltpu.VMEM((block, DIM), f32)],
        compiler_params=params(18),
    )(dq, dk, dv, normed, mixed, gmid, wqkv, convp, spread)


def conv_weight_kernel(frames_ref, xsource, gsource, gvec, out, xpad, gpad, moved, sums, tiles, flat, xsem, gsem):
    frames = frames_ref[0]
    count = xpad.shape[0]
    copies = []
    for group in range(count // 4):
        place = pl.ds(4 * group, 4)
        copies.append(pltpu.make_async_copy(xsource.at[place], xpad.at[place], xsem.at[group]))
        copies.append(pltpu.make_async_copy(gsource.at[place], gpad.at[place], gsem.at[group]))
    for copy in copies:
        copy.start()
    sums[...] = jnp.zeros(sums.shape, f32)

    def weight_frame(frame, carry):
        for low, high in TILES:
            body = gpad[frame, 16 : 16 + BODY, low:high]
            moved[0, :, low:high] = pltpu.roll(body, BODY - 1, axis=0)
            moved[1, :, low:high] = pltpu.roll(body, 1, axis=0)
        for a in (-1, 0, 1):
            at = frame + a

            @pl.when((at >= 0) & (at < frames))
            def _():
                for low, high in TILES:
                    for b in (-1, 0, 1):
                        cells = xpad[at, 16 + b * 16 : 16 + b * 16 + BODY, low:high]
                        for c in range(3):
                            body = (
                                gpad[frame, 16 : 16 + BODY, low:high]
                                if c == 1
                                else moved[c // 2, :, low:high]
                            )
                            product = (body * cells).reshape(BODY // 8, 8, high - low)
                            tap = 9 * (a + 1) + 3 * (b + 1) + c
                            sums[tap, :, low:high] += jnp.sum(product, axis=0)

        return carry

    for group in range(count // 4):
        copies[2 * group].wait()
        copies[2 * group + 1].wait()
        start = max(4 * group - 1, 0)
        stop = 4 * group + 3 if group < count // 4 - 1 else count
        lax.fori_loop(jnp.minimum(start, frames), jnp.minimum(stop, frames), weight_frame, 0)
    tiles[...] = jnp.zeros(tiles.shape, f32)
    flat[...] = jnp.zeros(flat.shape, f32)
    for tile, (low, high) in enumerate(TILES):
        tiles[tile, 0:27, : high - low] = jnp.sum(sums[:, :, low:high], axis=1)
        tiles[tile, 27:30, : high - low] = gvec[0:3, low:high]
    for parity in range(2):
        for j in range(5):
            value = tiles[j // 2, pl.ds(parity, 15, stride=2), :]
            put_half(flat, AT_CONV + parity * 5 + j, value, j % 2, 5, 15)
    out[...] = flat[...].astype(bf16)


def conv_weight_grads(frames, xpad, gpad, gvec):
    return pl.pallas_call(
        conv_weight_kernel,
        name="conv_weight_grads",
        in_specs=[SMEM_SPEC, HBM_SPEC, HBM_SPEC, VMEM_SPEC],
        out_shape=jax.ShapeDtypeStruct((80, LANES), bf16),
        scratch_shapes=[
            pltpu.VMEM(xpad.shape, f32),
            pltpu.VMEM(gpad.shape, f32),
            pltpu.VMEM((2, BODY, DIM), f32),
            pltpu.VMEM((27, 8, DIM), f32),
            pltpu.VMEM((3, 32, LANES), f32),
            pltpu.VMEM((80, LANES), f32),
            pltpu.SemaphoreType.DMA((xpad.shape[0] // 4,)),
            pltpu.SemaphoreType.DMA((xpad.shape[0] // 4,)),
        ],
        compiler_params=params(18),
    )(frames, in_hbm(xpad), in_hbm(gpad), gvec)


def token_piece_kernel(piece, frames_ref, convp, gsource, back, *refs):
    if piece > 0:
        refs = refs[1:]
    gtok, passed, masked, slots, sums, comp, rows, sem = refs
    frames = frames_ref[0]
    passed[0] = frames
    copies = fetch_frames(gsource, slots, sem, piece)
    for copy in copies:
        copy.start()
    rows[...] = jnp.zeros(rows.shape, f32)
    copies[0].wait()

    def each(member, carry):
        @pl.when(member == 1)
        def _():
            copies[1].wait()

        frame = 4 * piece + member
        there = frame < frames
        before = there & (frame > 0)
        after = frame + 1 < frames
        mask_weights(convp, masked, after, there, before)
        at = (member + jnp.where(before, 0, 1), member + 1, member + jnp.where(after, 2, 1))
        mix_frame(slots, at, masked, sums, comp, -1)
        place = pl.ds(pl.multiple_of(192 * member, 16), 208)
        rows[place, :] += dot(back[member], comp[...].astype(bf16))
        return carry

    lax.fori_loop(0, 4, each, 0)
    gtok[...] = rows[...].astype(bf16)


def token_piece(piece, frames, convp, gpad, back, gtok):
    count = gpad.shape[0]
    operands = [frames, convp, in_hbm(gpad), back] + ([] if piece == 0 else [gtok])
    return pl.pallas_call(
        functools.partial(token_piece_kernel, piece),
        name=f"token_piece{piece}",
        grid=(1,),
        in_specs=[SMEM_SPEC, VMEM_SPEC, HBM_SPEC, VMEM_SPEC] + [ANY_SPEC] * (piece > 0),
        out_specs=[pl.BlockSpec((PIECE, DIM), lambda i: (piece, 0)), SMEM_SPEC],
        out_shape=[
            jax.ShapeDtypeStruct((count * FRAME, DIM), bf16),
            jax.ShapeDtypeStruct((1,), jnp.int32),
        ],
        input_output_aliases={4: 0} if piece else {},
        scratch_shapes=[
            pltpu.VMEM((32, DIM), f32),
            pltpu.VMEM((6, PAD_ROWS, DIM), f32),
            pltpu.VMEM((3, BODY, DIM), f32),
            pltpu.VMEM((BODY, DIM), f32),
            pltpu.VMEM((PIECE, DIM), f32),
            pltpu.SemaphoreType.DMA((2,)),
        ],
        compiler_params=params(10),
    )(*operands)


def put_half(flat, index, value, side, step=1, count=1):
    row, wanted = divmod(index, 2)
    place = pl.ds(row, count, stride=step) if step > 1 else pl.ds(row, count)
    lane = lane_of(value.shape)
    if wanted == 0:
        flat[place, :] += jnp.where(lane < 64, low_half(value, side), 0.0)
    else:
        flat[place, :] += jnp.where(lane >= 64, high_half(value, side), 0.0)


def put_vector(flat, index, value):
    width = value.shape[1]
    for j in range(width // 64):
        low = (j // 2) * LANES
        part = value[:, low : min(low + LANES, width)]
        if part.shape[1] < LANES:
            part = jnp.concatenate([part, jnp.zeros((1, 64), f32)], axis=1)
        put_half(flat, index + j, part, j % 2)


PACK_BASE = 2432


def pack_main_kernel(gproj, gfc1, gfc2, gvec, gfc1b, out, flat):
    flat[...] = jnp.zeros(flat.shape, f32)
    for parity in range(2):
        for j in range(5):
            for head in range(HEADS):
                value = gproj[j // 2, pl.ds(head * LANES + parity, 32, stride=2), :]
                put_half(flat, AT_PROJ + (64 * head + parity) * 5 + j, value, j % 2, 5, 32)
            value = gfc2[j // 2, pl.ds(parity, FFN // 2, stride=2), :]
            put_half(flat, AT_FC2 + parity * 5 + j, value, j % 2, 5, FFN // 2)
    for j in range(20):
        value = gfc1[:, (j // 2) * LANES : (j // 2 + 1) * LANES]
        put_half(flat, AT_FC1 + j, value, j % 2, 10, DIM)
    for row in range(3):
        put_vector(flat, AT_VEC + 5 * row, gvec[row : row + 1, :])
    put_vector(flat, AT_FC2B, gvec[3:4, :])
    put_vector(flat, AT_FC1B, gfc1b[...])
    out[...] = flat[...].astype(bf16)


def pack_main(gproj, gfc1, gfc2, gvec, gfc1b, rows):
    return pl.pallas_call(
        pack_main_kernel,
        name="pack_main",
        out_shape=jax.ShapeDtypeStruct((rows, LANES), bf16),
        scratch_shapes=[pltpu.VMEM((rows, LANES), f32)],
        compiler_params=params(14),
    )(gproj, gfc1, gfc2, gvec, gfc1b)


QKV_ROWS = 2480


def pack_qkv_kernel(gqkv, gbias, out, end, flat):
    flat[...] = jnp.zeros(flat.shape, f32)
    for parity in range(2):
        for j in range(15):
            value = gqkv[j, pl.ds(parity, DIM // 2, stride=2), :]
            put_half(flat, AT_QKV + parity * 15 + j, value, 0, 15, DIM // 2)
    for j in range(10):
        tile = j if j < 5 else j + 5
        put_half(flat, AT_QV + j, gbias[:, tile * LANES : (tile + 1) * LANES], 0)
    out[...] = flat[:PACK_BASE, :].astype(bf16)
    end[...] = flat[PACK_BASE:, :].astype(bf16)


def pack_qkv(gqkv, gbias):
    return pl.pallas_call(
        pack_qkv_kernel,
        name="pack_qkv",
        out_shape=[
            jax.ShapeDtypeStruct((PACK_BASE, LANES), bf16),
            jax.ShapeDtypeStruct((QKV_ROWS - PACK_BASE, LANES), bf16),
        ],
        scratch_shapes=[pltpu.VMEM((QKV_ROWS, LANES), f32)],
        compiler_params=params(10),
    )(gqkv, gbias)


AXES = ("wide", "narrow")


def exchange(value, bit):
    count = lax.axis_size(AXES)
    return lax.ppermute(value, AXES, [(i, i ^ (1 << bit)) for i in range(count)])


def my_bit(bit):
    return (lax.axis_index(AXES) >> bit) & 1


def tie(*values):
    return lax.optimization_barrier(values)


def halve(value, bits):
    for bit in range(bits):
        value = value.reshape(value.shape[0] // 2, 2, -1, LANES)
        mine = my_bit(bit)
        keep = lax.dynamic_index_in_dim(value, mine, 1, keepdims=False)
        give = lax.dynamic_index_in_dim(value, 1 - mine, 1, keepdims=False)
        value = keep + exchange(give, bit)
    return value[0]


def on_device(master, momentum, average, tokens, clip_ids, borders, cotangent):
    wide_count, narrow_count = lax.axis_size("wide"), lax.axis_size("narrow")
    count = wide_count * narrow_count
    bits = count.bit_length() - 1
    own_rows = master.shape[0]
    frames = (jnp.sum((clip_ids >= 0).astype(jnp.int32)) // FRAME).reshape(1)
    me = lax.axis_index(AXES)
    quarter = me >> (bits - 2)
    blocks = master.astype(bf16)[None]
    other = exchange(blocks, bits - 2)
    xpad, spread, back, frames = prepare(frames, tokens.T)
    other, frames = tie(other, frames)
    blocks = jnp.concatenate([blocks, other], axis=0)
    blocks, frames = tie(blocks, frames)
    other = exchange(blocks, bits - 1)
    cotangent, frames = turn(frames, cotangent.T)
    other, frames = tie(other, frames)
    blocks = jnp.concatenate([blocks, other], axis=0)
    first = lax.dynamic_index_in_dim(blocks, quarter, 0)
    rest = [lax.dynamic_index_in_dim(blocks, quarter ^ index, 0) for index in (1, 2, 3)]
    rest = jnp.concatenate(rest, axis=0)[None]
    low_bits = list(range(bits - 3, -1, -1))
    for step, bit in enumerate(low_bits):
        first = jnp.concatenate([first, exchange(first, bit)], axis=0)
        if step == 0:
            first, rest, frames = tie(first, rest, frames)
            rest = jnp.concatenate([rest, exchange(rest, bit)], axis=0)
    order = [0] * (count // 4)
    for step, bit in enumerate(low_bits):
        order = [place | (((index >> bit) & 1) << step) for index, place in enumerate(order)]
    mine = sum((((me >> bit) & 1) << step) for step, bit in enumerate(low_bits))
    order = jnp.array(order, jnp.int32) ^ mine
    head = lax.dynamic_index_in_dim(first, mine, 0, keepdims=False)
    head = jnp.concatenate([head, jnp.zeros((4, LANES), bf16)], axis=0)[:80] if own_rows < 80 else head[:80]
    mixed, convp = None, None
    for step, bit in enumerate(low_bits[1:]):
        if step < 2:
            rest, frames = tie(rest, frames)
        other = exchange(rest, bit)
        if step == 0:
            mixed, convp, frames = conv_piece(0, frames, head, xpad, back, None)
        elif step == 1:
            mixed, convp, frames = conv_piece(1, frames, head, xpad, back, mixed)
            mixed, convp, frames = conv_piece(2, frames, head, xpad, back, mixed)
        other, frames = tie(other, frames)
        rest = jnp.concatenate([rest, other], axis=0)
    wqkv, wproj, fc1, fc2, bqkv, vecs, fc1b = unpack(order, first, rest)
    normed, q, k, v, size = project(frames, mixed, convp, wqkv, bqkv)
    o, q_back = attend(q, k, v, size)
    output, gmid, do, gproj, gfc1, gfc2, gvec, gfc1b = feed_forward(
        frames, o, mixed, cotangent, wproj, fc1, fc2, vecs, fc1b
    )
    main = pack_main(gproj, gfc1, gfc2, gvec, gfc1b, count * own_rows)
    main = main.reshape(wide_count, narrow_count, own_rows, LANES)
    main = lax.psum_scatter(main, "wide", scatter_dimension=0, tiled=True)[0]
    q_back, do, k, v = (in_hbm(value) for value in (q_back, do, k, v))
    dq, dk, dv = attend_back(q_back, do, k, v)
    gpad, gqkv, gbias, gvec_one = project_back(dq, dk, dv, normed, mixed, gmid, wqkv, convp, spread)
    qkv, qkv_end = pack_qkv(gqkv, gbias)
    qkv = halve(qkv.reshape(count // 4, own_rows, LANES), bits - 2)
    for bit in (bits - 2, bits - 1):
        qkv = qkv + exchange(qkv, bit)
    conv = conv_weight_grads(frames, xpad, gpad, gvec_one)
    late = jnp.concatenate([conv, qkv_end], axis=0)
    main, late = tie(main, late)
    main = halve(main, narrow_count.bit_length() - 1)
    gtok = None
    for bit in range(bits):
        late, frames = tie(late, frames)
        other = exchange(late, bit)
        if bit < 3:
            gtok, frames = token_piece(bit, frames, convp, gpad, back, gtok)
        elif bit == 3:
            output, frames = turn(frames, output)
        elif bit == 4:
            gtok, frames = turn(frames, gtok)
        other, frames = tie(other, frames)
        late = late + other
    early = jnp.where(me < count // 4, qkv.astype(f32), main.astype(f32))
    conv, qkv_end = late[:80].astype(f32), late[80:].astype(f32)
    if own_rows < 80:
        conv = conv[:own_rows]
    conv = jnp.pad(conv, ((0, own_rows - conv.shape[0]), (0, 0)))
    qkv_end = jnp.pad(qkv_end, ((0, own_rows - qkv_end.shape[0]), (0, 0)))
    owned = early + jnp.where(me == 0, conv, jnp.where(me == count // 4, qkv_end, 0.0))
    rate = RATE_FACTOR / math.sqrt(tokens.shape[0] * count)
    decayed = owned + DECAY_RATE * master
    new_momentum = MOMENTUM * momentum + decayed
    new_master = master - rate * (decayed + MOMENTUM * new_momentum)
    new_average = AVERAGE_KEEP * average + (1.0 - AVERAGE_KEEP) * new_master
    return (output.T, gtok.T, owned, new_master, new_momentum, new_average, new_master.astype(bf16))


def solution(mesh):
    rows = P(("wide", "narrow"), None)
    return jax.shard_map(
        on_device,
        mesh=mesh,
        in_specs=(rows, rows, rows, rows, P(("wide", "narrow")), P(("wide", "narrow")), rows),
        out_specs=(rows,) * 7,
        check_vma=False,
    )
```

```python
import functools
import math

import jax
import jax.numpy as jnp
from jax import lax
from jax.experimental import pallas as pl
from jax.experimental.pallas import tpu as pltpu
from jax.sharding import PartitionSpec as P

HEADS = 5
HEAD_DIM = 64
DIM = 320
FFN = 1280
SIDE = 14
FRAME = SIDE * SIDE
LANES = 128
WIDE_HEADS = HEADS * LANES

EPSILON = 1e-06
MOMENTUM = 0.9
DECAY_RATE = 0.0001
AVERAGE_KEEP = 0.8
RATE_FACTOR = 0.03
LOG2E = 1.0 / math.log(2.0)
LN2 = math.log(2.0)
INVERSE_ROOT_TWO_PI = 1.0 / math.sqrt(2.0 * math.pi)
BLOCKED = -(2.0**30)
SAFE_BOUND = 80.0

bf16 = jnp.bfloat16
f32 = jnp.float32

AT_CONV = 0
AT_QKV = 150
AT_QV = 4950
AT_PROJ = 4960
AT_VEC = 6560
AT_FC1 = 6575
AT_FC1B = 12975
AT_FC2 = 12995
AT_FC2B = 19395
HALF_END = 19400


SMEM_SPEC = pl.BlockSpec(memory_space=pltpu.SMEM)
VMEM_SPEC = pl.BlockSpec(memory_space=pltpu.VMEM)
ANY_SPEC = pl.BlockSpec(memory_space=pl.ANY)
HBM_SPEC = pl.BlockSpec(memory_space=pltpu.HBM)


def in_hbm(value):
    return pltpu.with_memory_space_constraint(value, pltpu.HBM)


def dot(a, b):
    return lax.dot_general(a, b, (((1,), (0,)), ((), ())), preferred_element_type=f32)


def dot_nt(a, b):
    return lax.dot_general(a, b, (((1,), (1,)), ((), ())), preferred_element_type=f32)


def dot_tn(a, b):
    return lax.dot_general(a, b, (((0,), (0,)), ((), ())), preferred_element_type=f32)


def params(limit=58):
    return pltpu.CompilerParams(vmem_limit_bytes=limit << 20)


def lane_of(shape):
    return lax.broadcasted_iota(jnp.int32, shape, len(shape) - 1)


def row_of(shape):
    return lax.broadcasted_iota(jnp.int32, shape, 0)


def low_half(value, side):
    return value if side == 0 else pltpu.roll(value, 64, axis=1)


def high_half(value, side):
    return value if side == 1 else pltpu.roll(value, 64, axis=1)


def split3(value):
    first = value.astype(bf16).astype(f32)
    rest = value - first
    second = rest.astype(bf16).astype(f32)
    return first, second, rest - second


def read_half(flat, at, length, step, count, parity, j):
    index = at + parity * length + j
    return flat[pl.ds(index // 2, count, stride=step), :], index % 2


def read_vector(flat, at, length):
    tiles = []
    lane = lane_of((1, LANES))
    for j in range(0, length, 2):
        row, side = divmod(at + j, 2)
        low = low_half(flat[row : row + 1, :], side)
        if j + 1 < length:
            row, side = divmod(at + j + 1, 2)
            tiles.append(jnp.where(lane < 64, low, high_half(flat[row : row + 1, :], side)))
        else:
            tiles.append(low[:, :64])
    return jnp.concatenate(tiles, axis=1)


def odd_matrix(flat, out, at, length, rows):
    pairs = rows // 2
    for parity in range(2):
        for tile in range((length + 1) // 2):
            low, side = read_half(flat, at, length, length, pairs, parity, 2 * tile)
            low = low_half(low, side)
            place = pl.ds(parity, pairs, stride=2)
            if 2 * tile + 1 < length:
                high, side = read_half(flat, at, length, length, pairs, parity, 2 * tile + 1)
                merged = jnp.where(lane_of(low.shape) < 64, low, high_half(high, side))
            else:
                merged = low
            out[tile, place, :] = merged


def unpack_kernel(order, first, rest, wqkv, wproj, fc1, fc2, bqkv, vecs, fc1b, flat, wide, tall):
    blocks, rows = first.shape[:2]
    for block in range(blocks):
        place = order[block]
        for quarter in range(4):
            start = (quarter * blocks + block) * rows
            value = first[place] if quarter == 0 else rest[place, quarter - 1]
            flat[start : start + rows, :] = value.astype(f32)
    for parity in range(2):
        for j in range(15):
            value, side = read_half(flat, AT_QKV, 15, 15, 160, parity, j)
            value = jnp.where(lane_of(value.shape) < 64, low_half(value, side), 0.0)
            wide[j, pl.ds(parity, 160, stride=2), :] = value
    for j in range(15):
        wqkv[:, j * LANES : (j + 1) * LANES] = wide[j].astype(bf16)
    lane = lane_of((1, LANES))
    for j in range(15):
        if 5 <= j < 10:
            bqkv[:, j * LANES : (j + 1) * LANES] = jnp.zeros((1, LANES), f32)
        else:
            row, side = divmod(AT_QV + (j if j < 5 else j - 5), 2)
            value = low_half(flat[row : row + 1, :], side)
            bqkv[:, j * LANES : (j + 1) * LANES] = jnp.where(lane < 64, value, 0.0)
    odd_matrix(flat, wide, AT_PROJ, 5, DIM)
    for head in range(HEADS):
        for tile in range(3):
            width = LANES if tile < 2 else 64
            columns = slice(tile * LANES, tile * LANES + width)
            part = wide[tile, head * 64 : head * 64 + 64, :width].astype(bf16)
            wproj[head * LANES : head * LANES + 64, columns] = part
        wproj[head * LANES + 64 : (head + 1) * LANES, :] = jnp.zeros((64, DIM), bf16)
    for row in range(3):
        vecs[row : row + 1, :] = read_vector(flat, AT_VEC + 5 * row, 5)
    vecs[3:4, :] = read_vector(flat, AT_FC2B, 5)
    vecs[4:8, :] = jnp.zeros((4, DIM), f32)
    fc1b[...] = read_vector(flat, AT_FC1B, 20)
    for tile in range(10):
        low, side = read_half(flat, AT_FC1, 20, 10, DIM, 0, 2 * tile)
        high, side_high = read_half(flat, AT_FC1, 20, 10, DIM, 0, 2 * tile + 1)
        merged = jnp.where(lane_of(low.shape) < 64, low_half(low, side), high_half(high, side_high))
        fc1[:, tile * LANES : (tile + 1) * LANES] = merged.astype(bf16)
    odd_matrix(flat, tall, AT_FC2, 5, FFN)
    for tile in range(3):
        width = LANES if tile < 2 else 64
        fc2[:, tile * LANES : tile * LANES + width] = tall[tile, :, :width].astype(bf16)


def unpack(order, first, rest):
    rows = 4 * first.shape[0] * first.shape[1]
    return pl.pallas_call(
        unpack_kernel,
        name="unpack",
        in_specs=[SMEM_SPEC, VMEM_SPEC, VMEM_SPEC],
        out_shape=[
            jax.ShapeDtypeStruct((DIM, 3 * WIDE_HEADS), bf16),
            jax.ShapeDtypeStruct((WIDE_HEADS, DIM), bf16),
            jax.ShapeDtypeStruct((DIM, FFN), bf16),
            jax.ShapeDtypeStruct((FFN, DIM), bf16),
            jax.ShapeDtypeStruct((1, 3 * WIDE_HEADS), f32),
            jax.ShapeDtypeStruct((8, DIM), f32),
            jax.ShapeDtypeStruct((1, FFN), f32),
        ],
        scratch_shapes=[
            pltpu.VMEM((rows, LANES), f32),
            pltpu.VMEM((15, DIM, LANES), f32),
            pltpu.VMEM((3, FFN, LANES), f32),
        ],
        compiler_params=params(16),
    )(order, first, rest)


PAD_ROWS = 16 * 16
BODY = SIDE * 16


def spread_matrix(shift):
    cell = lax.broadcasted_iota(jnp.int32, (PAD_ROWS, 208), 0)
    source = lax.broadcasted_iota(jnp.int32, (PAD_ROWS, 208), 1)
    row, column = cell >> 4, cell & 15
    inside = (row >= 1) & (row <= SIDE) & (column < SIDE)
    wanted = (row - 1) * SIDE + column + shift
    return jnp.where(inside & (source == wanted), 1.0, 0.0).astype(bf16)


def gather_matrix(shift):
    target = lax.broadcasted_iota(jnp.int32, (208, BODY), 0)
    cell = lax.broadcasted_iota(jnp.int32, (208, BODY), 1)
    row, column = cell >> 4, cell & 15
    wanted = row * SIDE + column + shift
    return jnp.where((column < SIDE) & (target == wanted), 1.0, 0.0).astype(bf16)


TILES = ((0, 128), (128, 256), (256, 320))


def pieces(value):
    first = value.astype(bf16)
    return first, (value - first.astype(f32)).astype(bf16)


def prepare_kernel(frames, turned, target, spread, back, passed, tokens, padded, sems):
    for member in range(4):
        spread[member] = spread_matrix(4 * member)
        back[member] = gather_matrix(4 * member)
    passed[0] = frames[0]
    tokens[...] = turned[...].T

    def fill(frame, carry):
        member = frame & 3
        place = pl.ds(pl.multiple_of(frame * FRAME - 4 * member, 16), 208)
        padded[frame] = dot(spread[member], tokens[place, :])
        return carry

    copies = []
    for group in range(padded.shape[0] // 4):
        lax.fori_loop(4 * group, 4 * group + 4, fill, 0)
        place = pl.ds(4 * group, 4)
        copies.append(pltpu.make_async_copy(padded.at[place], target.at[place], sems.at[group]))
        copies[-1].start()
    for copy in copies:
        copy.wait()


def prepare(frames, turned):
    rows = turned.shape[1]
    return pl.pallas_call(
        prepare_kernel,
        name="prepare",
        in_specs=[SMEM_SPEC, VMEM_SPEC],
        out_specs=[HBM_SPEC, VMEM_SPEC, VMEM_SPEC, SMEM_SPEC],
        out_shape=[
            pltpu.HBM((rows // FRAME, PAD_ROWS, DIM), f32),
            jax.ShapeDtypeStruct((4, PAD_ROWS, 208), bf16),
            jax.ShapeDtypeStruct((4, 208, BODY), bf16),
            jax.ShapeDtypeStruct((1,), jnp.int32),
        ],
        scratch_shapes=[
            pltpu.VMEM((rows, DIM), bf16),
            pltpu.VMEM((rows // FRAME, PAD_ROWS, DIM), f32),
            pltpu.SemaphoreType.DMA((rows // FRAME // 4,)),
        ],
        compiler_params=params(16),
    )(frames, turned)


PIECE = 4 * FRAME


def fetch_frames(source, slots, sems, piece):
    first, last = max(4 * piece - 1, 0), min(4 * piece + 5, source.shape[0])
    middle = 4 * piece + 2
    copies = []
    for index, (start, stop) in enumerate(((first, middle), (middle, last))):
        slot = start - (4 * piece - 1)
        copies.append(
            pltpu.make_async_copy(
                source.at[pl.ds(start, stop - start)], slots.at[pl.ds(slot, stop - start)], sems.at[index]
            )
        )
    return copies


def mix_frame(slots, at, weights, sums, out, sign):
    for low, high in TILES:
        for start in range(0, BODY, 56):
            parts = [None, None, None]
            for a in (-1, 0, 1):
                for b in (-1, 0, 1):
                    begin = 16 + sign * b * 16 + start
                    cells = slots[at[1 + sign * a], begin : begin + 56, low:high]
                    for c in range(3):
                        tap = 9 * (a + 1) + 3 * (b + 1) + c
                        term = cells * weights[tap : tap + 1, low:high]
                        parts[c] = term if parts[c] is None else parts[c] + term
            parts[1] = parts[1] + slots[at[1], 16 + start : 16 + start + 56, low:high]
            for c in range(3):
                sums[c, start : start + 56, low:high] = parts[c]
    before, after = (0, 2) if sign == 1 else (2, 0)
    for low, high in TILES:
        out[:, low:high] = (
            sums[1, :, low:high]
            + pltpu.roll(sums[before, :, low:high], 1, axis=0)
            + pltpu.roll(sums[after, :, low:high], BODY - 1, axis=0)
        )


def mask_weights(weights, masked, first, middle, last):
    for tap in range(27):
        keep = (first, middle, last)[tap // 9]
        scale = 1.0 if tap == 13 else jnp.where(keep, 1.0, 0.0)
        masked[tap : tap + 1, :] = weights[tap : tap + 1, :] * scale


def conv_params(head, flat, weights):
    flat[...] = head[...].astype(f32)
    for parity in range(2):
        for tile in range(3):
            low, side = read_half(flat, AT_CONV, 5, 5, 15, parity, 2 * tile)
            low = low_half(low, side)
            place = pl.ds(parity, 15, stride=2)
            if tile < 2:
                high, side = read_half(flat, AT_CONV, 5, 5, 15, parity, 2 * tile + 1)
                low = jnp.where(lane_of(low.shape) < 64, low, high_half(high, side))
            weights[tile, place, :] = low


def turn_kernel(frames, source, out, passed):
    passed[0] = frames[0]
    out[...] = source[...].T


def turn(frames, value):
    rows, columns = value.shape
    return pl.pallas_call(
        turn_kernel,
        name="turn",
        in_specs=[SMEM_SPEC, VMEM_SPEC],
        out_specs=[VMEM_SPEC, SMEM_SPEC],
        out_shape=[
            jax.ShapeDtypeStruct((columns, rows), value.dtype),
            jax.ShapeDtypeStruct((1,), jnp.int32),
        ],
        compiler_params=params(10),
        cost_estimate=pl.CostEstimate(flops=0, bytes_accessed=4 * rows * columns, transcendentals=0),
    )(frames, value)


def conv_piece_kernel(piece, frames_ref, head, padded, back, *refs):
    if piece > 0:
        refs = refs[1:]
    mixed, convp, passed, flat, weights, masked, slots, sums, comp, sem = refs
    passed[0] = frames_ref[0]
    copies = fetch_frames(padded, slots, sem, piece)
    for copy in copies:
        copy.start()
    frames = frames_ref[0]
    conv_params(head, flat, weights)
    for tile, (low, high) in enumerate(TILES):
        convp[:, low:high] = weights[tile, :, : high - low]
    mixed[...] = jnp.zeros(mixed.shape, f32)
    copies[0].wait()

    def each(member, carry):
        @pl.when(member == 1)
        def _():
            copies[1].wait()

        frame = 4 * piece + member
        there = frame < frames
        before = there & (frame > 0)
        after = frame + 1 < frames
        mask_weights(convp, masked, before, there, after)
        at = (member + jnp.where(before, 0, 1), member + 1, member + jnp.where(after, 2, 1))
        mix_frame(slots, at, masked, sums, comp, 1)
        high, low = pieces(comp[...] + convp[27:28, :])
        place = pl.ds(pl.multiple_of(192 * member, 16), 208)
        mixed[place, :] += dot(back[member], high) + dot(back[member], low)
        return carry

    lax.fori_loop(0, 4, each, 0)


def conv_piece(piece, frames, head, padded, back, mixed):
    rows = padded.shape[0] * FRAME
    operands = [frames, head, in_hbm(padded), back] + ([] if piece == 0 else [mixed])
    return pl.pallas_call(
        functools.partial(conv_piece_kernel, piece),
        name=f"conv_piece{piece}",
        grid=(1,),
        in_specs=[SMEM_SPEC, VMEM_SPEC, HBM_SPEC, VMEM_SPEC] + [ANY_SPEC] * (piece > 0),
        out_specs=[
            pl.BlockSpec((PIECE, DIM), lambda i: (piece, 0)),
            pl.BlockSpec((32, DIM), lambda i: (0, 0)),
            SMEM_SPEC,
        ],
        out_shape=[
            jax.ShapeDtypeStruct((rows, DIM), f32),
            jax.ShapeDtypeStruct((32, DIM), f32),
            jax.ShapeDtypeStruct((1,), jnp.int32),
        ],
        input_output_aliases={4: 0} if piece else {},
        scratch_shapes=[
            pltpu.VMEM(head.shape, f32),
            pltpu.VMEM((3, 32, LANES), f32),
            pltpu.VMEM((32, DIM), f32),
            pltpu.VMEM((6, PAD_ROWS, DIM), f32),
            pltpu.VMEM((3, BODY, DIM), f32),
            pltpu.VMEM((BODY, DIM), f32),
            pltpu.SemaphoreType.DMA((2,)),
        ],
        compiler_params=params(10),
    )(*operands)


def normalize(values):
    centered = values - jnp.mean(values, axis=-1, keepdims=True)
    variance = jnp.mean(centered * centered, axis=-1, keepdims=True)
    inverse = lax.rsqrt(variance + EPSILON)
    return centered * inverse, inverse


def row_size(value):
    part = jnp.where(lane_of(value.shape) < HEAD_DIM, value.astype(f32), 0.0)
    return jnp.sum(part * part, axis=-1, keepdims=True)


def qkv_kernel(frames_ref, mixed, convp, wqkv, bqkv, normed_out, q_out, k_out, v_out, size):
    block = pl.program_id(0)
    rows = mixed.shape[0]
    frames = frames_ref[0]
    normal, unused_inverse = normalize(mixed[...])
    normed = (normal * convp[28:29, :] + convp[29:30, :]).astype(bf16)
    normed_out[...] = normed
    lane = lane_of((rows, LANES))
    inside = row_of((rows, LANES)) + block * rows < frames * FRAME
    q_mask = jnp.where(
        ((lane == 64) & ~inside) | ((lane == 65) & inside), BLOCKED, 0.0
    )
    k_mask = jnp.where(
        ((lane == 64) & inside) | ((lane == 65) & ~inside) | ((lane >= 66) & (lane < 69)), 1.0, 0.0
    )
    v_mask = jnp.where((lane >= 64) & (lane < 67), 1.0, 0.0)
    scale = HEAD_DIM ** (-0.5) * LOG2E

    @pl.when(block == 0)
    def _():
        size[...] = jnp.zeros(size.shape, f32)

    projected = dot(normed, wqkv[...])
    for head in range(HEADS):

        def columns(kind, head=head):
            place = slice((kind * HEADS + head) * LANES, (kind * HEADS + head + 1) * LANES)
            return projected[:, place] + bqkv[:, place]

        query = (columns(0) * scale + q_mask).astype(bf16)
        key = (columns(1) + k_mask).astype(bf16)
        query_size = jnp.max(row_size(query), axis=0, keepdims=True)
        key_size = jnp.max(row_size(key), axis=0, keepdims=True)
        q_out[head] = query
        k_out[head] = key
        v_out[head] = (columns(2) + v_mask).astype(bf16)
        size[head : head + 1, :] = jnp.maximum(size[head : head + 1, :], query_size)
        size[head + 8 : head + 9, :] = jnp.maximum(size[head + 8 : head + 9, :], key_size)


def project(frames, mixed, convp, wqkv, bqkv, block=784):
    rows = mixed.shape[0]
    heads_spec = pl.BlockSpec((HEADS, block, LANES), lambda i: (0, i, 0))
    rows_spec = pl.BlockSpec((block, DIM), lambda i: (i, 0))
    heads_shape = jax.ShapeDtypeStruct((HEADS, rows, LANES), bf16)
    return pl.pallas_call(
        qkv_kernel,
        name="qkv_forward",
        grid=(rows // block,),
        in_specs=[
            SMEM_SPEC,
            rows_spec,
            pl.BlockSpec((32, DIM), lambda i: (0, 0)),
            pl.BlockSpec((DIM, 3 * WIDE_HEADS), lambda i: (0, 0)),
            pl.BlockSpec((1, 3 * WIDE_HEADS), lambda i: (0, 0)),
        ],
        out_specs=[rows_spec, heads_spec, heads_spec, heads_spec, pl.BlockSpec((16, LANES), lambda i: (0, 0))],
        out_shape=[
            pltpu.HBM((rows, DIM), bf16),
            heads_shape,
            heads_shape,
            heads_shape,
            jax.ShapeDtypeStruct((16, LANES), f32),
        ],
        compiler_params=params(14),
    )(frames, mixed, convp, wqkv, bqkv)


def attend_kernel(chunk, q, k, v, size, o_out, q_back, query, shift):
    head = pl.program_id(0)
    keys = k.shape[1]
    tall = q.shape[1]
    bound = jnp.max(size[pl.ds(head, 1), :] * size[pl.ds(head + 8, 1), :])
    query[...] = q[0]
    shift[...] = jnp.zeros(shift.shape, f32)

    @pl.when(bound > SAFE_BOUND * SAFE_BOUND)
    def _():
        shift[...] = jnp.full(shift.shape, -jnp.inf, f32)

        def peak(step, carry):
            scores = dot_nt(k[0, pl.ds(pl.multiple_of(step * 112, 16), 112), :], q[0])
            shift[...] = jnp.maximum(shift[...], jnp.max(scores, axis=0, keepdims=True))
            return carry

        lax.fori_loop(0, keys // 112, peak, 0)
        first, second, third = split3(-shift[...])
        row = row_of((LANES, tall))
        tail = jnp.where(row == 66, first, jnp.where(row == 67, second, jnp.where(row == 68, third, 0.0)))
        query[...] = (q[0].astype(f32) + tail.T).astype(bf16)

    total = None
    for start in range(0, keys, chunk):
        place = slice(start, min(start + chunk, keys))
        weights = jnp.exp2(dot_nt(k[0, place, :], query[...])).astype(bf16)
        part = dot_tn(v[0, place, :], weights)
        total = part if total is None else total + part
    sums = total[64:65, :]
    first, second, third = split3(-(shift[...] + jnp.log2(sums)))
    row = row_of((8, tall))
    tail = jnp.where(row == 2, first, jnp.where(row == 3, second, jnp.where(row == 4, third, 0.0)))
    stacked = jnp.concatenate([total[:64, :] / sums, tail, jnp.zeros((56, tall), f32)], axis=0).T
    lane = lane_of((tall, LANES))
    o_out[0] = jnp.where(lane < 64, stacked, 0.0).astype(bf16)
    q_back[0] = jnp.where((lane >= 66) & (lane < 69), stacked, q[0].astype(f32)).astype(bf16)


def attend(q, k, v, size, chunk=512):
    rows = q.shape[1]
    whole = pl.BlockSpec((1, rows, LANES), lambda h: (h, 0, 0))
    shape = jax.ShapeDtypeStruct((HEADS, rows, LANES), bf16)
    return pl.pallas_call(
        functools.partial(attend_kernel, chunk),
        name="attend",
        grid=(HEADS,),
        in_specs=[whole, whole, whole, pl.BlockSpec((16, LANES), lambda h: (0, 0))],
        out_specs=[whole, whole],
        out_shape=[shape, pltpu.HBM(shape.shape, bf16)],
        scratch_shapes=[pltpu.VMEM((rows, LANES), bf16), pltpu.VMEM((1, rows), f32)],
        compiler_params=params(18),
    )(q, k, v, size)


def attend_back_kernel(rows, q, do, k, v, dq_out, dk_out, dv_out, dq):
    step = pl.program_id(1)
    wide = k.shape[1]
    inside = row_of((wide, LANES)) + step * wide < rows
    key = jnp.where(inside, k[0], jnp.zeros((), bf16))
    value = jnp.where(inside, v[0], jnp.zeros((), bf16))
    weights = jnp.exp2(dot_nt(q[0], key))
    grad_scores = (weights * dot_nt(do[0], value)).astype(bf16)
    weights = weights.astype(bf16)
    dv_out[0] = dot_tn(do[0], weights).T.astype(bf16)
    dk_out[0] = (dot_tn(q[0], grad_scores) * LN2).T.astype(bf16)
    part = dot_nt(key.T, grad_scores)

    @pl.when(step == 0)
    def _():
        dq[...] = part

    @pl.when(step > 0)
    def _():
        dq[...] += part

    @pl.when(step == pl.num_programs(1) - 1)
    def _():
        dq_out[0] = (dq[...] * HEAD_DIM ** (-0.5)).T.astype(bf16)


def attend_back(q, do, k, v, wide=1280):
    heads, rows = q.shape[:2]
    block = pl.BlockSpec((1, wide, LANES), lambda h, i: (h, i, 0))
    whole = pl.BlockSpec((1, rows, LANES), lambda h, i: (h, 0, 0))
    shape = jax.ShapeDtypeStruct((heads, rows, LANES), bf16)
    return pl.pallas_call(
        functools.partial(attend_back_kernel, rows),
        name="attend_back",
        grid=(heads, pl.cdiv(rows, wide)),
        in_specs=[whole, whole, block, block],
        out_specs=[whole, block, block],
        out_shape=[shape, shape, shape],
        scratch_shapes=[pltpu.VMEM((LANES, rows), f32)],
        compiler_params=params(30),
    )(q, do, k, v)


def erf_parts(value):
    bell = jnp.exp(-0.5 * value * value)
    return bell, 0.5 * (1.0 + lax.erf(value * (1.0 / math.sqrt(2.0))))


def add_tiles(ref, place, value):
    for tile, (low, high) in enumerate(TILES):
        ref[tile, place, : high - low] += value[:, low:high]


def middle_kernel(
    frames_ref, o, mixed, cot, wproj, fc1, fc2, vecs, fc1b,
    output, gmid_out, do_out, gproj, gfc1, gfc2, gvec, gfc1b, chunk,
):
    block = pl.program_id(0)
    rows = mixed.shape[0]
    inside = row_of((rows, DIM)) + block * rows < frames_ref[0] * FRAME

    @pl.when(block == 0)
    def _():
        for ref in (gproj, gfc1, gfc2, gvec, gfc1b):
            ref[...] = jnp.zeros(ref.shape, f32)

    attended = jnp.concatenate([o[head] for head in range(HEADS)], axis=1)
    middle = mixed[...] + (dot(attended, wproj[...]) + vecs[0:1, :])
    normal, inverse = normalize(middle)
    normed = (normal * vecs[1:2, :] + vecs[2:3, :]).astype(bf16)
    grad_output = jnp.where(inside, cot[...].astype(f32), 0.0)
    grad_outer = grad_output.astype(bf16)
    total = middle + vecs[3:4, :]
    grad_normed = jnp.zeros((rows, DIM), f32)
    for start in range(0, FFN, chunk):
        place = slice(start, start + chunk)
        inner = dot(normed, fc1[:, place]) + fc1b[:, place]
        bell, gate = erf_parts(inner)
        activated = (inner * gate).astype(bf16)
        total += dot(activated, fc2[place, :])
        slope = gate + inner * bell * INVERSE_ROOT_TWO_PI
        grad_inner = (dot_nt(grad_outer, fc2[place, :]) * slope)
        gfc1b[:, place] += jnp.sum(grad_inner, axis=0, keepdims=True)
        grad_inner = grad_inner.astype(bf16)
        add_tiles(gfc2, place, dot_tn(activated, grad_outer))
        gfc1[:, place] += dot_tn(normed, grad_inner)
        grad_normed += dot_nt(grad_inner, fc1[:, place])
    output[...] = total.astype(bf16)
    scaled = grad_normed * vecs[1:2, :]
    grad_middle = grad_output + inverse * (
        scaled
        - jnp.mean(scaled, axis=-1, keepdims=True)
        - normal * jnp.mean(scaled * normal, axis=-1, keepdims=True)
    )
    gmid_out[...] = grad_middle
    grad_branch = grad_middle.astype(bf16)
    add_tiles(gproj, slice(None), dot_tn(attended, grad_branch))
    gvec[0:1, :] += jnp.sum(grad_branch.astype(f32), axis=0, keepdims=True)
    gvec[1:2, :] += jnp.sum(grad_normed * normal, axis=0, keepdims=True)
    gvec[2:3, :] += jnp.sum(grad_normed, axis=0, keepdims=True)
    gvec[3:4, :] += jnp.sum(grad_output, axis=0, keepdims=True)
    lane = lane_of((rows, LANES))
    grad_attended = dot_nt(grad_branch, wproj[...])
    for head in range(HEADS):
        grad_head = grad_attended[:, head * LANES : (head + 1) * LANES]
        delta = jnp.sum(grad_head * o[head].astype(f32), axis=-1, keepdims=True)
        first, second, third = split3(-delta)
        tail = jnp.where(lane == 64, first, jnp.where(lane == 65, second, third))
        do_out[head] = jnp.where((lane >= 64) & (lane < 67), tail, grad_head).astype(bf16)


def feed_forward(frames, o, mixed, cot, wproj, fc1, fc2, vecs, fc1b, block=784, chunk=256):
    rows = mixed.shape[0]
    heads_spec = pl.BlockSpec((HEADS, block, LANES), lambda i: (0, i, 0))
    rows_spec = pl.BlockSpec((block, DIM), lambda i: (i, 0))

    def full(*shape):
        return pl.BlockSpec(shape, lambda i: (0,) * len(shape))

    return pl.pallas_call(
        functools.partial(middle_kernel, chunk=chunk),
        name="feed_forward",
        grid=(rows // block,),
        in_specs=[
            SMEM_SPEC, heads_spec, rows_spec, rows_spec,
            full(WIDE_HEADS, DIM), full(DIM, FFN), full(FFN, DIM), full(8, DIM), full(1, FFN),
        ],
        out_specs=[
            rows_spec, rows_spec, heads_spec,
            full(3, WIDE_HEADS, LANES), full(DIM, FFN), full(3, FFN, LANES), full(8, DIM), full(1, FFN),
        ],
        out_shape=[
            pltpu.HBM((rows, DIM), bf16),
            pltpu.HBM((rows, DIM), f32),
            pltpu.HBM((HEADS, rows, LANES), bf16),
            jax.ShapeDtypeStruct((3, WIDE_HEADS, LANES), f32),
            jax.ShapeDtypeStruct((DIM, FFN), f32),
            jax.ShapeDtypeStruct((3, FFN, LANES), f32),
            jax.ShapeDtypeStruct((8, DIM), f32),
            jax.ShapeDtypeStruct((1, FFN), f32),
        ],
        compiler_params=params(22),
    )(frames, o, mixed, cot, wproj, fc1, fc2, vecs, fc1b)


def qkv_back_kernel(dq, dk, dv, normed, mixed, gmid, wqkv, convp, spread, padded, gqkv, gbias, gvec, gmix):
    block = pl.program_id(0)

    @pl.when(block == 0)
    def _():
        for ref in (gqkv, gbias, gvec):
            ref[...] = jnp.zeros(ref.shape, f32)

    normal, inverse = normalize(mixed[...])
    grads = jnp.concatenate([part[head] for part in (dq, dk, dv) for head in range(HEADS)], axis=1)
    grad_qkv = dot_tn(normed[...], grads)
    for tile in range(15):
        gqkv[tile] += grad_qkv[:, tile * LANES : (tile + 1) * LANES]
    gbias[...] += jnp.sum(grads.astype(f32), axis=0, keepdims=True)
    grad_normed = dot_nt(grads, wqkv[...])
    gvec[1:2, :] += jnp.sum(grad_normed * normal, axis=0, keepdims=True)
    gvec[2:3, :] += jnp.sum(grad_normed, axis=0, keepdims=True)
    scaled = grad_normed * convp[28:29, :]
    grad_mixed = gmid[...] + inverse * (
        scaled
        - jnp.mean(scaled, axis=-1, keepdims=True)
        - normal * jnp.mean(scaled * normal, axis=-1, keepdims=True)
    )
    gvec[0:1, :] += jnp.sum(grad_mixed, axis=0, keepdims=True)
    gmix[...] = grad_mixed
    for member in range(mixed.shape[0] // FRAME):
        high, low = pieces(gmix[192 * member : 192 * member + 208, :])
        padded[member] = dot(spread[member], high) + dot(spread[member], low)


def project_back(dq, dk, dv, normed, mixed, gmid, wqkv, convp, spread, block=PIECE):
    rows = mixed.shape[0]
    heads_spec = pl.BlockSpec((HEADS, block, LANES), lambda i: (0, i, 0))
    rows_spec = pl.BlockSpec((block, DIM), lambda i: (i, 0))

    def full(*shape):
        return pl.BlockSpec(shape, lambda i: (0,) * len(shape))

    return pl.pallas_call(
        qkv_back_kernel,
        name="qkv_back",
        grid=(rows // block,),
        in_specs=[heads_spec, heads_spec, heads_spec, rows_spec, rows_spec, rows_spec,
                  full(DIM, 3 * WIDE_HEADS), full(32, DIM), full(4, PAD_ROWS, 208)],
        out_specs=[pl.BlockSpec((4, PAD_ROWS, DIM), lambda i: (i, 0, 0)), full(15, DIM, LANES), full(1, 3 * WIDE_HEADS), full(8, DIM)],
        out_shape=[
            pltpu.HBM((rows // FRAME, PAD_ROWS, DIM), f32),
            jax.ShapeDtypeStruct((15, DIM, LANES), f32),
            jax.ShapeDtypeStruct((1, 3 * WIDE_HEADS), f32),
            jax.ShapeDtypeStruct((8, DIM), f32),
        ],
        scratch_shapes=[pltpu.VMEM((block, DIM), f32)],
        compiler_params=params(18),
    )(dq, dk, dv, normed, mixed, gmid, wqkv, convp, spread)


def conv_weight_kernel(frames_ref, xsource, gsource, gvec, out, xpad, gpad, moved, sums, tiles, flat, xsem, gsem):
    frames = frames_ref[0]
    count = xpad.shape[0]
    copies = []
    for group in range(count // 4):
        place = pl.ds(4 * group, 4)
        copies.append(pltpu.make_async_copy(xsource.at[place], xpad.at[place], xsem.at[group]))
        copies.append(pltpu.make_async_copy(gsource.at[place], gpad.at[place], gsem.at[group]))
    for copy in copies:
        copy.start()
    sums[...] = jnp.zeros(sums.shape, f32)

    def weight_frame(frame, carry):
        for low, high in TILES:
            body = gpad[frame, 16 : 16 + BODY, low:high]
            moved[0, :, low:high] = pltpu.roll(body, BODY - 1, axis=0)
            moved[1, :, low:high] = pltpu.roll(body, 1, axis=0)
        for a in (-1, 0, 1):
            at = frame + a

            @pl.when((at >= 0) & (at < frames))
            def _():
                for low, high in TILES:
                    for b in (-1, 0, 1):
                        cells = xpad[at, 16 + b * 16 : 16 + b * 16 + BODY, low:high]
                        for c in range(3):
                            body = (
                                gpad[frame, 16 : 16 + BODY, low:high]
                                if c == 1
                                else moved[c // 2, :, low:high]
                            )
                            product = (body * cells).reshape(BODY // 8, 8, high - low)
                            tap = 9 * (a + 1) + 3 * (b + 1) + c
                            sums[tap, :, low:high] += jnp.sum(product, axis=0)

        return carry

    for group in range(count // 4):
        copies[2 * group].wait()
        copies[2 * group + 1].wait()
        start = max(4 * group - 1, 0)
        stop = 4 * group + 3 if group < count // 4 - 1 else count
        lax.fori_loop(jnp.minimum(start, frames), jnp.minimum(stop, frames), weight_frame, 0)
    tiles[...] = jnp.zeros(tiles.shape, f32)
    flat[...] = jnp.zeros(flat.shape, f32)
    for tile, (low, high) in enumerate(TILES):
        tiles[tile, 0:27, : high - low] = jnp.sum(sums[:, :, low:high], axis=1)
        tiles[tile, 27:30, : high - low] = gvec[0:3, low:high]
    for parity in range(2):
        for j in range(5):
            value = tiles[j // 2, pl.ds(parity, 15, stride=2), :]
            put_half(flat, AT_CONV + parity * 5 + j, value, j % 2, 5, 15)
    out[...] = flat[...].astype(bf16)


def conv_weight_grads(frames, xpad, gpad, gvec):
    return pl.pallas_call(
        conv_weight_kernel,
        name="conv_weight_grads",
        in_specs=[SMEM_SPEC, HBM_SPEC, HBM_SPEC, VMEM_SPEC],
        out_shape=jax.ShapeDtypeStruct((80, LANES), bf16),
        scratch_shapes=[
            pltpu.VMEM(xpad.shape, f32),
            pltpu.VMEM(gpad.shape, f32),
            pltpu.VMEM((2, BODY, DIM), f32),
            pltpu.VMEM((27, 8, DIM), f32),
            pltpu.VMEM((3, 32, LANES), f32),
            pltpu.VMEM((80, LANES), f32),
            pltpu.SemaphoreType.DMA((xpad.shape[0] // 4,)),
            pltpu.SemaphoreType.DMA((xpad.shape[0] // 4,)),
        ],
        compiler_params=params(18),
    )(frames, in_hbm(xpad), in_hbm(gpad), gvec)


def token_piece_kernel(piece, frames_ref, convp, gsource, back, *refs):
    if piece > 0:
        refs = refs[1:]
    gtok, passed, masked, slots, sums, comp, rows, sem = refs
    frames = frames_ref[0]
    passed[0] = frames
    copies = fetch_frames(gsource, slots, sem, piece)
    for copy in copies:
        copy.start()
    rows[...] = jnp.zeros(rows.shape, f32)
    copies[0].wait()

    def each(member, carry):
        @pl.when(member == 1)
        def _():
            copies[1].wait()

        frame = 4 * piece + member
        there = frame < frames
        before = there & (frame > 0)
        after = frame + 1 < frames
        mask_weights(convp, masked, after, there, before)
        at = (member + jnp.where(before, 0, 1), member + 1, member + jnp.where(after, 2, 1))
        mix_frame(slots, at, masked, sums, comp, -1)
        place = pl.ds(pl.multiple_of(192 * member, 16), 208)
        rows[place, :] += dot(back[member], comp[...].astype(bf16))
        return carry

    lax.fori_loop(0, 4, each, 0)
    gtok[...] = rows[...].astype(bf16)


def token_piece(piece, frames, convp, gpad, back, gtok):
    count = gpad.shape[0]
    operands = [frames, convp, in_hbm(gpad), back] + ([] if piece == 0 else [gtok])
    return pl.pallas_call(
        functools.partial(token_piece_kernel, piece),
        name=f"token_piece{piece}",
        grid=(1,),
        in_specs=[SMEM_SPEC, VMEM_SPEC, HBM_SPEC, VMEM_SPEC] + [ANY_SPEC] * (piece > 0),
        out_specs=[pl.BlockSpec((PIECE, DIM), lambda i: (piece, 0)), SMEM_SPEC],
        out_shape=[
            jax.ShapeDtypeStruct((count * FRAME, DIM), bf16),
            jax.ShapeDtypeStruct((1,), jnp.int32),
        ],
        input_output_aliases={4: 0} if piece else {},
        scratch_shapes=[
            pltpu.VMEM((32, DIM), f32),
            pltpu.VMEM((6, PAD_ROWS, DIM), f32),
            pltpu.VMEM((3, BODY, DIM), f32),
            pltpu.VMEM((BODY, DIM), f32),
            pltpu.VMEM((PIECE, DIM), f32),
            pltpu.SemaphoreType.DMA((2,)),
        ],
        compiler_params=params(10),
    )(*operands)


def put_half(flat, index, value, side, step=1, count=1):
    row, wanted = divmod(index, 2)
    place = pl.ds(row, count, stride=step) if step > 1 else pl.ds(row, count)
    lane = lane_of(value.shape)
    if wanted == 0:
        flat[place, :] += jnp.where(lane < 64, low_half(value, side), 0.0)
    else:
        flat[place, :] += jnp.where(lane >= 64, high_half(value, side), 0.0)


def put_vector(flat, index, value):
    width = value.shape[1]
    for j in range(width // 64):
        low = (j // 2) * LANES
        part = value[:, low : min(low + LANES, width)]
        if part.shape[1] < LANES:
            part = jnp.concatenate([part, jnp.zeros((1, 64), f32)], axis=1)
        put_half(flat, index + j, part, j % 2)


PACK_BASE = 2432


def pack_main_kernel(gproj, gfc1, gfc2, gvec, gfc1b, out, flat):
    flat[...] = jnp.zeros(flat.shape, f32)
    for parity in range(2):
        for j in range(5):
            for head in range(HEADS):
                value = gproj[j // 2, pl.ds(head * LANES + parity, 32, stride=2), :]
                put_half(flat, AT_PROJ + (64 * head + parity) * 5 + j, value, j % 2, 5, 32)
            value = gfc2[j // 2, pl.ds(parity, FFN // 2, stride=2), :]
            put_half(flat, AT_FC2 + parity * 5 + j, value, j % 2, 5, FFN // 2)
    for j in range(20):
        value = gfc1[:, (j // 2) * LANES : (j // 2 + 1) * LANES]
        put_half(flat, AT_FC1 + j, value, j % 2, 10, DIM)
    for row in range(3):
        put_vector(flat, AT_VEC + 5 * row, gvec[row : row + 1, :])
    put_vector(flat, AT_FC2B, gvec[3:4, :])
    put_vector(flat, AT_FC1B, gfc1b[...])
    out[...] = flat[...].astype(bf16)


def pack_main(gproj, gfc1, gfc2, gvec, gfc1b, rows):
    return pl.pallas_call(
        pack_main_kernel,
        name="pack_main",
        out_shape=jax.ShapeDtypeStruct((rows, LANES), bf16),
        scratch_shapes=[pltpu.VMEM((rows, LANES), f32)],
        compiler_params=params(14),
    )(gproj, gfc1, gfc2, gvec, gfc1b)


QKV_ROWS = 2480


def pack_qkv_kernel(gqkv, gbias, out, end, flat):
    flat[...] = jnp.zeros(flat.shape, f32)
    for parity in range(2):
        for j in range(15):
            value = gqkv[j, pl.ds(parity, DIM // 2, stride=2), :]
            put_half(flat, AT_QKV + parity * 15 + j, value, 0, 15, DIM // 2)
    for j in range(10):
        tile = j if j < 5 else j + 5
        put_half(flat, AT_QV + j, gbias[:, tile * LANES : (tile + 1) * LANES], 0)
    out[...] = flat[:PACK_BASE, :].astype(bf16)
    end[...] = flat[PACK_BASE:, :].astype(bf16)


def pack_qkv(gqkv, gbias):
    return pl.pallas_call(
        pack_qkv_kernel,
        name="pack_qkv",
        out_shape=[
            jax.ShapeDtypeStruct((PACK_BASE, LANES), bf16),
            jax.ShapeDtypeStruct((QKV_ROWS - PACK_BASE, LANES), bf16),
        ],
        scratch_shapes=[pltpu.VMEM((QKV_ROWS, LANES), f32)],
        compiler_params=params(10),
    )(gqkv, gbias)


AXES = ("wide", "narrow")


def exchange(value, bit):
    count = lax.axis_size(AXES)
    return lax.ppermute(value, AXES, [(i, i ^ (1 << bit)) for i in range(count)])


def my_bit(bit):
    return (lax.axis_index(AXES) >> bit) & 1


def tie(*values):
    return lax.optimization_barrier(values)


def split(value, bit):
    value = value.reshape(value.shape[0] // 2, 2, -1, LANES)
    mine = my_bit(bit)
    keep = lax.dynamic_index_in_dim(value, mine, 1, keepdims=False)
    return keep, lax.dynamic_index_in_dim(value, 1 - mine, 1, keepdims=False)


def on_device(master, momentum, average, tokens, clip_ids, borders, cotangent):
    wide_count, narrow_count = lax.axis_size("wide"), lax.axis_size("narrow")
    count = wide_count * narrow_count
    bits = count.bit_length() - 1
    own_rows = master.shape[0]
    frames = (jnp.sum((clip_ids >= 0).astype(jnp.int32)) // FRAME).reshape(1)
    me = lax.axis_index(AXES)
    quarter = me >> (bits - 2)
    blocks = master.astype(bf16)[None]
    other = exchange(blocks, bits - 2)
    other, frames = tie(other, frames)
    blocks = jnp.concatenate([blocks, other], axis=0)
    blocks, frames = tie(blocks, frames)
    other = exchange(blocks, bits - 1)
    xpad, spread, back, frames = prepare(frames, tokens.T)
    other, frames = tie(other, frames)
    blocks = jnp.concatenate([blocks, other], axis=0)
    first = lax.dynamic_index_in_dim(blocks, quarter, 0)
    rest = [lax.dynamic_index_in_dim(blocks, quarter ^ index, 0) for index in (1, 2, 3)]
    rest = jnp.concatenate(rest, axis=0)[None]
    low_bits = list(range(bits - 3, -1, -1))
    for step, bit in enumerate(low_bits):
        if step == 0:
            first, frames = tie(first, frames)
        other = exchange(first, bit)
        if step == 0:
            cotangent, frames = turn(frames, cotangent.T)
            other, frames = tie(other, frames)
        first = jnp.concatenate([first, other], axis=0)
        if step == 0:
            first, rest, frames = tie(first, rest, frames)
            rest = jnp.concatenate([rest, exchange(rest, bit)], axis=0)
    order = [0] * (count // 4)
    for step, bit in enumerate(low_bits):
        order = [place | (((index >> bit) & 1) << step) for index, place in enumerate(order)]
    mine = sum((((me >> bit) & 1) << step) for step, bit in enumerate(low_bits))
    order = jnp.array(order, jnp.int32) ^ mine
    head = lax.dynamic_index_in_dim(first, mine, 0, keepdims=False)
    head = jnp.concatenate([head, jnp.zeros((4, LANES), bf16)], axis=0)[:80] if own_rows < 80 else head[:80]
    mixed, convp = None, None
    for step, bit in enumerate(low_bits[1:]):
        if step < 2:
            rest, frames = tie(rest, frames)
        other = exchange(rest, bit)
        if step == 0:
            mixed, convp, frames = conv_piece(0, frames, head, xpad, back, None)
            mixed, convp, frames = conv_piece(1, frames, head, xpad, back, mixed)
        elif step == 1:
            mixed, convp, frames = conv_piece(2, frames, head, xpad, back, mixed)
        other, frames = tie(other, frames)
        rest = jnp.concatenate([rest, other], axis=0)
    wqkv, wproj, fc1, fc2, bqkv, vecs, fc1b = unpack(order, first, rest)
    normed, q, k, v, size = project(frames, mixed, convp, wqkv, bqkv)
    o, q_back = attend(q, k, v, size)
    output, gmid, do, gproj, gfc1, gfc2, gvec, gfc1b = feed_forward(
        frames, o, mixed, cotangent, wproj, fc1, fc2, vecs, fc1b
    )
    main = pack_main(gproj, gfc1, gfc2, gvec, gfc1b, count * own_rows)
    main = main.reshape(wide_count, narrow_count, own_rows, LANES)
    main = lax.psum_scatter(main, "wide", scatter_dimension=0, tiled=True)[0]
    q_back, do, k, v = (in_hbm(value) for value in (q_back, do, k, v))
    dq, dk, dv = attend_back(q_back, do, k, v)
    gpad, gqkv, gbias, gvec_one = project_back(dq, dk, dv, normed, mixed, gmid, wqkv, convp, spread)
    qkv, qkv_end = pack_qkv(gqkv, gbias)
    qkv = qkv.reshape(count // 4, own_rows, LANES)
    narrow_bits = narrow_count.bit_length() - 1
    for bit in range(narrow_bits):
        keep, give = split(qkv, bit)
        qkv = keep + exchange(give, bit)
    conv = conv_weight_grads(frames, xpad, gpad, gvec_one)
    late = jnp.concatenate([conv, qkv_end], axis=0)
    main, late = tie(main, late)
    gtok = None
    for bit in range(bits):
        if bit < narrow_bits:
            keep, give = split(main, bit)
        elif bit < bits - 2:
            keep, give = split(qkv, bit)
        else:
            keep, give = qkv, qkv
        sent = give.shape[0] * own_rows
        packet = jnp.concatenate([give.reshape(sent, LANES), late], axis=0)
        packet, frames = tie(packet, frames)
        other = exchange(packet, bit)
        if bit < 3:
            gtok, frames = token_piece(bit, frames, convp, gpad, back, gtok)
        elif bit == 3:
            output, frames = turn(frames, output)
        elif bit == 4:
            gtok, frames = turn(frames, gtok)
        other, frames = tie(other, frames)
        summed = keep + other[:sent].reshape(keep.shape)
        late = late + other[sent:]
        if bit < narrow_bits:
            main = summed
        else:
            qkv = summed
    main, qkv = main[0], qkv[0]
    early = jnp.where(me < count // 4, qkv.astype(f32), main.astype(f32))
    conv, qkv_end = late[:80].astype(f32), late[80:].astype(f32)
    if own_rows < 80:
        conv = conv[:own_rows]
    conv = jnp.pad(conv, ((0, own_rows - conv.shape[0]), (0, 0)))
    qkv_end = jnp.pad(qkv_end, ((0, own_rows - qkv_end.shape[0]), (0, 0)))
    owned = early + jnp.where(me == 0, conv, jnp.where(me == count // 4, qkv_end, 0.0))
    rate = RATE_FACTOR / math.sqrt(tokens.shape[0] * count)
    decayed = owned + DECAY_RATE * master
    new_momentum = MOMENTUM * momentum + decayed
    new_master = master - rate * (decayed + MOMENTUM * new_momentum)
    new_average = AVERAGE_KEEP * average + (1.0 - AVERAGE_KEEP) * new_master
    return (output.T, gtok.T, owned, new_master, new_momentum, new_average, new_master.astype(bf16))


def solution(mesh):
    rows = P(("wide", "narrow"), None)
    return jax.shard_map(
        on_device,
        mesh=mesh,
        in_specs=(rows, rows, rows, rows, P(("wide", "narrow")), P(("wide", "narrow")), rows),
        out_specs=(rows,) * 7,
        check_vma=False,
    )
```

```python
import functools
import math

import jax
import jax.numpy as jnp
from jax import lax
from jax.experimental import pallas as pl
from jax.experimental.pallas import tpu as pltpu
from jax.sharding import PartitionSpec as P

HEADS = 5
HEAD_DIM = 64
DIM = 320
FFN = 1280
SIDE = 14
FRAME = SIDE * SIDE
LANES = 128
WIDE_HEADS = HEADS * LANES
QKV_COLUMNS = 8 * LANES

EPSILON = 1e-06
MOMENTUM = 0.9
DECAY_RATE = 0.0001
AVERAGE_KEEP = 0.8
RATE_FACTOR = 0.03
LOG2E = 1.0 / math.log(2.0)
LN2 = math.log(2.0)
INVERSE_ROOT_TWO_PI = 1.0 / math.sqrt(2.0 * math.pi)
BLOCKED = -(2.0**30)
SAFE_BOUND = 80.0

bf16 = jnp.bfloat16
f32 = jnp.float32

AT_CONV = 0
AT_QKV = 150
AT_QV = 4950
AT_PROJ = 4960
AT_VEC = 6560
AT_FC1 = 6575
AT_FC1B = 12975
AT_FC2 = 12995
AT_FC2B = 19395
HALF_END = 19400


SMEM_SPEC = pl.BlockSpec(memory_space=pltpu.SMEM)
VMEM_SPEC = pl.BlockSpec(memory_space=pltpu.VMEM)
ANY_SPEC = pl.BlockSpec(memory_space=pl.ANY)
HBM_SPEC = pl.BlockSpec(memory_space=pltpu.HBM)


def in_hbm(value):
    return pltpu.with_memory_space_constraint(value, pltpu.HBM)


def dot(a, b):
    return lax.dot_general(a, b, (((1,), (0,)), ((), ())), preferred_element_type=f32)


def dot_nt(a, b):
    return lax.dot_general(a, b, (((1,), (1,)), ((), ())), preferred_element_type=f32)


def dot_tn(a, b):
    return lax.dot_general(a, b, (((0,), (0,)), ((), ())), preferred_element_type=f32)


def params(limit=58):
    return pltpu.CompilerParams(vmem_limit_bytes=limit << 20)


def lane_of(shape):
    return lax.broadcasted_iota(jnp.int32, shape, len(shape) - 1)


def row_of(shape):
    return lax.broadcasted_iota(jnp.int32, shape, 0)


def low_half(value, side):
    return value if side == 0 else pltpu.roll(value, 64, axis=1)


def high_half(value, side):
    return value if side == 1 else pltpu.roll(value, 64, axis=1)


def split3(value):
    first = value.astype(bf16).astype(f32)
    rest = value - first
    second = rest.astype(bf16).astype(f32)
    return first, second, rest - second


def read_half(flat, at, length, step, count, parity, j):
    index = at + parity * length + j
    return flat[pl.ds(index // 2, count, stride=step), :], index % 2


def read_vector(flat, at, length):
    tiles = []
    lane = lane_of((1, LANES))
    for j in range(0, length, 2):
        row, side = divmod(at + j, 2)
        low = low_half(flat[row : row + 1, :], side)
        if j + 1 < length:
            row, side = divmod(at + j + 1, 2)
            tiles.append(jnp.where(lane < 64, low, high_half(flat[row : row + 1, :], side)))
        else:
            tiles.append(low[:, :64])
    return jnp.concatenate(tiles, axis=1)


def odd_matrix(flat, out, at, length, rows):
    pairs = rows // 2
    for parity in range(2):
        for tile in range((length + 1) // 2):
            low, side = read_half(flat, at, length, length, pairs, parity, 2 * tile)
            low = low_half(low, side)
            place = pl.ds(parity, pairs, stride=2)
            if 2 * tile + 1 < length:
                high, side = read_half(flat, at, length, length, pairs, parity, 2 * tile + 1)
                merged = jnp.where(lane_of(low.shape) < 64, low, high_half(high, side))
            else:
                merged = low
            out[tile, place, :] = merged


def unpack_kernel(order, first, rest, wide_qkv, wqkv, wproj, fc1, fc2, bqkv, vecs, fc1b, flat, wide, tall):
    blocks, rows = first.shape[:2]
    for block in range(blocks):
        place = order[block]
        for quarter in range(4):
            start = (quarter * blocks + block) * rows
            value = first[place] if quarter == 0 else rest[place, quarter - 1]
            flat[start : start + rows, :] = value.astype(f32)
    odd_matrix(flat, wide, AT_QKV, 15, DIM)
    for tile in range(8):
        value = wide[tile]
        if tile == 7:
            value = jnp.where(lane_of(value.shape) < 64, value, 0.0)
        wqkv[:, tile * LANES : (tile + 1) * LANES] = value.astype(bf16)
        inside = lane_of(value.shape) < 64
        for side in range(2 if tile < 7 else 1):
            place = pl.ds((2 * tile + side) * LANES, LANES)
            wide_qkv[:, place] = jnp.where(inside, low_half(value, side), 0.0).astype(bf16)
    lane = lane_of((1, LANES))
    for j in range(15):
        if 5 <= j < 10:
            bqkv[:, j * LANES : (j + 1) * LANES] = jnp.zeros((1, LANES), f32)
        else:
            row, side = divmod(AT_QV + (j if j < 5 else j - 5), 2)
            value = low_half(flat[row : row + 1, :], side)
            bqkv[:, j * LANES : (j + 1) * LANES] = jnp.where(lane < 64, value, 0.0)
    odd_matrix(flat, wide, AT_PROJ, 5, DIM)
    for head in range(HEADS):
        for tile in range(3):
            width = LANES if tile < 2 else 64
            columns = slice(tile * LANES, tile * LANES + width)
            part = wide[tile, head * 64 : head * 64 + 64, :width].astype(bf16)
            wproj[head * LANES : head * LANES + 64, columns] = part
        wproj[head * LANES + 64 : (head + 1) * LANES, :] = jnp.zeros((64, DIM), bf16)
    for row in range(3):
        vecs[row : row + 1, :] = read_vector(flat, AT_VEC + 5 * row, 5)
    vecs[3:4, :] = read_vector(flat, AT_FC2B, 5)
    vecs[4:8, :] = jnp.zeros((4, DIM), f32)
    fc1b[...] = read_vector(flat, AT_FC1B, 20)
    for tile in range(10):
        low, side = read_half(flat, AT_FC1, 20, 10, DIM, 0, 2 * tile)
        high, side_high = read_half(flat, AT_FC1, 20, 10, DIM, 0, 2 * tile + 1)
        merged = jnp.where(lane_of(low.shape) < 64, low_half(low, side), high_half(high, side_high))
        fc1[:, tile * LANES : (tile + 1) * LANES] = merged.astype(bf16)
    odd_matrix(flat, tall, AT_FC2, 5, FFN)
    for tile in range(3):
        width = LANES if tile < 2 else 64
        fc2[:, tile * LANES : tile * LANES + width] = tall[tile, :, :width].astype(bf16)


def unpack(order, first, rest):
    rows = 4 * first.shape[0] * first.shape[1]
    return pl.pallas_call(
        unpack_kernel,
        name="unpack",
        in_specs=[SMEM_SPEC, VMEM_SPEC, VMEM_SPEC],
        out_shape=[
            jax.ShapeDtypeStruct((DIM, 3 * WIDE_HEADS), bf16),
            jax.ShapeDtypeStruct((DIM, QKV_COLUMNS), bf16),
            jax.ShapeDtypeStruct((WIDE_HEADS, DIM), bf16),
            jax.ShapeDtypeStruct((DIM, FFN), bf16),
            jax.ShapeDtypeStruct((FFN, DIM), bf16),
            jax.ShapeDtypeStruct((1, 3 * WIDE_HEADS), f32),
            jax.ShapeDtypeStruct((8, DIM), f32),
            jax.ShapeDtypeStruct((1, FFN), f32),
        ],
        scratch_shapes=[
            pltpu.VMEM((rows, LANES), f32),
            pltpu.VMEM((15, DIM, LANES), f32),
            pltpu.VMEM((3, FFN, LANES), f32),
        ],
        compiler_params=params(16),
    )(order, first, rest)


PAD_ROWS = 16 * 16
BODY = SIDE * 16


def spread_matrix(shift):
    cell = lax.broadcasted_iota(jnp.int32, (PAD_ROWS, 208), 0)
    source = lax.broadcasted_iota(jnp.int32, (PAD_ROWS, 208), 1)
    row, column = cell >> 4, cell & 15
    inside = (row >= 1) & (row <= SIDE) & (column < SIDE)
    wanted = (row - 1) * SIDE + column + shift
    return jnp.where(inside & (source == wanted), 1.0, 0.0).astype(bf16)


def gather_matrix(shift):
    target = lax.broadcasted_iota(jnp.int32, (208, BODY), 0)
    cell = lax.broadcasted_iota(jnp.int32, (208, BODY), 1)
    row, column = cell >> 4, cell & 15
    wanted = row * SIDE + column + shift
    return jnp.where((column < SIDE) & (target == wanted), 1.0, 0.0).astype(bf16)


TILES = ((0, 128), (128, 256), (256, 320))


def pieces(value):
    first = value.astype(bf16)
    return first, (value - first.astype(f32)).astype(bf16)


def prepare_kernel(frames, turned, target, spread, back, passed, tokens, padded, sems):
    for member in range(4):
        spread[member] = spread_matrix(4 * member)
        back[member] = gather_matrix(4 * member)
    passed[0] = frames[0]
    tokens[...] = turned[...].T

    def fill(frame, carry):
        member = frame & 3
        place = pl.ds(pl.multiple_of(frame * FRAME - 4 * member, 16), 208)
        padded[frame] = dot(spread[member], tokens[place, :])
        return carry

    copies = []
    for group in range(padded.shape[0] // 4):
        lax.fori_loop(4 * group, 4 * group + 4, fill, 0)
        place = pl.ds(4 * group, 4)
        copies.append(pltpu.make_async_copy(padded.at[place], target.at[place], sems.at[group]))
        copies[-1].start()
    for copy in copies:
        copy.wait()


def prepare(frames, turned):
    rows = turned.shape[1]
    return pl.pallas_call(
        prepare_kernel,
        name="prepare",
        in_specs=[SMEM_SPEC, VMEM_SPEC],
        out_specs=[HBM_SPEC, VMEM_SPEC, VMEM_SPEC, SMEM_SPEC],
        out_shape=[
            pltpu.HBM((rows // FRAME, PAD_ROWS, DIM), f32),
            jax.ShapeDtypeStruct((4, PAD_ROWS, 208), bf16),
            jax.ShapeDtypeStruct((4, 208, BODY), bf16),
            jax.ShapeDtypeStruct((1,), jnp.int32),
        ],
        scratch_shapes=[
            pltpu.VMEM((rows, DIM), bf16),
            pltpu.VMEM((rows // FRAME, PAD_ROWS, DIM), f32),
            pltpu.SemaphoreType.DMA((rows // FRAME // 4,)),
        ],
        compiler_params=params(16),
    )(frames, turned)


PIECE = 4 * FRAME


def fetch_frames(source, slots, sems, start, count):
    first, last = max(start - 1, 0), min(start + count + 1, source.shape[0])
    middle = start + 2
    copies = []
    for index, (low, high) in enumerate(((first, middle), (middle, last))):
        copies.append(
            pltpu.make_async_copy(
                source.at[pl.ds(low, high - low)], slots.at[pl.ds(low - start + 1, high - low)], sems.at[index]
            )
        )
    return copies


def mix_frame(slots, at, weights, sums, out, sign):
    for low, high in TILES:
        for start in range(0, BODY, 56):
            parts = [None, None, None]
            for a in (-1, 0, 1):
                for b in (-1, 0, 1):
                    begin = 16 + sign * b * 16 + start
                    cells = slots[at[1 + sign * a], begin : begin + 56, low:high]
                    for c in range(3):
                        tap = 9 * (a + 1) + 3 * (b + 1) + c
                        term = cells * weights[tap : tap + 1, low:high]
                        parts[c] = term if parts[c] is None else parts[c] + term
            parts[1] = parts[1] + slots[at[1], 16 + start : 16 + start + 56, low:high]
            for c in range(3):
                sums[c, start : start + 56, low:high] = parts[c]
    before, after = (0, 2) if sign == 1 else (2, 0)
    for low, high in TILES:
        out[:, low:high] = (
            sums[1, :, low:high]
            + pltpu.roll(sums[before, :, low:high], 1, axis=0)
            + pltpu.roll(sums[after, :, low:high], BODY - 1, axis=0)
        )


def mask_weights(weights, masked, first, middle, last):
    for tap in range(27):
        keep = (first, middle, last)[tap // 9]
        scale = 1.0 if tap == 13 else jnp.where(keep, 1.0, 0.0)
        masked[tap : tap + 1, :] = weights[tap : tap + 1, :] * scale


def conv_params(head, flat, weights):
    flat[...] = head[...].astype(f32)
    for parity in range(2):
        for tile in range(3):
            low, side = read_half(flat, AT_CONV, 5, 5, 15, parity, 2 * tile)
            low = low_half(low, side)
            place = pl.ds(parity, 15, stride=2)
            if tile < 2:
                high, side = read_half(flat, AT_CONV, 5, 5, 15, parity, 2 * tile + 1)
                low = jnp.where(lane_of(low.shape) < 64, low, high_half(high, side))
            weights[tile, place, :] = low


def turn_kernel(frames, source, out, passed):
    passed[0] = frames[0]
    out[...] = source[...].T


def turn(frames, value):
    rows, columns = value.shape
    return pl.pallas_call(
        turn_kernel,
        name="turn",
        in_specs=[SMEM_SPEC, VMEM_SPEC],
        out_specs=[VMEM_SPEC, SMEM_SPEC],
        out_shape=[
            jax.ShapeDtypeStruct((columns, rows), value.dtype),
            jax.ShapeDtypeStruct((1,), jnp.int32),
        ],
        compiler_params=params(10),
        cost_estimate=pl.CostEstimate(flops=0, bytes_accessed=4 * rows * columns, transcendentals=0),
    )(frames, value)


def conv_piece_kernel(start, count, frames_ref, head, padded, back, *refs):
    if start > 0:
        refs = refs[1:]
    mixed, convp, passed, flat, weights, masked, slots, sums, comp, sem = refs
    passed[0] = frames_ref[0]
    copies = fetch_frames(padded, slots, sem, start, count)
    for copy in copies:
        copy.start()
    frames = frames_ref[0]
    conv_params(head, flat, weights)
    for tile, (low, high) in enumerate(TILES):
        convp[:, low:high] = weights[tile, :, : high - low]
    mixed[...] = jnp.zeros(mixed.shape, f32)
    copies[0].wait()

    def each(member, carry):
        @pl.when(member == 1)
        def _():
            copies[1].wait()

        frame = start + member
        there = frame < frames
        before = there & (frame > 0)
        after = frame + 1 < frames
        mask_weights(convp, masked, before, there, after)
        at = (member + jnp.where(before, 0, 1), member + 1, member + jnp.where(after, 2, 1))
        mix_frame(slots, at, masked, sums, comp, 1)
        high, low = pieces(comp[...] + convp[27:28, :])
        shift = member & 3
        place = pl.ds(pl.multiple_of(FRAME * member - 4 * shift, 16), 208)
        mixed[place, :] += dot(back[shift], high) + dot(back[shift], low)
        return carry

    lax.fori_loop(0, count, each, 0)


def conv_piece(start, count, frames, head, padded, back, mixed):
    rows = padded.shape[0] * FRAME
    operands = [frames, head, in_hbm(padded), back] + ([] if start == 0 else [mixed])
    return pl.pallas_call(
        functools.partial(conv_piece_kernel, start, count),
        name=f"conv_piece{start}",
        grid=(1,),
        in_specs=[SMEM_SPEC, VMEM_SPEC, HBM_SPEC, VMEM_SPEC] + [ANY_SPEC] * (start > 0),
        out_specs=[
            pl.BlockSpec((count * FRAME, DIM), lambda i: (start // count, 0)),
            pl.BlockSpec((32, DIM), lambda i: (0, 0)),
            SMEM_SPEC,
        ],
        out_shape=[
            jax.ShapeDtypeStruct((rows, DIM), f32),
            jax.ShapeDtypeStruct((32, DIM), f32),
            jax.ShapeDtypeStruct((1,), jnp.int32),
        ],
        input_output_aliases={4: 0} if start else {},
        scratch_shapes=[
            pltpu.VMEM(head.shape, f32),
            pltpu.VMEM((3, 32, LANES), f32),
            pltpu.VMEM((32, DIM), f32),
            pltpu.VMEM((count + 2, PAD_ROWS, DIM), f32),
            pltpu.VMEM((3, BODY, DIM), f32),
            pltpu.VMEM((BODY, DIM), f32),
            pltpu.SemaphoreType.DMA((2,)),
        ],
        compiler_params=params(20),
    )(*operands)


def normalize(values):
    centered = values - jnp.mean(values, axis=-1, keepdims=True)
    variance = jnp.mean(centered * centered, axis=-1, keepdims=True)
    inverse = lax.rsqrt(variance + EPSILON)
    return centered * inverse, inverse


def row_size(value):
    part = jnp.where(lane_of(value.shape) < HEAD_DIM, value.astype(f32), 0.0)
    return jnp.sum(part * part, axis=-1, keepdims=True)


def qkv_kernel(frames_ref, mixed, convp, wqkv, bqkv, normed_out, q_out, k_out, v_out, size):
    block = pl.program_id(0)
    rows = mixed.shape[0]
    frames = frames_ref[0]
    normal, unused_inverse = normalize(mixed[...])
    normed = (normal * convp[28:29, :] + convp[29:30, :]).astype(bf16)
    normed_out[...] = normed
    lane = lane_of((rows, LANES))
    inside = row_of((rows, LANES)) + block * rows < frames * FRAME
    q_mask = jnp.where(
        ((lane == 64) & ~inside) | ((lane == 65) & inside), BLOCKED, 0.0
    )
    k_mask = jnp.where(
        ((lane == 64) & inside) | ((lane == 65) & ~inside) | ((lane >= 66) & (lane < 69)), 1.0, 0.0
    )
    v_mask = jnp.where((lane >= 64) & (lane < 67), 1.0, 0.0)
    scale = HEAD_DIM ** (-0.5) * LOG2E

    @pl.when(block == 0)
    def _():
        size[...] = jnp.zeros(size.shape, f32)

    projected = dot(normed, wqkv[...])
    for head in range(HEADS):

        def columns(kind, head=head):
            place = slice((kind * HEADS + head) * LANES, (kind * HEADS + head + 1) * LANES)
            return projected[:, place] + bqkv[:, place]

        query = (columns(0) * scale + q_mask).astype(bf16)
        key = (columns(1) + k_mask).astype(bf16)
        query_size = jnp.max(row_size(query), axis=0, keepdims=True)
        key_size = jnp.max(row_size(key), axis=0, keepdims=True)
        q_out[head] = query
        k_out[head] = key
        v_out[head] = (columns(2) + v_mask).astype(bf16)
        size[head : head + 1, :] = jnp.maximum(size[head : head + 1, :], query_size)
        size[head + 8 : head + 9, :] = jnp.maximum(size[head + 8 : head + 9, :], key_size)


def project(frames, mixed, convp, wqkv, bqkv, block=784):
    rows = mixed.shape[0]
    heads_spec = pl.BlockSpec((HEADS, block, LANES), lambda i: (0, i, 0))
    rows_spec = pl.BlockSpec((block, DIM), lambda i: (i, 0))
    heads_shape = jax.ShapeDtypeStruct((HEADS, rows, LANES), bf16)
    return pl.pallas_call(
        qkv_kernel,
        name="qkv_forward",
        grid=(rows // block,),
        in_specs=[
            SMEM_SPEC,
            rows_spec,
            pl.BlockSpec((32, DIM), lambda i: (0, 0)),
            pl.BlockSpec((DIM, 3 * WIDE_HEADS), lambda i: (0, 0)),
            pl.BlockSpec((1, 3 * WIDE_HEADS), lambda i: (0, 0)),
        ],
        out_specs=[rows_spec, heads_spec, heads_spec, heads_spec, pl.BlockSpec((16, LANES), lambda i: (0, 0))],
        out_shape=[
            pltpu.HBM((rows, DIM), bf16),
            heads_shape,
            heads_shape,
            heads_shape,
            jax.ShapeDtypeStruct((16, LANES), f32),
        ],
        compiler_params=params(14),
    )(frames, mixed, convp, wqkv, bqkv)


def attend_kernel(chunk, q, k, v, size, o_out, q_back, query, shift):
    head = pl.program_id(0)
    keys = k.shape[1]
    tall = q.shape[1]
    bound = jnp.max(size[pl.ds(head, 1), :] * size[pl.ds(head + 8, 1), :])
    query[...] = q[0]
    shift[...] = jnp.zeros(shift.shape, f32)

    @pl.when(bound > SAFE_BOUND * SAFE_BOUND)
    def _():
        shift[...] = jnp.full(shift.shape, -jnp.inf, f32)

        def peak(step, carry):
            scores = dot_nt(k[0, pl.ds(pl.multiple_of(step * 112, 16), 112), :], q[0])
            shift[...] = jnp.maximum(shift[...], jnp.max(scores, axis=0, keepdims=True))
            return carry

        lax.fori_loop(0, keys // 112, peak, 0)
        first, second, third = split3(-shift[...])
        row = row_of((LANES, tall))
        tail = jnp.where(row == 66, first, jnp.where(row == 67, second, jnp.where(row == 68, third, 0.0)))
        query[...] = (q[0].astype(f32) + tail.T).astype(bf16)

    total = None
    for start in range(0, keys, chunk):
        place = slice(start, min(start + chunk, keys))
        weights = jnp.exp2(dot_nt(k[0, place, :], query[...])).astype(bf16)
        part = dot_tn(v[0, place, :], weights)
        total = part if total is None else total + part
    sums = total[64:65, :]
    first, second, third = split3(-(shift[...] + jnp.log2(sums)))
    row = row_of((8, tall))
    tail = jnp.where(row == 2, first, jnp.where(row == 3, second, jnp.where(row == 4, third, 0.0)))
    stacked = jnp.concatenate([total[:64, :] / sums, tail, jnp.zeros((56, tall), f32)], axis=0).T
    lane = lane_of((tall, LANES))
    o_out[0] = jnp.where(lane < 64, stacked, 0.0).astype(bf16)
    q_back[0] = jnp.where((lane >= 66) & (lane < 69), stacked, q[0].astype(f32)).astype(bf16)


def attend(q, k, v, size, chunk=512):
    rows = q.shape[1]
    whole = pl.BlockSpec((1, rows, LANES), lambda h: (h, 0, 0))
    shape = jax.ShapeDtypeStruct((HEADS, rows, LANES), bf16)
    return pl.pallas_call(
        functools.partial(attend_kernel, chunk),
        name="attend",
        grid=(HEADS,),
        in_specs=[whole, whole, whole, pl.BlockSpec((16, LANES), lambda h: (0, 0))],
        out_specs=[whole, whole],
        out_shape=[shape, pltpu.HBM(shape.shape, bf16)],
        scratch_shapes=[pltpu.VMEM((rows, LANES), bf16), pltpu.VMEM((1, rows), f32)],
        compiler_params=params(18),
    )(q, k, v, size)


def attend_back_kernel(rows, q, do, k, v, dq_out, dk_out, dv_out, dq):
    step = pl.program_id(1)
    wide = k.shape[1]
    inside = row_of((wide, LANES)) + step * wide < rows
    key = jnp.where(inside, k[0], jnp.zeros((), bf16))
    value = jnp.where(inside, v[0], jnp.zeros((), bf16))
    weights = jnp.exp2(dot_nt(q[0], key))
    grad_scores = (weights * dot_nt(do[0], value)).astype(bf16)
    weights = weights.astype(bf16)
    dv_out[0] = dot_tn(do[0], weights).T.astype(bf16)
    dk_out[0] = (dot_tn(q[0], grad_scores) * LN2).T.astype(bf16)
    part = dot_nt(key.T, grad_scores)

    @pl.when(step == 0)
    def _():
        dq[...] = part

    @pl.when(step > 0)
    def _():
        dq[...] += part

    @pl.when(step == pl.num_programs(1) - 1)
    def _():
        dq_out[0] = (dq[...] * HEAD_DIM ** (-0.5)).T.astype(bf16)


def attend_back(q, do, k, v, wide=1280):
    heads, rows = q.shape[:2]
    block = pl.BlockSpec((1, wide, LANES), lambda h, i: (h, i, 0))
    whole = pl.BlockSpec((1, rows, LANES), lambda h, i: (h, 0, 0))
    shape = jax.ShapeDtypeStruct((heads, rows, LANES), bf16)
    return pl.pallas_call(
        functools.partial(attend_back_kernel, rows),
        name="attend_back",
        grid=(heads, pl.cdiv(rows, wide)),
        in_specs=[whole, whole, block, block],
        out_specs=[whole, block, block],
        out_shape=[shape, shape, shape],
        scratch_shapes=[pltpu.VMEM((LANES, rows), f32)],
        compiler_params=params(30),
    )(q, do, k, v)


def erf_parts(value):
    bell = jnp.exp(-0.5 * value * value)
    return bell, 0.5 * (1.0 + lax.erf(value * (1.0 / math.sqrt(2.0))))


def add_tiles(ref, place, value):
    for tile, (low, high) in enumerate(TILES):
        ref[tile, place, : high - low] += value[:, low:high]


def middle_kernel(
    frames_ref, o, mixed, cot, wproj, fc1, fc2, vecs, fc1b,
    output, gmid_out, do_out, gproj, gfc1, gfc2, gvec, gfc1b, chunk,
):
    block = pl.program_id(0)
    rows = mixed.shape[0]
    inside = row_of((rows, DIM)) + block * rows < frames_ref[0] * FRAME

    @pl.when(block == 0)
    def _():
        for ref in (gproj, gfc1, gfc2, gvec, gfc1b):
            ref[...] = jnp.zeros(ref.shape, f32)

    attended = jnp.concatenate([o[head] for head in range(HEADS)], axis=1)
    middle = mixed[...] + (dot(attended, wproj[...]) + vecs[0:1, :])
    normal, inverse = normalize(middle)
    normed = (normal * vecs[1:2, :] + vecs[2:3, :]).astype(bf16)
    grad_output = jnp.where(inside, cot[...].astype(f32), 0.0)
    grad_outer = grad_output.astype(bf16)
    total = middle + vecs[3:4, :]
    grad_normed = jnp.zeros((rows, DIM), f32)
    for start in range(0, FFN, chunk):
        place = slice(start, start + chunk)
        inner = dot(normed, fc1[:, place]) + fc1b[:, place]
        bell, gate = erf_parts(inner)
        activated = (inner * gate).astype(bf16)
        total += dot(activated, fc2[place, :])
        slope = gate + inner * bell * INVERSE_ROOT_TWO_PI
        grad_inner = (dot_nt(grad_outer, fc2[place, :]) * slope)
        gfc1b[:, place] += jnp.sum(grad_inner, axis=0, keepdims=True)
        grad_inner = grad_inner.astype(bf16)
        add_tiles(gfc2, place, dot_tn(activated, grad_outer))
        gfc1[:, place] += dot_tn(normed, grad_inner)
        grad_normed += dot_nt(grad_inner, fc1[:, place])
    output[...] = total.astype(bf16)
    scaled = grad_normed * vecs[1:2, :]
    grad_middle = grad_output + inverse * (
        scaled
        - jnp.mean(scaled, axis=-1, keepdims=True)
        - normal * jnp.mean(scaled * normal, axis=-1, keepdims=True)
    )
    gmid_out[...] = grad_middle
    grad_branch = grad_middle.astype(bf16)
    add_tiles(gproj, slice(None), dot_tn(attended, grad_branch))
    gvec[0:1, :] += jnp.sum(grad_branch.astype(f32), axis=0, keepdims=True)
    gvec[1:2, :] += jnp.sum(grad_normed * normal, axis=0, keepdims=True)
    gvec[2:3, :] += jnp.sum(grad_normed, axis=0, keepdims=True)
    gvec[3:4, :] += jnp.sum(grad_output, axis=0, keepdims=True)
    lane = lane_of((rows, LANES))
    grad_attended = dot_nt(grad_branch, wproj[...])
    for head in range(HEADS):
        grad_head = grad_attended[:, head * LANES : (head + 1) * LANES]
        delta = jnp.sum(grad_head * o[head].astype(f32), axis=-1, keepdims=True)
        first, second, third = split3(-delta)
        tail = jnp.where(lane == 64, first, jnp.where(lane == 65, second, third))
        do_out[head] = jnp.where((lane >= 64) & (lane < 67), tail, grad_head).astype(bf16)


def feed_forward(frames, o, mixed, cot, wproj, fc1, fc2, vecs, fc1b, block=784, chunk=256):
    rows = mixed.shape[0]
    heads_spec = pl.BlockSpec((HEADS, block, LANES), lambda i: (0, i, 0))
    rows_spec = pl.BlockSpec((block, DIM), lambda i: (i, 0))

    def full(*shape):
        return pl.BlockSpec(shape, lambda i: (0,) * len(shape))

    return pl.pallas_call(
        functools.partial(middle_kernel, chunk=chunk),
        name="feed_forward",
        grid=(rows // block,),
        in_specs=[
            SMEM_SPEC, heads_spec, rows_spec, rows_spec,
            full(WIDE_HEADS, DIM), full(DIM, FFN), full(FFN, DIM), full(8, DIM), full(1, FFN),
        ],
        out_specs=[
            rows_spec, rows_spec, heads_spec,
            full(3, WIDE_HEADS, LANES), full(DIM, FFN), full(3, FFN, LANES), full(8, DIM), full(1, FFN),
        ],
        out_shape=[
            pltpu.HBM((rows, DIM), bf16),
            pltpu.HBM((rows, DIM), f32),
            pltpu.HBM((HEADS, rows, LANES), bf16),
            jax.ShapeDtypeStruct((3, WIDE_HEADS, LANES), f32),
            jax.ShapeDtypeStruct((DIM, FFN), f32),
            jax.ShapeDtypeStruct((3, FFN, LANES), f32),
            jax.ShapeDtypeStruct((8, DIM), f32),
            jax.ShapeDtypeStruct((1, FFN), f32),
        ],
        compiler_params=params(22),
    )(frames, o, mixed, cot, wproj, fc1, fc2, vecs, fc1b)


def qkv_back_kernel(dq, dk, dv, normed, mixed, gmid, wqkv, convp, spread, padded, gqkv, gbias, gvec, gmix):
    block = pl.program_id(0)

    @pl.when(block == 0)
    def _():
        for ref in (gqkv, gbias, gvec):
            ref[...] = jnp.zeros(ref.shape, f32)

    normal, inverse = normalize(mixed[...])
    heads = [part[head][:, :HEAD_DIM] for part in (dq, dk, dv) for head in range(HEADS)]
    heads.append(jnp.zeros_like(heads[0]))
    grads = jnp.concatenate(heads, axis=1)
    grad_qkv = dot_tn(normed[...], grads)
    for tile in range(8):
        gqkv[tile] += grad_qkv[:, tile * LANES : (tile + 1) * LANES]
    gbias[...] += jnp.sum(grads.astype(f32), axis=0, keepdims=True)
    grad_normed = dot_nt(grads, wqkv[...])
    gvec[1:2, :] += jnp.sum(grad_normed * normal, axis=0, keepdims=True)
    gvec[2:3, :] += jnp.sum(grad_normed, axis=0, keepdims=True)
    scaled = grad_normed * convp[28:29, :]
    grad_mixed = gmid[...] + inverse * (
        scaled
        - jnp.mean(scaled, axis=-1, keepdims=True)
        - normal * jnp.mean(scaled * normal, axis=-1, keepdims=True)
    )
    gvec[0:1, :] += jnp.sum(grad_mixed, axis=0, keepdims=True)
    gmix[...] = grad_mixed
    for member in range(mixed.shape[0] // FRAME):
        high, low = pieces(gmix[192 * member : 192 * member + 208, :])
        padded[member] = dot(spread[member], high) + dot(spread[member], low)


def project_back(dq, dk, dv, normed, mixed, gmid, wqkv, convp, spread, block=PIECE):
    rows = mixed.shape[0]
    heads_spec = pl.BlockSpec((HEADS, block, LANES), lambda i: (0, i, 0))
    rows_spec = pl.BlockSpec((block, DIM), lambda i: (i, 0))

    def full(*shape):
        return pl.BlockSpec(shape, lambda i: (0,) * len(shape))

    return pl.pallas_call(
        qkv_back_kernel,
        name="qkv_back",
        grid=(rows // block,),
        in_specs=[heads_spec, heads_spec, heads_spec, rows_spec, rows_spec, rows_spec,
                  full(DIM, QKV_COLUMNS), full(32, DIM), full(4, PAD_ROWS, 208)],
        out_specs=[pl.BlockSpec((4, PAD_ROWS, DIM), lambda i: (i, 0, 0)), full(8, DIM, LANES), full(1, QKV_COLUMNS), full(8, DIM)],
        out_shape=[
            pltpu.HBM((rows // FRAME, PAD_ROWS, DIM), f32),
            jax.ShapeDtypeStruct((8, DIM, LANES), f32),
            jax.ShapeDtypeStruct((1, QKV_COLUMNS), f32),
            jax.ShapeDtypeStruct((8, DIM), f32),
        ],
        scratch_shapes=[pltpu.VMEM((block, DIM), f32)],
        compiler_params=params(18),
    )(dq, dk, dv, normed, mixed, gmid, wqkv, convp, spread)


def conv_weight_kernel(frames_ref, xsource, gsource, gvec, out, xpad, gpad, moved, sums, tiles, flat, xsem, gsem):
    frames = frames_ref[0]
    count = xpad.shape[0]
    copies = []
    for group in range(count // 4):
        place = pl.ds(4 * group, 4)
        copies.append(pltpu.make_async_copy(xsource.at[place], xpad.at[place], xsem.at[group]))
        copies.append(pltpu.make_async_copy(gsource.at[place], gpad.at[place], gsem.at[group]))
    for copy in copies:
        copy.start()
    sums[...] = jnp.zeros(sums.shape, f32)

    def weight_frame(frame, carry):
        for low, high in TILES:
            body = gpad[frame, 16 : 16 + BODY, low:high]
            moved[0, :, low:high] = pltpu.roll(body, BODY - 1, axis=0)
            moved[1, :, low:high] = pltpu.roll(body, 1, axis=0)
        for a in (-1, 0, 1):
            at = frame + a

            @pl.when((at >= 0) & (at < frames))
            def _():
                for low, high in TILES:
                    for b in (-1, 0, 1):
                        cells = xpad[at, 16 + b * 16 : 16 + b * 16 + BODY, low:high]
                        for c in range(3):
                            body = (
                                gpad[frame, 16 : 16 + BODY, low:high]
                                if c == 1
                                else moved[c // 2, :, low:high]
                            )
                            product = (body * cells).reshape(BODY // 8, 8, high - low)
                            tap = 9 * (a + 1) + 3 * (b + 1) + c
                            sums[tap, :, low:high] += jnp.sum(product, axis=0)

        return carry

    for group in range(count // 4):
        copies[2 * group].wait()
        copies[2 * group + 1].wait()
        start = max(4 * group - 1, 0)
        stop = 4 * group + 3 if group < count // 4 - 1 else count
        lax.fori_loop(jnp.minimum(start, frames), jnp.minimum(stop, frames), weight_frame, 0)
    tiles[...] = jnp.zeros(tiles.shape, f32)
    flat[...] = jnp.zeros(flat.shape, f32)
    for tile, (low, high) in enumerate(TILES):
        tiles[tile, 0:27, : high - low] = jnp.sum(sums[:, :, low:high], axis=1)
        tiles[tile, 27:30, : high - low] = gvec[0:3, low:high]
    for parity in range(2):
        for j in range(5):
            value = tiles[j // 2, pl.ds(parity, 15, stride=2), :]
            put_half(flat, AT_CONV + parity * 5 + j, value, j % 2, 5, 15)
    out[...] = flat[...].astype(bf16)


def conv_weight_grads(frames, xpad, gpad, gvec):
    return pl.pallas_call(
        conv_weight_kernel,
        name="conv_weight_grads",
        in_specs=[SMEM_SPEC, HBM_SPEC, HBM_SPEC, VMEM_SPEC],
        out_shape=jax.ShapeDtypeStruct((80, LANES), bf16),
        scratch_shapes=[
            pltpu.VMEM(xpad.shape, f32),
            pltpu.VMEM(gpad.shape, f32),
            pltpu.VMEM((2, BODY, DIM), f32),
            pltpu.VMEM((27, 8, DIM), f32),
            pltpu.VMEM((3, 32, LANES), f32),
            pltpu.VMEM((80, LANES), f32),
            pltpu.SemaphoreType.DMA((xpad.shape[0] // 4,)),
            pltpu.SemaphoreType.DMA((xpad.shape[0] // 4,)),
        ],
        compiler_params=params(18),
    )(frames, in_hbm(xpad), in_hbm(gpad), gvec)


def token_piece_kernel(piece, frames_ref, convp, gsource, back, *refs):
    if piece > 0:
        refs = refs[1:]
    gtok, passed, masked, slots, sums, comp, rows, sem = refs
    frames = frames_ref[0]
    passed[0] = frames
    copies = fetch_frames(gsource, slots, sem, 4 * piece, 4)
    for copy in copies:
        copy.start()
    rows[...] = jnp.zeros(rows.shape, f32)
    copies[0].wait()

    def each(member, carry):
        @pl.when(member == 1)
        def _():
            copies[1].wait()

        frame = 4 * piece + member
        there = frame < frames
        before = there & (frame > 0)
        after = frame + 1 < frames
        mask_weights(convp, masked, after, there, before)
        at = (member + jnp.where(before, 0, 1), member + 1, member + jnp.where(after, 2, 1))
        mix_frame(slots, at, masked, sums, comp, -1)
        place = pl.ds(pl.multiple_of(192 * member, 16), 208)
        rows[place, :] += dot(back[member], comp[...].astype(bf16))
        return carry

    lax.fori_loop(0, 4, each, 0)
    gtok[...] = rows[...].astype(bf16)


def token_piece(piece, frames, convp, gpad, back, gtok):
    count = gpad.shape[0]
    operands = [frames, convp, in_hbm(gpad), back] + ([] if piece == 0 else [gtok])
    return pl.pallas_call(
        functools.partial(token_piece_kernel, piece),
        name=f"token_piece{piece}",
        grid=(1,),
        in_specs=[SMEM_SPEC, VMEM_SPEC, HBM_SPEC, VMEM_SPEC] + [ANY_SPEC] * (piece > 0),
        out_specs=[pl.BlockSpec((PIECE, DIM), lambda i: (piece, 0)), SMEM_SPEC],
        out_shape=[
            jax.ShapeDtypeStruct((count * FRAME, DIM), bf16),
            jax.ShapeDtypeStruct((1,), jnp.int32),
        ],
        input_output_aliases={4: 0} if piece else {},
        scratch_shapes=[
            pltpu.VMEM((32, DIM), f32),
            pltpu.VMEM((6, PAD_ROWS, DIM), f32),
            pltpu.VMEM((3, BODY, DIM), f32),
            pltpu.VMEM((BODY, DIM), f32),
            pltpu.VMEM((PIECE, DIM), f32),
            pltpu.SemaphoreType.DMA((2,)),
        ],
        compiler_params=params(10),
    )(*operands)


def put_half(flat, index, value, side, step=1, count=1):
    row, wanted = divmod(index, 2)
    place = pl.ds(row, count, stride=step) if step > 1 else pl.ds(row, count)
    lane = lane_of(value.shape)
    if wanted == 0:
        flat[place, :] += jnp.where(lane < 64, low_half(value, side), 0.0)
    else:
        flat[place, :] += jnp.where(lane >= 64, high_half(value, side), 0.0)


def put_vector(flat, index, value):
    width = value.shape[1]
    for j in range(width // 64):
        low = (j // 2) * LANES
        part = value[:, low : min(low + LANES, width)]
        if part.shape[1] < LANES:
            part = jnp.concatenate([part, jnp.zeros((1, 64), f32)], axis=1)
        put_half(flat, index + j, part, j % 2)


PACK_BASE = 2432


def pack_main_kernel(gproj, gfc1, gfc2, gvec, gfc1b, out, flat):
    flat[...] = jnp.zeros(flat.shape, f32)
    for parity in range(2):
        for j in range(5):
            for head in range(HEADS):
                value = gproj[j // 2, pl.ds(head * LANES + parity, 32, stride=2), :]
                put_half(flat, AT_PROJ + (64 * head + parity) * 5 + j, value, j % 2, 5, 32)
            value = gfc2[j // 2, pl.ds(parity, FFN // 2, stride=2), :]
            put_half(flat, AT_FC2 + parity * 5 + j, value, j % 2, 5, FFN // 2)
    for j in range(20):
        value = gfc1[:, (j // 2) * LANES : (j // 2 + 1) * LANES]
        put_half(flat, AT_FC1 + j, value, j % 2, 10, DIM)
    for row in range(3):
        put_vector(flat, AT_VEC + 5 * row, gvec[row : row + 1, :])
    put_vector(flat, AT_FC2B, gvec[3:4, :])
    put_vector(flat, AT_FC1B, gfc1b[...])
    out[...] = flat[...].astype(bf16)


def pack_main(gproj, gfc1, gfc2, gvec, gfc1b, rows):
    return pl.pallas_call(
        pack_main_kernel,
        name="pack_main",
        out_shape=jax.ShapeDtypeStruct((rows, LANES), bf16),
        scratch_shapes=[pltpu.VMEM((rows, LANES), f32)],
        compiler_params=params(14),
    )(gproj, gfc1, gfc2, gvec, gfc1b)


QKV_ROWS = 2480


def pack_qkv_kernel(gqkv, gbias, out, end, flat):
    flat[...] = jnp.zeros(flat.shape, f32)
    for parity in range(2):
        for j in range(15):
            value = gqkv[j // 2, pl.ds(parity, DIM // 2, stride=2), :]
            put_half(flat, AT_QKV + parity * 15 + j, value, j % 2, 15, DIM // 2)
    for j in range(10):
        index = j if j < 5 else j + 5
        pair = gbias[:, index // 2 * LANES : (index // 2 + 1) * LANES]
        put_half(flat, AT_QV + j, pair, index % 2)
    out[...] = flat[:PACK_BASE, :].astype(bf16)
    end[...] = flat[PACK_BASE:, :].astype(bf16)


def pack_qkv(gqkv, gbias):
    return pl.pallas_call(
        pack_qkv_kernel,
        name="pack_qkv",
        out_shape=[
            jax.ShapeDtypeStruct((PACK_BASE, LANES), bf16),
            jax.ShapeDtypeStruct((QKV_ROWS - PACK_BASE, LANES), bf16),
        ],
        scratch_shapes=[pltpu.VMEM((QKV_ROWS, LANES), f32)],
        compiler_params=params(10),
    )(gqkv, gbias)


AXES = ("wide", "narrow")


def exchange(value, bit):
    count = lax.axis_size(AXES)
    return lax.ppermute(value, AXES, [(i, i ^ (1 << bit)) for i in range(count)])


def my_bit(bit):
    return (lax.axis_index(AXES) >> bit) & 1


def tie(*values):
    return lax.optimization_barrier(values)


def split(value, bit):
    value = value.reshape(value.shape[0] // 2, 2, -1, LANES)
    mine = my_bit(bit)
    keep = lax.dynamic_index_in_dim(value, mine, 1, keepdims=False)
    return keep, lax.dynamic_index_in_dim(value, 1 - mine, 1, keepdims=False)


def on_device(master, momentum, average, tokens, clip_ids, borders, cotangent):
    wide_count, narrow_count = lax.axis_size("wide"), lax.axis_size("narrow")
    count = wide_count * narrow_count
    bits = count.bit_length() - 1
    own_rows = master.shape[0]
    filled = jnp.sum((clip_ids >= 0).astype(jnp.int32))
    frames = jnp.where(filled > 6 * FRAME, 12, jnp.where(filled > 3 * FRAME, 6, 3)).reshape(1)
    me = lax.axis_index(AXES)
    quarter = me >> (bits - 2)
    blocks = master.astype(bf16)[None]
    other = exchange(blocks, bits - 2)
    other, frames = tie(other, frames)
    blocks = jnp.concatenate([blocks, other], axis=0)
    blocks, frames = tie(blocks, frames)
    other = exchange(blocks, bits - 1)
    xpad, spread, back, frames = prepare(frames, tokens.T)
    other, frames = tie(other, frames)
    blocks = jnp.concatenate([blocks, other], axis=0)
    first = lax.dynamic_index_in_dim(blocks, quarter, 0)
    rest = [lax.dynamic_index_in_dim(blocks, quarter ^ index, 0) for index in (1, 2, 3)]
    rest = jnp.concatenate(rest, axis=0)[None]
    low_bits = list(range(bits - 3, -1, -1))
    for step, bit in enumerate(low_bits):
        if step == 0:
            first, frames = tie(first, frames)
        other = exchange(first, bit)
        if step == 0:
            cotangent, frames = turn(frames, cotangent.T)
            other, frames = tie(other, frames)
        first = jnp.concatenate([first, other], axis=0)
        if step == 0:
            first, rest, frames = tie(first, rest, frames)
            rest = jnp.concatenate([rest, exchange(rest, bit)], axis=0)
    order = [0] * (count // 4)
    for step, bit in enumerate(low_bits):
        order = [place | (((index >> bit) & 1) << step) for index, place in enumerate(order)]
    mine = sum((((me >> bit) & 1) << step) for step, bit in enumerate(low_bits))
    order = jnp.array(order, jnp.int32) ^ mine
    head = lax.dynamic_index_in_dim(first, mine, 0, keepdims=False)
    head = jnp.concatenate([head, jnp.zeros((4, LANES), bf16)], axis=0)[:80] if own_rows < 80 else head[:80]
    mixed, convp = None, None
    for step, bit in enumerate(low_bits[1:]):
        if step < 2:
            rest, frames = tie(rest, frames)
        other = exchange(rest, bit)
        if step == 0:
            mixed, convp, frames = conv_piece(0, 8, frames, head, xpad, back, None)
        elif step == 1:
            mixed, convp, frames = conv_piece(8, 4, frames, head, xpad, back, mixed)
        other, frames = tie(other, frames)
        rest = jnp.concatenate([rest, other], axis=0)
    wide_qkv, wqkv, wproj, fc1, fc2, bqkv, vecs, fc1b = unpack(order, first, rest)
    normed, q, k, v, size = project(frames, mixed, convp, wide_qkv, bqkv)
    o, q_back = attend(q, k, v, size)
    output, gmid, do, gproj, gfc1, gfc2, gvec, gfc1b = feed_forward(
        frames, o, mixed, cotangent, wproj, fc1, fc2, vecs, fc1b
    )
    main = pack_main(gproj, gfc1, gfc2, gvec, gfc1b, count * own_rows)
    main = main.reshape(wide_count, narrow_count, own_rows, LANES)
    main = lax.psum_scatter(main, "wide", scatter_dimension=0, tiled=True)[0]
    q_back, do, k, v = (in_hbm(value) for value in (q_back, do, k, v))
    dq, dk, dv = attend_back(q_back, do, k, v)
    gpad, gqkv, gbias, gvec_one = project_back(dq, dk, dv, normed, mixed, gmid, wqkv, convp, spread)
    qkv, qkv_end = pack_qkv(gqkv, gbias)
    qkv = qkv.reshape(count // 4, own_rows, LANES)
    narrow_bits = narrow_count.bit_length() - 1
    for bit in range(narrow_bits):
        keep, give = split(qkv, bit)
        if bit == narrow_bits - 1:
            gvec_one, give = tie(gvec_one, give)
        qkv = keep + exchange(give, bit)
    conv = conv_weight_grads(frames, xpad, gpad, gvec_one)
    late = jnp.concatenate([conv, qkv_end], axis=0)
    main, late = tie(main, late)
    gtok = None
    for bit in range(bits):
        if bit < narrow_bits:
            keep, give = split(main, bit)
        elif bit < bits - 2:
            keep, give = split(qkv, bit)
        else:
            keep, give = qkv, qkv
        sent = give.shape[0] * own_rows
        packet = jnp.concatenate([give.reshape(sent, LANES), late], axis=0)
        packet, frames = tie(packet, frames)
        other = exchange(packet, bit)
        if bit < 3:
            gtok, frames = token_piece(bit, frames, convp, gpad, back, gtok)
        elif bit == 3:
            output, frames = turn(frames, output)
        elif bit == 4:
            gtok, frames = turn(frames, gtok)
        other, frames = tie(other, frames)
        summed = keep + other[:sent].reshape(keep.shape)
        late = late + other[sent:]
        if bit < narrow_bits:
            main = summed
        else:
            qkv = summed
    main, qkv = main[0], qkv[0]
    early = jnp.where(me < count // 4, qkv.astype(f32), main.astype(f32))
    conv, qkv_end = late[:80].astype(f32), late[80:].astype(f32)
    if own_rows < 80:
        conv = conv[:own_rows]
    conv = jnp.pad(conv, ((0, own_rows - conv.shape[0]), (0, 0)))
    qkv_end = jnp.pad(qkv_end, ((0, own_rows - qkv_end.shape[0]), (0, 0)))
    owned = early + jnp.where(me == 0, conv, jnp.where(me == count // 4, qkv_end, 0.0))
    rate = RATE_FACTOR / math.sqrt(tokens.shape[0] * count)
    decayed = owned + DECAY_RATE * master
    new_momentum = MOMENTUM * momentum + decayed
    new_master = master - rate * (decayed + MOMENTUM * new_momentum)
    new_average = AVERAGE_KEEP * average + (1.0 - AVERAGE_KEEP) * new_master
    return (output.T, gtok.T, owned, new_master, new_momentum, new_average, new_master.astype(bf16))


def solution(mesh):
    rows = P(("wide", "narrow"), None)
    return jax.shard_map(
        on_device,
        mesh=mesh,
        in_specs=(rows, rows, rows, rows, P(("wide", "narrow")), P(("wide", "narrow")), rows),
        out_specs=(rows,) * 7,
        check_vma=False,
    )
```

```python
import functools
import math

import jax
import jax.numpy as jnp
from jax import lax
from jax.experimental import pallas as pl
from jax.experimental.pallas import tpu as pltpu
from jax.sharding import PartitionSpec as P

HEADS = 5
HEAD_DIM = 64
DIM = 320
FFN = 1280
SIDE = 14
FRAME = SIDE * SIDE
LANES = 128
PAIRS = (HEADS + 1) // 2
PAIR_COLUMNS = PAIRS * LANES
QKV_COLUMNS = 3 * PAIR_COLUMNS

EPSILON = 1e-06
MOMENTUM = 0.9
DECAY_RATE = 0.0001
AVERAGE_KEEP = 0.8
RATE_FACTOR = 0.03
LOG2E = 1.0 / math.log(2.0)
LN2 = math.log(2.0)
INVERSE_ROOT_TWO_PI = 1.0 / math.sqrt(2.0 * math.pi)
BLOCKED = -(2.0**30)
SAFE_BOUND = 80.0

TILES = ((0, 128), (128, 256), (256, 320))

bf16 = jnp.bfloat16
f32 = jnp.float32

AT_CONV = 0
AT_QKV = 150
AT_QV = 4950
AT_PROJ = 4960
AT_VEC = 6560
AT_FC1 = 6575
AT_FC1B = 12975
AT_FC2 = 12995
AT_FC2B = 19395
HALF_END = 19400


SMEM_SPEC = pl.BlockSpec(memory_space=pltpu.SMEM)
VMEM_SPEC = pl.BlockSpec(memory_space=pltpu.VMEM)
ANY_SPEC = pl.BlockSpec(memory_space=pl.ANY)
HBM_SPEC = pl.BlockSpec(memory_space=pltpu.HBM)


def in_hbm(value):
    return pltpu.with_memory_space_constraint(value, pltpu.HBM)


def dot(a, b):
    return lax.dot_general(a, b, (((1,), (0,)), ((), ())), preferred_element_type=f32)


def dot_nt(a, b):
    return lax.dot_general(a, b, (((1,), (1,)), ((), ())), preferred_element_type=f32)


def dot_tn(a, b):
    return lax.dot_general(a, b, (((0,), (0,)), ((), ())), preferred_element_type=f32)


def params(limit=58):
    return pltpu.CompilerParams(vmem_limit_bytes=limit << 20)


def lane_of(shape):
    return lax.broadcasted_iota(jnp.int32, shape, len(shape) - 1)


def row_of(shape):
    return lax.broadcasted_iota(jnp.int32, shape, 0)


def low_half(value, side):
    return value if side == 0 else pltpu.roll(value, 64, axis=1)


def high_half(value, side):
    return value if side == 1 else pltpu.roll(value, 64, axis=1)


def split3(value):
    first = value.astype(bf16).astype(f32)
    rest = value - first
    second = rest.astype(bf16).astype(f32)
    return first, second, rest - second


def read_half(flat, at, length, step, count, parity, j):
    index = at + parity * length + j
    return flat[pl.ds(index // 2, count, stride=step), :], index % 2


def read_vector(flat, at, length):
    tiles = []
    lane = lane_of((1, LANES))
    for j in range(0, length, 2):
        row, side = divmod(at + j, 2)
        low = low_half(flat[row : row + 1, :], side)
        if j + 1 < length:
            row, side = divmod(at + j + 1, 2)
            tiles.append(jnp.where(lane < 64, low, high_half(flat[row : row + 1, :], side)))
        else:
            tiles.append(low[:, :64])
    return jnp.concatenate(tiles, axis=1)


def odd_matrix(flat, out, at, length, rows):
    pairs = rows // 2
    for parity in range(2):
        for tile in range((length + 1) // 2):
            low, side = read_half(flat, at, length, length, pairs, parity, 2 * tile)
            low = low_half(low, side)
            place = pl.ds(parity, pairs, stride=2)
            if 2 * tile + 1 < length:
                high, side = read_half(flat, at, length, length, pairs, parity, 2 * tile + 1)
                merged = jnp.where(lane_of(low.shape) < 64, low, high_half(high, side))
            else:
                merged = low
            out[tile, place, :] = merged


def unpack_kernel(order, first, rest, wqkv, wproj, fc1, fc2, bqkv, vecs, fc1b, flat, wide, tall):
    blocks, rows = first.shape[:2]
    for block in range(blocks):
        place = order[block]
        for quarter in range(4):
            start = (quarter * blocks + block) * rows
            value = first[place] if quarter == 0 else rest[place, quarter - 1]
            flat[start : start + rows, :] = value.astype(f32)
    for parity in range(2):
        place = pl.ds(parity, DIM // 2, stride=2)
        for kind in range(3):
            for pair in range(PAIRS):
                j = kind * HEADS + 2 * pair
                low, side = read_half(flat, AT_QKV, 15, 15, DIM // 2, parity, j)
                low = low_half(low, side)
                high = jnp.zeros_like(low)
                if 2 * pair + 1 < HEADS:
                    high, side = read_half(flat, AT_QKV, 15, 15, DIM // 2, parity, j + 1)
                    high = high_half(high, side)
                wide[kind * PAIRS + pair, place, :] = jnp.where(lane_of(low.shape) < 64, low, high)
    for tile in range(3 * PAIRS):
        wqkv[:, tile * LANES : (tile + 1) * LANES] = wide[tile].astype(bf16)
    bqkv[...] = jnp.zeros(bqkv.shape, f32)
    for index, kind in enumerate((0, 2)):
        start = kind * PAIR_COLUMNS
        bqkv[:, start : start + DIM] = read_vector(flat, AT_QV + index * HEADS, HEADS)
    odd_matrix(flat, wide, AT_PROJ, 5, DIM)
    for tile, (low, high) in enumerate(TILES):
        wproj[:DIM, low:high] = wide[tile, :, : high - low].astype(bf16)
    wproj[DIM:, :] = jnp.zeros((PAIR_COLUMNS - DIM, DIM), bf16)
    for row in range(3):
        vecs[row : row + 1, :] = read_vector(flat, AT_VEC + 5 * row, 5)
    vecs[3:4, :] = read_vector(flat, AT_FC2B, 5)
    vecs[4:8, :] = jnp.zeros((4, DIM), f32)
    fc1b[...] = read_vector(flat, AT_FC1B, 20)
    for tile in range(10):
        low, side = read_half(flat, AT_FC1, 20, 10, DIM, 0, 2 * tile)
        high, side_high = read_half(flat, AT_FC1, 20, 10, DIM, 0, 2 * tile + 1)
        merged = jnp.where(lane_of(low.shape) < 64, low_half(low, side), high_half(high, side_high))
        fc1[:, tile * LANES : (tile + 1) * LANES] = merged.astype(bf16)
    odd_matrix(flat, tall, AT_FC2, 5, FFN)
    for tile in range(3):
        width = LANES if tile < 2 else 64
        fc2[:, tile * LANES : tile * LANES + width] = tall[tile, :, :width].astype(bf16)


def unpack(order, first, rest):
    rows = 4 * first.shape[0] * first.shape[1]
    return pl.pallas_call(
        unpack_kernel,
        name="unpack",
        in_specs=[SMEM_SPEC, VMEM_SPEC, VMEM_SPEC],
        out_shape=[
            jax.ShapeDtypeStruct((DIM, QKV_COLUMNS), bf16),
            jax.ShapeDtypeStruct((PAIR_COLUMNS, DIM), bf16),
            jax.ShapeDtypeStruct((DIM, FFN), bf16),
            jax.ShapeDtypeStruct((FFN, DIM), bf16),
            jax.ShapeDtypeStruct((1, QKV_COLUMNS), f32),
            jax.ShapeDtypeStruct((8, DIM), f32),
            jax.ShapeDtypeStruct((1, FFN), f32),
        ],
        scratch_shapes=[
            pltpu.VMEM((rows, LANES), f32),
            pltpu.VMEM((15, DIM, LANES), f32),
            pltpu.VMEM((3, FFN, LANES), f32),
        ],
        compiler_params=params(18),
    )(order, first, rest)


PAD_ROWS = 16 * 16
BODY = SIDE * 16


def spread_matrix(shift):
    cell = lax.broadcasted_iota(jnp.int32, (PAD_ROWS, 208), 0)
    source = lax.broadcasted_iota(jnp.int32, (PAD_ROWS, 208), 1)
    row, column = cell >> 4, cell & 15
    inside = (row >= 1) & (row <= SIDE) & (column < SIDE)
    wanted = (row - 1) * SIDE + column + shift
    return jnp.where(inside & (source == wanted), 1.0, 0.0).astype(bf16)


def gather_matrix(shift):
    target = lax.broadcasted_iota(jnp.int32, (208, BODY), 0)
    cell = lax.broadcasted_iota(jnp.int32, (208, BODY), 1)
    row, column = cell >> 4, cell & 15
    wanted = row * SIDE + column + shift
    return jnp.where((column < SIDE) & (target == wanted), 1.0, 0.0).astype(bf16)


def pieces(value):
    first = value.astype(bf16)
    return first, (value - first.astype(f32)).astype(bf16)


def prepare_kernel(frames, turned, target, spread, back, passed, tokens, padded, sems):
    for member in range(4):
        spread[member] = spread_matrix(4 * member)
        back[member] = gather_matrix(4 * member)
    passed[0] = frames[0]
    tokens[...] = turned[...].T

    def fill(frame, carry):
        member = frame & 3
        place = pl.ds(pl.multiple_of(frame * FRAME - 4 * member, 16), 208)
        padded[frame] = dot(spread[member], tokens[place, :])
        return carry

    copies = []
    for group in range(padded.shape[0] // 4):
        lax.fori_loop(4 * group, 4 * group + 4, fill, 0)
        place = pl.ds(4 * group, 4)
        copies.append(pltpu.make_async_copy(padded.at[place], target.at[place], sems.at[group]))
        copies[-1].start()
    for copy in copies:
        copy.wait()


def prepare(frames, turned):
    rows = turned.shape[1]
    return pl.pallas_call(
        prepare_kernel,
        name="prepare",
        in_specs=[SMEM_SPEC, VMEM_SPEC],
        out_specs=[HBM_SPEC, VMEM_SPEC, VMEM_SPEC, SMEM_SPEC],
        out_shape=[
            pltpu.HBM((rows // FRAME, PAD_ROWS, DIM), f32),
            jax.ShapeDtypeStruct((4, PAD_ROWS, 208), bf16),
            jax.ShapeDtypeStruct((4, 208, BODY), bf16),
            jax.ShapeDtypeStruct((1,), jnp.int32),
        ],
        scratch_shapes=[
            pltpu.VMEM((rows, DIM), bf16),
            pltpu.VMEM((rows // FRAME, PAD_ROWS, DIM), f32),
            pltpu.SemaphoreType.DMA((rows // FRAME // 4,)),
        ],
        compiler_params=params(16),
    )(frames, turned)


PIECE = 4 * FRAME


def fetch_frames(source, slots, sems, start, count):
    first, last = max(start - 1, 0), min(start + count + 1, source.shape[0])
    middle = start + 2
    copies = []
    for index, (low, high) in enumerate(((first, middle), (middle, last))):
        copies.append(
            pltpu.make_async_copy(
                source.at[pl.ds(low, high - low)], slots.at[pl.ds(low - start + 1, high - low)], sems.at[index]
            )
        )
    return copies


def mix_frame(slots, at, weights, sums, out, sign):
    for low, high in TILES:
        for start in range(0, BODY, 56):
            parts = [None, None, None]
            for a in (-1, 0, 1):
                for b in (-1, 0, 1):
                    begin = 16 + sign * b * 16 + start
                    cells = slots[at[1 + sign * a], begin : begin + 56, low:high]
                    for c in range(3):
                        tap = 9 * (a + 1) + 3 * (b + 1) + c
                        term = cells * weights[tap : tap + 1, low:high]
                        parts[c] = term if parts[c] is None else parts[c] + term
            parts[1] = parts[1] + slots[at[1], 16 + start : 16 + start + 56, low:high]
            for c in range(3):
                sums[c, start : start + 56, low:high] = parts[c]
    before, after = (0, 2) if sign == 1 else (2, 0)
    for low, high in TILES:
        out[:, low:high] = (
            sums[1, :, low:high]
            + pltpu.roll(sums[before, :, low:high], 1, axis=0)
            + pltpu.roll(sums[after, :, low:high], BODY - 1, axis=0)
        )


def mask_weights(weights, masked, first, middle, last):
    for tap in range(27):
        keep = (first, middle, last)[tap // 9]
        scale = 1.0 if tap == 13 else jnp.where(keep, 1.0, 0.0)
        masked[tap : tap + 1, :] = weights[tap : tap + 1, :] * scale


def conv_params(head, flat, weights):
    flat[...] = head[...].astype(f32)
    for parity in range(2):
        for tile in range(3):
            low, side = read_half(flat, AT_CONV, 5, 5, 15, parity, 2 * tile)
            low = low_half(low, side)
            place = pl.ds(parity, 15, stride=2)
            if tile < 2:
                high, side = read_half(flat, AT_CONV, 5, 5, 15, parity, 2 * tile + 1)
                low = jnp.where(lane_of(low.shape) < 64, low, high_half(high, side))
            weights[tile, place, :] = low


def turn_kernel(frames, source, out, passed):
    passed[0] = frames[0]
    out[...] = source[...].T


def turn(frames, value):
    rows, columns = value.shape
    return pl.pallas_call(
        turn_kernel,
        name="turn",
        in_specs=[SMEM_SPEC, VMEM_SPEC],
        out_specs=[VMEM_SPEC, SMEM_SPEC],
        out_shape=[
            jax.ShapeDtypeStruct((columns, rows), value.dtype),
            jax.ShapeDtypeStruct((1,), jnp.int32),
        ],
        compiler_params=params(10),
        cost_estimate=pl.CostEstimate(flops=0, bytes_accessed=4 * rows * columns, transcendentals=0),
    )(frames, value)


def conv_piece_kernel(start, count, frames_ref, head, padded, back, *refs):
    if start > 0:
        refs = refs[1:]
    mixed, convp, passed, flat, weights, masked, slots, sums, comp, sem = refs
    passed[0] = frames_ref[0]
    copies = fetch_frames(padded, slots, sem, start, count)
    for copy in copies:
        copy.start()
    frames = frames_ref[0]
    conv_params(head, flat, weights)
    for tile, (low, high) in enumerate(TILES):
        convp[:, low:high] = weights[tile, :, : high - low]
    mixed[...] = jnp.zeros(mixed.shape, f32)
    copies[0].wait()

    def each(member, carry):
        @pl.when(member == 1)
        def _():
            copies[1].wait()

        frame = start + member
        there = frame < frames
        before = there & (frame > 0)
        after = frame + 1 < frames
        mask_weights(convp, masked, before, there, after)
        at = (member + jnp.where(before, 0, 1), member + 1, member + jnp.where(after, 2, 1))
        mix_frame(slots, at, masked, sums, comp, 1)
        high, low = pieces(comp[...] + convp[27:28, :])
        shift = member & 3
        place = pl.ds(pl.multiple_of(FRAME * member - 4 * shift, 16), 208)
        mixed[place, :] += dot(back[shift], high) + dot(back[shift], low)
        return carry

    lax.fori_loop(0, count, each, 0)


def conv_piece(start, count, frames, head, padded, back, mixed):
    rows = padded.shape[0] * FRAME
    operands = [frames, head, in_hbm(padded), back] + ([] if start == 0 else [mixed])
    return pl.pallas_call(
        functools.partial(conv_piece_kernel, start, count),
        name=f"conv_piece{start}",
        grid=(1,),
        in_specs=[SMEM_SPEC, VMEM_SPEC, HBM_SPEC, VMEM_SPEC] + [ANY_SPEC] * (start > 0),
        out_specs=[
            pl.BlockSpec((count * FRAME, DIM), lambda i: (start // count, 0)),
            pl.BlockSpec((32, DIM), lambda i: (0, 0)),
            SMEM_SPEC,
        ],
        out_shape=[
            jax.ShapeDtypeStruct((rows, DIM), f32),
            jax.ShapeDtypeStruct((32, DIM), f32),
            jax.ShapeDtypeStruct((1,), jnp.int32),
        ],
        input_output_aliases={4: 0} if start else {},
        scratch_shapes=[
            pltpu.VMEM(head.shape, f32),
            pltpu.VMEM((3, 32, LANES), f32),
            pltpu.VMEM((32, DIM), f32),
            pltpu.VMEM((count + 2, PAD_ROWS, DIM), f32),
            pltpu.VMEM((3, BODY, DIM), f32),
            pltpu.VMEM((BODY, DIM), f32),
            pltpu.SemaphoreType.DMA((2,)),
        ],
        compiler_params=params(20),
    )(*operands)


def normalize(values):
    centered = values - jnp.mean(values, axis=-1, keepdims=True)
    variance = jnp.mean(centered * centered, axis=-1, keepdims=True)
    inverse = lax.rsqrt(variance + EPSILON)
    return centered * inverse, inverse


def flag_base(head):
    return HEAD_DIM if head % 2 == 0 else 0


def own_lanes(lane, head):
    return lane < HEAD_DIM if head % 2 == 0 else lane >= HEAD_DIM


def row_size(value, own):
    part = jnp.where(own, value.astype(f32), 0.0)
    return jnp.sum(part * part, axis=-1, keepdims=True)


def qkv_kernel(frames_ref, mixed, convp, wqkv, bqkv, normed_out, q_out, k_out, v_out, size):
    block = pl.program_id(0)
    rows = mixed.shape[0]
    frames = frames_ref[0]
    normal, unused_inverse = normalize(mixed[...])
    normed = (normal * convp[28:29, :] + convp[29:30, :]).astype(bf16)
    normed_out[...] = normed
    lane = lane_of((rows, LANES))
    inside = row_of((rows, LANES)) + block * rows < frames * FRAME
    scale = HEAD_DIM ** (-0.5) * LOG2E

    @pl.when(block == 0)
    def _():
        size[...] = jnp.zeros(size.shape, f32)

    projected = dot(normed, wqkv[...]) + bqkv[...]
    masks = []
    for base in (flag_base(0), flag_base(1)):
        flag = lane - base
        q_flags = jnp.where(((flag == 0) & ~inside) | ((flag == 1) & inside), BLOCKED, 0.0)
        k_flags = jnp.where(
            ((flag == 0) & inside) | ((flag == 1) & ~inside) | ((flag >= 2) & (flag < 5)), 1.0, 0.0
        )
        v_flags = jnp.where((flag >= 0) & (flag < 3), 1.0, 0.0)
        masks.append((q_flags, k_flags, v_flags))
    for head in range(HEADS):
        q_mask, k_mask, v_mask = masks[head % 2]
        own = own_lanes(lane, head)

        def columns(kind, head=head):
            start = (kind * PAIRS + head // 2) * LANES
            return projected[:, start : start + LANES]

        query = jnp.where(own, columns(0) * scale, q_mask).astype(bf16)
        key = jnp.where(own, columns(1), k_mask).astype(bf16)
        query_size = jnp.max(row_size(query, own), axis=0, keepdims=True)
        key_size = jnp.max(row_size(key, own), axis=0, keepdims=True)
        q_out[head] = query
        k_out[head] = key
        v_out[head] = jnp.where(own, columns(2), v_mask).astype(bf16)
        size[head : head + 1, :] = jnp.maximum(size[head : head + 1, :], query_size)
        size[head + 8 : head + 9, :] = jnp.maximum(size[head + 8 : head + 9, :], key_size)


def project(frames, mixed, convp, wqkv, bqkv, block=784):
    rows = mixed.shape[0]
    heads_spec = pl.BlockSpec((HEADS, block, LANES), lambda i: (0, i, 0))
    rows_spec = pl.BlockSpec((block, DIM), lambda i: (i, 0))
    heads_shape = jax.ShapeDtypeStruct((HEADS, rows, LANES), bf16)
    return pl.pallas_call(
        qkv_kernel,
        name="qkv_forward",
        grid=(rows // block,),
        in_specs=[
            SMEM_SPEC,
            rows_spec,
            pl.BlockSpec((32, DIM), lambda i: (0, 0)),
            pl.BlockSpec((DIM, QKV_COLUMNS), lambda i: (0, 0)),
            pl.BlockSpec((1, QKV_COLUMNS), lambda i: (0, 0)),
        ],
        out_specs=[rows_spec, heads_spec, heads_spec, heads_spec, pl.BlockSpec((16, LANES), lambda i: (0, 0))],
        out_shape=[
            pltpu.HBM((rows, DIM), bf16),
            heads_shape,
            heads_shape,
            heads_shape,
            jax.ShapeDtypeStruct((16, LANES), f32),
        ],
        compiler_params=params(14),
    )(frames, mixed, convp, wqkv, bqkv)


def attend_kernel(chunk, q, k, v, size, o_out, q_back, query, shift):
    head = pl.program_id(0)
    keys = k.shape[1]
    tall = q.shape[1]
    bound = jnp.max(size[pl.ds(head, 1), :] * size[pl.ds(head + 8, 1), :])
    query[...] = q[0]
    shift[...] = jnp.zeros(shift.shape, f32)

    @pl.when(bound > SAFE_BOUND * SAFE_BOUND)
    def _():
        shift[...] = jnp.full(shift.shape, -jnp.inf, f32)

        def peak(step, carry):
            scores = dot_nt(k[0, pl.ds(pl.multiple_of(step * 112, 16), 112), :], q[0])
            shift[...] = jnp.maximum(shift[...], jnp.max(scores, axis=0, keepdims=True))
            return carry

        lax.fori_loop(0, keys // 112, peak, 0)
        first, second, third = split3(-shift[...])
        flag = row_of((LANES, tall)) - jnp.where(lax.rem(head, 2) == 0, HEAD_DIM, 0)
        tail = jnp.where(flag == 2, first, jnp.where(flag == 3, second, jnp.where(flag == 4, third, 0.0)))
        query[...] = (q[0].astype(f32) + tail.T).astype(bf16)

    total = None
    for start in range(0, keys, chunk):
        place = slice(start, min(start + chunk, keys))
        weights = jnp.exp2(dot_nt(k[0, place, :], query[...])).astype(bf16)
        part = dot_tn(v[0, place, :], weights)
        total = part if total is None else total + part
    def finish(parity):
        base = flag_base(parity)
        sums = total[base : base + 1, :]
        first, second, third = split3(-(shift[...] + jnp.log2(sums)))
        row = row_of((8, tall))
        tail = jnp.where(row == 2, first, jnp.where(row == 3, second, jnp.where(row == 4, third, 0.0)))
        flags = [tail, jnp.zeros((56, tall), f32)]
        own = [total[HEAD_DIM - base : 2 * HEAD_DIM - base, :] / sums]
        stacked = jnp.concatenate(own + flags if parity == 0 else flags + own, axis=0).T
        lane = lane_of((tall, LANES))
        o_out[0] = jnp.where(own_lanes(lane, parity), stacked, 0.0).astype(bf16)
        place = (lane >= base + 2) & (lane < base + 5)
        q_back[0] = jnp.where(place, stacked, q[0].astype(f32)).astype(bf16)

    for parity in range(2):
        pl.when(lax.rem(head, 2) == parity)(functools.partial(finish, parity))


def attend(q, k, v, size, chunk=512):
    rows = q.shape[1]
    whole = pl.BlockSpec((1, rows, LANES), lambda h: (h, 0, 0))
    shape = jax.ShapeDtypeStruct((HEADS, rows, LANES), bf16)
    return pl.pallas_call(
        functools.partial(attend_kernel, chunk),
        name="attend",
        grid=(HEADS,),
        in_specs=[whole, whole, whole, pl.BlockSpec((16, LANES), lambda h: (0, 0))],
        out_specs=[whole, whole],
        out_shape=[shape, pltpu.HBM(shape.shape, bf16)],
        scratch_shapes=[pltpu.VMEM((rows, LANES), bf16), pltpu.VMEM((1, rows), f32)],
        compiler_params=params(18),
    )(q, k, v, size)


def attend_back_kernel(q, do, k, v, dq_out, dk_out, dv_out):
    weights = jnp.exp2(dot_nt(q[0], k[0]))
    grad_scores = (weights * dot_nt(do[0], v[0])).astype(bf16)
    dv_out[0] = dot_tn(do[0], weights.astype(bf16)).T.astype(bf16)
    dk_out[0] = (dot_tn(q[0], grad_scores) * LN2).T.astype(bf16)
    dq_out[0] = (dot_nt(k[0].T, grad_scores) * HEAD_DIM ** (-0.5)).T.astype(bf16)


def attend_back(q, do, k, v):
    heads, rows = q.shape[:2]
    whole = pl.BlockSpec((1, rows, LANES), lambda h: (h, 0, 0))
    shape = jax.ShapeDtypeStruct((heads, rows, LANES), bf16)
    return pl.pallas_call(
        attend_back_kernel,
        name="attend_back",
        grid=(heads,),
        in_specs=[whole] * 4,
        out_specs=[whole] * 3,
        out_shape=[shape] * 3,
        compiler_params=params(40),
    )(q, do, k, v)


def erf_parts(value):
    bell = jnp.exp(-0.5 * value * value)
    return bell, 0.5 * (1.0 + lax.erf(value * (1.0 / math.sqrt(2.0))))


def paired(heads):
    tiles = []
    for head in range(0, HEADS, 2):
        high = heads[head + 1] if head + 1 < HEADS else jnp.zeros_like(heads[head])
        tiles.append(jnp.where(lane_of(high.shape) < HEAD_DIM, heads[head], high))
    return jnp.concatenate(tiles, axis=1)


def add_tiles(ref, place, value):
    for tile, (low, high) in enumerate(TILES):
        ref[tile, place, : high - low] += value[:, low:high]


def middle_kernel(
    frames_ref, o, mixed, cot, wproj, fc1, fc2, vecs, fc1b,
    output, gmid_out, do_out, gproj, gfc1, gfc2, gvec, gfc1b, chunk,
):
    block = pl.program_id(0)
    rows = mixed.shape[0]
    inside = row_of((rows, DIM)) + block * rows < frames_ref[0] * FRAME

    @pl.when(block == 0)
    def _():
        for ref in (gproj, gfc1, gfc2, gvec, gfc1b):
            ref[...] = jnp.zeros(ref.shape, f32)

    attended = paired(o)
    middle = mixed[...] + (dot(attended, wproj[...]) + vecs[0:1, :])
    normal, inverse = normalize(middle)
    normed = (normal * vecs[1:2, :] + vecs[2:3, :]).astype(bf16)
    grad_output = jnp.where(inside, cot[...].astype(f32), 0.0)
    grad_outer = grad_output.astype(bf16)
    total = middle + vecs[3:4, :]
    grad_normed = jnp.zeros((rows, DIM), f32)
    for start in range(0, FFN, chunk):
        place = slice(start, start + chunk)
        inner = dot(normed, fc1[:, place]) + fc1b[:, place]
        bell, gate = erf_parts(inner)
        activated = (inner * gate).astype(bf16)
        total += dot(activated, fc2[place, :])
        slope = gate + inner * bell * INVERSE_ROOT_TWO_PI
        grad_inner = (dot_nt(grad_outer, fc2[place, :]) * slope)
        gfc1b[:, place] += jnp.sum(grad_inner, axis=0, keepdims=True)
        grad_inner = grad_inner.astype(bf16)
        add_tiles(gfc2, place, dot_tn(activated, grad_outer))
        gfc1[:, place] += dot_tn(normed, grad_inner)
        grad_normed += dot_nt(grad_inner, fc1[:, place])
    output[...] = total.astype(bf16)
    scaled = grad_normed * vecs[1:2, :]
    grad_middle = grad_output + inverse * (
        scaled
        - jnp.mean(scaled, axis=-1, keepdims=True)
        - normal * jnp.mean(scaled * normal, axis=-1, keepdims=True)
    )
    gmid_out[...] = grad_middle
    grad_branch = grad_middle.astype(bf16)
    add_tiles(gproj, slice(None), dot_tn(attended, grad_branch))
    gvec[0:1, :] += jnp.sum(grad_branch.astype(f32), axis=0, keepdims=True)
    gvec[1:2, :] += jnp.sum(grad_normed * normal, axis=0, keepdims=True)
    gvec[2:3, :] += jnp.sum(grad_normed, axis=0, keepdims=True)
    gvec[3:4, :] += jnp.sum(grad_output, axis=0, keepdims=True)
    lane = lane_of((rows, LANES))
    grad_attended = dot_nt(grad_branch, wproj[...])
    for head in range(HEADS):
        grad_head = grad_attended[:, head // 2 * LANES : (head // 2 + 1) * LANES]
        flag = lane - flag_base(head)
        delta = jnp.sum(grad_head * o[head].astype(f32), axis=-1, keepdims=True)
        first, second, third = split3(-delta)
        tail = jnp.where(flag == 0, first, jnp.where(flag == 1, second, third))
        do_out[head] = jnp.where((flag >= 0) & (flag < 3), tail, grad_head).astype(bf16)


def feed_forward(frames, o, mixed, cot, wproj, fc1, fc2, vecs, fc1b, block=784, chunk=256):
    rows = mixed.shape[0]
    heads_spec = pl.BlockSpec((HEADS, block, LANES), lambda i: (0, i, 0))
    rows_spec = pl.BlockSpec((block, DIM), lambda i: (i, 0))

    def full(*shape):
        return pl.BlockSpec(shape, lambda i: (0,) * len(shape))

    return pl.pallas_call(
        functools.partial(middle_kernel, chunk=chunk),
        name="feed_forward",
        grid=(rows // block,),
        in_specs=[
            SMEM_SPEC, heads_spec, rows_spec, rows_spec,
            full(PAIR_COLUMNS, DIM), full(DIM, FFN), full(FFN, DIM), full(8, DIM), full(1, FFN),
        ],
        out_specs=[
            rows_spec, rows_spec, heads_spec,
            full(3, PAIR_COLUMNS, LANES), full(DIM, FFN), full(3, FFN, LANES), full(8, DIM), full(1, FFN),
        ],
        out_shape=[
            pltpu.HBM((rows, DIM), bf16),
            pltpu.HBM((rows, DIM), f32),
            pltpu.HBM((HEADS, rows, LANES), bf16),
            jax.ShapeDtypeStruct((3, PAIR_COLUMNS, LANES), f32),
            jax.ShapeDtypeStruct((DIM, FFN), f32),
            jax.ShapeDtypeStruct((3, FFN, LANES), f32),
            jax.ShapeDtypeStruct((8, DIM), f32),
            jax.ShapeDtypeStruct((1, FFN), f32),
        ],
        compiler_params=params(22),
    )(frames, o, mixed, cot, wproj, fc1, fc2, vecs, fc1b)


def qkv_back_kernel(dq, dk, dv, normed, mixed, gmid, wqkv, convp, spread, padded, gqkv, gbias, gvec, gmix):
    block = pl.program_id(0)

    @pl.when(block == 0)
    def _():
        for ref in (gqkv, gbias, gvec):
            ref[...] = jnp.zeros(ref.shape, f32)

    normal, inverse = normalize(mixed[...])
    grads = jnp.concatenate([paired(part) for part in (dq, dk, dv)], axis=1)
    grad_qkv = dot_tn(normed[...], grads)
    for tile in range(3 * PAIRS):
        gqkv[tile] += grad_qkv[:, tile * LANES : (tile + 1) * LANES]
    gbias[...] += jnp.sum(grads.astype(f32), axis=0, keepdims=True)
    grad_normed = dot_nt(grads, wqkv[...])
    gvec[1:2, :] += jnp.sum(grad_normed * normal, axis=0, keepdims=True)
    gvec[2:3, :] += jnp.sum(grad_normed, axis=0, keepdims=True)
    scaled = grad_normed * convp[28:29, :]
    grad_mixed = gmid[...] + inverse * (
        scaled
        - jnp.mean(scaled, axis=-1, keepdims=True)
        - normal * jnp.mean(scaled * normal, axis=-1, keepdims=True)
    )
    gvec[0:1, :] += jnp.sum(grad_mixed, axis=0, keepdims=True)
    gmix[...] = grad_mixed
    for member in range(mixed.shape[0] // FRAME):
        high, low = pieces(gmix[192 * member : 192 * member + 208, :])
        padded[member] = dot(spread[member], high) + dot(spread[member], low)


def project_back(dq, dk, dv, normed, mixed, gmid, wqkv, convp, spread, block=PIECE):
    rows = mixed.shape[0]
    heads_spec = pl.BlockSpec((HEADS, block, LANES), lambda i: (0, i, 0))
    rows_spec = pl.BlockSpec((block, DIM), lambda i: (i, 0))

    def full(*shape):
        return pl.BlockSpec(shape, lambda i: (0,) * len(shape))

    return pl.pallas_call(
        qkv_back_kernel,
        name="qkv_back",
        grid=(rows // block,),
        in_specs=[heads_spec, heads_spec, heads_spec, rows_spec, rows_spec, rows_spec,
                  full(DIM, QKV_COLUMNS), full(32, DIM), full(4, PAD_ROWS, 208)],
        out_specs=[pl.BlockSpec((4, PAD_ROWS, DIM), lambda i: (i, 0, 0)), full(3 * PAIRS, DIM, LANES), full(1, QKV_COLUMNS), full(8, DIM)],
        out_shape=[
            pltpu.HBM((rows // FRAME, PAD_ROWS, DIM), f32),
            jax.ShapeDtypeStruct((3 * PAIRS, DIM, LANES), f32),
            jax.ShapeDtypeStruct((1, QKV_COLUMNS), f32),
            jax.ShapeDtypeStruct((8, DIM), f32),
        ],
        scratch_shapes=[pltpu.VMEM((block, DIM), f32)],
        compiler_params=params(18),
    )(dq, dk, dv, normed, mixed, gmid, wqkv, convp, spread)


def conv_weight_kernel(frames_ref, xsource, gsource, gvec, out, xpad, gpad, moved, sums, tiles, flat, xsem, gsem):
    frames = frames_ref[0]
    count = xpad.shape[0]
    copies = []
    for group in range(count // 4):
        place = pl.ds(4 * group, 4)
        copies.append(pltpu.make_async_copy(xsource.at[place], xpad.at[place], xsem.at[group]))
        copies.append(pltpu.make_async_copy(gsource.at[place], gpad.at[place], gsem.at[group]))
    for copy in copies:
        copy.start()
    sums[...] = jnp.zeros(sums.shape, f32)

    def weight_frame(frame, carry):
        for low, high in TILES:
            body = gpad[frame, 16 : 16 + BODY, low:high]
            moved[0, :, low:high] = pltpu.roll(body, BODY - 1, axis=0)
            moved[1, :, low:high] = pltpu.roll(body, 1, axis=0)
        for a in (-1, 0, 1):
            at = frame + a

            @pl.when((at >= 0) & (at < frames))
            def _():
                for low, high in TILES:
                    for b in (-1, 0, 1):
                        cells = xpad[at, 16 + b * 16 : 16 + b * 16 + BODY, low:high]
                        for c in range(3):
                            body = (
                                gpad[frame, 16 : 16 + BODY, low:high]
                                if c == 1
                                else moved[c // 2, :, low:high]
                            )
                            product = (body * cells).reshape(BODY // 8, 8, high - low)
                            tap = 9 * (a + 1) + 3 * (b + 1) + c
                            sums[tap, :, low:high] += jnp.sum(product, axis=0)

        return carry

    for group in range(count // 4):
        copies[2 * group].wait()
        copies[2 * group + 1].wait()
        start = max(4 * group - 1, 0)
        stop = 4 * group + 3 if group < count // 4 - 1 else count
        lax.fori_loop(jnp.minimum(start, frames), jnp.minimum(stop, frames), weight_frame, 0)
    tiles[...] = jnp.zeros(tiles.shape, f32)
    flat[...] = jnp.zeros(flat.shape, f32)
    for tile, (low, high) in enumerate(TILES):
        tiles[tile, 0:27, : high - low] = jnp.sum(sums[:, :, low:high], axis=1)
        tiles[tile, 27:30, : high - low] = gvec[0:3, low:high]
    for parity in range(2):
        for j in range(5):
            value = tiles[j // 2, pl.ds(parity, 15, stride=2), :]
            put_half(flat, AT_CONV + parity * 5 + j, value, j % 2, 5, 15)
    out[...] = flat[...].astype(bf16)


def conv_weight_grads(frames, xpad, gpad, gvec):
    return pl.pallas_call(
        conv_weight_kernel,
        name="conv_weight_grads",
        in_specs=[SMEM_SPEC, HBM_SPEC, HBM_SPEC, VMEM_SPEC],
        out_shape=jax.ShapeDtypeStruct((80, LANES), bf16),
        scratch_shapes=[
            pltpu.VMEM(xpad.shape, f32),
            pltpu.VMEM(gpad.shape, f32),
            pltpu.VMEM((2, BODY, DIM), f32),
            pltpu.VMEM((27, 8, DIM), f32),
            pltpu.VMEM((3, 32, LANES), f32),
            pltpu.VMEM((80, LANES), f32),
            pltpu.SemaphoreType.DMA((xpad.shape[0] // 4,)),
            pltpu.SemaphoreType.DMA((xpad.shape[0] // 4,)),
        ],
        compiler_params=params(18),
    )(frames, in_hbm(xpad), in_hbm(gpad), gvec)


def token_piece_kernel(piece, frames_ref, convp, gsource, back, *refs):
    if piece > 0:
        refs = refs[1:]
    gtok, passed, masked, slots, sums, comp, rows, sem = refs
    frames = frames_ref[0]
    passed[0] = frames
    copies = fetch_frames(gsource, slots, sem, 4 * piece, 4)
    for copy in copies:
        copy.start()
    rows[...] = jnp.zeros(rows.shape, f32)
    copies[0].wait()

    def each(member, carry):
        @pl.when(member == 1)
        def _():
            copies[1].wait()

        frame = 4 * piece + member
        there = frame < frames
        before = there & (frame > 0)
        after = frame + 1 < frames
        mask_weights(convp, masked, after, there, before)
        at = (member + jnp.where(before, 0, 1), member + 1, member + jnp.where(after, 2, 1))
        mix_frame(slots, at, masked, sums, comp, -1)
        place = pl.ds(pl.multiple_of(192 * member, 16), 208)
        rows[place, :] += dot(back[member], comp[...].astype(bf16))
        return carry

    lax.fori_loop(0, 4, each, 0)
    gtok[...] = rows[...].astype(bf16)


def token_piece(piece, frames, convp, gpad, back, gtok):
    count = gpad.shape[0]
    operands = [frames, convp, in_hbm(gpad), back] + ([] if piece == 0 else [gtok])
    return pl.pallas_call(
        functools.partial(token_piece_kernel, piece),
        name=f"token_piece{piece}",
        grid=(1,),
        in_specs=[SMEM_SPEC, VMEM_SPEC, HBM_SPEC, VMEM_SPEC] + [ANY_SPEC] * (piece > 0),
        out_specs=[pl.BlockSpec((PIECE, DIM), lambda i: (piece, 0)), SMEM_SPEC],
        out_shape=[
            jax.ShapeDtypeStruct((count * FRAME, DIM), bf16),
            jax.ShapeDtypeStruct((1,), jnp.int32),
        ],
        input_output_aliases={4: 0} if piece else {},
        scratch_shapes=[
            pltpu.VMEM((32, DIM), f32),
            pltpu.VMEM((6, PAD_ROWS, DIM), f32),
            pltpu.VMEM((3, BODY, DIM), f32),
            pltpu.VMEM((BODY, DIM), f32),
            pltpu.VMEM((PIECE, DIM), f32),
            pltpu.SemaphoreType.DMA((2,)),
        ],
        compiler_params=params(10),
    )(*operands)


def put_half(flat, index, value, side, step=1, count=1):
    row, wanted = divmod(index, 2)
    place = pl.ds(row, count, stride=step) if step > 1 else pl.ds(row, count)
    lane = lane_of(value.shape)
    if wanted == 0:
        flat[place, :] += jnp.where(lane < 64, low_half(value, side), 0.0)
    else:
        flat[place, :] += jnp.where(lane >= 64, high_half(value, side), 0.0)


def put_vector(flat, index, value):
    width = value.shape[1]
    for j in range(width // 64):
        low = (j // 2) * LANES
        part = value[:, low : min(low + LANES, width)]
        if part.shape[1] < LANES:
            part = jnp.concatenate([part, jnp.zeros((1, 64), f32)], axis=1)
        put_half(flat, index + j, part, j % 2)


PACK_BASE = 2432


def pack_main_kernel(gproj, gfc1, gfc2, gvec, gfc1b, out, flat):
    flat[...] = jnp.zeros(flat.shape, f32)
    for parity in range(2):
        for j in range(5):
            value = gproj[j // 2, pl.ds(parity, DIM // 2, stride=2), :]
            put_half(flat, AT_PROJ + parity * 5 + j, value, j % 2, 5, DIM // 2)
            value = gfc2[j // 2, pl.ds(parity, FFN // 2, stride=2), :]
            put_half(flat, AT_FC2 + parity * 5 + j, value, j % 2, 5, FFN // 2)
    for j in range(20):
        value = gfc1[:, (j // 2) * LANES : (j // 2 + 1) * LANES]
        put_half(flat, AT_FC1 + j, value, j % 2, 10, DIM)
    for row in range(3):
        put_vector(flat, AT_VEC + 5 * row, gvec[row : row + 1, :])
    put_vector(flat, AT_FC2B, gvec[3:4, :])
    put_vector(flat, AT_FC1B, gfc1b[...])
    out[...] = flat[...].astype(bf16)


def pack_main(gproj, gfc1, gfc2, gvec, gfc1b, rows):
    return pl.pallas_call(
        pack_main_kernel,
        name="pack_main",
        out_shape=jax.ShapeDtypeStruct((rows, LANES), bf16),
        scratch_shapes=[pltpu.VMEM((rows, LANES), f32)],
        compiler_params=params(14),
    )(gproj, gfc1, gfc2, gvec, gfc1b)


QKV_ROWS = 2480


def pack_qkv_kernel(gqkv, gbias, out, end, flat):
    flat[...] = jnp.zeros(flat.shape, f32)
    for parity in range(2):
        for j in range(15):
            kind, head = divmod(j, HEADS)
            value = gqkv[kind * PAIRS + head // 2, pl.ds(parity, DIM // 2, stride=2), :]
            put_half(flat, AT_QKV + parity * 15 + j, value, head % 2, 15, DIM // 2)
    for j in range(10):
        start = (0 if j < HEADS else 2 * PAIR_COLUMNS) + j % HEADS // 2 * LANES
        put_half(flat, AT_QV + j, gbias[:, start : start + LANES], j % HEADS % 2)
    out[...] = flat[:PACK_BASE, :].astype(bf16)
    end[...] = flat[PACK_BASE:, :].astype(bf16)


def pack_qkv(gqkv, gbias):
    return pl.pallas_call(
        pack_qkv_kernel,
        name="pack_qkv",
        out_shape=[
            jax.ShapeDtypeStruct((PACK_BASE, LANES), bf16),
            jax.ShapeDtypeStruct((QKV_ROWS - PACK_BASE, LANES), bf16),
        ],
        scratch_shapes=[pltpu.VMEM((QKV_ROWS, LANES), f32)],
        compiler_params=params(10),
    )(gqkv, gbias)


AXES = ("wide", "narrow")


def exchange(value, bit):
    count = lax.axis_size(AXES)
    return lax.ppermute(value, AXES, [(i, i ^ (1 << bit)) for i in range(count)])


def my_bit(bit):
    return (lax.axis_index(AXES) >> bit) & 1


def tie(*values):
    return lax.optimization_barrier(values)


def split(value, bit):
    value = value.reshape(value.shape[0] // 2, 2, -1, LANES)
    mine = my_bit(bit)
    keep = lax.dynamic_index_in_dim(value, mine, 1, keepdims=False)
    return keep, lax.dynamic_index_in_dim(value, 1 - mine, 1, keepdims=False)


def on_device(master, momentum, average, tokens, clip_ids, borders, cotangent):
    wide_count, narrow_count = lax.axis_size("wide"), lax.axis_size("narrow")
    count = wide_count * narrow_count
    bits = count.bit_length() - 1
    own_rows = master.shape[0]
    filled = jnp.sum((clip_ids >= 0).astype(jnp.int32))
    frames = jnp.where(filled > 6 * FRAME, 12, jnp.where(filled > 3 * FRAME, 6, 3)).reshape(1)
    me = lax.axis_index(AXES)
    quarter = me >> (bits - 2)
    blocks = master.astype(bf16)[None]
    other = exchange(blocks, bits - 2)
    other, frames = tie(other, frames)
    blocks = jnp.concatenate([blocks, other], axis=0)
    blocks, frames = tie(blocks, frames)
    other = exchange(blocks, bits - 1)
    xpad, spread, back, frames = prepare(frames, tokens.T)
    other, frames = tie(other, frames)
    blocks = jnp.concatenate([blocks, other], axis=0)
    first = lax.dynamic_index_in_dim(blocks, quarter, 0)
    rest = [lax.dynamic_index_in_dim(blocks, quarter ^ index, 0) for index in (1, 2, 3)]
    rest = jnp.concatenate(rest, axis=0)[None]
    low_bits = list(range(bits - 3, -1, -1))
    for step, bit in enumerate(low_bits):
        if step == 0:
            first, frames = tie(first, frames)
        other = exchange(first, bit)
        if step == 0:
            cotangent, frames = turn(frames, cotangent.T)
            other, frames = tie(other, frames)
        first = jnp.concatenate([first, other], axis=0)
        if step == 0:
            first, rest, frames = tie(first, rest, frames)
            rest = jnp.concatenate([rest, exchange(rest, bit)], axis=0)
    order = [0] * (count // 4)
    for step, bit in enumerate(low_bits):
        order = [place | (((index >> bit) & 1) << step) for index, place in enumerate(order)]
    mine = sum((((me >> bit) & 1) << step) for step, bit in enumerate(low_bits))
    order = jnp.array(order, jnp.int32) ^ mine
    head = lax.dynamic_index_in_dim(first, mine, 0, keepdims=False)
    head = jnp.concatenate([head, jnp.zeros((4, LANES), bf16)], axis=0)[:80] if own_rows < 80 else head[:80]
    mixed, convp = None, None
    for step, bit in enumerate(low_bits[1:]):
        if step < 2:
            rest, frames = tie(rest, frames)
        other = exchange(rest, bit)
        if step == 0:
            mixed, convp, frames = conv_piece(0, 8, frames, head, xpad, back, None)
        elif step == 1:
            mixed, convp, frames = conv_piece(8, 4, frames, head, xpad, back, mixed)
        other, frames = tie(other, frames)
        rest = jnp.concatenate([rest, other], axis=0)
    wqkv, wproj, fc1, fc2, bqkv, vecs, fc1b = unpack(order, first, rest)
    normed, q, k, v, size = project(frames, mixed, convp, wqkv, bqkv)
    o, q_back = attend(q, k, v, size)
    output, gmid, do, gproj, gfc1, gfc2, gvec, gfc1b = feed_forward(
        frames, o, mixed, cotangent, wproj, fc1, fc2, vecs, fc1b
    )
    main = pack_main(gproj, gfc1, gfc2, gvec, gfc1b, count * own_rows)
    main = main.reshape(wide_count, narrow_count, own_rows, LANES)
    main = lax.psum_scatter(main, "wide", scatter_dimension=0, tiled=True)[0]
    q_back, do, k, v = (in_hbm(value) for value in (q_back, do, k, v))
    dq, dk, dv = attend_back(q_back, do, k, v)
    gpad, gqkv, gbias, gvec_one = project_back(dq, dk, dv, normed, mixed, gmid, wqkv, convp, spread)
    qkv, qkv_end = pack_qkv(gqkv, gbias)
    qkv = qkv.reshape(count // 4, own_rows, LANES)
    narrow_bits = narrow_count.bit_length() - 1
    for bit in range(narrow_bits):
        keep, give = split(qkv, bit)
        if bit == narrow_bits - 1:
            gvec_one, give = tie(gvec_one, give)
        qkv = keep + exchange(give, bit)
    conv = conv_weight_grads(frames, xpad, gpad, gvec_one)
    late = jnp.concatenate([conv, qkv_end], axis=0)
    main, late = tie(main, late)
    gtok = None
    for bit in range(bits):
        if bit < narrow_bits:
            keep, give = split(main, bit)
        elif bit < bits - 2:
            keep, give = split(qkv, bit)
        else:
            keep, give = qkv, qkv
        sent = give.shape[0] * own_rows
        packet = jnp.concatenate([give.reshape(sent, LANES), late], axis=0)
        packet, frames = tie(packet, frames)
        other = exchange(packet, bit)
        if bit < 3:
            gtok, frames = token_piece(bit, frames, convp, gpad, back, gtok)
        elif bit == 3:
            output, frames = turn(frames, output)
        elif bit == 4:
            gtok, frames = turn(frames, gtok)
        other, frames = tie(other, frames)
        summed = keep + other[:sent].reshape(keep.shape)
        late = late + other[sent:]
        if bit < narrow_bits:
            main = summed
        else:
            qkv = summed
    main, qkv = main[0], qkv[0]
    early = jnp.where(me < count // 4, qkv.astype(f32), main.astype(f32))
    conv, qkv_end = late[:80].astype(f32), late[80:].astype(f32)
    if own_rows < 80:
        conv = conv[:own_rows]
    conv = jnp.pad(conv, ((0, own_rows - conv.shape[0]), (0, 0)))
    qkv_end = jnp.pad(qkv_end, ((0, own_rows - qkv_end.shape[0]), (0, 0)))
    owned = early + jnp.where(me == 0, conv, jnp.where(me == count // 4, qkv_end, 0.0))
    rate = RATE_FACTOR / math.sqrt(tokens.shape[0] * count)
    decayed = owned + DECAY_RATE * master
    new_momentum = MOMENTUM * momentum + decayed
    new_master = master - rate * (decayed + MOMENTUM * new_momentum)
    new_average = AVERAGE_KEEP * average + (1.0 - AVERAGE_KEEP) * new_master
    return (output.T, gtok.T, owned, new_master, new_momentum, new_average, new_master.astype(bf16))


def solution(mesh):
    rows = P(("wide", "narrow"), None)
    return jax.shard_map(
        on_device,
        mesh=mesh,
        in_specs=(rows, rows, rows, rows, P(("wide", "narrow")), P(("wide", "narrow")), rows),
        out_specs=(rows,) * 7,
        check_vma=False,
    )
```

```python
import functools
import math

import jax
import jax.numpy as jnp
from jax import lax
from jax.experimental import pallas as pl
from jax.experimental.pallas import tpu as pltpu
from jax.sharding import PartitionSpec as P

HEADS = 5
HEAD_DIM = 64
DIM = 320
FFN = 1280
SIDE = 14
FRAME = SIDE * SIDE
LANES = 128
PAIRS = (HEADS + 1) // 2
PAIR_COLUMNS = PAIRS * LANES
QKV_COLUMNS = 3 * PAIR_COLUMNS

EPSILON = 1e-06
MOMENTUM = 0.9
DECAY_RATE = 0.0001
AVERAGE_KEEP = 0.8
RATE_FACTOR = 0.03
LOG2E = 1.0 / math.log(2.0)
LN2 = math.log(2.0)
INVERSE_ROOT_TWO_PI = 1.0 / math.sqrt(2.0 * math.pi)
BLOCKED = -(2.0**30)
SAFE_BOUND = 80.0

TILES = ((0, 128), (128, 256), (256, 320))

bf16 = jnp.bfloat16
f32 = jnp.float32

AT_CONV = 0
AT_QKV = 150
AT_QV = 4950
AT_PROJ = 4960
AT_VEC = 6560
AT_FC1 = 6575
AT_FC1B = 12975
AT_FC2 = 12995
AT_FC2B = 19395
HALF_END = 19400


SMEM_SPEC = pl.BlockSpec(memory_space=pltpu.SMEM)
VMEM_SPEC = pl.BlockSpec(memory_space=pltpu.VMEM)
ANY_SPEC = pl.BlockSpec(memory_space=pl.ANY)
HBM_SPEC = pl.BlockSpec(memory_space=pltpu.HBM)


def in_hbm(value):
    return pltpu.with_memory_space_constraint(value, pltpu.HBM)


def dot(a, b):
    return lax.dot_general(a, b, (((1,), (0,)), ((), ())), preferred_element_type=f32)


def dot_nt(a, b):
    return lax.dot_general(a, b, (((1,), (1,)), ((), ())), preferred_element_type=f32)


def dot_tn(a, b):
    return lax.dot_general(a, b, (((0,), (0,)), ((), ())), preferred_element_type=f32)


def params(limit=58):
    return pltpu.CompilerParams(vmem_limit_bytes=limit << 20)


def lane_of(shape):
    return lax.broadcasted_iota(jnp.int32, shape, len(shape) - 1)


def row_of(shape):
    return lax.broadcasted_iota(jnp.int32, shape, 0)


def low_half(value, side):
    return value if side == 0 else pltpu.roll(value, 64, axis=1)


def high_half(value, side):
    return value if side == 1 else pltpu.roll(value, 64, axis=1)


def split3(value):
    first = value.astype(bf16).astype(f32)
    rest = value - first
    second = rest.astype(bf16).astype(f32)
    return first, second, rest - second


def read_half(flat, at, length, step, count, parity, j):
    index = at + parity * length + j
    return flat[pl.ds(index // 2, count, stride=step), :], index % 2


def read_vector(flat, at, length):
    tiles = []
    lane = lane_of((1, LANES))
    for j in range(0, length, 2):
        row, side = divmod(at + j, 2)
        low = low_half(flat[row : row + 1, :], side)
        if j + 1 < length:
            row, side = divmod(at + j + 1, 2)
            tiles.append(jnp.where(lane < 64, low, high_half(flat[row : row + 1, :], side)))
        else:
            tiles.append(low[:, :64])
    return jnp.concatenate(tiles, axis=1)


def odd_matrix(flat, out, at, length, rows):
    pairs = rows // 2
    for parity in range(2):
        for tile in range((length + 1) // 2):
            low, side = read_half(flat, at, length, length, pairs, parity, 2 * tile)
            low = low_half(low, side)
            place = pl.ds(parity, pairs, stride=2)
            if 2 * tile + 1 < length:
                high, side = read_half(flat, at, length, length, pairs, parity, 2 * tile + 1)
                merged = jnp.where(lane_of(low.shape) < 64, low, high_half(high, side))
            else:
                merged = low
            out[tile, place, :] = merged


def unpack_kernel(order, first, rest, wqkv, wproj, fc1, fc2, bqkv, vecs, fc1b, flat, wide, tall):
    blocks, rows = first.shape[:2]
    for block in range(blocks):
        place = order[block]
        for quarter in range(4):
            start = (quarter * blocks + block) * rows
            value = first[place] if quarter == 0 else rest[place, quarter - 1]
            flat[start : start + rows, :] = value.astype(f32)
    for parity in range(2):
        place = pl.ds(parity, DIM // 2, stride=2)
        for kind in range(3):
            for pair in range(PAIRS):
                j = kind * HEADS + 2 * pair
                low, side = read_half(flat, AT_QKV, 15, 15, DIM // 2, parity, j)
                low = low_half(low, side)
                high = jnp.zeros_like(low)
                if 2 * pair + 1 < HEADS:
                    high, side = read_half(flat, AT_QKV, 15, 15, DIM // 2, parity, j + 1)
                    high = high_half(high, side)
                wide[kind * PAIRS + pair, place, :] = jnp.where(lane_of(low.shape) < 64, low, high)
    for tile in range(3 * PAIRS):
        wqkv[:, tile * LANES : (tile + 1) * LANES] = wide[tile].astype(bf16)
    bqkv[...] = jnp.zeros(bqkv.shape, f32)
    for index, kind in enumerate((0, 2)):
        start = kind * PAIR_COLUMNS
        bqkv[:, start : start + DIM] = read_vector(flat, AT_QV + index * HEADS, HEADS)
    odd_matrix(flat, wide, AT_PROJ, 5, DIM)
    for tile, (low, high) in enumerate(TILES):
        wproj[:DIM, low:high] = wide[tile, :, : high - low].astype(bf16)
    wproj[DIM:, :] = jnp.zeros((PAIR_COLUMNS - DIM, DIM), bf16)
    for row in range(3):
        vecs[row : row + 1, :] = read_vector(flat, AT_VEC + 5 * row, 5)
    vecs[3:4, :] = read_vector(flat, AT_FC2B, 5)
    vecs[4:8, :] = jnp.zeros((4, DIM), f32)
    fc1b[...] = read_vector(flat, AT_FC1B, 20)
    for tile in range(10):
        low, side = read_half(flat, AT_FC1, 20, 10, DIM, 0, 2 * tile)
        high, side_high = read_half(flat, AT_FC1, 20, 10, DIM, 0, 2 * tile + 1)
        merged = jnp.where(lane_of(low.shape) < 64, low_half(low, side), high_half(high, side_high))
        fc1[:, tile * LANES : (tile + 1) * LANES] = merged.astype(bf16)
    odd_matrix(flat, tall, AT_FC2, 5, FFN)
    for tile in range(3):
        width = LANES if tile < 2 else 64
        fc2[:, tile * LANES : tile * LANES + width] = tall[tile, :, :width].astype(bf16)


def unpack(order, first, rest):
    rows = 4 * first.shape[0] * first.shape[1]
    return pl.pallas_call(
        unpack_kernel,
        name="unpack",
        in_specs=[SMEM_SPEC, VMEM_SPEC, VMEM_SPEC],
        out_shape=[
            jax.ShapeDtypeStruct((DIM, QKV_COLUMNS), bf16),
            jax.ShapeDtypeStruct((PAIR_COLUMNS, DIM), bf16),
            jax.ShapeDtypeStruct((DIM, FFN), bf16),
            jax.ShapeDtypeStruct((FFN, DIM), bf16),
            jax.ShapeDtypeStruct((1, QKV_COLUMNS), f32),
            jax.ShapeDtypeStruct((8, DIM), f32),
            jax.ShapeDtypeStruct((1, FFN), f32),
        ],
        scratch_shapes=[
            pltpu.VMEM((rows, LANES), f32),
            pltpu.VMEM((15, DIM, LANES), f32),
            pltpu.VMEM((3, FFN, LANES), f32),
        ],
        compiler_params=params(18),
    )(order, first, rest)


PAD_ROWS = 16 * 16
BODY = SIDE * 16


def spread_matrix(shift):
    cell = lax.broadcasted_iota(jnp.int32, (PAD_ROWS, 208), 0)
    source = lax.broadcasted_iota(jnp.int32, (PAD_ROWS, 208), 1)
    row, column = cell >> 4, cell & 15
    inside = (row >= 1) & (row <= SIDE) & (column < SIDE)
    wanted = (row - 1) * SIDE + column + shift
    return jnp.where(inside & (source == wanted), 1.0, 0.0).astype(bf16)


def gather_matrix(shift):
    target = lax.broadcasted_iota(jnp.int32, (208, BODY), 0)
    cell = lax.broadcasted_iota(jnp.int32, (208, BODY), 1)
    row, column = cell >> 4, cell & 15
    wanted = row * SIDE + column + shift
    return jnp.where((column < SIDE) & (target == wanted), 1.0, 0.0).astype(bf16)


def pieces(value):
    first = value.astype(bf16)
    return first, (value - first.astype(f32)).astype(bf16)


def prepare_kernel(first, lanes, frames, turned, *refs):
    if first == 0:
        target, passed, spread, back, tokens, padded, sems = refs
        for member in range(4):
            spread[member] = spread_matrix(4 * member)
            back[member] = gather_matrix(4 * member)
    else:
        spread, unused_target, target, passed, tokens, padded, sems = refs
    passed[0] = frames[0]
    tokens[...] = turned[:, lanes].T
    count = padded.shape[0]

    def fill(index, carry):
        frame = first + index
        member = frame & 3
        place = pl.ds(pl.multiple_of(frame * FRAME - 4 * member - lanes.start, 16), 208)
        padded[index] = dot(spread[member], tokens[place, :])
        return carry

    copies = []
    for group in range(2):
        low, high = group * count // 2, (group + 1) * count // 2
        lax.fori_loop(low, high, fill, 0)
        own, there = pl.ds(low, high - low), pl.ds(first + low, high - low)
        copies.append(pltpu.make_async_copy(padded.at[own], target.at[there], sems.at[group]))
        copies[-1].start()
    for copy in copies:
        copy.wait()


def prepare(first, count, frames, turned, spread=None, target=None):
    rows = turned.shape[1]
    low = max(first * FRAME - 16, 0) // LANES * LANES
    high = min(pl.cdiv((first + count) * FRAME + 16, LANES) * LANES, rows)
    tables = [
        jax.ShapeDtypeStruct((4, PAD_ROWS, 208), bf16),
        jax.ShapeDtypeStruct((4, 208, BODY), bf16),
    ]
    fresh = first == 0
    return pl.pallas_call(
        functools.partial(prepare_kernel, first, slice(low, high)),
        name="prepare",
        in_specs=[SMEM_SPEC, VMEM_SPEC] + ([] if fresh else [VMEM_SPEC, HBM_SPEC]),
        out_specs=[HBM_SPEC, SMEM_SPEC] + ([VMEM_SPEC] * 2 if fresh else []),
        out_shape=[
            pltpu.HBM((rows // FRAME, PAD_ROWS, DIM), f32),
            jax.ShapeDtypeStruct((1,), jnp.int32),
        ]
        + (tables if fresh else []),
        input_output_aliases={} if fresh else {3: 0},
        scratch_shapes=[
            pltpu.VMEM((high - low, DIM), bf16),
            pltpu.VMEM((count, PAD_ROWS, DIM), f32),
            pltpu.SemaphoreType.DMA((2,)),
        ],
        compiler_params=params(16),
    )(frames, turned, *([] if fresh else [spread, target]))


PIECE = 4 * FRAME


def fetch_frames(source, slots, sems, start, count):
    first, last = max(start - 1, 0), min(start + count + 1, source.shape[0])
    middle = start + 2
    copies = []
    for index, (low, high) in enumerate(((first, middle), (middle, last))):
        copies.append(
            pltpu.make_async_copy(
                source.at[pl.ds(low, high - low)], slots.at[pl.ds(low - start + 1, high - low)], sems.at[index]
            )
        )
    return copies


def mix_frame(slots, at, weights, sums, out, sign):
    for low, high in TILES:
        for start in range(0, BODY, 56):
            parts = [None, None, None]
            for a in (-1, 0, 1):
                for b in (-1, 0, 1):
                    begin = 16 + sign * b * 16 + start
                    cells = slots[at[1 + sign * a], begin : begin + 56, low:high]
                    for c in range(3):
                        tap = 9 * (a + 1) + 3 * (b + 1) + c
                        term = cells * weights[tap : tap + 1, low:high]
                        parts[c] = term if parts[c] is None else parts[c] + term
            parts[1] = parts[1] + slots[at[1], 16 + start : 16 + start + 56, low:high]
            for c in range(3):
                sums[c, start : start + 56, low:high] = parts[c]
    before, after = (0, 2) if sign == 1 else (2, 0)
    for low, high in TILES:
        out[:, low:high] = (
            sums[1, :, low:high]
            + pltpu.roll(sums[before, :, low:high], 1, axis=0)
            + pltpu.roll(sums[after, :, low:high], BODY - 1, axis=0)
        )


def mask_weights(weights, masked, first, middle, last):
    for tap in range(27):
        keep = (first, middle, last)[tap // 9]
        scale = 1.0 if tap == 13 else jnp.where(keep, 1.0, 0.0)
        masked[tap : tap + 1, :] = weights[tap : tap + 1, :] * scale


def conv_params(head, flat, weights):
    flat[...] = head[...].astype(f32)
    for parity in range(2):
        for tile in range(3):
            low, side = read_half(flat, AT_CONV, 5, 5, 15, parity, 2 * tile)
            low = low_half(low, side)
            place = pl.ds(parity, 15, stride=2)
            if tile < 2:
                high, side = read_half(flat, AT_CONV, 5, 5, 15, parity, 2 * tile + 1)
                low = jnp.where(lane_of(low.shape) < 64, low, high_half(high, side))
            weights[tile, place, :] = low


def turn_kernel(frames, source, out, passed):
    passed[0] = frames[0]
    out[...] = source[...].T


def turn(frames, value):
    rows, columns = value.shape
    return pl.pallas_call(
        turn_kernel,
        name="turn",
        in_specs=[SMEM_SPEC, VMEM_SPEC],
        out_specs=[VMEM_SPEC, SMEM_SPEC],
        out_shape=[
            jax.ShapeDtypeStruct((columns, rows), value.dtype),
            jax.ShapeDtypeStruct((1,), jnp.int32),
        ],
        compiler_params=params(10),
        cost_estimate=pl.CostEstimate(flops=0, bytes_accessed=4 * rows * columns, transcendentals=0),
    )(frames, value)


def conv_piece_kernel(start, count, frames_ref, head, padded, back, *refs):
    if start > 0:
        refs = refs[1:]
    mixed, convp, passed, flat, weights, masked, slots, sums, comp, sem = refs
    passed[0] = frames_ref[0]
    copies = fetch_frames(padded, slots, sem, start, count)
    for copy in copies:
        copy.start()
    frames = frames_ref[0]
    conv_params(head, flat, weights)
    for tile, (low, high) in enumerate(TILES):
        convp[:, low:high] = weights[tile, :, : high - low]
    mixed[...] = jnp.zeros(mixed.shape, f32)
    copies[0].wait()

    def each(member, carry):
        @pl.when(member == 1)
        def _():
            copies[1].wait()

        frame = start + member
        there = frame < frames
        before = there & (frame > 0)
        after = frame + 1 < frames
        mask_weights(convp, masked, before, there, after)
        at = (member + jnp.where(before, 0, 1), member + 1, member + jnp.where(after, 2, 1))
        mix_frame(slots, at, masked, sums, comp, 1)
        high, low = pieces(comp[...] + convp[27:28, :])
        shift = member & 3
        place = pl.ds(pl.multiple_of(FRAME * member - 4 * shift, 16), 208)
        mixed[place, :] += dot(back[shift], high) + dot(back[shift], low)
        return carry

    lax.fori_loop(0, count, each, 0)


def conv_piece(start, count, frames, head, padded, back, mixed):
    rows = padded.shape[0] * FRAME
    operands = [frames, head, in_hbm(padded), back] + ([] if start == 0 else [mixed])
    return pl.pallas_call(
        functools.partial(conv_piece_kernel, start, count),
        name=f"conv_piece{start}",
        grid=(1,),
        in_specs=[SMEM_SPEC, VMEM_SPEC, HBM_SPEC, VMEM_SPEC] + [ANY_SPEC] * (start > 0),
        out_specs=[
            pl.BlockSpec((count * FRAME, DIM), lambda i: (start // count, 0)),
            pl.BlockSpec((32, DIM), lambda i: (0, 0)),
            SMEM_SPEC,
        ],
        out_shape=[
            jax.ShapeDtypeStruct((rows, DIM), f32),
            jax.ShapeDtypeStruct((32, DIM), f32),
            jax.ShapeDtypeStruct((1,), jnp.int32),
        ],
        input_output_aliases={4: 0} if start else {},
        scratch_shapes=[
            pltpu.VMEM(head.shape, f32),
            pltpu.VMEM((3, 32, LANES), f32),
            pltpu.VMEM((32, DIM), f32),
            pltpu.VMEM((count + 2, PAD_ROWS, DIM), f32),
            pltpu.VMEM((3, BODY, DIM), f32),
            pltpu.VMEM((BODY, DIM), f32),
            pltpu.SemaphoreType.DMA((2,)),
        ],
        compiler_params=params(20),
    )(*operands)


def normalize(values):
    centered = values - jnp.mean(values, axis=-1, keepdims=True)
    variance = jnp.mean(centered * centered, axis=-1, keepdims=True)
    inverse = lax.rsqrt(variance + EPSILON)
    return centered * inverse, inverse


def flag_base(head):
    return HEAD_DIM if head % 2 == 0 else 0


def own_lanes(lane, head):
    return lane < HEAD_DIM if head % 2 == 0 else lane >= HEAD_DIM


def row_size(value, own):
    part = jnp.where(own, value.astype(f32), 0.0)
    return jnp.sum(part * part, axis=-1, keepdims=True)


def qkv_kernel(frames_ref, mixed, convp, wqkv, bqkv, normed_out, q_out, k_out, v_out, size):
    block = pl.program_id(0)
    rows = mixed.shape[0]
    frames = frames_ref[0]
    normal, unused_inverse = normalize(mixed[...])
    normed = (normal * convp[28:29, :] + convp[29:30, :]).astype(bf16)
    normed_out[...] = normed
    lane = lane_of((rows, LANES))
    inside = row_of((rows, LANES)) + block * rows < frames * FRAME
    scale = HEAD_DIM ** (-0.5) * LOG2E

    @pl.when(block == 0)
    def _():
        size[...] = jnp.zeros(size.shape, f32)

    projected = dot(normed, wqkv[...]) + bqkv[...]
    masks = []
    for base in (flag_base(0), flag_base(1)):
        flag = lane - base
        q_flags = jnp.where(((flag == 0) & ~inside) | ((flag == 1) & inside), BLOCKED, 0.0)
        k_flags = jnp.where(
            ((flag == 0) & inside) | ((flag == 1) & ~inside) | ((flag >= 2) & (flag < 5)), 1.0, 0.0
        )
        v_flags = jnp.where((flag >= 0) & (flag < 3), 1.0, 0.0)
        masks.append((q_flags, k_flags, v_flags))
    for head in range(HEADS):
        q_mask, k_mask, v_mask = masks[head % 2]
        own = own_lanes(lane, head)

        def columns(kind, head=head):
            start = (kind * PAIRS + head // 2) * LANES
            return projected[:, start : start + LANES]

        query = jnp.where(own, columns(0) * scale, q_mask).astype(bf16)
        key = jnp.where(own, columns(1), k_mask).astype(bf16)
        query_size = jnp.max(row_size(query, own), axis=0, keepdims=True)
        key_size = jnp.max(row_size(key, own), axis=0, keepdims=True)
        q_out[head] = query
        k_out[head] = key
        v_out[head] = jnp.where(own, columns(2), v_mask).astype(bf16)
        size[head : head + 1, :] = jnp.maximum(size[head : head + 1, :], query_size)
        size[head + 8 : head + 9, :] = jnp.maximum(size[head + 8 : head + 9, :], key_size)


def project(frames, mixed, convp, wqkv, bqkv, block=784):
    rows = mixed.shape[0]
    heads_spec = pl.BlockSpec((HEADS, block, LANES), lambda i: (0, i, 0))
    rows_spec = pl.BlockSpec((block, DIM), lambda i: (i, 0))
    heads_shape = jax.ShapeDtypeStruct((HEADS, rows, LANES), bf16)
    return pl.pallas_call(
        qkv_kernel,
        name="qkv_forward",
        grid=(rows // block,),
        in_specs=[
            SMEM_SPEC,
            rows_spec,
            pl.BlockSpec((32, DIM), lambda i: (0, 0)),
            pl.BlockSpec((DIM, QKV_COLUMNS), lambda i: (0, 0)),
            pl.BlockSpec((1, QKV_COLUMNS), lambda i: (0, 0)),
        ],
        out_specs=[rows_spec, heads_spec, heads_spec, heads_spec, pl.BlockSpec((16, LANES), lambda i: (0, 0))],
        out_shape=[
            pltpu.HBM((rows, DIM), bf16),
            heads_shape,
            heads_shape,
            heads_shape,
            jax.ShapeDtypeStruct((16, LANES), f32),
        ],
        compiler_params=params(14),
    )(frames, mixed, convp, wqkv, bqkv)


def attend_kernel(chunk, q, k, v, size, o_out, q_back, query, shift):
    head = pl.program_id(0)
    keys = k.shape[1]
    tall = q.shape[1]
    bound = jnp.max(size[pl.ds(head, 1), :] * size[pl.ds(head + 8, 1), :])
    query[...] = q[0]
    shift[...] = jnp.zeros(shift.shape, f32)

    @pl.when(bound > SAFE_BOUND * SAFE_BOUND)
    def _():
        shift[...] = jnp.full(shift.shape, -jnp.inf, f32)

        def peak(step, carry):
            scores = dot_nt(k[0, pl.ds(pl.multiple_of(step * 112, 16), 112), :], q[0])
            shift[...] = jnp.maximum(shift[...], jnp.max(scores, axis=0, keepdims=True))
            return carry

        lax.fori_loop(0, keys // 112, peak, 0)
        first, second, third = split3(-shift[...])
        flag = row_of((LANES, tall)) - jnp.where(lax.rem(head, 2) == 0, HEAD_DIM, 0)
        tail = jnp.where(flag == 2, first, jnp.where(flag == 3, second, jnp.where(flag == 4, third, 0.0)))
        query[...] = (q[0].astype(f32) + tail.T).astype(bf16)

    total = None
    for start in range(0, keys, chunk):
        place = slice(start, min(start + chunk, keys))
        weights = jnp.exp2(dot_nt(k[0, place, :], query[...])).astype(bf16)
        part = dot_tn(v[0, place, :], weights)
        total = part if total is None else total + part
    def finish(parity):
        base = flag_base(parity)
        sums = total[base : base + 1, :]
        first, second, third = split3(-(shift[...] + jnp.log2(sums)))
        row = row_of((8, tall))
        tail = jnp.where(row == 2, first, jnp.where(row == 3, second, jnp.where(row == 4, third, 0.0)))
        flags = [tail, jnp.zeros((56, tall), f32)]
        own = [total[HEAD_DIM - base : 2 * HEAD_DIM - base, :] / sums]
        stacked = jnp.concatenate(own + flags if parity == 0 else flags + own, axis=0).T
        lane = lane_of((tall, LANES))
        o_out[0] = jnp.where(own_lanes(lane, parity), stacked, 0.0).astype(bf16)
        place = (lane >= base + 2) & (lane < base + 5)
        q_back[0] = jnp.where(place, stacked, q[0].astype(f32)).astype(bf16)

    for parity in range(2):
        pl.when(lax.rem(head, 2) == parity)(functools.partial(finish, parity))


def attend(q, k, v, size, chunk=512):
    rows = q.shape[1]
    whole = pl.BlockSpec((1, rows, LANES), lambda h: (h, 0, 0))
    shape = jax.ShapeDtypeStruct((HEADS, rows, LANES), bf16)
    return pl.pallas_call(
        functools.partial(attend_kernel, chunk),
        name="attend",
        grid=(HEADS,),
        in_specs=[whole, whole, whole, pl.BlockSpec((16, LANES), lambda h: (0, 0))],
        out_specs=[whole, whole],
        out_shape=[shape, pltpu.HBM(shape.shape, bf16)],
        scratch_shapes=[pltpu.VMEM((rows, LANES), bf16), pltpu.VMEM((1, rows), f32)],
        compiler_params=params(18),
    )(q, k, v, size)


def attend_back_kernel(q, do, k, v, dq_out, dk_out, dv_out):
    weights = jnp.exp2(dot_nt(q[0], k[0]))
    grad_scores = (weights * dot_nt(do[0], v[0])).astype(bf16)
    dv_out[0] = dot_tn(do[0], weights.astype(bf16)).T.astype(bf16)
    dk_out[0] = (dot_tn(q[0], grad_scores) * LN2).T.astype(bf16)
    dq_out[0] = (dot_nt(k[0].T, grad_scores) * HEAD_DIM ** (-0.5)).T.astype(bf16)


def attend_back(q, do, k, v):
    heads, rows = q.shape[:2]
    whole = pl.BlockSpec((1, rows, LANES), lambda h: (h, 0, 0))
    shape = jax.ShapeDtypeStruct((heads, rows, LANES), bf16)
    return pl.pallas_call(
        attend_back_kernel,
        name="attend_back",
        grid=(heads,),
        in_specs=[whole] * 4,
        out_specs=[whole] * 3,
        out_shape=[shape] * 3,
        compiler_params=params(40),
    )(q, do, k, v)


def erf_parts(value):
    bell = jnp.exp(-0.5 * value * value)
    return bell, 0.5 * (1.0 + lax.erf(value * (1.0 / math.sqrt(2.0))))


def paired(heads):
    tiles = []
    for head in range(0, HEADS, 2):
        high = heads[head + 1] if head + 1 < HEADS else jnp.zeros_like(heads[head])
        tiles.append(jnp.where(lane_of(high.shape) < HEAD_DIM, heads[head], high))
    return jnp.concatenate(tiles, axis=1)


def add_tiles(ref, place, value):
    for tile, (low, high) in enumerate(TILES):
        ref[tile, place, : high - low] += value[:, low:high]


def middle_kernel(
    frames_ref, o, mixed, cot, wproj, fc1, fc2, vecs, fc1b,
    output, gmid_out, do_out, gproj, gfc1, gfc2, gvec, gfc1b, chunk,
):
    block = pl.program_id(0)
    rows = mixed.shape[0]
    inside = row_of((rows, DIM)) + block * rows < frames_ref[0] * FRAME

    @pl.when(block == 0)
    def _():
        for ref in (gproj, gfc1, gfc2, gvec, gfc1b):
            ref[...] = jnp.zeros(ref.shape, f32)

    attended = paired(o)
    middle = mixed[...] + (dot(attended, wproj[...]) + vecs[0:1, :])
    normal, inverse = normalize(middle)
    normed = (normal * vecs[1:2, :] + vecs[2:3, :]).astype(bf16)
    grad_output = jnp.where(inside, cot[...].astype(f32), 0.0)
    grad_outer = grad_output.astype(bf16)
    total = middle + vecs[3:4, :]
    grad_normed = jnp.zeros((rows, DIM), f32)
    for start in range(0, FFN, chunk):
        place = slice(start, start + chunk)
        inner = dot(normed, fc1[:, place]) + fc1b[:, place]
        bell, gate = erf_parts(inner)
        activated = (inner * gate).astype(bf16)
        total += dot(activated, fc2[place, :])
        slope = gate + inner * bell * INVERSE_ROOT_TWO_PI
        grad_inner = (dot_nt(grad_outer, fc2[place, :]) * slope)
        gfc1b[:, place] += jnp.sum(grad_inner, axis=0, keepdims=True)
        grad_inner = grad_inner.astype(bf16)
        add_tiles(gfc2, place, dot_tn(activated, grad_outer))
        gfc1[:, place] += dot_tn(normed, grad_inner)
        grad_normed += dot_nt(grad_inner, fc1[:, place])
    output[...] = total.astype(bf16)
    scaled = grad_normed * vecs[1:2, :]
    grad_middle = grad_output + inverse * (
        scaled
        - jnp.mean(scaled, axis=-1, keepdims=True)
        - normal * jnp.mean(scaled * normal, axis=-1, keepdims=True)
    )
    gmid_out[...] = grad_middle
    grad_branch = grad_middle.astype(bf16)
    add_tiles(gproj, slice(None), dot_tn(attended, grad_branch))
    gvec[0:1, :] += jnp.sum(grad_branch.astype(f32), axis=0, keepdims=True)
    gvec[1:2, :] += jnp.sum(grad_normed * normal, axis=0, keepdims=True)
    gvec[2:3, :] += jnp.sum(grad_normed, axis=0, keepdims=True)
    gvec[3:4, :] += jnp.sum(grad_output, axis=0, keepdims=True)
    lane = lane_of((rows, LANES))
    grad_attended = dot_nt(grad_branch, wproj[...])
    for head in range(HEADS):
        grad_head = grad_attended[:, head // 2 * LANES : (head // 2 + 1) * LANES]
        flag = lane - flag_base(head)
        delta = jnp.sum(grad_head * o[head].astype(f32), axis=-1, keepdims=True)
        first, second, third = split3(-delta)
        tail = jnp.where(flag == 0, first, jnp.where(flag == 1, second, third))
        do_out[head] = jnp.where((flag >= 0) & (flag < 3), tail, grad_head).astype(bf16)


def feed_forward(frames, o, mixed, cot, wproj, fc1, fc2, vecs, fc1b, block=784, chunk=256):
    rows = mixed.shape[0]
    heads_spec = pl.BlockSpec((HEADS, block, LANES), lambda i: (0, i, 0))
    rows_spec = pl.BlockSpec((block, DIM), lambda i: (i, 0))

    def full(*shape):
        return pl.BlockSpec(shape, lambda i: (0,) * len(shape))

    return pl.pallas_call(
        functools.partial(middle_kernel, chunk=chunk),
        name="feed_forward",
        grid=(rows // block,),
        in_specs=[
            SMEM_SPEC, heads_spec, rows_spec, rows_spec,
            full(PAIR_COLUMNS, DIM), full(DIM, FFN), full(FFN, DIM), full(8, DIM), full(1, FFN),
        ],
        out_specs=[
            rows_spec, rows_spec, heads_spec,
            full(3, PAIR_COLUMNS, LANES), full(DIM, FFN), full(3, FFN, LANES), full(8, DIM), full(1, FFN),
        ],
        out_shape=[
            pltpu.HBM((rows, DIM), bf16),
            pltpu.HBM((rows, DIM), f32),
            pltpu.HBM((HEADS, rows, LANES), bf16),
            jax.ShapeDtypeStruct((3, PAIR_COLUMNS, LANES), f32),
            jax.ShapeDtypeStruct((DIM, FFN), f32),
            jax.ShapeDtypeStruct((3, FFN, LANES), f32),
            jax.ShapeDtypeStruct((8, DIM), f32),
            jax.ShapeDtypeStruct((1, FFN), f32),
        ],
        compiler_params=params(22),
    )(frames, o, mixed, cot, wproj, fc1, fc2, vecs, fc1b)


def qkv_back_kernel(dq, dk, dv, normed, mixed, gmid, wqkv, convp, spread, padded, gqkv, gbias, gvec, gmix):
    block = pl.program_id(0)

    @pl.when(block == 0)
    def _():
        for ref in (gqkv, gbias, gvec):
            ref[...] = jnp.zeros(ref.shape, f32)

    normal, inverse = normalize(mixed[...])
    grads = jnp.concatenate([paired(part) for part in (dq, dk, dv)], axis=1)
    grad_qkv = dot_tn(normed[...], grads)
    for tile in range(3 * PAIRS):
        gqkv[tile] += grad_qkv[:, tile * LANES : (tile + 1) * LANES]
    gbias[...] += jnp.sum(grads.astype(f32), axis=0, keepdims=True)
    grad_normed = dot_nt(grads, wqkv[...])
    gvec[1:2, :] += jnp.sum(grad_normed * normal, axis=0, keepdims=True)
    gvec[2:3, :] += jnp.sum(grad_normed, axis=0, keepdims=True)
    scaled = grad_normed * convp[28:29, :]
    grad_mixed = gmid[...] + inverse * (
        scaled
        - jnp.mean(scaled, axis=-1, keepdims=True)
        - normal * jnp.mean(scaled * normal, axis=-1, keepdims=True)
    )
    gvec[0:1, :] += jnp.sum(grad_mixed, axis=0, keepdims=True)
    gmix[...] = grad_mixed
    for member in range(mixed.shape[0] // FRAME):
        high, low = pieces(gmix[192 * member : 192 * member + 208, :])
        padded[member] = dot(spread[member], high) + dot(spread[member], low)


def project_back(dq, dk, dv, normed, mixed, gmid, wqkv, convp, spread, block=PIECE):
    rows = mixed.shape[0]
    heads_spec = pl.BlockSpec((HEADS, block, LANES), lambda i: (0, i, 0))
    rows_spec = pl.BlockSpec((block, DIM), lambda i: (i, 0))

    def full(*shape):
        return pl.BlockSpec(shape, lambda i: (0,) * len(shape))

    return pl.pallas_call(
        qkv_back_kernel,
        name="qkv_back",
        grid=(rows // block,),
        in_specs=[heads_spec, heads_spec, heads_spec, rows_spec, rows_spec, rows_spec,
                  full(DIM, QKV_COLUMNS), full(32, DIM), full(4, PAD_ROWS, 208)],
        out_specs=[pl.BlockSpec((4, PAD_ROWS, DIM), lambda i: (i, 0, 0)), full(3 * PAIRS, DIM, LANES), full(1, QKV_COLUMNS), full(8, DIM)],
        out_shape=[
            pltpu.HBM((rows // FRAME, PAD_ROWS, DIM), f32),
            jax.ShapeDtypeStruct((3 * PAIRS, DIM, LANES), f32),
            jax.ShapeDtypeStruct((1, QKV_COLUMNS), f32),
            jax.ShapeDtypeStruct((8, DIM), f32),
        ],
        scratch_shapes=[pltpu.VMEM((block, DIM), f32)],
        compiler_params=params(18),
    )(dq, dk, dv, normed, mixed, gmid, wqkv, convp, spread)


def conv_weight_kernel(frames_ref, xsource, gsource, gvec, out, xpad, gpad, moved, sums, tiles, flat, xsem, gsem):
    frames = frames_ref[0]
    count = xpad.shape[0]
    copies = []
    for group in range(count // 4):
        place = pl.ds(4 * group, 4)
        copies.append(pltpu.make_async_copy(xsource.at[place], xpad.at[place], xsem.at[group]))
        copies.append(pltpu.make_async_copy(gsource.at[place], gpad.at[place], gsem.at[group]))
    for copy in copies:
        copy.start()
    sums[...] = jnp.zeros(sums.shape, f32)

    def weight_frame(frame, carry):
        for low, high in TILES:
            body = gpad[frame, 16 : 16 + BODY, low:high]
            moved[0, :, low:high] = pltpu.roll(body, BODY - 1, axis=0)
            moved[1, :, low:high] = pltpu.roll(body, 1, axis=0)
        for a in (-1, 0, 1):
            at = frame + a

            @pl.when((at >= 0) & (at < frames))
            def _():
                for low, high in TILES:
                    for b in (-1, 0, 1):
                        cells = xpad[at, 16 + b * 16 : 16 + b * 16 + BODY, low:high]
                        for c in range(3):
                            body = (
                                gpad[frame, 16 : 16 + BODY, low:high]
                                if c == 1
                                else moved[c // 2, :, low:high]
                            )
                            product = (body * cells).reshape(BODY // 8, 8, high - low)
                            tap = 9 * (a + 1) + 3 * (b + 1) + c
                            sums[tap, :, low:high] += jnp.sum(product, axis=0)

        return carry

    for group in range(count // 4):
        copies[2 * group].wait()
        copies[2 * group + 1].wait()
        start = max(4 * group - 1, 0)
        stop = 4 * group + 3 if group < count // 4 - 1 else count
        lax.fori_loop(jnp.minimum(start, frames), jnp.minimum(stop, frames), weight_frame, 0)
    tiles[...] = jnp.zeros(tiles.shape, f32)
    flat[...] = jnp.zeros(flat.shape, f32)
    for tile, (low, high) in enumerate(TILES):
        tiles[tile, 0:27, : high - low] = jnp.sum(sums[:, :, low:high], axis=1)
        tiles[tile, 27:30, : high - low] = gvec[0:3, low:high]
    for parity in range(2):
        for j in range(5):
            value = tiles[j // 2, pl.ds(parity, 15, stride=2), :]
            put_half(flat, AT_CONV + parity * 5 + j, value, j % 2, 5, 15)
    out[...] = flat[...].astype(bf16)


def conv_weight_grads(frames, xpad, gpad, gvec):
    return pl.pallas_call(
        conv_weight_kernel,
        name="conv_weight_grads",
        in_specs=[SMEM_SPEC, HBM_SPEC, HBM_SPEC, VMEM_SPEC],
        out_shape=jax.ShapeDtypeStruct((80, LANES), bf16),
        scratch_shapes=[
            pltpu.VMEM(xpad.shape, f32),
            pltpu.VMEM(gpad.shape, f32),
            pltpu.VMEM((2, BODY, DIM), f32),
            pltpu.VMEM((27, 8, DIM), f32),
            pltpu.VMEM((3, 32, LANES), f32),
            pltpu.VMEM((80, LANES), f32),
            pltpu.SemaphoreType.DMA((xpad.shape[0] // 4,)),
            pltpu.SemaphoreType.DMA((xpad.shape[0] // 4,)),
        ],
        compiler_params=params(18),
    )(frames, in_hbm(xpad), in_hbm(gpad), gvec)


def token_piece_kernel(piece, frames_ref, convp, gsource, back, *refs):
    if piece > 0:
        refs = refs[1:]
    gtok, passed, masked, slots, sums, comp, rows, sem = refs
    frames = frames_ref[0]
    passed[0] = frames
    copies = fetch_frames(gsource, slots, sem, 4 * piece, 4)
    for copy in copies:
        copy.start()
    rows[...] = jnp.zeros(rows.shape, f32)
    copies[0].wait()

    def each(member, carry):
        @pl.when(member == 1)
        def _():
            copies[1].wait()

        frame = 4 * piece + member
        there = frame < frames
        before = there & (frame > 0)
        after = frame + 1 < frames
        mask_weights(convp, masked, after, there, before)
        at = (member + jnp.where(before, 0, 1), member + 1, member + jnp.where(after, 2, 1))
        mix_frame(slots, at, masked, sums, comp, -1)
        place = pl.ds(pl.multiple_of(192 * member, 16), 208)
        rows[place, :] += dot(back[member], comp[...].astype(bf16))
        return carry

    lax.fori_loop(0, 4, each, 0)
    gtok[...] = rows[...].astype(bf16)


def token_piece(piece, frames, convp, gpad, back, gtok):
    count = gpad.shape[0]
    operands = [frames, convp, in_hbm(gpad), back] + ([] if piece == 0 else [gtok])
    return pl.pallas_call(
        functools.partial(token_piece_kernel, piece),
        name=f"token_piece{piece}",
        grid=(1,),
        in_specs=[SMEM_SPEC, VMEM_SPEC, HBM_SPEC, VMEM_SPEC] + [ANY_SPEC] * (piece > 0),
        out_specs=[pl.BlockSpec((PIECE, DIM), lambda i: (piece, 0)), SMEM_SPEC],
        out_shape=[
            jax.ShapeDtypeStruct((count * FRAME, DIM), bf16),
            jax.ShapeDtypeStruct((1,), jnp.int32),
        ],
        input_output_aliases={4: 0} if piece else {},
        scratch_shapes=[
            pltpu.VMEM((32, DIM), f32),
            pltpu.VMEM((6, PAD_ROWS, DIM), f32),
            pltpu.VMEM((3, BODY, DIM), f32),
            pltpu.VMEM((BODY, DIM), f32),
            pltpu.VMEM((PIECE, DIM), f32),
            pltpu.SemaphoreType.DMA((2,)),
        ],
        compiler_params=params(10),
    )(*operands)


def put_half(flat, index, value, side, step=1, count=1):
    row, wanted = divmod(index, 2)
    place = pl.ds(row, count, stride=step) if step > 1 else pl.ds(row, count)
    lane = lane_of(value.shape)
    if wanted == 0:
        flat[place, :] += jnp.where(lane < 64, low_half(value, side), 0.0)
    else:
        flat[place, :] += jnp.where(lane >= 64, high_half(value, side), 0.0)


def put_vector(flat, index, value):
    width = value.shape[1]
    for j in range(width // 64):
        low = (j // 2) * LANES
        part = value[:, low : min(low + LANES, width)]
        if part.shape[1] < LANES:
            part = jnp.concatenate([part, jnp.zeros((1, 64), f32)], axis=1)
        put_half(flat, index + j, part, j % 2)


PACK_BASE = 2432


def pack_main_kernel(gproj, gfc1, gfc2, gvec, gfc1b, out, flat):
    flat[...] = jnp.zeros(flat.shape, f32)
    for parity in range(2):
        for j in range(5):
            value = gproj[j // 2, pl.ds(parity, DIM // 2, stride=2), :]
            put_half(flat, AT_PROJ + parity * 5 + j, value, j % 2, 5, DIM // 2)
            value = gfc2[j // 2, pl.ds(parity, FFN // 2, stride=2), :]
            put_half(flat, AT_FC2 + parity * 5 + j, value, j % 2, 5, FFN // 2)
    for j in range(20):
        value = gfc1[:, (j // 2) * LANES : (j // 2 + 1) * LANES]
        put_half(flat, AT_FC1 + j, value, j % 2, 10, DIM)
    for row in range(3):
        put_vector(flat, AT_VEC + 5 * row, gvec[row : row + 1, :])
    put_vector(flat, AT_FC2B, gvec[3:4, :])
    put_vector(flat, AT_FC1B, gfc1b[...])
    out[...] = flat[...].astype(bf16)


def pack_main(gproj, gfc1, gfc2, gvec, gfc1b, rows):
    return pl.pallas_call(
        pack_main_kernel,
        name="pack_main",
        out_shape=jax.ShapeDtypeStruct((rows, LANES), bf16),
        scratch_shapes=[pltpu.VMEM((rows, LANES), f32)],
        compiler_params=params(14),
    )(gproj, gfc1, gfc2, gvec, gfc1b)


QKV_ROWS = 2480


def pack_qkv_kernel(gqkv, gbias, out, end, flat):
    flat[...] = jnp.zeros(flat.shape, f32)
    for parity in range(2):
        for j in range(15):
            kind, head = divmod(j, HEADS)
            value = gqkv[kind * PAIRS + head // 2, pl.ds(parity, DIM // 2, stride=2), :]
            put_half(flat, AT_QKV + parity * 15 + j, value, head % 2, 15, DIM // 2)
    for j in range(10):
        start = (0 if j < HEADS else 2 * PAIR_COLUMNS) + j % HEADS // 2 * LANES
        put_half(flat, AT_QV + j, gbias[:, start : start + LANES], j % HEADS % 2)
    out[...] = flat[:PACK_BASE, :].astype(bf16)
    end[...] = flat[PACK_BASE:, :].astype(bf16)


def pack_qkv(gqkv, gbias):
    return pl.pallas_call(
        pack_qkv_kernel,
        name="pack_qkv",
        out_shape=[
            jax.ShapeDtypeStruct((PACK_BASE, LANES), bf16),
            jax.ShapeDtypeStruct((QKV_ROWS - PACK_BASE, LANES), bf16),
        ],
        scratch_shapes=[pltpu.VMEM((QKV_ROWS, LANES), f32)],
        compiler_params=params(10),
    )(gqkv, gbias)


AXES = ("wide", "narrow")


def exchange(value, bit):
    count = lax.axis_size(AXES)
    return lax.ppermute(value, AXES, [(i, i ^ (1 << bit)) for i in range(count)])


def my_bit(bit):
    return (lax.axis_index(AXES) >> bit) & 1


def tie(*values):
    return lax.optimization_barrier(values)


def split(value, bit):
    value = value.reshape(value.shape[0] // 2, 2, -1, LANES)
    mine = my_bit(bit)
    keep = lax.dynamic_index_in_dim(value, mine, 1, keepdims=False)
    return keep, lax.dynamic_index_in_dim(value, 1 - mine, 1, keepdims=False)


def on_device(master, momentum, average, tokens, clip_ids, borders, cotangent):
    wide_count, narrow_count = lax.axis_size("wide"), lax.axis_size("narrow")
    count = wide_count * narrow_count
    bits = count.bit_length() - 1
    own_rows = master.shape[0]
    filled = jnp.sum((clip_ids >= 0).astype(jnp.int32))
    frames = jnp.where(filled > 6 * FRAME, 12, jnp.where(filled > 3 * FRAME, 6, 3)).reshape(1)
    me = lax.axis_index(AXES)
    quarter = me >> (bits - 2)
    blocks = master.astype(bf16)[None]
    other = exchange(blocks, bits - 2)
    other, frames = tie(other, frames)
    blocks = jnp.concatenate([blocks, other], axis=0)
    blocks, frames = tie(blocks, frames)
    other = exchange(blocks, bits - 1)
    xpad, frames, spread, back = prepare(0, 6, frames, tokens.T)
    other, frames = tie(other, frames)
    blocks = jnp.concatenate([blocks, other], axis=0)
    first = lax.dynamic_index_in_dim(blocks, quarter, 0)
    rest = [lax.dynamic_index_in_dim(blocks, quarter ^ index, 0) for index in (1, 2, 3)]
    rest = jnp.concatenate(rest, axis=0)[None]
    low_bits = list(range(bits - 3, -1, -1))
    for step, bit in enumerate(low_bits):
        if step < 2:
            first, frames = tie(first, frames)
        other = exchange(first, bit)
        if step == 0:
            xpad, frames = prepare(6, 6, frames, tokens.T, spread, xpad)
        elif step == 1:
            cotangent, frames = turn(frames, cotangent.T)
        if step < 2:
            other, frames = tie(other, frames)
        first = jnp.concatenate([first, other], axis=0)
        if step == 0:
            first, rest, frames = tie(first, rest, frames)
            rest = jnp.concatenate([rest, exchange(rest, bit)], axis=0)
    order = [0] * (count // 4)
    for step, bit in enumerate(low_bits):
        order = [place | (((index >> bit) & 1) << step) for index, place in enumerate(order)]
    mine = sum((((me >> bit) & 1) << step) for step, bit in enumerate(low_bits))
    order = jnp.array(order, jnp.int32) ^ mine
    head = lax.dynamic_index_in_dim(first, mine, 0, keepdims=False)
    head = jnp.concatenate([head, jnp.zeros((4, LANES), bf16)], axis=0)[:80] if own_rows < 80 else head[:80]
    mixed, convp = None, None
    for step, bit in enumerate(low_bits[1:]):
        if step < 2:
            rest, frames = tie(rest, frames)
        other = exchange(rest, bit)
        if step == 0:
            mixed, convp, frames = conv_piece(0, 8, frames, head, xpad, back, None)
        elif step == 1:
            mixed, convp, frames = conv_piece(8, 4, frames, head, xpad, back, mixed)
        other, frames = tie(other, frames)
        rest = jnp.concatenate([rest, other], axis=0)
    wqkv, wproj, fc1, fc2, bqkv, vecs, fc1b = unpack(order, first, rest)
    normed, q, k, v, size = project(frames, mixed, convp, wqkv, bqkv)
    o, q_back = attend(q, k, v, size)
    output, gmid, do, gproj, gfc1, gfc2, gvec, gfc1b = feed_forward(
        frames, o, mixed, cotangent, wproj, fc1, fc2, vecs, fc1b
    )
    main = pack_main(gproj, gfc1, gfc2, gvec, gfc1b, count * own_rows)
    main = main.reshape(wide_count, narrow_count, own_rows, LANES)
    main = lax.psum_scatter(main, "wide", scatter_dimension=0, tiled=True)[0]
    q_back, do, k, v = (in_hbm(value) for value in (q_back, do, k, v))
    dq, dk, dv = attend_back(q_back, do, k, v)
    gpad, gqkv, gbias, gvec_one = project_back(dq, dk, dv, normed, mixed, gmid, wqkv, convp, spread)
    qkv, qkv_end = pack_qkv(gqkv, gbias)
    qkv = qkv.reshape(count // 4, own_rows, LANES)
    narrow_bits = narrow_count.bit_length() - 1
    conv = conv_weight_grads(frames, xpad, gpad, gvec_one)
    late = jnp.concatenate([conv, qkv_end], axis=0)
    main, late = tie(main, late)
    gtok = None
    for bit in range(bits):
        main_keep, main_give = split(main, bit) if bit < narrow_bits else (main, main[:0])
        qkv_keep, qkv_give = split(qkv, bit) if bit < bits - 2 else (qkv, qkv)
        gives = [main_give.reshape(-1, LANES), qkv_give.reshape(-1, LANES), late]
        packet = jnp.concatenate(gives if bit < narrow_bits else gives[1:], axis=0)
        packet, frames = tie(packet, frames)
        other = exchange(packet, bit)
        if bit == 0:
            output, frames = turn(frames, output)
        elif bit < 4:
            gtok, frames = token_piece(bit - 1, frames, convp, gpad, back, gtok)
        elif bit == 4:
            gtok, frames = turn(frames, gtok)
        other, frames = tie(other, frames)
        ends = [gives[0].shape[0], gives[0].shape[0] + gives[1].shape[0]]
        if bit < narrow_bits:
            main = main_keep + other[: ends[0]].reshape(main_keep.shape)
        qkv = qkv_keep + other[ends[0] : ends[1]].reshape(qkv_keep.shape)
        late = late + other[ends[1] :]
    main, qkv = main[0], qkv[0]
    early = jnp.where(me < count // 4, qkv.astype(f32), main.astype(f32))
    conv, qkv_end = late[:80].astype(f32), late[80:].astype(f32)
    if own_rows < 80:
        conv = conv[:own_rows]
    conv = jnp.pad(conv, ((0, own_rows - conv.shape[0]), (0, 0)))
    qkv_end = jnp.pad(qkv_end, ((0, own_rows - qkv_end.shape[0]), (0, 0)))
    owned = early + jnp.where(me == 0, conv, jnp.where(me == count // 4, qkv_end, 0.0))
    rate = RATE_FACTOR / math.sqrt(tokens.shape[0] * count)
    decayed = owned + DECAY_RATE * master
    new_momentum = MOMENTUM * momentum + decayed
    new_master = master - rate * (decayed + MOMENTUM * new_momentum)
    new_average = AVERAGE_KEEP * average + (1.0 - AVERAGE_KEEP) * new_master
    return (output.T, gtok.T, owned, new_master, new_momentum, new_average, new_master.astype(bf16))


def solution(mesh):
    rows = P(("wide", "narrow"), None)
    return jax.shard_map(
        on_device,
        mesh=mesh,
        in_specs=(rows, rows, rows, rows, P(("wide", "narrow")), P(("wide", "narrow")), rows),
        out_specs=(rows,) * 7,
        check_vma=False,
    )
```

```python
import functools
import math

import jax
import jax.numpy as jnp
from jax import lax
from jax.experimental import pallas as pl
from jax.experimental.pallas import tpu as pltpu
from jax.sharding import PartitionSpec as P

HEADS = 5
HEAD_DIM = 64
DIM = 320
FFN = 1280
SIDE = 14
FRAME = SIDE * SIDE
LANES = 128
PAIRS = (HEADS + 1) // 2
PAIR_COLUMNS = PAIRS * LANES
QKV_COLUMNS = 3 * PAIR_COLUMNS

EPSILON = 1e-06
MOMENTUM = 0.9
DECAY_RATE = 0.0001
AVERAGE_KEEP = 0.8
RATE_FACTOR = 0.03
LOG2E = 1.0 / math.log(2.0)
LN2 = math.log(2.0)
INVERSE_ROOT_TWO_PI = 1.0 / math.sqrt(2.0 * math.pi)
BLOCKED = -(2.0**30)
SAFE_BOUND = 80.0

TILES = ((0, 128), (128, 256), (256, 320))

bf16 = jnp.bfloat16
f32 = jnp.float32

AT_CONV = 0
AT_QKV = 150
AT_QV = 4950
AT_PROJ = 4960
AT_VEC = 6560
AT_FC1 = 6575
AT_FC1B = 12975
AT_FC2 = 12995
AT_FC2B = 19395
HALF_END = 19400


SMEM_SPEC = pl.BlockSpec(memory_space=pltpu.SMEM)
VMEM_SPEC = pl.BlockSpec(memory_space=pltpu.VMEM)
ANY_SPEC = pl.BlockSpec(memory_space=pl.ANY)
HBM_SPEC = pl.BlockSpec(memory_space=pltpu.HBM)


def in_hbm(value):
    return pltpu.with_memory_space_constraint(value, pltpu.HBM)


def dot(a, b):
    return lax.dot_general(a, b, (((1,), (0,)), ((), ())), preferred_element_type=f32)


def dot_nt(a, b):
    return lax.dot_general(a, b, (((1,), (1,)), ((), ())), preferred_element_type=f32)


def dot_tn(a, b):
    return lax.dot_general(a, b, (((0,), (0,)), ((), ())), preferred_element_type=f32)


def params(limit=58):
    return pltpu.CompilerParams(vmem_limit_bytes=limit << 20)


def lane_of(shape):
    return lax.broadcasted_iota(jnp.int32, shape, len(shape) - 1)


def row_of(shape):
    return lax.broadcasted_iota(jnp.int32, shape, 0)


def low_half(value, side):
    return value if side == 0 else pltpu.roll(value, 64, axis=1)


def high_half(value, side):
    return value if side == 1 else pltpu.roll(value, 64, axis=1)


def split3(value):
    first = value.astype(bf16).astype(f32)
    rest = value - first
    second = rest.astype(bf16).astype(f32)
    return first, second, rest - second


def read_half(flat, at, length, step, count, parity, j):
    index = at + parity * length + j
    return flat[pl.ds(index // 2, count, stride=step), :], index % 2


def read_vector(flat, at, length):
    tiles = []
    lane = lane_of((1, LANES))
    for j in range(0, length, 2):
        row, side = divmod(at + j, 2)
        low = low_half(flat[row : row + 1, :], side)
        if j + 1 < length:
            row, side = divmod(at + j + 1, 2)
            tiles.append(jnp.where(lane < 64, low, high_half(flat[row : row + 1, :], side)))
        else:
            tiles.append(low[:, :64])
    return jnp.concatenate(tiles, axis=1)


def odd_matrix(flat, out, at, length, rows):
    pairs = rows // 2
    for parity in range(2):
        for tile in range((length + 1) // 2):
            low, side = read_half(flat, at, length, length, pairs, parity, 2 * tile)
            low = low_half(low, side)
            place = pl.ds(parity, pairs, stride=2)
            if 2 * tile + 1 < length:
                high, side = read_half(flat, at, length, length, pairs, parity, 2 * tile + 1)
                merged = jnp.where(lane_of(low.shape) < 64, low, high_half(high, side))
            else:
                merged = low
            out[tile, place, :] = merged


def unpack_kernel(order, first, rest, wqkv, wproj, fc1, fc2, bqkv, vecs, fc1b, flat, wide, tall):
    blocks, rows = first.shape[:2]
    for block in range(blocks):
        place = order[block]
        for quarter in range(4):
            start = (quarter * blocks + block) * rows
            value = first[place] if quarter == 0 else rest[place, quarter - 1]
            flat[start : start + rows, :] = value.astype(f32)
    for parity in range(2):
        place = pl.ds(parity, DIM // 2, stride=2)
        for kind in range(3):
            for pair in range(PAIRS):
                j = kind * HEADS + 2 * pair
                low, side = read_half(flat, AT_QKV, 15, 15, DIM // 2, parity, j)
                low = low_half(low, side)
                high = jnp.zeros_like(low)
                if 2 * pair + 1 < HEADS:
                    high, side = read_half(flat, AT_QKV, 15, 15, DIM // 2, parity, j + 1)
                    high = high_half(high, side)
                wide[kind * PAIRS + pair, place, :] = jnp.where(lane_of(low.shape) < 64, low, high)
    for tile in range(3 * PAIRS):
        wqkv[:, tile * LANES : (tile + 1) * LANES] = wide[tile].astype(bf16)
    bqkv[...] = jnp.zeros(bqkv.shape, f32)
    for index, kind in enumerate((0, 2)):
        start = kind * PAIR_COLUMNS
        bqkv[:, start : start + DIM] = read_vector(flat, AT_QV + index * HEADS, HEADS)
    odd_matrix(flat, wide, AT_PROJ, 5, DIM)
    for tile, (low, high) in enumerate(TILES):
        wproj[:DIM, low:high] = wide[tile, :, : high - low].astype(bf16)
    wproj[DIM:, :] = jnp.zeros((PAIR_COLUMNS - DIM, DIM), bf16)
    for row in range(3):
        vecs[row : row + 1, :] = read_vector(flat, AT_VEC + 5 * row, 5)
    vecs[3:4, :] = read_vector(flat, AT_FC2B, 5)
    vecs[4:8, :] = jnp.zeros((4, DIM), f32)
    fc1b[...] = read_vector(flat, AT_FC1B, 20)
    for tile in range(10):
        low, side = read_half(flat, AT_FC1, 20, 10, DIM, 0, 2 * tile)
        high, side_high = read_half(flat, AT_FC1, 20, 10, DIM, 0, 2 * tile + 1)
        merged = jnp.where(lane_of(low.shape) < 64, low_half(low, side), high_half(high, side_high))
        fc1[:, tile * LANES : (tile + 1) * LANES] = merged.astype(bf16)
    odd_matrix(flat, tall, AT_FC2, 5, FFN)
    for tile in range(3):
        width = LANES if tile < 2 else 64
        fc2[:, tile * LANES : tile * LANES + width] = tall[tile, :, :width].astype(bf16)


def unpack(order, first, rest):
    rows = 4 * first.shape[0] * first.shape[1]
    return pl.pallas_call(
        unpack_kernel,
        name="unpack",
        in_specs=[SMEM_SPEC, VMEM_SPEC, VMEM_SPEC],
        out_shape=[
            jax.ShapeDtypeStruct((DIM, QKV_COLUMNS), bf16),
            jax.ShapeDtypeStruct((PAIR_COLUMNS, DIM), bf16),
            jax.ShapeDtypeStruct((DIM, FFN), bf16),
            jax.ShapeDtypeStruct((FFN, DIM), bf16),
            jax.ShapeDtypeStruct((1, QKV_COLUMNS), f32),
            jax.ShapeDtypeStruct((8, DIM), f32),
            jax.ShapeDtypeStruct((1, FFN), f32),
        ],
        scratch_shapes=[
            pltpu.VMEM((rows, LANES), f32),
            pltpu.VMEM((15, DIM, LANES), f32),
            pltpu.VMEM((3, FFN, LANES), f32),
        ],
        compiler_params=params(18),
    )(order, first, rest)


PAD_ROWS = 16 * 16
BODY = SIDE * 16


def spread_matrix(shift):
    cell = lax.broadcasted_iota(jnp.int32, (PAD_ROWS, 208), 0)
    source = lax.broadcasted_iota(jnp.int32, (PAD_ROWS, 208), 1)
    row, column = cell >> 4, cell & 15
    inside = (row >= 1) & (row <= SIDE) & (column < SIDE)
    wanted = (row - 1) * SIDE + column + shift
    return jnp.where(inside & (source == wanted), 1.0, 0.0).astype(bf16)


def gather_matrix(shift):
    target = lax.broadcasted_iota(jnp.int32, (208, BODY), 0)
    cell = lax.broadcasted_iota(jnp.int32, (208, BODY), 1)
    row, column = cell >> 4, cell & 15
    wanted = row * SIDE + column + shift
    return jnp.where((column < SIDE) & (target == wanted), 1.0, 0.0).astype(bf16)


def pieces(value):
    first = value.astype(bf16)
    return first, (value - first.astype(f32)).astype(bf16)


def prepare_kernel(frames, turned, target, spread, back, passed, tokens, padded, sems):
    for member in range(4):
        spread[member] = spread_matrix(4 * member)
        back[member] = gather_matrix(4 * member)
    passed[0] = frames[0]
    tokens[...] = turned[...].T

    def fill(frame, carry):
        member = frame & 3
        place = pl.ds(pl.multiple_of(frame * FRAME - 4 * member, 16), 208)
        padded[frame] = dot(spread[member], tokens[place, :])
        return carry

    copies = []
    for group in range(padded.shape[0] // 4):
        lax.fori_loop(4 * group, 4 * group + 4, fill, 0)
        place = pl.ds(4 * group, 4)
        copies.append(pltpu.make_async_copy(padded.at[place], target.at[place], sems.at[group]))
        copies[-1].start()
    for copy in copies:
        copy.wait()


def prepare(frames, turned):
    rows = turned.shape[1]
    return pl.pallas_call(
        prepare_kernel,
        name="prepare",
        in_specs=[SMEM_SPEC, VMEM_SPEC],
        out_specs=[HBM_SPEC, VMEM_SPEC, VMEM_SPEC, SMEM_SPEC],
        out_shape=[
            pltpu.HBM((rows // FRAME, PAD_ROWS, DIM), f32),
            jax.ShapeDtypeStruct((4, PAD_ROWS, 208), bf16),
            jax.ShapeDtypeStruct((4, 208, BODY), bf16),
            jax.ShapeDtypeStruct((1,), jnp.int32),
        ],
        scratch_shapes=[
            pltpu.VMEM((rows, DIM), bf16),
            pltpu.VMEM((rows // FRAME, PAD_ROWS, DIM), f32),
            pltpu.SemaphoreType.DMA((rows // FRAME // 4,)),
        ],
        compiler_params=params(16),
    )(frames, turned)


PIECE = 4 * FRAME


def fetch_frames(source, slots, sems, start, count):
    first, last = max(start - 1, 0), min(start + count + 1, source.shape[0])
    middle = start + 2
    copies = []
    for index, (low, high) in enumerate(((first, middle), (middle, last))):
        copies.append(
            pltpu.make_async_copy(
                source.at[pl.ds(low, high - low)], slots.at[pl.ds(low - start + 1, high - low)], sems.at[index]
            )
        )
    return copies


def mix_frame(slots, at, weights, sums, out, sign):
    for low, high in TILES:
        for start in range(0, BODY, 56):
            parts = [None, None, None]
            for a in (-1, 0, 1):
                for b in (-1, 0, 1):
                    begin = 16 + sign * b * 16 + start
                    cells = slots[at[1 + sign * a], begin : begin + 56, low:high]
                    for c in range(3):
                        tap = 9 * (a + 1) + 3 * (b + 1) + c
                        term = cells * weights[tap : tap + 1, low:high]
                        parts[c] = term if parts[c] is None else parts[c] + term
            parts[1] = parts[1] + slots[at[1], 16 + start : 16 + start + 56, low:high]
            for c in range(3):
                sums[c, start : start + 56, low:high] = parts[c]
    before, after = (0, 2) if sign == 1 else (2, 0)
    for low, high in TILES:
        out[:, low:high] = (
            sums[1, :, low:high]
            + pltpu.roll(sums[before, :, low:high], 1, axis=0)
            + pltpu.roll(sums[after, :, low:high], BODY - 1, axis=0)
        )


def mask_weights(weights, masked, first, middle, last):
    for tap in range(27):
        keep = (first, middle, last)[tap // 9]
        scale = 1.0 if tap == 13 else jnp.where(keep, 1.0, 0.0)
        masked[tap : tap + 1, :] = weights[tap : tap + 1, :] * scale


def conv_params(head, flat, weights):
    flat[...] = head[...].astype(f32)
    for parity in range(2):
        for tile in range(3):
            low, side = read_half(flat, AT_CONV, 5, 5, 15, parity, 2 * tile)
            low = low_half(low, side)
            place = pl.ds(parity, 15, stride=2)
            if tile < 2:
                high, side = read_half(flat, AT_CONV, 5, 5, 15, parity, 2 * tile + 1)
                low = jnp.where(lane_of(low.shape) < 64, low, high_half(high, side))
            weights[tile, place, :] = low


def turn_kernel(frames, source, out, passed):
    passed[0] = frames[0]
    out[...] = source[...].T


def turn(frames, value):
    rows, columns = value.shape
    return pl.pallas_call(
        turn_kernel,
        name="turn",
        in_specs=[SMEM_SPEC, VMEM_SPEC],
        out_specs=[VMEM_SPEC, SMEM_SPEC],
        out_shape=[
            jax.ShapeDtypeStruct((columns, rows), value.dtype),
            jax.ShapeDtypeStruct((1,), jnp.int32),
        ],
        compiler_params=params(10),
        cost_estimate=pl.CostEstimate(flops=0, bytes_accessed=4 * rows * columns, transcendentals=0),
    )(frames, value)


def conv_piece_kernel(start, count, frames_ref, head, padded, back, *refs):
    if start > 0:
        refs = refs[1:]
    mixed, convp, passed, flat, weights, masked, slots, sums, comp, sem = refs
    passed[0] = frames_ref[0]
    copies = fetch_frames(padded, slots, sem, start, count)
    for copy in copies:
        copy.start()
    frames = frames_ref[0]
    conv_params(head, flat, weights)
    for tile, (low, high) in enumerate(TILES):
        convp[:, low:high] = weights[tile, :, : high - low]
    mixed[...] = jnp.zeros(mixed.shape, f32)
    copies[0].wait()

    def each(member, carry):
        @pl.when(member == 1)
        def _():
            copies[1].wait()

        frame = start + member
        there = frame < frames
        before = there & (frame > 0)
        after = frame + 1 < frames
        mask_weights(convp, masked, before, there, after)
        at = (member + jnp.where(before, 0, 1), member + 1, member + jnp.where(after, 2, 1))
        mix_frame(slots, at, masked, sums, comp, 1)
        high, low = pieces(comp[...] + convp[27:28, :])
        shift = member & 3
        place = pl.ds(pl.multiple_of(FRAME * member - 4 * shift, 16), 208)
        mixed[place, :] += dot(back[shift], high) + dot(back[shift], low)
        return carry

    lax.fori_loop(0, count, each, 0)


def conv_piece(start, count, frames, head, padded, back, mixed):
    rows = padded.shape[0] * FRAME
    operands = [frames, head, in_hbm(padded), back] + ([] if start == 0 else [mixed])
    return pl.pallas_call(
        functools.partial(conv_piece_kernel, start, count),
        name=f"conv_piece{start}",
        grid=(1,),
        in_specs=[SMEM_SPEC, VMEM_SPEC, HBM_SPEC, VMEM_SPEC] + [ANY_SPEC] * (start > 0),
        out_specs=[
            pl.BlockSpec((count * FRAME, DIM), lambda i: (start // count, 0)),
            pl.BlockSpec((32, DIM), lambda i: (0, 0)),
            SMEM_SPEC,
        ],
        out_shape=[
            jax.ShapeDtypeStruct((rows, DIM), f32),
            jax.ShapeDtypeStruct((32, DIM), f32),
            jax.ShapeDtypeStruct((1,), jnp.int32),
        ],
        input_output_aliases={4: 0} if start else {},
        scratch_shapes=[
            pltpu.VMEM(head.shape, f32),
            pltpu.VMEM((3, 32, LANES), f32),
            pltpu.VMEM((32, DIM), f32),
            pltpu.VMEM((count + 2, PAD_ROWS, DIM), f32),
            pltpu.VMEM((3, BODY, DIM), f32),
            pltpu.VMEM((BODY, DIM), f32),
            pltpu.SemaphoreType.DMA((2,)),
        ],
        compiler_params=params(20),
    )(*operands)


def normalize(values):
    centered = values - jnp.mean(values, axis=-1, keepdims=True)
    variance = jnp.mean(centered * centered, axis=-1, keepdims=True)
    inverse = lax.rsqrt(variance + EPSILON)
    return centered * inverse, inverse


def flag_base(head):
    return HEAD_DIM if head % 2 == 0 else 0


def own_lanes(lane, head):
    return lane < HEAD_DIM if head % 2 == 0 else lane >= HEAD_DIM


def row_size(value, own):
    part = jnp.where(own, value.astype(f32), 0.0)
    return jnp.sum(part * part, axis=-1, keepdims=True)


def qkv_kernel(frames_ref, mixed, convp, wqkv, bqkv, normed_out, q_out, k_out, v_out, size):
    block = pl.program_id(0)
    rows = mixed.shape[0]
    frames = frames_ref[0]
    normal, unused_inverse = normalize(mixed[...])
    normed = (normal * convp[28:29, :] + convp[29:30, :]).astype(bf16)
    normed_out[...] = normed
    lane = lane_of((rows, LANES))
    inside = row_of((rows, LANES)) + block * rows < frames * FRAME
    scale = HEAD_DIM ** (-0.5) * LOG2E

    @pl.when(block == 0)
    def _():
        size[...] = jnp.zeros(size.shape, f32)

    projected = dot(normed, wqkv[...]) + bqkv[...]
    masks = []
    for base in (flag_base(0), flag_base(1)):
        flag = lane - base
        q_flags = jnp.where(((flag == 0) & ~inside) | ((flag == 1) & inside), BLOCKED, 0.0)
        k_flags = jnp.where(
            ((flag == 0) & inside) | ((flag == 1) & ~inside) | ((flag >= 2) & (flag < 5)), 1.0, 0.0
        )
        v_flags = jnp.where((flag >= 0) & (flag < 3), 1.0, 0.0)
        masks.append((q_flags, k_flags, v_flags))
    for head in range(HEADS):
        q_mask, k_mask, v_mask = masks[head % 2]
        own = own_lanes(lane, head)

        def columns(kind, head=head):
            start = (kind * PAIRS + head // 2) * LANES
            return projected[:, start : start + LANES]

        query = jnp.where(own, columns(0) * scale, q_mask).astype(bf16)
        key = jnp.where(own, columns(1), k_mask).astype(bf16)
        query_size = jnp.max(row_size(query, own), axis=0, keepdims=True)
        key_size = jnp.max(row_size(key, own), axis=0, keepdims=True)
        q_out[head] = query
        k_out[head] = key
        v_out[head] = jnp.where(own, columns(2), v_mask).astype(bf16)
        size[head : head + 1, :] = jnp.maximum(size[head : head + 1, :], query_size)
        size[head + 8 : head + 9, :] = jnp.maximum(size[head + 8 : head + 9, :], key_size)


def project(frames, mixed, convp, wqkv, bqkv, block=784):
    rows = mixed.shape[0]
    heads_spec = pl.BlockSpec((HEADS, block, LANES), lambda i: (0, i, 0))
    rows_spec = pl.BlockSpec((block, DIM), lambda i: (i, 0))
    heads_shape = jax.ShapeDtypeStruct((HEADS, rows, LANES), bf16)
    return pl.pallas_call(
        qkv_kernel,
        name="qkv_forward",
        grid=(rows // block,),
        in_specs=[
            SMEM_SPEC,
            rows_spec,
            pl.BlockSpec((32, DIM), lambda i: (0, 0)),
            pl.BlockSpec((DIM, QKV_COLUMNS), lambda i: (0, 0)),
            pl.BlockSpec((1, QKV_COLUMNS), lambda i: (0, 0)),
        ],
        out_specs=[rows_spec, heads_spec, heads_spec, heads_spec, pl.BlockSpec((16, LANES), lambda i: (0, 0))],
        out_shape=[
            pltpu.HBM((rows, DIM), bf16),
            heads_shape,
            heads_shape,
            heads_shape,
            jax.ShapeDtypeStruct((16, LANES), f32),
        ],
        compiler_params=params(14),
    )(frames, mixed, convp, wqkv, bqkv)


def attend_kernel(chunk, q, k, v, size, o_out, q_back, query, shift):
    head = pl.program_id(0)
    keys = k.shape[1]
    tall = q.shape[1]
    bound = jnp.max(size[pl.ds(head, 1), :] * size[pl.ds(head + 8, 1), :])
    query[...] = q[0]
    shift[...] = jnp.zeros(shift.shape, f32)

    @pl.when(bound > SAFE_BOUND * SAFE_BOUND)
    def _():
        shift[...] = jnp.full(shift.shape, -jnp.inf, f32)

        def peak(step, carry):
            scores = dot_nt(k[0, pl.ds(pl.multiple_of(step * 112, 16), 112), :], q[0])
            shift[...] = jnp.maximum(shift[...], jnp.max(scores, axis=0, keepdims=True))
            return carry

        lax.fori_loop(0, keys // 112, peak, 0)
        first, second, third = split3(-shift[...])
        flag = row_of((LANES, tall)) - jnp.where(lax.rem(head, 2) == 0, HEAD_DIM, 0)
        tail = jnp.where(flag == 2, first, jnp.where(flag == 3, second, jnp.where(flag == 4, third, 0.0)))
        query[...] = (q[0].astype(f32) + tail.T).astype(bf16)

    total = None
    for start in range(0, keys, chunk):
        place = slice(start, min(start + chunk, keys))
        weights = jnp.exp2(dot_nt(k[0, place, :], query[...])).astype(bf16)
        part = dot_tn(v[0, place, :], weights)
        total = part if total is None else total + part
    def finish(parity):
        base = flag_base(parity)
        sums = total[base : base + 1, :]
        first, second, third = split3(-(shift[...] + jnp.log2(sums)))
        row = row_of((8, tall))
        tail = jnp.where(row == 2, first, jnp.where(row == 3, second, jnp.where(row == 4, third, 0.0)))
        flags = [tail, jnp.zeros((56, tall), f32)]
        own = [total[HEAD_DIM - base : 2 * HEAD_DIM - base, :] / sums]
        stacked = jnp.concatenate(own + flags if parity == 0 else flags + own, axis=0).T
        lane = lane_of((tall, LANES))
        o_out[0] = jnp.where(own_lanes(lane, parity), stacked, 0.0).astype(bf16)
        place = (lane >= base + 2) & (lane < base + 5)
        q_back[0] = jnp.where(place, stacked, q[0].astype(f32)).astype(bf16)

    for parity in range(2):
        pl.when(lax.rem(head, 2) == parity)(functools.partial(finish, parity))


def attend(q, k, v, size, chunk=512):
    rows = q.shape[1]
    whole = pl.BlockSpec((1, rows, LANES), lambda h: (h, 0, 0))
    shape = jax.ShapeDtypeStruct((HEADS, rows, LANES), bf16)
    return pl.pallas_call(
        functools.partial(attend_kernel, chunk),
        name="attend",
        grid=(HEADS,),
        in_specs=[whole, whole, whole, pl.BlockSpec((16, LANES), lambda h: (0, 0))],
        out_specs=[whole, whole],
        out_shape=[shape, pltpu.HBM(shape.shape, bf16)],
        scratch_shapes=[pltpu.VMEM((rows, LANES), bf16), pltpu.VMEM((1, rows), f32)],
        compiler_params=params(18),
    )(q, k, v, size)


def attend_back_kernel(q, do, k, v, dq_out, dk_out, dv_out):
    weights = jnp.exp2(dot_nt(q[0], k[0]))
    grad_scores = (weights * dot_nt(do[0], v[0])).astype(bf16)
    dv_out[0] = dot_tn(do[0], weights.astype(bf16)).T.astype(bf16)
    dk_out[0] = (dot_tn(q[0], grad_scores) * LN2).T.astype(bf16)
    dq_out[0] = (dot_nt(k[0].T, grad_scores) * HEAD_DIM ** (-0.5)).T.astype(bf16)


def attend_back(q, do, k, v):
    heads, rows = q.shape[:2]
    whole = pl.BlockSpec((1, rows, LANES), lambda h: (h, 0, 0))
    shape = jax.ShapeDtypeStruct((heads, rows, LANES), bf16)
    return pl.pallas_call(
        attend_back_kernel,
        name="attend_back",
        grid=(heads,),
        in_specs=[whole] * 4,
        out_specs=[whole] * 3,
        out_shape=[shape] * 3,
        compiler_params=params(40),
    )(q, do, k, v)


def erf_parts(value):
    bell = jnp.exp(-0.5 * value * value)
    return bell, 0.5 * (1.0 + lax.erf(value * (1.0 / math.sqrt(2.0))))


def paired(heads):
    tiles = []
    for head in range(0, HEADS, 2):
        high = heads[head + 1] if head + 1 < HEADS else jnp.zeros_like(heads[head])
        tiles.append(jnp.where(lane_of(high.shape) < HEAD_DIM, heads[head], high))
    return jnp.concatenate(tiles, axis=1)


def add_tiles(ref, place, value):
    for tile, (low, high) in enumerate(TILES):
        ref[tile, place, : high - low] += value[:, low:high]


def middle_kernel(
    frames_ref, o, mixed, cot, wproj, fc1, fc2, vecs, fc1b,
    output, gmid_out, do_out, gproj, gfc1, gfc2, gvec, gfc1b, chunk,
):
    block = pl.program_id(0)
    rows = mixed.shape[0]
    inside = row_of((rows, DIM)) + block * rows < frames_ref[0] * FRAME

    @pl.when(block == 0)
    def _():
        for ref in (gproj, gfc1, gfc2, gvec, gfc1b):
            ref[...] = jnp.zeros(ref.shape, f32)

    attended = paired(o)
    middle = mixed[...] + (dot(attended, wproj[...]) + vecs[0:1, :])
    normal, inverse = normalize(middle)
    normed = (normal * vecs[1:2, :] + vecs[2:3, :]).astype(bf16)
    grad_output = jnp.where(inside, cot[...].astype(f32), 0.0)
    grad_outer = grad_output.astype(bf16)
    total = middle + vecs[3:4, :]
    grad_normed = jnp.zeros((rows, DIM), f32)
    for start in range(0, FFN, chunk):
        place = slice(start, start + chunk)
        inner = dot(normed, fc1[:, place]) + fc1b[:, place]
        bell, gate = erf_parts(inner)
        activated = (inner * gate).astype(bf16)
        total += dot(activated, fc2[place, :])
        slope = gate + inner * bell * INVERSE_ROOT_TWO_PI
        grad_inner = (dot_nt(grad_outer, fc2[place, :]) * slope)
        gfc1b[:, place] += jnp.sum(grad_inner, axis=0, keepdims=True)
        grad_inner = grad_inner.astype(bf16)
        add_tiles(gfc2, place, dot_tn(activated, grad_outer))
        gfc1[:, place] += dot_tn(normed, grad_inner)
        grad_normed += dot_nt(grad_inner, fc1[:, place])
    output[...] = total.astype(bf16)
    scaled = grad_normed * vecs[1:2, :]
    grad_middle = grad_output + inverse * (
        scaled
        - jnp.mean(scaled, axis=-1, keepdims=True)
        - normal * jnp.mean(scaled * normal, axis=-1, keepdims=True)
    )
    gmid_out[...] = grad_middle
    grad_branch = grad_middle.astype(bf16)
    add_tiles(gproj, slice(None), dot_tn(attended, grad_branch))
    gvec[0:1, :] += jnp.sum(grad_branch.astype(f32), axis=0, keepdims=True)
    gvec[1:2, :] += jnp.sum(grad_normed * normal, axis=0, keepdims=True)
    gvec[2:3, :] += jnp.sum(grad_normed, axis=0, keepdims=True)
    gvec[3:4, :] += jnp.sum(grad_output, axis=0, keepdims=True)
    lane = lane_of((rows, LANES))
    grad_attended = dot_nt(grad_branch, wproj[...])
    for head in range(HEADS):
        grad_head = grad_attended[:, head // 2 * LANES : (head // 2 + 1) * LANES]
        flag = lane - flag_base(head)
        delta = jnp.sum(grad_head * o[head].astype(f32), axis=-1, keepdims=True)
        first, second, third = split3(-delta)
        tail = jnp.where(flag == 0, first, jnp.where(flag == 1, second, third))
        do_out[head] = jnp.where((flag >= 0) & (flag < 3), tail, grad_head).astype(bf16)


def feed_forward(frames, o, mixed, cot, wproj, fc1, fc2, vecs, fc1b, block=784, chunk=256):
    rows = mixed.shape[0]
    heads_spec = pl.BlockSpec((HEADS, block, LANES), lambda i: (0, i, 0))
    rows_spec = pl.BlockSpec((block, DIM), lambda i: (i, 0))

    def full(*shape):
        return pl.BlockSpec(shape, lambda i: (0,) * len(shape))

    return pl.pallas_call(
        functools.partial(middle_kernel, chunk=chunk),
        name="feed_forward",
        grid=(rows // block,),
        in_specs=[
            SMEM_SPEC, heads_spec, rows_spec, rows_spec,
            full(PAIR_COLUMNS, DIM), full(DIM, FFN), full(FFN, DIM), full(8, DIM), full(1, FFN),
        ],
        out_specs=[
            rows_spec, rows_spec, heads_spec,
            full(3, PAIR_COLUMNS, LANES), full(DIM, FFN), full(3, FFN, LANES), full(8, DIM), full(1, FFN),
        ],
        out_shape=[
            pltpu.HBM((rows, DIM), bf16),
            pltpu.HBM((rows, DIM), f32),
            pltpu.HBM((HEADS, rows, LANES), bf16),
            jax.ShapeDtypeStruct((3, PAIR_COLUMNS, LANES), f32),
            jax.ShapeDtypeStruct((DIM, FFN), f32),
            jax.ShapeDtypeStruct((3, FFN, LANES), f32),
            jax.ShapeDtypeStruct((8, DIM), f32),
            jax.ShapeDtypeStruct((1, FFN), f32),
        ],
        compiler_params=params(22),
    )(frames, o, mixed, cot, wproj, fc1, fc2, vecs, fc1b)


def qkv_back_kernel(dq, dk, dv, normed, mixed, gmid, wqkv, convp, spread, padded, gqkv, gbias, gvec, gmix):
    block = pl.program_id(0)

    @pl.when(block == 0)
    def _():
        for ref in (gqkv, gbias, gvec):
            ref[...] = jnp.zeros(ref.shape, f32)

    normal, inverse = normalize(mixed[...])
    grads = jnp.concatenate([paired(part) for part in (dq, dk, dv)], axis=1)
    grad_qkv = dot_tn(normed[...], grads)
    for tile in range(3 * PAIRS):
        gqkv[tile] += grad_qkv[:, tile * LANES : (tile + 1) * LANES]
    gbias[...] += jnp.sum(grads.astype(f32), axis=0, keepdims=True)
    grad_normed = dot_nt(grads, wqkv[...])
    gvec[1:2, :] += jnp.sum(grad_normed * normal, axis=0, keepdims=True)
    gvec[2:3, :] += jnp.sum(grad_normed, axis=0, keepdims=True)
    scaled = grad_normed * convp[28:29, :]
    grad_mixed = gmid[...] + inverse * (
        scaled
        - jnp.mean(scaled, axis=-1, keepdims=True)
        - normal * jnp.mean(scaled * normal, axis=-1, keepdims=True)
    )
    gvec[0:1, :] += jnp.sum(grad_mixed, axis=0, keepdims=True)
    gmix[...] = grad_mixed
    for member in range(mixed.shape[0] // FRAME):
        high, low = pieces(gmix[192 * member : 192 * member + 208, :])
        padded[member] = dot(spread[member], high) + dot(spread[member], low)


def project_back(dq, dk, dv, normed, mixed, gmid, wqkv, convp, spread, block=PIECE):
    rows = mixed.shape[0]
    heads_spec = pl.BlockSpec((HEADS, block, LANES), lambda i: (0, i, 0))
    rows_spec = pl.BlockSpec((block, DIM), lambda i: (i, 0))

    def full(*shape):
        return pl.BlockSpec(shape, lambda i: (0,) * len(shape))

    return pl.pallas_call(
        qkv_back_kernel,
        name="qkv_back",
        grid=(rows // block,),
        in_specs=[heads_spec, heads_spec, heads_spec, rows_spec, rows_spec, rows_spec,
                  full(DIM, QKV_COLUMNS), full(32, DIM), full(4, PAD_ROWS, 208)],
        out_specs=[pl.BlockSpec((4, PAD_ROWS, DIM), lambda i: (i, 0, 0)), full(3 * PAIRS, DIM, LANES), full(1, QKV_COLUMNS), full(8, DIM)],
        out_shape=[
            pltpu.HBM((rows // FRAME, PAD_ROWS, DIM), f32),
            jax.ShapeDtypeStruct((3 * PAIRS, DIM, LANES), f32),
            jax.ShapeDtypeStruct((1, QKV_COLUMNS), f32),
            jax.ShapeDtypeStruct((8, DIM), f32),
        ],
        scratch_shapes=[pltpu.VMEM((block, DIM), f32)],
        compiler_params=params(18),
    )(dq, dk, dv, normed, mixed, gmid, wqkv, convp, spread)


def conv_weight_kernel(frames_ref, xsource, gsource, gvec, out, xpad, gpad, moved, sums, tiles, flat, xsem, gsem):
    frames = frames_ref[0]
    count = xpad.shape[0]
    copies = []
    for group in range(count // 4):
        place = pl.ds(4 * group, 4)
        copies.append(pltpu.make_async_copy(xsource.at[place], xpad.at[place], xsem.at[group]))
        copies.append(pltpu.make_async_copy(gsource.at[place], gpad.at[place], gsem.at[group]))
    for copy in copies:
        copy.start()
    sums[...] = jnp.zeros(sums.shape, f32)

    def weight_frame(frame, carry):
        for low, high in TILES:
            body = gpad[frame, 16 : 16 + BODY, low:high]
            moved[0, :, low:high] = pltpu.roll(body, BODY - 1, axis=0)
            moved[1, :, low:high] = pltpu.roll(body, 1, axis=0)
        for a in (-1, 0, 1):
            at = frame + a

            @pl.when((at >= 0) & (at < frames))
            def _():
                for low, high in TILES:
                    for b in (-1, 0, 1):
                        cells = xpad[at, 16 + b * 16 : 16 + b * 16 + BODY, low:high]
                        for c in range(3):
                            body = (
                                gpad[frame, 16 : 16 + BODY, low:high]
                                if c == 1
                                else moved[c // 2, :, low:high]
                            )
                            product = (body * cells).reshape(BODY // 8, 8, high - low)
                            tap = 9 * (a + 1) + 3 * (b + 1) + c
                            sums[tap, :, low:high] += jnp.sum(product, axis=0)

        return carry

    for group in range(count // 4):
        copies[2 * group].wait()
        copies[2 * group + 1].wait()
        start = max(4 * group - 1, 0)
        stop = 4 * group + 3 if group < count // 4 - 1 else count
        lax.fori_loop(jnp.minimum(start, frames), jnp.minimum(stop, frames), weight_frame, 0)
    tiles[...] = jnp.zeros(tiles.shape, f32)
    flat[...] = jnp.zeros(flat.shape, f32)
    for tile, (low, high) in enumerate(TILES):
        tiles[tile, 0:27, : high - low] = jnp.sum(sums[:, :, low:high], axis=1)
        tiles[tile, 27:30, : high - low] = gvec[0:3, low:high]
    for parity in range(2):
        for j in range(5):
            value = tiles[j // 2, pl.ds(parity, 15, stride=2), :]
            put_half(flat, AT_CONV + parity * 5 + j, value, j % 2, 5, 15)
    out[...] = flat[...].astype(bf16)


def conv_weight_grads(frames, xpad, gpad, gvec):
    return pl.pallas_call(
        conv_weight_kernel,
        name="conv_weight_grads",
        in_specs=[SMEM_SPEC, HBM_SPEC, HBM_SPEC, VMEM_SPEC],
        out_shape=jax.ShapeDtypeStruct((80, LANES), bf16),
        scratch_shapes=[
            pltpu.VMEM(xpad.shape, f32),
            pltpu.VMEM(gpad.shape, f32),
            pltpu.VMEM((2, BODY, DIM), f32),
            pltpu.VMEM((27, 8, DIM), f32),
            pltpu.VMEM((3, 32, LANES), f32),
            pltpu.VMEM((80, LANES), f32),
            pltpu.SemaphoreType.DMA((xpad.shape[0] // 4,)),
            pltpu.SemaphoreType.DMA((xpad.shape[0] // 4,)),
        ],
        compiler_params=params(18),
    )(frames, in_hbm(xpad), in_hbm(gpad), gvec)


def token_piece_kernel(piece, frames_ref, convp, gsource, back, *refs):
    if piece > 0:
        refs = refs[1:]
    gtok, passed, masked, slots, sums, comp, rows, sem = refs
    frames = frames_ref[0]
    passed[0] = frames
    copies = fetch_frames(gsource, slots, sem, 4 * piece, 4)
    for copy in copies:
        copy.start()
    rows[...] = jnp.zeros(rows.shape, f32)
    copies[0].wait()

    def each(member, carry):
        @pl.when(member == 1)
        def _():
            copies[1].wait()

        frame = 4 * piece + member
        there = frame < frames
        before = there & (frame > 0)
        after = frame + 1 < frames
        mask_weights(convp, masked, after, there, before)
        at = (member + jnp.where(before, 0, 1), member + 1, member + jnp.where(after, 2, 1))
        mix_frame(slots, at, masked, sums, comp, -1)
        place = pl.ds(pl.multiple_of(192 * member, 16), 208)
        rows[place, :] += dot(back[member], comp[...].astype(bf16))
        return carry

    lax.fori_loop(0, 4, each, 0)
    gtok[...] = rows[...].astype(bf16)


def token_piece(piece, frames, convp, gpad, back, gtok):
    count = gpad.shape[0]
    operands = [frames, convp, in_hbm(gpad), back] + ([] if piece == 0 else [gtok])
    return pl.pallas_call(
        functools.partial(token_piece_kernel, piece),
        name=f"token_piece{piece}",
        grid=(1,),
        in_specs=[SMEM_SPEC, VMEM_SPEC, HBM_SPEC, VMEM_SPEC] + [ANY_SPEC] * (piece > 0),
        out_specs=[pl.BlockSpec((PIECE, DIM), lambda i: (piece, 0)), SMEM_SPEC],
        out_shape=[
            jax.ShapeDtypeStruct((count * FRAME, DIM), bf16),
            jax.ShapeDtypeStruct((1,), jnp.int32),
        ],
        input_output_aliases={4: 0} if piece else {},
        scratch_shapes=[
            pltpu.VMEM((32, DIM), f32),
            pltpu.VMEM((6, PAD_ROWS, DIM), f32),
            pltpu.VMEM((3, BODY, DIM), f32),
            pltpu.VMEM((BODY, DIM), f32),
            pltpu.VMEM((PIECE, DIM), f32),
            pltpu.SemaphoreType.DMA((2,)),
        ],
        compiler_params=params(10),
    )(*operands)


def put_half(flat, index, value, side, step=1, count=1):
    row, wanted = divmod(index, 2)
    place = pl.ds(row, count, stride=step) if step > 1 else pl.ds(row, count)
    lane = lane_of(value.shape)
    if wanted == 0:
        flat[place, :] += jnp.where(lane < 64, low_half(value, side), 0.0)
    else:
        flat[place, :] += jnp.where(lane >= 64, high_half(value, side), 0.0)


def put_vector(flat, index, value):
    width = value.shape[1]
    for j in range(width // 64):
        low = (j // 2) * LANES
        part = value[:, low : min(low + LANES, width)]
        if part.shape[1] < LANES:
            part = jnp.concatenate([part, jnp.zeros((1, 64), f32)], axis=1)
        put_half(flat, index + j, part, j % 2)


PACK_BASE = 2432


def pack_main_kernel(gproj, gfc1, gfc2, gvec, gfc1b, out, flat):
    flat[...] = jnp.zeros(flat.shape, f32)
    for parity in range(2):
        for j in range(5):
            value = gproj[j // 2, pl.ds(parity, DIM // 2, stride=2), :]
            put_half(flat, AT_PROJ + parity * 5 + j, value, j % 2, 5, DIM // 2)
            value = gfc2[j // 2, pl.ds(parity, FFN // 2, stride=2), :]
            put_half(flat, AT_FC2 + parity * 5 + j, value, j % 2, 5, FFN // 2)
    for j in range(20):
        value = gfc1[:, (j // 2) * LANES : (j // 2 + 1) * LANES]
        put_half(flat, AT_FC1 + j, value, j % 2, 10, DIM)
    for row in range(3):
        put_vector(flat, AT_VEC + 5 * row, gvec[row : row + 1, :])
    put_vector(flat, AT_FC2B, gvec[3:4, :])
    put_vector(flat, AT_FC1B, gfc1b[...])
    out[...] = flat[...].astype(bf16)


def pack_main(gproj, gfc1, gfc2, gvec, gfc1b, rows):
    return pl.pallas_call(
        pack_main_kernel,
        name="pack_main",
        out_shape=jax.ShapeDtypeStruct((rows, LANES), bf16),
        scratch_shapes=[pltpu.VMEM((rows, LANES), f32)],
        compiler_params=params(14),
    )(gproj, gfc1, gfc2, gvec, gfc1b)


QKV_ROWS = 2480


def pack_qkv_kernel(gqkv, gbias, out, end, flat):
    flat[...] = jnp.zeros(flat.shape, f32)
    for parity in range(2):
        for j in range(15):
            kind, head = divmod(j, HEADS)
            value = gqkv[kind * PAIRS + head // 2, pl.ds(parity, DIM // 2, stride=2), :]
            put_half(flat, AT_QKV + parity * 15 + j, value, head % 2, 15, DIM // 2)
    for j in range(10):
        start = (0 if j < HEADS else 2 * PAIR_COLUMNS) + j % HEADS // 2 * LANES
        put_half(flat, AT_QV + j, gbias[:, start : start + LANES], j % HEADS % 2)
    out[...] = flat[:PACK_BASE, :].astype(bf16)
    end[...] = flat[PACK_BASE:, :].astype(bf16)


def pack_qkv(gqkv, gbias):
    return pl.pallas_call(
        pack_qkv_kernel,
        name="pack_qkv",
        out_shape=[
            jax.ShapeDtypeStruct((PACK_BASE, LANES), bf16),
            jax.ShapeDtypeStruct((QKV_ROWS - PACK_BASE, LANES), bf16),
        ],
        scratch_shapes=[pltpu.VMEM((QKV_ROWS, LANES), f32)],
        compiler_params=params(10),
    )(gqkv, gbias)


AXES = ("wide", "narrow")


def exchange(value, bit):
    count = lax.axis_size(AXES)
    return lax.ppermute(value, AXES, [(i, i ^ (1 << bit)) for i in range(count)])


def my_bit(bit):
    return (lax.axis_index(AXES) >> bit) & 1


def tie(*values):
    return lax.optimization_barrier(values)


def split(value, bit):
    value = value.reshape(value.shape[0] // 2, 2, -1, LANES)
    mine = my_bit(bit)
    keep = lax.dynamic_index_in_dim(value, mine, 1, keepdims=False)
    return keep, lax.dynamic_index_in_dim(value, 1 - mine, 1, keepdims=False)


def on_device(master, momentum, average, tokens, clip_ids, borders, cotangent):
    wide_count, narrow_count = lax.axis_size("wide"), lax.axis_size("narrow")
    count = wide_count * narrow_count
    bits = count.bit_length() - 1
    own_rows = master.shape[0]
    filled = jnp.sum((clip_ids >= 0).astype(jnp.int32))
    frames = jnp.where(filled > 6 * FRAME, 12, jnp.where(filled > 3 * FRAME, 6, 3)).reshape(1)
    me = lax.axis_index(AXES)
    quarter = me >> (bits - 2)
    blocks = master.astype(bf16)[None]
    other = exchange(blocks, bits - 2)
    other, frames = tie(other, frames)
    blocks = jnp.concatenate([blocks, other], axis=0)
    blocks, frames = tie(blocks, frames)
    other = exchange(blocks, bits - 1)
    xpad, spread, back, frames = prepare(frames, tokens.T)
    other, frames = tie(other, frames)
    blocks = jnp.concatenate([blocks, other], axis=0)
    first = lax.dynamic_index_in_dim(blocks, quarter, 0)
    rest = [lax.dynamic_index_in_dim(blocks, quarter ^ index, 0) for index in (1, 2, 3)]
    rest = jnp.concatenate(rest, axis=0)[None]
    low_bits = list(range(bits - 3, -1, -1))
    for step, bit in enumerate(low_bits):
        if step == 0:
            first, frames = tie(first, frames)
        other = exchange(first, bit)
        if step == 0:
            cotangent, frames = turn(frames, cotangent.T)
            other, frames = tie(other, frames)
        first = jnp.concatenate([first, other], axis=0)
        if step == 0:
            first, rest, frames = tie(first, rest, frames)
            rest = jnp.concatenate([rest, exchange(rest, bit)], axis=0)
    order = [0] * (count // 4)
    for step, bit in enumerate(low_bits):
        order = [place | (((index >> bit) & 1) << step) for index, place in enumerate(order)]
    mine = sum((((me >> bit) & 1) << step) for step, bit in enumerate(low_bits))
    order = jnp.array(order, jnp.int32) ^ mine
    head = lax.dynamic_index_in_dim(first, mine, 0, keepdims=False)
    head = jnp.concatenate([head, jnp.zeros((4, LANES), bf16)], axis=0)[:80] if own_rows < 80 else head[:80]
    mixed, convp = None, None
    for step, bit in enumerate(low_bits[1:]):
        if step < 2:
            rest, frames = tie(rest, frames)
        other = exchange(rest, bit)
        if step == 0:
            mixed, convp, frames = conv_piece(0, 8, frames, head, xpad, back, None)
        elif step == 1:
            mixed, convp, frames = conv_piece(8, 4, frames, head, xpad, back, mixed)
        other, frames = tie(other, frames)
        rest = jnp.concatenate([rest, other], axis=0)
    wqkv, wproj, fc1, fc2, bqkv, vecs, fc1b = unpack(order, first, rest)
    normed, q, k, v, size = project(frames, mixed, convp, wqkv, bqkv)
    o, q_back = attend(q, k, v, size)
    output, gmid, do, gproj, gfc1, gfc2, gvec, gfc1b = feed_forward(
        frames, o, mixed, cotangent, wproj, fc1, fc2, vecs, fc1b
    )
    main = pack_main(gproj, gfc1, gfc2, gvec, gfc1b, count * own_rows)
    main = main.reshape(wide_count, narrow_count, own_rows, LANES)
    main = lax.psum_scatter(main, "wide", scatter_dimension=0, tiled=True)[0]
    q_back, do, k, v = (in_hbm(value) for value in (q_back, do, k, v))
    dq, dk, dv = attend_back(q_back, do, k, v)
    gpad, gqkv, gbias, gvec_one = project_back(dq, dk, dv, normed, mixed, gmid, wqkv, convp, spread)
    qkv, qkv_end = pack_qkv(gqkv, gbias)
    qkv = qkv.reshape(count // 4, own_rows, LANES)
    narrow_bits = narrow_count.bit_length() - 1
    keep, give = split(qkv, 0)
    gvec_one, give = tie(gvec_one, give)
    arriving = exchange(give, 0)
    conv = conv_weight_grads(frames, xpad, gpad, gvec_one)
    late = jnp.concatenate([conv, qkv_end], axis=0)
    main, late = tie(main, late)
    for bit in range(1, narrow_bits):
        keep, give = split(keep + arriving, bit)
        arriving = exchange(give, bit)
    gtok = None
    for bit in range(bits):
        if bit < narrow_bits:
            stays, give = split(main, bit)
        elif bit < bits - 2:
            stays, give = split(qkv, bit)
        else:
            stays, give = qkv, qkv
        sent = give.shape[0] * own_rows
        packet = jnp.concatenate([give.reshape(sent, LANES), late], axis=0)
        packet, frames = tie(packet, frames)
        other = exchange(packet, bit)
        if bit == 0:
            output, frames = turn(frames, output)
        elif bit < 4:
            gtok, frames = token_piece(bit - 1, frames, convp, gpad, back, gtok)
        elif bit == 4:
            gtok, frames = turn(frames, gtok)
        other, frames = tie(other, frames)
        if bit == narrow_bits - 1:
            other, arriving = tie(other, arriving)
            qkv = keep + arriving
        summed = stays + other[:sent].reshape(stays.shape)
        late = late + other[sent:]
        if bit < narrow_bits:
            main = summed
        else:
            qkv = summed
    main, qkv = main[0], qkv[0]
    early = jnp.where(me < count // 4, qkv.astype(f32), main.astype(f32))
    conv, qkv_end = late[:80].astype(f32), late[80:].astype(f32)
    if own_rows < 80:
        conv = conv[:own_rows]
    conv = jnp.pad(conv, ((0, own_rows - conv.shape[0]), (0, 0)))
    qkv_end = jnp.pad(qkv_end, ((0, own_rows - qkv_end.shape[0]), (0, 0)))
    owned = early + jnp.where(me == 0, conv, jnp.where(me == count // 4, qkv_end, 0.0))
    rate = RATE_FACTOR / math.sqrt(tokens.shape[0] * count)
    decayed = owned + DECAY_RATE * master
    new_momentum = MOMENTUM * momentum + decayed
    new_master = master - rate * (decayed + MOMENTUM * new_momentum)
    new_average = AVERAGE_KEEP * average + (1.0 - AVERAGE_KEEP) * new_master
    return (output.T, gtok.T, owned, new_master, new_momentum, new_average, new_master.astype(bf16))


def solution(mesh):
    rows = P(("wide", "narrow"), None)
    return jax.shard_map(
        on_device,
        mesh=mesh,
        in_specs=(rows, rows, rows, rows, P(("wide", "narrow")), P(("wide", "narrow")), rows),
        out_specs=(rows,) * 7,
        check_vma=False,
    )
```

```python
import functools
import math

import jax
import jax.numpy as jnp
from jax import lax
from jax.experimental import pallas as pl
from jax.experimental.pallas import tpu as pltpu
from jax.sharding import PartitionSpec as P

HEADS = 5
HEAD_DIM = 64
DIM = 320
FFN = 1280
SIDE = 14
FRAME = SIDE * SIDE
LANES = 128
PAIRS = (HEADS + 1) // 2
PAIR_COLUMNS = PAIRS * LANES
QKV_COLUMNS = 3 * PAIR_COLUMNS

EPSILON = 1e-06
MOMENTUM = 0.9
DECAY_RATE = 0.0001
AVERAGE_KEEP = 0.8
RATE_FACTOR = 0.03
LOG2E = 1.0 / math.log(2.0)
LN2 = math.log(2.0)
INVERSE_ROOT_TWO_PI = 1.0 / math.sqrt(2.0 * math.pi)
BLOCKED = -(2.0**30)
SAFE_BOUND = 80.0

TILES = ((0, 128), (128, 256), (256, 320))

bf16 = jnp.bfloat16
f32 = jnp.float32

AT_CONV = 0
AT_QKV = 150
AT_QV = 4950
AT_PROJ = 4960
AT_VEC = 6560
AT_FC1 = 6575
AT_FC1B = 12975
AT_FC2 = 12995
AT_FC2B = 19395
HALF_END = 19400


SMEM_SPEC = pl.BlockSpec(memory_space=pltpu.SMEM)
VMEM_SPEC = pl.BlockSpec(memory_space=pltpu.VMEM)
ANY_SPEC = pl.BlockSpec(memory_space=pl.ANY)
HBM_SPEC = pl.BlockSpec(memory_space=pltpu.HBM)


def in_hbm(value):
    return pltpu.with_memory_space_constraint(value, pltpu.HBM)


def dot(a, b):
    return lax.dot_general(a, b, (((1,), (0,)), ((), ())), preferred_element_type=f32)


def dot_nt(a, b):
    return lax.dot_general(a, b, (((1,), (1,)), ((), ())), preferred_element_type=f32)


def dot_tn(a, b):
    return lax.dot_general(a, b, (((0,), (0,)), ((), ())), preferred_element_type=f32)


def params(limit=58):
    return pltpu.CompilerParams(vmem_limit_bytes=limit << 20)


def lane_of(shape):
    return lax.broadcasted_iota(jnp.int32, shape, len(shape) - 1)


def row_of(shape):
    return lax.broadcasted_iota(jnp.int32, shape, 0)


def low_half(value, side):
    return value if side == 0 else pltpu.roll(value, 64, axis=1)


def high_half(value, side):
    return value if side == 1 else pltpu.roll(value, 64, axis=1)


def split3(value):
    first = value.astype(bf16).astype(f32)
    rest = value - first
    second = rest.astype(bf16).astype(f32)
    return first, second, rest - second


def read_half(flat, at, length, step, count, parity, j):
    index = at + parity * length + j
    return flat[pl.ds(index // 2, count, stride=step), :], index % 2


def read_vector(flat, at, length):
    tiles = []
    lane = lane_of((1, LANES))
    for j in range(0, length, 2):
        row, side = divmod(at + j, 2)
        low = low_half(flat[row : row + 1, :], side)
        if j + 1 < length:
            row, side = divmod(at + j + 1, 2)
            tiles.append(jnp.where(lane < 64, low, high_half(flat[row : row + 1, :], side)))
        else:
            tiles.append(low[:, :64])
    return jnp.concatenate(tiles, axis=1)


def odd_matrix(flat, out, at, length, rows):
    pairs = rows // 2
    for parity in range(2):
        for tile in range((length + 1) // 2):
            low, side = read_half(flat, at, length, length, pairs, parity, 2 * tile)
            low = low_half(low, side)
            place = pl.ds(parity, pairs, stride=2)
            if 2 * tile + 1 < length:
                high, side = read_half(flat, at, length, length, pairs, parity, 2 * tile + 1)
                merged = jnp.where(lane_of(low.shape) < 64, low, high_half(high, side))
            else:
                merged = low
            out[tile, place, :] = merged


def unpack_kernel(order, first, rest, wqkv, wproj, fc1, fc2, bqkv, vecs, fc1b, flat, wide, tall):
    blocks, rows = first.shape[:2]
    for block in range(blocks):
        place = order[block]
        for quarter in range(4):
            start = (quarter * blocks + block) * rows
            value = first[place] if quarter == 0 else rest[place, quarter - 1]
            flat[start : start + rows, :] = value.astype(f32)
    for parity in range(2):
        place = pl.ds(parity, DIM // 2, stride=2)
        for kind in range(3):
            for pair in range(PAIRS):
                j = kind * HEADS + 2 * pair
                low, side = read_half(flat, AT_QKV, 15, 15, DIM // 2, parity, j)
                low = low_half(low, side)
                high = jnp.zeros_like(low)
                if 2 * pair + 1 < HEADS:
                    high, side = read_half(flat, AT_QKV, 15, 15, DIM // 2, parity, j + 1)
                    high = high_half(high, side)
                wide[kind * PAIRS + pair, place, :] = jnp.where(lane_of(low.shape) < 64, low, high)
    for tile in range(3 * PAIRS):
        wqkv[:, tile * LANES : (tile + 1) * LANES] = wide[tile].astype(bf16)
    bqkv[...] = jnp.zeros(bqkv.shape, f32)
    for index, kind in enumerate((0, 2)):
        start = kind * PAIR_COLUMNS
        bqkv[:, start : start + DIM] = read_vector(flat, AT_QV + index * HEADS, HEADS)
    odd_matrix(flat, wide, AT_PROJ, 5, DIM)
    for tile, (low, high) in enumerate(TILES):
        wproj[:DIM, low:high] = wide[tile, :, : high - low].astype(bf16)
    wproj[DIM:, :] = jnp.zeros((PAIR_COLUMNS - DIM, DIM), bf16)
    for row in range(3):
        vecs[row : row + 1, :] = read_vector(flat, AT_VEC + 5 * row, 5)
    vecs[3:4, :] = read_vector(flat, AT_FC2B, 5)
    vecs[4:8, :] = jnp.zeros((4, DIM), f32)
    fc1b[...] = read_vector(flat, AT_FC1B, 20)
    for tile in range(10):
        low, side = read_half(flat, AT_FC1, 20, 10, DIM, 0, 2 * tile)
        high, side_high = read_half(flat, AT_FC1, 20, 10, DIM, 0, 2 * tile + 1)
        merged = jnp.where(lane_of(low.shape) < 64, low_half(low, side), high_half(high, side_high))
        fc1[:, tile * LANES : (tile + 1) * LANES] = merged.astype(bf16)
    odd_matrix(flat, tall, AT_FC2, 5, FFN)
    for tile in range(3):
        width = LANES if tile < 2 else 64
        fc2[:, tile * LANES : tile * LANES + width] = tall[tile, :, :width].astype(bf16)


def unpack(order, first, rest):
    rows = 4 * first.shape[0] * first.shape[1]
    return pl.pallas_call(
        unpack_kernel,
        name="unpack",
        in_specs=[SMEM_SPEC, VMEM_SPEC, VMEM_SPEC],
        out_shape=[
            jax.ShapeDtypeStruct((DIM, QKV_COLUMNS), bf16),
            jax.ShapeDtypeStruct((PAIR_COLUMNS, DIM), bf16),
            jax.ShapeDtypeStruct((DIM, FFN), bf16),
            jax.ShapeDtypeStruct((FFN, DIM), bf16),
            jax.ShapeDtypeStruct((1, QKV_COLUMNS), f32),
            jax.ShapeDtypeStruct((8, DIM), f32),
            jax.ShapeDtypeStruct((1, FFN), f32),
        ],
        scratch_shapes=[
            pltpu.VMEM((rows, LANES), f32),
            pltpu.VMEM((15, DIM, LANES), f32),
            pltpu.VMEM((3, FFN, LANES), f32),
        ],
        compiler_params=params(18),
    )(order, first, rest)


PAD_ROWS = 16 * 16
BODY = SIDE * 16


def spread_matrix(shift):
    cell = lax.broadcasted_iota(jnp.int32, (PAD_ROWS, 208), 0)
    source = lax.broadcasted_iota(jnp.int32, (PAD_ROWS, 208), 1)
    row, column = cell >> 4, cell & 15
    inside = (row >= 1) & (row <= SIDE) & (column < SIDE)
    wanted = (row - 1) * SIDE + column + shift
    return jnp.where(inside & (source == wanted), 1.0, 0.0).astype(bf16)


def gather_matrix(shift):
    target = lax.broadcasted_iota(jnp.int32, (208, BODY), 0)
    cell = lax.broadcasted_iota(jnp.int32, (208, BODY), 1)
    row, column = cell >> 4, cell & 15
    wanted = row * SIDE + column + shift
    return jnp.where((column < SIDE) & (target == wanted), 1.0, 0.0).astype(bf16)


def pieces(value):
    first = value.astype(bf16)
    return first, (value - first.astype(f32)).astype(bf16)


def prepare_kernel(frames, turned, target, spread, back, passed, tokens, padded, sems):
    for member in range(4):
        spread[member] = spread_matrix(4 * member)
        back[member] = gather_matrix(4 * member)
    passed[0] = frames[0]
    tokens[...] = turned[...].T

    def fill(frame, carry):
        member = frame & 3
        place = pl.ds(pl.multiple_of(frame * FRAME - 4 * member, 16), 208)
        padded[frame] = dot(spread[member], tokens[place, :])
        return carry

    copies = []
    for group in range(padded.shape[0] // 4):
        lax.fori_loop(4 * group, 4 * group + 4, fill, 0)
        place = pl.ds(4 * group, 4)
        copies.append(pltpu.make_async_copy(padded.at[place], target.at[place], sems.at[group]))
        copies[-1].start()
    for copy in copies:
        copy.wait()


def prepare(frames, turned):
    rows = turned.shape[1]
    return pl.pallas_call(
        prepare_kernel,
        name="prepare",
        in_specs=[SMEM_SPEC, VMEM_SPEC],
        out_specs=[HBM_SPEC, VMEM_SPEC, VMEM_SPEC, SMEM_SPEC],
        out_shape=[
            pltpu.HBM((rows // FRAME, PAD_ROWS, DIM), f32),
            jax.ShapeDtypeStruct((4, PAD_ROWS, 208), bf16),
            jax.ShapeDtypeStruct((4, 208, BODY), bf16),
            jax.ShapeDtypeStruct((1,), jnp.int32),
        ],
        scratch_shapes=[
            pltpu.VMEM((rows, DIM), bf16),
            pltpu.VMEM((rows // FRAME, PAD_ROWS, DIM), f32),
            pltpu.SemaphoreType.DMA((rows // FRAME // 4,)),
        ],
        compiler_params=params(16),
    )(frames, turned)


PIECE = 4 * FRAME


def fetch_frames(source, slots, sems, start, count):
    first, last = max(start - 1, 0), min(start + count + 1, source.shape[0])
    middle = start + 2
    copies = []
    for index, (low, high) in enumerate(((first, middle), (middle, last))):
        copies.append(
            pltpu.make_async_copy(
                source.at[pl.ds(low, high - low)], slots.at[pl.ds(low - start + 1, high - low)], sems.at[index]
            )
        )
    return copies


def mix_frame(slots, at, weights, sums, out, sign):
    for low, high in TILES:
        for start in range(0, BODY, 56):
            parts = [None, None, None]
            for a in (-1, 0, 1):
                for b in (-1, 0, 1):
                    begin = 16 + sign * b * 16 + start
                    cells = slots[at[1 + sign * a], begin : begin + 56, low:high]
                    for c in range(3):
                        tap = 9 * (a + 1) + 3 * (b + 1) + c
                        term = cells * weights[tap : tap + 1, low:high]
                        parts[c] = term if parts[c] is None else parts[c] + term
            parts[1] = parts[1] + slots[at[1], 16 + start : 16 + start + 56, low:high]
            for c in range(3):
                sums[c, start : start + 56, low:high] = parts[c]
    before, after = (0, 2) if sign == 1 else (2, 0)
    for low, high in TILES:
        out[:, low:high] = (
            sums[1, :, low:high]
            + pltpu.roll(sums[before, :, low:high], 1, axis=0)
            + pltpu.roll(sums[after, :, low:high], BODY - 1, axis=0)
        )


def mask_weights(weights, masked, first, middle, last):
    for tap in range(27):
        keep = (first, middle, last)[tap // 9]
        scale = 1.0 if tap == 13 else jnp.where(keep, 1.0, 0.0)
        masked[tap : tap + 1, :] = weights[tap : tap + 1, :] * scale


def conv_params(head, flat, weights):
    flat[...] = head[...].astype(f32)
    for parity in range(2):
        for tile in range(3):
            low, side = read_half(flat, AT_CONV, 5, 5, 15, parity, 2 * tile)
            low = low_half(low, side)
            place = pl.ds(parity, 15, stride=2)
            if tile < 2:
                high, side = read_half(flat, AT_CONV, 5, 5, 15, parity, 2 * tile + 1)
                low = jnp.where(lane_of(low.shape) < 64, low, high_half(high, side))
            weights[tile, place, :] = low


def turn_kernel(frames, source, out, passed):
    passed[0] = frames[0]
    out[...] = source[...].T


def turn(frames, value):
    rows, columns = value.shape
    return pl.pallas_call(
        turn_kernel,
        name="turn",
        in_specs=[SMEM_SPEC, VMEM_SPEC],
        out_specs=[VMEM_SPEC, SMEM_SPEC],
        out_shape=[
            jax.ShapeDtypeStruct((columns, rows), value.dtype),
            jax.ShapeDtypeStruct((1,), jnp.int32),
        ],
        compiler_params=params(10),
        cost_estimate=pl.CostEstimate(flops=0, bytes_accessed=4 * rows * columns, transcendentals=0),
    )(frames, value)


def conv_piece_kernel(start, count, frames_ref, head, padded, back, *refs):
    if start > 0:
        refs = refs[1:]
    mixed, convp, passed, flat, weights, masked, slots, sums, comp, sem = refs
    passed[0] = frames_ref[0]
    copies = fetch_frames(padded, slots, sem, start, count)
    for copy in copies:
        copy.start()
    frames = frames_ref[0]
    conv_params(head, flat, weights)
    for tile, (low, high) in enumerate(TILES):
        convp[:, low:high] = weights[tile, :, : high - low]
    mixed[...] = jnp.zeros(mixed.shape, f32)
    copies[0].wait()

    def each(member, carry):
        @pl.when(member == 1)
        def _():
            copies[1].wait()

        frame = start + member
        there = frame < frames
        before = there & (frame > 0)
        after = frame + 1 < frames
        mask_weights(convp, masked, before, there, after)
        at = (member + jnp.where(before, 0, 1), member + 1, member + jnp.where(after, 2, 1))
        mix_frame(slots, at, masked, sums, comp, 1)
        high, low = pieces(comp[...] + convp[27:28, :])
        shift = member & 3
        place = pl.ds(pl.multiple_of(FRAME * member - 4 * shift, 16), 208)
        mixed[place, :] += dot(back[shift], high) + dot(back[shift], low)
        return carry

    lax.fori_loop(0, count, each, 0)


def conv_piece(start, count, frames, head, padded, back, mixed):
    rows = padded.shape[0] * FRAME
    operands = [frames, head, in_hbm(padded), back] + ([] if start == 0 else [mixed])
    return pl.pallas_call(
        functools.partial(conv_piece_kernel, start, count),
        name=f"conv_piece{start}",
        grid=(1,),
        in_specs=[SMEM_SPEC, VMEM_SPEC, HBM_SPEC, VMEM_SPEC] + [ANY_SPEC] * (start > 0),
        out_specs=[
            pl.BlockSpec((count * FRAME, DIM), lambda i: (start // count, 0)),
            pl.BlockSpec((32, DIM), lambda i: (0, 0)),
            SMEM_SPEC,
        ],
        out_shape=[
            jax.ShapeDtypeStruct((rows, DIM), f32),
            jax.ShapeDtypeStruct((32, DIM), f32),
            jax.ShapeDtypeStruct((1,), jnp.int32),
        ],
        input_output_aliases={4: 0} if start else {},
        scratch_shapes=[
            pltpu.VMEM(head.shape, f32),
            pltpu.VMEM((3, 32, LANES), f32),
            pltpu.VMEM((32, DIM), f32),
            pltpu.VMEM((count + 2, PAD_ROWS, DIM), f32),
            pltpu.VMEM((3, BODY, DIM), f32),
            pltpu.VMEM((BODY, DIM), f32),
            pltpu.SemaphoreType.DMA((2,)),
        ],
        compiler_params=params(20),
    )(*operands)


def normalize(values):
    centered = values - jnp.mean(values, axis=-1, keepdims=True)
    variance = jnp.mean(centered * centered, axis=-1, keepdims=True)
    inverse = lax.rsqrt(variance + EPSILON)
    return centered * inverse, inverse


def flag_base(head):
    return HEAD_DIM if head % 2 == 0 else 0


def own_lanes(lane, head):
    return lane < HEAD_DIM if head % 2 == 0 else lane >= HEAD_DIM


def row_size(value):
    return jnp.max(jnp.sum(value * value, axis=-1, keepdims=True), axis=0, keepdims=True)


def qkv_kernel(frames_ref, mixed, convp, wqkv, bqkv, normed_out, q_out, k_out, v_out, size):
    block = pl.program_id(0)
    rows = mixed.shape[0]
    frames = frames_ref[0]
    normal, unused_inverse = normalize(mixed[...])
    normed = (normal * convp[28:29, :] + convp[29:30, :]).astype(bf16)
    normed_out[...] = normed
    lane = lane_of((rows, LANES))
    inside = row_of((rows, LANES)) + block * rows < frames * FRAME
    scale = HEAD_DIM ** (-0.5) * LOG2E

    @pl.when(block == 0)
    def _():
        size[...] = jnp.zeros(size.shape, f32)

    projected = dot(normed, wqkv[...]) + bqkv[...]
    masks = []
    for base in (flag_base(0), flag_base(1)):
        flag = lane - base
        q_flags = jnp.where(((flag == 0) & ~inside) | ((flag == 1) & inside), BLOCKED, 0.0)
        k_flags = jnp.where(
            ((flag == 0) & inside) | ((flag == 1) & ~inside) | ((flag >= 2) & (flag < 5)), 1.0, 0.0
        )
        v_flags = jnp.where((flag >= 0) & (flag < 3), 1.0, 0.0)
        masks.append((q_flags, k_flags, v_flags))
    for head in range(HEADS):
        q_mask, k_mask, v_mask = masks[head % 2]
        own = own_lanes(lane, head)

        def columns(kind, head=head):
            start = (kind * PAIRS + head // 2) * LANES
            return projected[:, start : start + LANES]

        query = jnp.where(own, columns(0) * scale, q_mask).astype(bf16)
        key = jnp.where(own, columns(1), k_mask).astype(bf16)
        if head % 2 == 0:
            query_size = row_size(columns(0) * scale)
            key_size = row_size(columns(1))
        q_out[head] = query
        k_out[head] = key
        v_out[head] = jnp.where(own, columns(2), v_mask).astype(bf16)
        size[head : head + 1, :] = jnp.maximum(size[head : head + 1, :], query_size)
        size[head + 8 : head + 9, :] = jnp.maximum(size[head + 8 : head + 9, :], key_size)


def project(frames, mixed, convp, wqkv, bqkv, block=784):
    rows = mixed.shape[0]
    heads_spec = pl.BlockSpec((HEADS, block, LANES), lambda i: (0, i, 0))
    rows_spec = pl.BlockSpec((block, DIM), lambda i: (i, 0))
    heads_shape = jax.ShapeDtypeStruct((HEADS, rows, LANES), bf16)
    return pl.pallas_call(
        qkv_kernel,
        name="qkv_forward",
        grid=(rows // block,),
        in_specs=[
            SMEM_SPEC,
            rows_spec,
            pl.BlockSpec((32, DIM), lambda i: (0, 0)),
            pl.BlockSpec((DIM, QKV_COLUMNS), lambda i: (0, 0)),
            pl.BlockSpec((1, QKV_COLUMNS), lambda i: (0, 0)),
        ],
        out_specs=[rows_spec, heads_spec, heads_spec, heads_spec, pl.BlockSpec((16, LANES), lambda i: (0, 0))],
        out_shape=[
            pltpu.HBM((rows, DIM), bf16),
            heads_shape,
            heads_shape,
            heads_shape,
            jax.ShapeDtypeStruct((16, LANES), f32),
        ],
        compiler_params=params(14),
    )(frames, mixed, convp, wqkv, bqkv)


def attend_kernel(chunk, q, k, v, size, o_out, q_back, query, shift):
    head = pl.program_id(0)
    keys = k.shape[1]
    tall = q.shape[1]
    bound = jnp.max(size[pl.ds(head, 1), :] * size[pl.ds(head + 8, 1), :])
    query[...] = q[0]
    shift[...] = jnp.zeros(shift.shape, f32)

    @pl.when(bound > SAFE_BOUND * SAFE_BOUND)
    def _():
        shift[...] = jnp.full(shift.shape, -jnp.inf, f32)

        def peak(step, carry):
            scores = dot_nt(k[0, pl.ds(pl.multiple_of(step * 112, 16), 112), :], q[0])
            shift[...] = jnp.maximum(shift[...], jnp.max(scores, axis=0, keepdims=True))
            return carry

        lax.fori_loop(0, keys // 112, peak, 0)
        first, second, third = split3(-shift[...])
        flag = row_of((LANES, tall)) - jnp.where(lax.rem(head, 2) == 0, HEAD_DIM, 0)
        tail = jnp.where(flag == 2, first, jnp.where(flag == 3, second, jnp.where(flag == 4, third, 0.0)))
        query[...] = (q[0].astype(f32) + tail.T).astype(bf16)

    total = None
    for start in range(0, keys, chunk):
        place = slice(start, min(start + chunk, keys))
        weights = jnp.exp2(dot_nt(k[0, place, :], query[...])).astype(bf16)
        part = dot_tn(v[0, place, :], weights)
        total = part if total is None else total + part
    def finish(parity):
        base = flag_base(parity)
        sums = total[base : base + 1, :]
        first, second, third = split3(-(shift[...] + jnp.log2(sums)))
        row = row_of((8, tall))
        tail = jnp.where(row == 2, first, jnp.where(row == 3, second, jnp.where(row == 4, third, 0.0)))
        flags = [tail, jnp.zeros((56, tall), f32)]
        own = [total[HEAD_DIM - base : 2 * HEAD_DIM - base, :] / sums]
        stacked = jnp.concatenate(own + flags if parity == 0 else flags + own, axis=0).T
        lane = lane_of((tall, LANES))
        o_out[0] = jnp.where(own_lanes(lane, parity), stacked, 0.0).astype(bf16)
        place = (lane >= base + 2) & (lane < base + 5)
        q_back[0] = jnp.where(place, stacked, q[0].astype(f32)).astype(bf16)

    for parity in range(2):
        pl.when(lax.rem(head, 2) == parity)(functools.partial(finish, parity))


def attend(q, k, v, size, chunk=512):
    rows = q.shape[1]
    whole = pl.BlockSpec((1, rows, LANES), lambda h: (h, 0, 0))
    shape = jax.ShapeDtypeStruct((HEADS, rows, LANES), bf16)
    return pl.pallas_call(
        functools.partial(attend_kernel, chunk),
        name="attend",
        grid=(HEADS,),
        in_specs=[whole, whole, whole, pl.BlockSpec((16, LANES), lambda h: (0, 0))],
        out_specs=[whole, whole],
        out_shape=[shape, pltpu.HBM(shape.shape, bf16)],
        scratch_shapes=[pltpu.VMEM((rows, LANES), bf16), pltpu.VMEM((1, rows), f32)],
        compiler_params=params(18),
    )(q, k, v, size)


def attend_back_kernel(q, do, k, v, dq_out, dk_out, dv_out):
    weights = jnp.exp2(dot_nt(q[0], k[0]))
    grad_scores = (weights * dot_nt(do[0], v[0])).astype(bf16)
    dv_out[0] = dot_tn(do[0], weights.astype(bf16)).T.astype(bf16)
    dk_out[0] = (dot_tn(q[0], grad_scores) * LN2).T.astype(bf16)
    dq_out[0] = (dot_nt(k[0].T, grad_scores) * HEAD_DIM ** (-0.5)).T.astype(bf16)


def attend_back(q, do, k, v):
    heads, rows = q.shape[:2]
    whole = pl.BlockSpec((1, rows, LANES), lambda h: (h, 0, 0))
    shape = jax.ShapeDtypeStruct((heads, rows, LANES), bf16)
    return pl.pallas_call(
        attend_back_kernel,
        name="attend_back",
        grid=(heads,),
        in_specs=[whole] * 4,
        out_specs=[whole] * 3,
        out_shape=[shape] * 3,
        compiler_params=params(40),
    )(q, do, k, v)


def erf_parts(value):
    bell = jnp.exp(-0.5 * value * value)
    return bell, 0.5 * (1.0 + lax.erf(value * (1.0 / math.sqrt(2.0))))


def paired(heads):
    tiles = []
    for head in range(0, HEADS, 2):
        high = heads[head + 1] if head + 1 < HEADS else jnp.zeros_like(heads[head])
        tiles.append(jnp.where(lane_of(high.shape) < HEAD_DIM, heads[head], high))
    return jnp.concatenate(tiles, axis=1)


def add_tiles(ref, place, value):
    for tile, (low, high) in enumerate(TILES):
        ref[tile, place, : high - low] += value[:, low:high]


def middle_kernel(
    frames_ref, o, mixed, cot, wproj, fc1, fc2, vecs, fc1b,
    output, gmid_out, do_out, gproj, gfc1, gfc2, gvec, gfc1b, chunk,
):
    block = pl.program_id(0)
    rows = mixed.shape[0]
    inside = row_of((rows, DIM)) + block * rows < frames_ref[0] * FRAME

    @pl.when(block == 0)
    def _():
        for ref in (gproj, gfc1, gfc2, gvec, gfc1b):
            ref[...] = jnp.zeros(ref.shape, f32)

    attended = paired(o)
    middle = mixed[...] + (dot(attended, wproj[...]) + vecs[0:1, :])
    normal, inverse = normalize(middle)
    normed = (normal * vecs[1:2, :] + vecs[2:3, :]).astype(bf16)
    grad_output = jnp.where(inside, cot[...].astype(f32), 0.0)
    grad_outer = grad_output.astype(bf16)
    total = middle + vecs[3:4, :]
    grad_normed = jnp.zeros((rows, DIM), f32)
    for start in range(0, FFN, chunk):
        place = slice(start, start + chunk)
        inner = dot(normed, fc1[:, place]) + fc1b[:, place]
        bell, gate = erf_parts(inner)
        activated = (inner * gate).astype(bf16)
        total += dot(activated, fc2[place, :])
        slope = gate + inner * bell * INVERSE_ROOT_TWO_PI
        grad_inner = (dot_nt(grad_outer, fc2[place, :]) * slope)
        gfc1b[:, place] += jnp.sum(grad_inner, axis=0, keepdims=True)
        grad_inner = grad_inner.astype(bf16)
        add_tiles(gfc2, place, dot_tn(activated, grad_outer))
        gfc1[:, place] += dot_tn(normed, grad_inner)
        grad_normed += dot_nt(grad_inner, fc1[:, place])
    output[...] = total.astype(bf16)
    scaled = grad_normed * vecs[1:2, :]
    grad_middle = grad_output + inverse * (
        scaled
        - jnp.mean(scaled, axis=-1, keepdims=True)
        - normal * jnp.mean(scaled * normal, axis=-1, keepdims=True)
    )
    gmid_out[...] = grad_middle
    grad_branch = grad_middle.astype(bf16)
    add_tiles(gproj, slice(None), dot_tn(attended, grad_branch))
    gvec[0:1, :] += jnp.sum(grad_branch.astype(f32), axis=0, keepdims=True)
    gvec[1:2, :] += jnp.sum(grad_normed * normal, axis=0, keepdims=True)
    gvec[2:3, :] += jnp.sum(grad_normed, axis=0, keepdims=True)
    gvec[3:4, :] += jnp.sum(grad_output, axis=0, keepdims=True)
    lane = lane_of((rows, LANES))
    grad_attended = dot_nt(grad_branch, wproj[...])
    for head in range(HEADS):
        grad_head = grad_attended[:, head // 2 * LANES : (head // 2 + 1) * LANES]
        flag = lane - flag_base(head)
        delta = jnp.sum(grad_head * o[head].astype(f32), axis=-1, keepdims=True)
        first, second, third = split3(-delta)
        tail = jnp.where(flag == 0, first, jnp.where(flag == 1, second, third))
        do_out[head] = jnp.where((flag >= 0) & (flag < 3), tail, grad_head).astype(bf16)


def feed_forward(frames, o, mixed, cot, wproj, fc1, fc2, vecs, fc1b, block=784, chunk=256):
    rows = mixed.shape[0]
    heads_spec = pl.BlockSpec((HEADS, block, LANES), lambda i: (0, i, 0))
    rows_spec = pl.BlockSpec((block, DIM), lambda i: (i, 0))

    def full(*shape):
        return pl.BlockSpec(shape, lambda i: (0,) * len(shape))

    return pl.pallas_call(
        functools.partial(middle_kernel, chunk=chunk),
        name="feed_forward",
        grid=(rows // block,),
        in_specs=[
            SMEM_SPEC, heads_spec, rows_spec, rows_spec,
            full(PAIR_COLUMNS, DIM), full(DIM, FFN), full(FFN, DIM), full(8, DIM), full(1, FFN),
        ],
        out_specs=[
            rows_spec, rows_spec, heads_spec,
            full(3, PAIR_COLUMNS, LANES), full(DIM, FFN), full(3, FFN, LANES), full(8, DIM), full(1, FFN),
        ],
        out_shape=[
            pltpu.HBM((rows, DIM), bf16),
            pltpu.HBM((rows, DIM), f32),
            pltpu.HBM((HEADS, rows, LANES), bf16),
            jax.ShapeDtypeStruct((3, PAIR_COLUMNS, LANES), f32),
            jax.ShapeDtypeStruct((DIM, FFN), f32),
            jax.ShapeDtypeStruct((3, FFN, LANES), f32),
            jax.ShapeDtypeStruct((8, DIM), f32),
            jax.ShapeDtypeStruct((1, FFN), f32),
        ],
        compiler_params=params(22),
    )(frames, o, mixed, cot, wproj, fc1, fc2, vecs, fc1b)


def qkv_back_kernel(dq, dk, dv, normed, mixed, gmid, wqkv, convp, spread, padded, gqkv, gbias, gvec, gmix):
    block = pl.program_id(0)

    @pl.when(block == 0)
    def _():
        for ref in (gqkv, gbias, gvec):
            ref[...] = jnp.zeros(ref.shape, f32)

    normal, inverse = normalize(mixed[...])
    grads = jnp.concatenate([paired(part) for part in (dq, dk, dv)], axis=1)
    grad_qkv = dot_tn(normed[...], grads)
    for tile in range(3 * PAIRS):
        gqkv[tile] += grad_qkv[:, tile * LANES : (tile + 1) * LANES]
    gbias[...] += jnp.sum(grads.astype(f32), axis=0, keepdims=True)
    grad_normed = dot_nt(grads, wqkv[...])
    gvec[1:2, :] += jnp.sum(grad_normed * normal, axis=0, keepdims=True)
    gvec[2:3, :] += jnp.sum(grad_normed, axis=0, keepdims=True)
    scaled = grad_normed * convp[28:29, :]
    grad_mixed = gmid[...] + inverse * (
        scaled
        - jnp.mean(scaled, axis=-1, keepdims=True)
        - normal * jnp.mean(scaled * normal, axis=-1, keepdims=True)
    )
    gvec[0:1, :] += jnp.sum(grad_mixed, axis=0, keepdims=True)
    gmix[...] = grad_mixed
    for member in range(mixed.shape[0] // FRAME):
        high, low = pieces(gmix[192 * member : 192 * member + 208, :])
        padded[member] = dot(spread[member], high) + dot(spread[member], low)


def project_back(dq, dk, dv, normed, mixed, gmid, wqkv, convp, spread, block=PIECE):
    rows = mixed.shape[0]
    heads_spec = pl.BlockSpec((HEADS, block, LANES), lambda i: (0, i, 0))
    rows_spec = pl.BlockSpec((block, DIM), lambda i: (i, 0))

    def full(*shape):
        return pl.BlockSpec(shape, lambda i: (0,) * len(shape))

    return pl.pallas_call(
        qkv_back_kernel,
        name="qkv_back",
        grid=(rows // block,),
        in_specs=[heads_spec, heads_spec, heads_spec, rows_spec, rows_spec, rows_spec,
                  full(DIM, QKV_COLUMNS), full(32, DIM), full(4, PAD_ROWS, 208)],
        out_specs=[pl.BlockSpec((4, PAD_ROWS, DIM), lambda i: (i, 0, 0)), full(3 * PAIRS, DIM, LANES), full(1, QKV_COLUMNS), full(8, DIM)],
        out_shape=[
            pltpu.HBM((rows // FRAME, PAD_ROWS, DIM), f32),
            jax.ShapeDtypeStruct((3 * PAIRS, DIM, LANES), f32),
            jax.ShapeDtypeStruct((1, QKV_COLUMNS), f32),
            jax.ShapeDtypeStruct((8, DIM), f32),
        ],
        scratch_shapes=[pltpu.VMEM((block, DIM), f32)],
        compiler_params=params(18),
    )(dq, dk, dv, normed, mixed, gmid, wqkv, convp, spread)


FRAME_GROUPS = ((0, 2), (2, 5), (5, 12))


def conv_weight_kernel(frames_ref, xsource, gsource, gvec, out, xpad, gpad, moved, sums, tiles, flat, xsem, gsem):
    frames = frames_ref[0]
    count = xpad.shape[0]
    copies = []
    for group, (low, high) in enumerate(FRAME_GROUPS):
        place = pl.ds(low, high - low)
        copies.append(pltpu.make_async_copy(xsource.at[place], xpad.at[place], xsem.at[group]))
        copies.append(pltpu.make_async_copy(gsource.at[place], gpad.at[place], gsem.at[group]))
    for copy in copies:
        copy.start()
    sums[...] = jnp.zeros(sums.shape, f32)

    def weight_frame(frame, carry):
        for low, high in TILES:
            body = gpad[frame, 16 : 16 + BODY, low:high]
            moved[0, :, low:high] = pltpu.roll(body, BODY - 1, axis=0)
            moved[1, :, low:high] = pltpu.roll(body, 1, axis=0)
        for a in (-1, 0, 1):
            at = frame + a

            @pl.when((at >= 0) & (at < frames))
            def _():
                for low, high in TILES:
                    for b in (-1, 0, 1):
                        cells = xpad[at, 16 + b * 16 : 16 + b * 16 + BODY, low:high]
                        for c in range(3):
                            body = (
                                gpad[frame, 16 : 16 + BODY, low:high]
                                if c == 1
                                else moved[c // 2, :, low:high]
                            )
                            product = (body * cells).reshape(BODY // 8, 8, high - low)
                            tap = 9 * (a + 1) + 3 * (b + 1) + c
                            sums[tap, :, low:high] += jnp.sum(product, axis=0)

        return carry

    for group, (low, high) in enumerate(FRAME_GROUPS):
        copies[2 * group].wait()
        copies[2 * group + 1].wait()
        start = max(low - 1, 0)
        stop = high - 1 if high < count else count
        lax.fori_loop(jnp.minimum(start, frames), jnp.minimum(stop, frames), weight_frame, 0)
    tiles[...] = jnp.zeros(tiles.shape, f32)
    flat[...] = jnp.zeros(flat.shape, f32)
    for tile, (low, high) in enumerate(TILES):
        tiles[tile, 0:27, : high - low] = jnp.sum(sums[:, :, low:high], axis=1)
        tiles[tile, 27:30, : high - low] = gvec[0:3, low:high]
    for parity in range(2):
        for j in range(5):
            value = tiles[j // 2, pl.ds(parity, 15, stride=2), :]
            put_half(flat, AT_CONV + parity * 5 + j, value, j % 2, 5, 15)
    out[...] = flat[...].astype(bf16)


def conv_weight_grads(frames, xpad, gpad, gvec):
    return pl.pallas_call(
        conv_weight_kernel,
        name="conv_weight_grads",
        in_specs=[SMEM_SPEC, HBM_SPEC, HBM_SPEC, VMEM_SPEC],
        out_shape=jax.ShapeDtypeStruct((80, LANES), bf16),
        scratch_shapes=[
            pltpu.VMEM(xpad.shape, f32),
            pltpu.VMEM(gpad.shape, f32),
            pltpu.VMEM((2, BODY, DIM), f32),
            pltpu.VMEM((27, 8, DIM), f32),
            pltpu.VMEM((3, 32, LANES), f32),
            pltpu.VMEM((80, LANES), f32),
            pltpu.SemaphoreType.DMA((len(FRAME_GROUPS),)),
            pltpu.SemaphoreType.DMA((len(FRAME_GROUPS),)),
        ],
        compiler_params=params(18),
    )(frames, in_hbm(xpad), in_hbm(gpad), gvec)


def token_piece_kernel(piece, frames_ref, convp, gsource, back, *refs):
    if piece > 0:
        refs = refs[1:]
    gtok, passed, masked, slots, sums, comp, rows, sem = refs
    frames = frames_ref[0]
    passed[0] = frames
    copies = fetch_frames(gsource, slots, sem, 4 * piece, 4)
    for copy in copies:
        copy.start()
    rows[...] = jnp.zeros(rows.shape, f32)
    copies[0].wait()

    def each(member, carry):
        @pl.when(member == 1)
        def _():
            copies[1].wait()

        frame = 4 * piece + member
        there = frame < frames
        before = there & (frame > 0)
        after = frame + 1 < frames
        mask_weights(convp, masked, after, there, before)
        at = (member + jnp.where(before, 0, 1), member + 1, member + jnp.where(after, 2, 1))
        mix_frame(slots, at, masked, sums, comp, -1)
        place = pl.ds(pl.multiple_of(192 * member, 16), 208)
        rows[place, :] += dot(back[member], comp[...].astype(bf16))
        return carry

    lax.fori_loop(0, 4, each, 0)
    gtok[...] = rows[...].astype(bf16)


def token_piece(piece, frames, convp, gpad, back, gtok):
    count = gpad.shape[0]
    operands = [frames, convp, in_hbm(gpad), back] + ([] if piece == 0 else [gtok])
    return pl.pallas_call(
        functools.partial(token_piece_kernel, piece),
        name=f"token_piece{piece}",
        grid=(1,),
        in_specs=[SMEM_SPEC, VMEM_SPEC, HBM_SPEC, VMEM_SPEC] + [ANY_SPEC] * (piece > 0),
        out_specs=[pl.BlockSpec((PIECE, DIM), lambda i: (piece, 0)), SMEM_SPEC],
        out_shape=[
            jax.ShapeDtypeStruct((count * FRAME, DIM), bf16),
            jax.ShapeDtypeStruct((1,), jnp.int32),
        ],
        input_output_aliases={4: 0} if piece else {},
        scratch_shapes=[
            pltpu.VMEM((32, DIM), f32),
            pltpu.VMEM((6, PAD_ROWS, DIM), f32),
            pltpu.VMEM((3, BODY, DIM), f32),
            pltpu.VMEM((BODY, DIM), f32),
            pltpu.VMEM((PIECE, DIM), f32),
            pltpu.SemaphoreType.DMA((2,)),
        ],
        compiler_params=params(10),
    )(*operands)


def put_half(flat, index, value, side, step=1, count=1):
    row, wanted = divmod(index, 2)
    place = pl.ds(row, count, stride=step) if step > 1 else pl.ds(row, count)
    lane = lane_of(value.shape)
    if wanted == 0:
        flat[place, :] += jnp.where(lane < 64, low_half(value, side), 0.0)
    else:
        flat[place, :] += jnp.where(lane >= 64, high_half(value, side), 0.0)


def put_vector(flat, index, value):
    width = value.shape[1]
    for j in range(width // 64):
        low = (j // 2) * LANES
        part = value[:, low : min(low + LANES, width)]
        if part.shape[1] < LANES:
            part = jnp.concatenate([part, jnp.zeros((1, 64), f32)], axis=1)
        put_half(flat, index + j, part, j % 2)


PACK_BASE = 2432


def pack_main_kernel(gproj, gfc1, gfc2, gvec, gfc1b, out, flat):
    flat[...] = jnp.zeros(flat.shape, f32)
    for parity in range(2):
        for j in range(5):
            value = gproj[j // 2, pl.ds(parity, DIM // 2, stride=2), :]
            put_half(flat, AT_PROJ + parity * 5 + j, value, j % 2, 5, DIM // 2)
            value = gfc2[j // 2, pl.ds(parity, FFN // 2, stride=2), :]
            put_half(flat, AT_FC2 + parity * 5 + j, value, j % 2, 5, FFN // 2)
    for j in range(20):
        value = gfc1[:, (j // 2) * LANES : (j // 2 + 1) * LANES]
        put_half(flat, AT_FC1 + j, value, j % 2, 10, DIM)
    for row in range(3):
        put_vector(flat, AT_VEC + 5 * row, gvec[row : row + 1, :])
    put_vector(flat, AT_FC2B, gvec[3:4, :])
    put_vector(flat, AT_FC1B, gfc1b[...])
    out[...] = flat[...].astype(bf16)


def pack_main(gproj, gfc1, gfc2, gvec, gfc1b, rows):
    return pl.pallas_call(
        pack_main_kernel,
        name="pack_main",
        out_shape=jax.ShapeDtypeStruct((rows, LANES), bf16),
        scratch_shapes=[pltpu.VMEM((rows, LANES), f32)],
        compiler_params=params(14),
    )(gproj, gfc1, gfc2, gvec, gfc1b)


QKV_ROWS = 2480


def pack_qkv_kernel(gqkv, gbias, out, end, flat):
    flat[...] = jnp.zeros(flat.shape, f32)
    for parity in range(2):
        for j in range(15):
            kind, head = divmod(j, HEADS)
            value = gqkv[kind * PAIRS + head // 2, pl.ds(parity, DIM // 2, stride=2), :]
            put_half(flat, AT_QKV + parity * 15 + j, value, head % 2, 15, DIM // 2)
    for j in range(10):
        start = (0 if j < HEADS else 2 * PAIR_COLUMNS) + j % HEADS // 2 * LANES
        put_half(flat, AT_QV + j, gbias[:, start : start + LANES], j % HEADS % 2)
    out[...] = flat[:PACK_BASE, :].astype(bf16)
    end[...] = flat[PACK_BASE:, :].astype(bf16)


def pack_qkv(gqkv, gbias):
    return pl.pallas_call(
        pack_qkv_kernel,
        name="pack_qkv",
        out_shape=[
            jax.ShapeDtypeStruct((PACK_BASE, LANES), bf16),
            jax.ShapeDtypeStruct((QKV_ROWS - PACK_BASE, LANES), bf16),
        ],
        scratch_shapes=[pltpu.VMEM((QKV_ROWS, LANES), f32)],
        compiler_params=params(10),
    )(gqkv, gbias)


AXES = ("wide", "narrow")


def exchange(value, bit):
    count = lax.axis_size(AXES)
    return lax.ppermute(value, AXES, [(i, i ^ (1 << bit)) for i in range(count)])


def my_bit(bit):
    return (lax.axis_index(AXES) >> bit) & 1


def tie(*values):
    return lax.optimization_barrier(values)


def split(value, bit):
    value = value.reshape(value.shape[0] // 2, 2, -1, LANES)
    mine = my_bit(bit)
    keep = lax.dynamic_index_in_dim(value, mine, 1, keepdims=False)
    return keep, lax.dynamic_index_in_dim(value, 1 - mine, 1, keepdims=False)


def on_device(master, momentum, average, tokens, clip_ids, borders, cotangent):
    wide_count, narrow_count = lax.axis_size("wide"), lax.axis_size("narrow")
    count = wide_count * narrow_count
    bits = count.bit_length() - 1
    own_rows = master.shape[0]
    filled = jnp.sum((clip_ids >= 0).astype(jnp.int32))
    frames = jnp.where(filled > 6 * FRAME, 12, jnp.where(filled > 3 * FRAME, 6, 3)).reshape(1)
    me = lax.axis_index(AXES)
    quarter = me >> (bits - 2)
    blocks = master.astype(bf16)[None]
    other = exchange(blocks, bits - 2)
    other, frames = tie(other, frames)
    blocks = jnp.concatenate([blocks, other], axis=0)
    blocks, frames = tie(blocks, frames)
    other = exchange(blocks, bits - 1)
    xpad, spread, back, frames = prepare(frames, tokens.T)
    other, frames = tie(other, frames)
    blocks = jnp.concatenate([blocks, other], axis=0)
    first = lax.dynamic_index_in_dim(blocks, quarter, 0)
    rest = [lax.dynamic_index_in_dim(blocks, quarter ^ index, 0) for index in (1, 2, 3)]
    rest = jnp.concatenate(rest, axis=0)[None]
    low_bits = list(range(bits - 3, -1, -1))
    for step, bit in enumerate(low_bits):
        if step == 0:
            first, frames = tie(first, frames)
        other = exchange(first, bit)
        if step == 0:
            cotangent, frames = turn(frames, cotangent.T)
            other, frames = tie(other, frames)
        first = jnp.concatenate([first, other], axis=0)
        if step == 0:
            first, rest, frames = tie(first, rest, frames)
            rest = jnp.concatenate([rest, exchange(rest, bit)], axis=0)
    order = [0] * (count // 4)
    for step, bit in enumerate(low_bits):
        order = [place | (((index >> bit) & 1) << step) for index, place in enumerate(order)]
    mine = sum((((me >> bit) & 1) << step) for step, bit in enumerate(low_bits))
    order = jnp.array(order, jnp.int32) ^ mine
    head = lax.dynamic_index_in_dim(first, mine, 0, keepdims=False)
    head = jnp.concatenate([head, jnp.zeros((4, LANES), bf16)], axis=0)[:80] if own_rows < 80 else head[:80]
    mixed, convp = None, None
    for step, bit in enumerate(low_bits[1:]):
        if step < 2:
            rest, frames = tie(rest, frames)
        other = exchange(rest, bit)
        if step == 0:
            mixed, convp, frames = conv_piece(0, 8, frames, head, xpad, back, None)
        elif step == 1:
            mixed, convp, frames = conv_piece(8, 4, frames, head, xpad, back, mixed)
        other, frames = tie(other, frames)
        rest = jnp.concatenate([rest, other], axis=0)
    wqkv, wproj, fc1, fc2, bqkv, vecs, fc1b = unpack(order, first, rest)
    normed, q, k, v, size = project(frames, mixed, convp, wqkv, bqkv)
    o, q_back = attend(q, k, v, size)
    output, gmid, do, gproj, gfc1, gfc2, gvec, gfc1b = feed_forward(
        frames, o, mixed, cotangent, wproj, fc1, fc2, vecs, fc1b
    )
    main = pack_main(gproj, gfc1, gfc2, gvec, gfc1b, count * own_rows)
    main = main.reshape(wide_count, narrow_count, own_rows, LANES)
    main = lax.psum_scatter(main, "wide", scatter_dimension=0, tiled=True)[0]
    q_back, do, k, v = (in_hbm(value) for value in (q_back, do, k, v))
    dq, dk, dv = attend_back(q_back, do, k, v)
    gpad, gqkv, gbias, gvec_one = project_back(dq, dk, dv, normed, mixed, gmid, wqkv, convp, spread)
    qkv, qkv_end = pack_qkv(gqkv, gbias)
    qkv = qkv.reshape(count // 4, own_rows, LANES)
    narrow_bits = narrow_count.bit_length() - 1
    keep, give = split(qkv, 0)
    gvec_one, give = tie(gvec_one, give)
    arriving = exchange(give, 0)
    conv = conv_weight_grads(frames, xpad, gpad, gvec_one)
    late = jnp.concatenate([conv, qkv_end], axis=0)
    main, late = tie(main, late)
    for bit in range(1, narrow_bits):
        keep, give = split(keep + arriving, bit)
        arriving = exchange(give, bit)
    gtok = None
    for bit in range(bits):
        if bit < narrow_bits:
            stays, give = split(main, bit)
        elif bit < bits - 2:
            stays, give = split(qkv, bit)
        else:
            stays, give = qkv, qkv
        sent = give.shape[0] * own_rows
        packet = jnp.concatenate([give.reshape(sent, LANES), late], axis=0)
        packet, frames = tie(packet, frames)
        other = exchange(packet, bit)
        if bit == 0:
            output, frames = turn(frames, output)
        elif bit < 4:
            gtok, frames = token_piece(bit - 1, frames, convp, gpad, back, gtok)
        elif bit == 4:
            gtok, frames = turn(frames, gtok)
        other, frames = tie(other, frames)
        if bit == narrow_bits - 1:
            other, arriving = tie(other, arriving)
            qkv = keep + arriving
        summed = stays + other[:sent].reshape(stays.shape)
        late = late + other[sent:]
        if bit < narrow_bits:
            main = summed
        else:
            qkv = summed
    main, qkv = main[0], qkv[0]
    early = jnp.where(me < count // 4, qkv.astype(f32), main.astype(f32))
    conv, qkv_end = late[:80].astype(f32), late[80:].astype(f32)
    if own_rows < 80:
        conv = conv[:own_rows]
    conv = jnp.pad(conv, ((0, own_rows - conv.shape[0]), (0, 0)))
    qkv_end = jnp.pad(qkv_end, ((0, own_rows - qkv_end.shape[0]), (0, 0)))
    owned = early + jnp.where(me == 0, conv, jnp.where(me == count // 4, qkv_end, 0.0))
    rate = RATE_FACTOR / math.sqrt(tokens.shape[0] * count)
    decayed = owned + DECAY_RATE * master
    new_momentum = MOMENTUM * momentum + decayed
    new_master = master - rate * (decayed + MOMENTUM * new_momentum)
    new_average = AVERAGE_KEEP * average + (1.0 - AVERAGE_KEEP) * new_master
    return (output.T, gtok.T, owned, new_master, new_momentum, new_average, new_master.astype(bf16))


def solution(mesh):
    rows = P(("wide", "narrow"), None)
    return jax.shard_map(
        on_device,
        mesh=mesh,
        in_specs=(rows, rows, rows, rows, P(("wide", "narrow")), P(("wide", "narrow")), rows),
        out_specs=(rows,) * 7,
        check_vma=False,
    )
```

```python
import functools
import math

import jax
import jax.numpy as jnp
from jax import lax
from jax.experimental import pallas as pl
from jax.experimental.pallas import tpu as pltpu
from jax.sharding import PartitionSpec as P

HEADS = 5
HEAD_DIM = 64
DIM = 320
FFN = 1280
SIDE = 14
FRAME = SIDE * SIDE
LANES = 128
PAIRS = (HEADS + 1) // 2
PAIR_COLUMNS = PAIRS * LANES
QKV_COLUMNS = 3 * PAIR_COLUMNS

EPSILON = 1e-06
MOMENTUM = 0.9
DECAY_RATE = 0.0001
AVERAGE_KEEP = 0.8
RATE_FACTOR = 0.03
LOG2E = 1.0 / math.log(2.0)
LN2 = math.log(2.0)
INVERSE_ROOT_TWO_PI = 1.0 / math.sqrt(2.0 * math.pi)
BLOCKED = -(2.0**30)
SAFE_BOUND = 80.0

TILES = ((0, 128), (128, 256), (256, 320))

bf16 = jnp.bfloat16
f32 = jnp.float32

AT_CONV = 0
AT_QKV = 150
AT_QV = 4950
AT_PROJ = 4960
AT_VEC = 6560
AT_FC1 = 6575
AT_FC1B = 12975
AT_FC2 = 12995
AT_FC2B = 19395
HALF_END = 19400


SMEM_SPEC = pl.BlockSpec(memory_space=pltpu.SMEM)
VMEM_SPEC = pl.BlockSpec(memory_space=pltpu.VMEM)
ANY_SPEC = pl.BlockSpec(memory_space=pl.ANY)
HBM_SPEC = pl.BlockSpec(memory_space=pltpu.HBM)


def in_hbm(value):
    return pltpu.with_memory_space_constraint(value, pltpu.HBM)


def dot(a, b):
    return lax.dot_general(a, b, (((1,), (0,)), ((), ())), preferred_element_type=f32)


def dot_nt(a, b):
    return lax.dot_general(a, b, (((1,), (1,)), ((), ())), preferred_element_type=f32)


def dot_tn(a, b):
    return lax.dot_general(a, b, (((0,), (0,)), ((), ())), preferred_element_type=f32)


def params(limit=58):
    return pltpu.CompilerParams(vmem_limit_bytes=limit << 20)


def lane_of(shape):
    return lax.broadcasted_iota(jnp.int32, shape, len(shape) - 1)


def row_of(shape):
    return lax.broadcasted_iota(jnp.int32, shape, 0)


def low_half(value, side):
    return value if side == 0 else pltpu.roll(value, 64, axis=1)


def high_half(value, side):
    return value if side == 1 else pltpu.roll(value, 64, axis=1)


def split3(value):
    first = value.astype(bf16).astype(f32)
    rest = value - first
    second = rest.astype(bf16).astype(f32)
    return first, second, rest - second


def read_half(flat, at, length, step, count, parity, j):
    index = at + parity * length + j
    return flat[pl.ds(index // 2, count, stride=step), :], index % 2


def read_vector(flat, at, length):
    tiles = []
    lane = lane_of((1, LANES))
    for j in range(0, length, 2):
        row, side = divmod(at + j, 2)
        low = low_half(flat[row : row + 1, :], side)
        if j + 1 < length:
            row, side = divmod(at + j + 1, 2)
            tiles.append(jnp.where(lane < 64, low, high_half(flat[row : row + 1, :], side)))
        else:
            tiles.append(low[:, :64])
    return jnp.concatenate(tiles, axis=1)


def odd_matrix(flat, out, at, length, rows):
    pairs = rows // 2
    for parity in range(2):
        for tile in range((length + 1) // 2):
            low, side = read_half(flat, at, length, length, pairs, parity, 2 * tile)
            low = low_half(low, side)
            place = pl.ds(parity, pairs, stride=2)
            if 2 * tile + 1 < length:
                high, side = read_half(flat, at, length, length, pairs, parity, 2 * tile + 1)
                merged = jnp.where(lane_of(low.shape) < 64, low, high_half(high, side))
            else:
                merged = low
            out[tile, place, :] = merged


def unpack_kernel(order, first, rest, wqkv, wproj, fc1, fc2, bqkv, vecs, fc1b, flat, wide, tall):
    blocks, rows = first.shape[:2]
    for block in range(blocks):
        place = order[block]
        for quarter in range(4):
            start = (quarter * blocks + block) * rows
            value = first[place] if quarter == 0 else rest[place, quarter - 1]
            flat[start : start + rows, :] = value.astype(f32)
    for parity in range(2):
        place = pl.ds(parity, DIM // 2, stride=2)
        for kind in range(3):
            for pair in range(PAIRS):
                j = kind * HEADS + 2 * pair
                low, side = read_half(flat, AT_QKV, 15, 15, DIM // 2, parity, j)
                low = low_half(low, side)
                high = jnp.zeros_like(low)
                if 2 * pair + 1 < HEADS:
                    high, side = read_half(flat, AT_QKV, 15, 15, DIM // 2, parity, j + 1)
                    high = high_half(high, side)
                wide[kind * PAIRS + pair, place, :] = jnp.where(lane_of(low.shape) < 64, low, high)
    for tile in range(3 * PAIRS):
        wqkv[:, tile * LANES : (tile + 1) * LANES] = wide[tile].astype(bf16)
    bqkv[...] = jnp.zeros(bqkv.shape, f32)
    for index, kind in enumerate((0, 2)):
        start = kind * PAIR_COLUMNS
        bqkv[:, start : start + DIM] = read_vector(flat, AT_QV + index * HEADS, HEADS)
    odd_matrix(flat, wide, AT_PROJ, 5, DIM)
    for tile, (low, high) in enumerate(TILES):
        wproj[:DIM, low:high] = wide[tile, :, : high - low].astype(bf16)
    wproj[DIM:, :] = jnp.zeros((PAIR_COLUMNS - DIM, DIM), bf16)
    for row in range(3):
        vecs[row : row + 1, :] = read_vector(flat, AT_VEC + 5 * row, 5)
    vecs[3:4, :] = read_vector(flat, AT_FC2B, 5)
    vecs[4:8, :] = jnp.zeros((4, DIM), f32)
    fc1b[...] = read_vector(flat, AT_FC1B, 20)
    for tile in range(10):
        low, side = read_half(flat, AT_FC1, 20, 10, DIM, 0, 2 * tile)
        high, side_high = read_half(flat, AT_FC1, 20, 10, DIM, 0, 2 * tile + 1)
        merged = jnp.where(lane_of(low.shape) < 64, low_half(low, side), high_half(high, side_high))
        fc1[:, tile * LANES : (tile + 1) * LANES] = merged.astype(bf16)
    odd_matrix(flat, tall, AT_FC2, 5, FFN)
    for tile in range(3):
        width = LANES if tile < 2 else 64
        fc2[:, tile * LANES : tile * LANES + width] = tall[tile, :, :width].astype(bf16)


def unpack(order, first, rest):
    rows = 4 * first.shape[0] * first.shape[1]
    return pl.pallas_call(
        unpack_kernel,
        name="unpack",
        in_specs=[SMEM_SPEC, VMEM_SPEC, VMEM_SPEC],
        out_shape=[
            jax.ShapeDtypeStruct((DIM, QKV_COLUMNS), bf16),
            jax.ShapeDtypeStruct((PAIR_COLUMNS, DIM), bf16),
            jax.ShapeDtypeStruct((DIM, FFN), bf16),
            jax.ShapeDtypeStruct((FFN, DIM), bf16),
            jax.ShapeDtypeStruct((1, QKV_COLUMNS), f32),
            jax.ShapeDtypeStruct((8, DIM), f32),
            jax.ShapeDtypeStruct((1, FFN), f32),
        ],
        scratch_shapes=[
            pltpu.VMEM((rows, LANES), f32),
            pltpu.VMEM((15, DIM, LANES), f32),
            pltpu.VMEM((3, FFN, LANES), f32),
        ],
        compiler_params=params(18),
    )(order, first, rest)


PAD_ROWS = 16 * 16
BODY = SIDE * 16


def spread_matrix(shift):
    cell = lax.broadcasted_iota(jnp.int32, (PAD_ROWS, 208), 0)
    source = lax.broadcasted_iota(jnp.int32, (PAD_ROWS, 208), 1)
    row, column = cell >> 4, cell & 15
    inside = (row >= 1) & (row <= SIDE) & (column < SIDE)
    wanted = (row - 1) * SIDE + column + shift
    return jnp.where(inside & (source == wanted), 1.0, 0.0).astype(bf16)


def gather_matrix(shift):
    target = lax.broadcasted_iota(jnp.int32, (208, BODY), 0)
    cell = lax.broadcasted_iota(jnp.int32, (208, BODY), 1)
    row, column = cell >> 4, cell & 15
    wanted = row * SIDE + column + shift
    return jnp.where((column < SIDE) & (target == wanted), 1.0, 0.0).astype(bf16)


def pieces(value):
    first = value.astype(bf16)
    return first, (value - first.astype(f32)).astype(bf16)


def prepare_kernel(frames, turned, target, spread, back, passed, tokens, padded, sems):
    for member in range(4):
        spread[member] = spread_matrix(4 * member)
        back[member] = gather_matrix(4 * member)
    passed[0] = frames[0]
    tokens[...] = turned[...].T

    def fill(frame, carry):
        member = frame & 3
        place = pl.ds(pl.multiple_of(frame * FRAME - 4 * member, 16), 208)
        padded[frame] = dot(spread[member], tokens[place, :])
        return carry

    copies = []
    for group in range(padded.shape[0] // 4):
        lax.fori_loop(4 * group, 4 * group + 4, fill, 0)
        place = pl.ds(4 * group, 4)
        copies.append(pltpu.make_async_copy(padded.at[place], target.at[place], sems.at[group]))
        copies[-1].start()
    for copy in copies:
        copy.wait()


def prepare(frames, turned):
    rows = turned.shape[1]
    return pl.pallas_call(
        prepare_kernel,
        name="prepare",
        in_specs=[SMEM_SPEC, VMEM_SPEC],
        out_specs=[HBM_SPEC, VMEM_SPEC, VMEM_SPEC, SMEM_SPEC],
        out_shape=[
            pltpu.HBM((rows // FRAME, PAD_ROWS, DIM), f32),
            jax.ShapeDtypeStruct((4, PAD_ROWS, 208), bf16),
            jax.ShapeDtypeStruct((4, 208, BODY), bf16),
            jax.ShapeDtypeStruct((1,), jnp.int32),
        ],
        scratch_shapes=[
            pltpu.VMEM((rows, DIM), bf16),
            pltpu.VMEM((rows // FRAME, PAD_ROWS, DIM), f32),
            pltpu.SemaphoreType.DMA((rows // FRAME // 4,)),
        ],
        compiler_params=params(16),
    )(frames, turned)


PIECE = 4 * FRAME


def fetch_frames(source, slots, sems, start, count):
    first, last = max(start - 1, 0), min(start + count + 1, source.shape[0])
    middle = start + 2
    copies = []
    for index, (low, high) in enumerate(((first, middle), (middle, last))):
        copies.append(
            pltpu.make_async_copy(
                source.at[pl.ds(low, high - low)], slots.at[pl.ds(low - start + 1, high - low)], sems.at[index]
            )
        )
    return copies


def mix_frame(slots, at, weights, sums, out, sign):
    for low, high in TILES:
        for start in range(0, BODY, 56):
            parts = [None, None, None]
            for a in (-1, 0, 1):
                for b in (-1, 0, 1):
                    begin = 16 + sign * b * 16 + start
                    cells = slots[at[1 + sign * a], begin : begin + 56, low:high]
                    for c in range(3):
                        tap = 9 * (a + 1) + 3 * (b + 1) + c
                        term = cells * weights[tap : tap + 1, low:high]
                        parts[c] = term if parts[c] is None else parts[c] + term
            parts[1] = parts[1] + slots[at[1], 16 + start : 16 + start + 56, low:high]
            for c in range(3):
                sums[c, start : start + 56, low:high] = parts[c]
    before, after = (0, 2) if sign == 1 else (2, 0)
    for low, high in TILES:
        out[:, low:high] = (
            sums[1, :, low:high]
            + pltpu.roll(sums[before, :, low:high], 1, axis=0)
            + pltpu.roll(sums[after, :, low:high], BODY - 1, axis=0)
        )


def mask_weights(weights, masked, first, middle, last):
    for tap in range(27):
        keep = (first, middle, last)[tap // 9]
        scale = 1.0 if tap == 13 else jnp.where(keep, 1.0, 0.0)
        masked[tap : tap + 1, :] = weights[tap : tap + 1, :] * scale


def conv_params(head, flat, weights):
    flat[...] = head[...].astype(f32)
    for parity in range(2):
        for tile in range(3):
            low, side = read_half(flat, AT_CONV, 5, 5, 15, parity, 2 * tile)
            low = low_half(low, side)
            place = pl.ds(parity, 15, stride=2)
            if tile < 2:
                high, side = read_half(flat, AT_CONV, 5, 5, 15, parity, 2 * tile + 1)
                low = jnp.where(lane_of(low.shape) < 64, low, high_half(high, side))
            weights[tile, place, :] = low


def turn_kernel(frames, source, out, passed):
    passed[0] = frames[0]
    out[...] = source[...].T


def turn(frames, value):
    rows, columns = value.shape
    return pl.pallas_call(
        turn_kernel,
        name="turn",
        in_specs=[SMEM_SPEC, VMEM_SPEC],
        out_specs=[VMEM_SPEC, SMEM_SPEC],
        out_shape=[
            jax.ShapeDtypeStruct((columns, rows), value.dtype),
            jax.ShapeDtypeStruct((1,), jnp.int32),
        ],
        compiler_params=params(10),
        cost_estimate=pl.CostEstimate(flops=0, bytes_accessed=4 * rows * columns, transcendentals=0),
    )(frames, value)


def conv_piece_kernel(start, count, frames_ref, head, padded, back, *refs):
    if start > 0:
        refs = refs[1:]
    mixed, convp, passed, flat, weights, masked, slots, sums, comp, sem = refs
    passed[0] = frames_ref[0]
    copies = fetch_frames(padded, slots, sem, start, count)
    for copy in copies:
        copy.start()
    frames = frames_ref[0]
    conv_params(head, flat, weights)
    for tile, (low, high) in enumerate(TILES):
        convp[:, low:high] = weights[tile, :, : high - low]
    mixed[...] = jnp.zeros(mixed.shape, f32)
    copies[0].wait()

    def each(member, carry):
        @pl.when(member == 1)
        def _():
            copies[1].wait()

        frame = start + member
        there = frame < frames
        before = there & (frame > 0)
        after = frame + 1 < frames
        mask_weights(convp, masked, before, there, after)
        at = (member + jnp.where(before, 0, 1), member + 1, member + jnp.where(after, 2, 1))
        mix_frame(slots, at, masked, sums, comp, 1)
        high, low = pieces(comp[...] + convp[27:28, :])
        shift = member & 3
        place = pl.ds(pl.multiple_of(FRAME * member - 4 * shift, 16), 208)
        mixed[place, :] += dot(back[shift], high) + dot(back[shift], low)
        return carry

    lax.fori_loop(0, count, each, 0)


def conv_piece(start, count, frames, head, padded, back, mixed):
    rows = padded.shape[0] * FRAME
    operands = [frames, head, in_hbm(padded), back] + ([] if start == 0 else [mixed])
    return pl.pallas_call(
        functools.partial(conv_piece_kernel, start, count),
        name=f"conv_piece{start}",
        grid=(1,),
        in_specs=[SMEM_SPEC, VMEM_SPEC, HBM_SPEC, VMEM_SPEC] + [ANY_SPEC] * (start > 0),
        out_specs=[
            pl.BlockSpec((count * FRAME, DIM), lambda i: (start // count, 0)),
            pl.BlockSpec((32, DIM), lambda i: (0, 0)),
            SMEM_SPEC,
        ],
        out_shape=[
            jax.ShapeDtypeStruct((rows, DIM), f32),
            jax.ShapeDtypeStruct((32, DIM), f32),
            jax.ShapeDtypeStruct((1,), jnp.int32),
        ],
        input_output_aliases={4: 0} if start else {},
        scratch_shapes=[
            pltpu.VMEM(head.shape, f32),
            pltpu.VMEM((3, 32, LANES), f32),
            pltpu.VMEM((32, DIM), f32),
            pltpu.VMEM((count + 2, PAD_ROWS, DIM), f32),
            pltpu.VMEM((3, BODY, DIM), f32),
            pltpu.VMEM((BODY, DIM), f32),
            pltpu.SemaphoreType.DMA((2,)),
        ],
        compiler_params=params(20),
    )(*operands)


def normalize(values):
    centered = values - jnp.mean(values, axis=-1, keepdims=True)
    variance = jnp.mean(centered * centered, axis=-1, keepdims=True)
    inverse = lax.rsqrt(variance + EPSILON)
    return centered * inverse, inverse


def flag_base(head):
    return HEAD_DIM if head % 2 == 0 else 0


def own_lanes(lane, head):
    return lane < HEAD_DIM if head % 2 == 0 else lane >= HEAD_DIM


def row_size(value):
    return jnp.max(jnp.sum(value * value, axis=-1, keepdims=True), axis=0, keepdims=True)


def qkv_kernel(frames_ref, mixed, convp, wqkv, bqkv, normed_out, q_out, k_out, v_out, size):
    block = pl.program_id(0)
    rows = mixed.shape[0]
    frames = frames_ref[0]
    normal, unused_inverse = normalize(mixed[...])
    normed = (normal * convp[28:29, :] + convp[29:30, :]).astype(bf16)
    normed_out[...] = normed
    lane = lane_of((rows, LANES))
    inside = row_of((rows, LANES)) + block * rows < frames * FRAME
    scale = HEAD_DIM ** (-0.5) * LOG2E

    @pl.when(block == 0)
    def _():
        size[...] = jnp.zeros(size.shape, f32)

    projected = dot(normed, wqkv[...]) + bqkv[...]
    masks = []
    for base in (flag_base(0), flag_base(1)):
        flag = lane - base
        q_flags = jnp.where(((flag == 0) & ~inside) | ((flag == 1) & inside), BLOCKED, 0.0)
        k_flags = jnp.where(
            ((flag == 0) & inside) | ((flag == 1) & ~inside) | ((flag >= 2) & (flag < 5)), 1.0, 0.0
        )
        v_flags = jnp.where((flag >= 0) & (flag < 3), 1.0, 0.0)
        masks.append((q_flags, k_flags, v_flags))
    for head in range(HEADS):
        q_mask, k_mask, v_mask = masks[head % 2]
        own = own_lanes(lane, head)

        def columns(kind, head=head):
            start = (kind * PAIRS + head // 2) * LANES
            return projected[:, start : start + LANES]

        query = jnp.where(own, columns(0) * scale, q_mask).astype(bf16)
        key = jnp.where(own, columns(1), k_mask).astype(bf16)
        if head % 2 == 0:
            query_size = row_size(columns(0) * scale)
            key_size = row_size(columns(1))
        q_out[head] = query
        k_out[head] = key
        v_out[head] = jnp.where(own, columns(2), v_mask).astype(bf16)
        size[head : head + 1, :] = jnp.maximum(size[head : head + 1, :], query_size)
        size[head + 8 : head + 9, :] = jnp.maximum(size[head + 8 : head + 9, :], key_size)


def project(frames, mixed, convp, wqkv, bqkv, block=784):
    rows = mixed.shape[0]
    heads_spec = pl.BlockSpec((HEADS, block, LANES), lambda i: (0, i, 0))
    rows_spec = pl.BlockSpec((block, DIM), lambda i: (i, 0))
    heads_shape = jax.ShapeDtypeStruct((HEADS, rows, LANES), bf16)
    return pl.pallas_call(
        qkv_kernel,
        name="qkv_forward",
        grid=(rows // block,),
        in_specs=[
            SMEM_SPEC,
            rows_spec,
            pl.BlockSpec((32, DIM), lambda i: (0, 0)),
            pl.BlockSpec((DIM, QKV_COLUMNS), lambda i: (0, 0)),
            pl.BlockSpec((1, QKV_COLUMNS), lambda i: (0, 0)),
        ],
        out_specs=[rows_spec, heads_spec, heads_spec, heads_spec, pl.BlockSpec((16, LANES), lambda i: (0, 0))],
        out_shape=[
            pltpu.HBM((rows, DIM), bf16),
            heads_shape,
            heads_shape,
            heads_shape,
            jax.ShapeDtypeStruct((16, LANES), f32),
        ],
        compiler_params=params(14),
    )(frames, mixed, convp, wqkv, bqkv)


def attend_kernel(chunk, q, k, v, size, o_out, q_back, query, shift):
    head = pl.program_id(0)
    keys = k.shape[1]
    tall = q.shape[1]
    bound = jnp.max(size[pl.ds(head, 1), :] * size[pl.ds(head + 8, 1), :])
    query[...] = q[0]
    shift[...] = jnp.zeros(shift.shape, f32)

    @pl.when(bound > SAFE_BOUND * SAFE_BOUND)
    def _():
        shift[...] = jnp.full(shift.shape, -jnp.inf, f32)

        def peak(step, carry):
            scores = dot_nt(k[0, pl.ds(pl.multiple_of(step * 112, 16), 112), :], q[0])
            shift[...] = jnp.maximum(shift[...], jnp.max(scores, axis=0, keepdims=True))
            return carry

        lax.fori_loop(0, keys // 112, peak, 0)
        first, second, third = split3(-shift[...])
        flag = row_of((LANES, tall)) - jnp.where(lax.rem(head, 2) == 0, HEAD_DIM, 0)
        tail = jnp.where(flag == 2, first, jnp.where(flag == 3, second, jnp.where(flag == 4, third, 0.0)))
        query[...] = (q[0].astype(f32) + tail.T).astype(bf16)

    total = None
    for start in range(0, keys, chunk):
        place = slice(start, min(start + chunk, keys))
        weights = jnp.exp2(dot_nt(k[0, place, :], query[...])).astype(bf16)
        part = dot_tn(v[0, place, :], weights)
        total = part if total is None else total + part
    def finish(parity):
        base = flag_base(parity)
        sums = total[base : base + 1, :]
        first, second, third = split3(-(shift[...] + jnp.log2(sums)))
        row = row_of((8, tall))
        tail = jnp.where(row == 2, first, jnp.where(row == 3, second, jnp.where(row == 4, third, 0.0)))
        flags = [tail, jnp.zeros((56, tall), f32)]
        own = [total[HEAD_DIM - base : 2 * HEAD_DIM - base, :] / sums]
        stacked = jnp.concatenate(own + flags if parity == 0 else flags + own, axis=0).T
        lane = lane_of((tall, LANES))
        o_out[0] = jnp.where(own_lanes(lane, parity), stacked, 0.0).astype(bf16)
        place = (lane >= base + 2) & (lane < base + 5)
        q_back[0] = jnp.where(place, stacked, q[0].astype(f32)).astype(bf16)

    for parity in range(2):
        pl.when(lax.rem(head, 2) == parity)(functools.partial(finish, parity))


def attend(q, k, v, size, chunk=512):
    rows = q.shape[1]
    whole = pl.BlockSpec((1, rows, LANES), lambda h: (h, 0, 0))
    shape = jax.ShapeDtypeStruct((HEADS, rows, LANES), bf16)
    return pl.pallas_call(
        functools.partial(attend_kernel, chunk),
        name="attend",
        grid=(HEADS,),
        in_specs=[whole, whole, whole, pl.BlockSpec((16, LANES), lambda h: (0, 0))],
        out_specs=[whole, whole],
        out_shape=[shape, pltpu.HBM(shape.shape, bf16)],
        scratch_shapes=[pltpu.VMEM((rows, LANES), bf16), pltpu.VMEM((1, rows), f32)],
        compiler_params=params(18),
    )(q, k, v, size)


def attend_back_kernel(q, do, k, v, dq_out, dk_out, dv_out):
    weights = jnp.exp2(dot_nt(q[0], k[0]))
    grad_scores = (weights * dot_nt(do[0], v[0])).astype(bf16)
    dv_out[0] = dot_tn(do[0], weights.astype(bf16)).T.astype(bf16)
    dk_out[0] = (dot_tn(q[0], grad_scores) * LN2).T.astype(bf16)
    dq_out[0] = (dot_nt(k[0].T, grad_scores) * HEAD_DIM ** (-0.5)).T.astype(bf16)


def attend_back(q, do, k, v):
    heads, rows = q.shape[:2]
    whole = pl.BlockSpec((1, rows, LANES), lambda h: (h, 0, 0))
    shape = jax.ShapeDtypeStruct((heads, rows, LANES), bf16)
    return pl.pallas_call(
        attend_back_kernel,
        name="attend_back",
        grid=(heads,),
        in_specs=[whole] * 4,
        out_specs=[whole] * 3,
        out_shape=[shape] * 3,
        compiler_params=params(40),
    )(q, do, k, v)


def erf_parts(value):
    bell = jnp.exp(-0.5 * value * value)
    return bell, 0.5 * (1.0 + lax.erf(value * (1.0 / math.sqrt(2.0))))


def paired(heads):
    tiles = []
    for head in range(0, HEADS, 2):
        high = heads[head + 1] if head + 1 < HEADS else jnp.zeros_like(heads[head])
        tiles.append(jnp.where(lane_of(high.shape) < HEAD_DIM, heads[head], high))
    return jnp.concatenate(tiles, axis=1)


def add_tiles(ref, place, value):
    for tile, (low, high) in enumerate(TILES):
        ref[tile, place, : high - low] += value[:, low:high]


def middle_kernel(
    frames_ref, o, mixed, cot, wproj, fc1, fc2, vecs, fc1b,
    output, gmid_out, do_out, gproj, gfc1, gfc2, gvec, gfc1b, chunk,
):
    block = pl.program_id(0)
    rows = mixed.shape[0]
    inside = row_of((rows, DIM)) + block * rows < frames_ref[0] * FRAME

    @pl.when(block == 0)
    def _():
        for ref in (gproj, gfc1, gfc2, gvec, gfc1b):
            ref[...] = jnp.zeros(ref.shape, f32)

    attended = paired(o)
    middle = mixed[...] + (dot(attended, wproj[...]) + vecs[0:1, :])
    normal, inverse = normalize(middle)
    normed = (normal * vecs[1:2, :] + vecs[2:3, :]).astype(bf16)
    grad_output = jnp.where(inside, cot[...].astype(f32), 0.0)
    grad_outer = grad_output.astype(bf16)
    total = middle + vecs[3:4, :]
    grad_normed = jnp.zeros((rows, DIM), f32)
    for start in range(0, FFN, chunk):
        place = slice(start, start + chunk)
        inner = dot(normed, fc1[:, place]) + fc1b[:, place]
        bell, gate = erf_parts(inner)
        activated = (inner * gate).astype(bf16)
        total += dot(activated, fc2[place, :])
        slope = gate + inner * bell * INVERSE_ROOT_TWO_PI
        grad_inner = (dot_nt(grad_outer, fc2[place, :]) * slope)
        gfc1b[:, place] += jnp.sum(grad_inner, axis=0, keepdims=True)
        grad_inner = grad_inner.astype(bf16)
        add_tiles(gfc2, place, dot_tn(activated, grad_outer))
        gfc1[:, place] += dot_tn(normed, grad_inner)
        grad_normed += dot_nt(grad_inner, fc1[:, place])
    output[...] = total.astype(bf16)
    scaled = grad_normed * vecs[1:2, :]
    grad_middle = grad_output + inverse * (
        scaled
        - jnp.mean(scaled, axis=-1, keepdims=True)
        - normal * jnp.mean(scaled * normal, axis=-1, keepdims=True)
    )
    gmid_out[...] = grad_middle
    grad_branch = grad_middle.astype(bf16)
    add_tiles(gproj, slice(None), dot_tn(attended, grad_branch))
    gvec[0:1, :] += jnp.sum(grad_branch.astype(f32), axis=0, keepdims=True)
    gvec[1:2, :] += jnp.sum(grad_normed * normal, axis=0, keepdims=True)
    gvec[2:3, :] += jnp.sum(grad_normed, axis=0, keepdims=True)
    gvec[3:4, :] += jnp.sum(grad_output, axis=0, keepdims=True)
    lane = lane_of((rows, LANES))
    grad_attended = dot_nt(grad_branch, wproj[...])
    for head in range(HEADS):
        grad_head = grad_attended[:, head // 2 * LANES : (head // 2 + 1) * LANES]
        flag = lane - flag_base(head)
        delta = jnp.sum(grad_head * o[head].astype(f32), axis=-1, keepdims=True)
        first, second, third = split3(-delta)
        tail = jnp.where(flag == 0, first, jnp.where(flag == 1, second, third))
        do_out[head] = jnp.where((flag >= 0) & (flag < 3), tail, grad_head).astype(bf16)


def feed_forward(frames, o, mixed, cot, wproj, fc1, fc2, vecs, fc1b, block=784, chunk=256):
    rows = mixed.shape[0]
    heads_spec = pl.BlockSpec((HEADS, block, LANES), lambda i: (0, i, 0))
    rows_spec = pl.BlockSpec((block, DIM), lambda i: (i, 0))

    def full(*shape):
        return pl.BlockSpec(shape, lambda i: (0,) * len(shape))

    return pl.pallas_call(
        functools.partial(middle_kernel, chunk=chunk),
        name="feed_forward",
        grid=(rows // block,),
        in_specs=[
            SMEM_SPEC, heads_spec, rows_spec, rows_spec,
            full(PAIR_COLUMNS, DIM), full(DIM, FFN), full(FFN, DIM), full(8, DIM), full(1, FFN),
        ],
        out_specs=[
            rows_spec, rows_spec, heads_spec,
            full(3, PAIR_COLUMNS, LANES), full(DIM, FFN), full(3, FFN, LANES), full(8, DIM), full(1, FFN),
        ],
        out_shape=[
            pltpu.HBM((rows, DIM), bf16),
            pltpu.HBM((rows, DIM), f32),
            pltpu.HBM((HEADS, rows, LANES), bf16),
            jax.ShapeDtypeStruct((3, PAIR_COLUMNS, LANES), f32),
            jax.ShapeDtypeStruct((DIM, FFN), f32),
            jax.ShapeDtypeStruct((3, FFN, LANES), f32),
            jax.ShapeDtypeStruct((8, DIM), f32),
            jax.ShapeDtypeStruct((1, FFN), f32),
        ],
        compiler_params=params(22),
    )(frames, o, mixed, cot, wproj, fc1, fc2, vecs, fc1b)


def qkv_back_kernel(dq, dk, dv, normed, mixed, gmid, wqkv, convp, spread, padded, gqkv, gbias, gvec, gmix):
    block = pl.program_id(0)

    @pl.when(block == 0)
    def _():
        for ref in (gqkv, gbias, gvec):
            ref[...] = jnp.zeros(ref.shape, f32)

    normal, inverse = normalize(mixed[...])
    grads = jnp.concatenate([paired(part) for part in (dq, dk, dv)], axis=1)
    grad_qkv = dot_tn(normed[...], grads)
    for tile in range(3 * PAIRS):
        gqkv[tile] += grad_qkv[:, tile * LANES : (tile + 1) * LANES]
    gbias[...] += jnp.sum(grads.astype(f32), axis=0, keepdims=True)
    grad_normed = dot_nt(grads, wqkv[...])
    gvec[1:2, :] += jnp.sum(grad_normed * normal, axis=0, keepdims=True)
    gvec[2:3, :] += jnp.sum(grad_normed, axis=0, keepdims=True)
    scaled = grad_normed * convp[28:29, :]
    grad_mixed = gmid[...] + inverse * (
        scaled
        - jnp.mean(scaled, axis=-1, keepdims=True)
        - normal * jnp.mean(scaled * normal, axis=-1, keepdims=True)
    )
    gvec[0:1, :] += jnp.sum(grad_mixed, axis=0, keepdims=True)
    gmix[...] = grad_mixed
    for member in range(mixed.shape[0] // FRAME):
        high, low = pieces(gmix[192 * member : 192 * member + 208, :])
        padded[member] = dot(spread[member], high) + dot(spread[member], low)


def project_back(dq, dk, dv, normed, mixed, gmid, wqkv, convp, spread, block=PIECE):
    rows = mixed.shape[0]
    heads_spec = pl.BlockSpec((HEADS, block, LANES), lambda i: (0, i, 0))
    rows_spec = pl.BlockSpec((block, DIM), lambda i: (i, 0))

    def full(*shape):
        return pl.BlockSpec(shape, lambda i: (0,) * len(shape))

    return pl.pallas_call(
        qkv_back_kernel,
        name="qkv_back",
        grid=(rows // block,),
        in_specs=[heads_spec, heads_spec, heads_spec, rows_spec, rows_spec, rows_spec,
                  full(DIM, QKV_COLUMNS), full(32, DIM), full(4, PAD_ROWS, 208)],
        out_specs=[pl.BlockSpec((4, PAD_ROWS, DIM), lambda i: (i, 0, 0)), full(3 * PAIRS, DIM, LANES), full(1, QKV_COLUMNS), full(8, DIM)],
        out_shape=[
            pltpu.HBM((rows // FRAME, PAD_ROWS, DIM), f32),
            jax.ShapeDtypeStruct((3 * PAIRS, DIM, LANES), f32),
            jax.ShapeDtypeStruct((1, QKV_COLUMNS), f32),
            jax.ShapeDtypeStruct((8, DIM), f32),
        ],
        scratch_shapes=[pltpu.VMEM((block, DIM), f32)],
        compiler_params=params(18),
    )(dq, dk, dv, normed, mixed, gmid, wqkv, convp, spread)


FRAME_GROUPS = ((0, 2), (2, 5), (5, 12))


def conv_weight_kernel(frames_ref, xsource, gsource, gvec, out, xpad, gpad, moved, sums, tiles, flat, xsem, gsem):
    frames = frames_ref[0]
    count = xpad.shape[0]
    copies = []
    for group, (low, high) in enumerate(FRAME_GROUPS):
        place = pl.ds(low, high - low)
        copies.append(pltpu.make_async_copy(xsource.at[place], xpad.at[place], xsem.at[group]))
        copies.append(pltpu.make_async_copy(gsource.at[place], gpad.at[place], gsem.at[group]))
    for copy in copies:
        copy.start()
    sums[...] = jnp.zeros(sums.shape, f32)

    def weight_frame(frame, carry):
        for low, high in TILES:
            body = gpad[frame, 16 : 16 + BODY, low:high]
            moved[0, :, low:high] = pltpu.roll(body, BODY - 1, axis=0)
            moved[1, :, low:high] = pltpu.roll(body, 1, axis=0)
        for a in (-1, 0, 1):
            at = frame + a

            @pl.when((at >= 0) & (at < frames))
            def _():
                for low, high in TILES:
                    for b in (-1, 0, 1):
                        cells = xpad[at, 16 + b * 16 : 16 + b * 16 + BODY, low:high]
                        for c in range(3):
                            body = (
                                gpad[frame, 16 : 16 + BODY, low:high]
                                if c == 1
                                else moved[c // 2, :, low:high]
                            )
                            product = (body * cells).reshape(BODY // 8, 8, high - low)
                            tap = 9 * (a + 1) + 3 * (b + 1) + c
                            sums[tap, :, low:high] += jnp.sum(product, axis=0)

        return carry

    for group, (low, high) in enumerate(FRAME_GROUPS):
        copies[2 * group].wait()
        copies[2 * group + 1].wait()
        start = max(low - 1, 0)
        stop = high - 1 if high < count else count
        lax.fori_loop(jnp.minimum(start, frames), jnp.minimum(stop, frames), weight_frame, 0)
    tiles[...] = jnp.zeros(tiles.shape, f32)
    flat[...] = jnp.zeros(flat.shape, f32)
    for tile, (low, high) in enumerate(TILES):
        tiles[tile, 0:27, : high - low] = jnp.sum(sums[:, :, low:high], axis=1)
        tiles[tile, 27:30, : high - low] = gvec[0:3, low:high]
    for parity in range(2):
        for j in range(5):
            value = tiles[j // 2, pl.ds(parity, 15, stride=2), :]
            put_half(flat, AT_CONV + parity * 5 + j, value, j % 2, 5, 15)
    out[...] = flat[...].astype(bf16)


def conv_weight_grads(frames, xpad, gpad, gvec):
    return pl.pallas_call(
        conv_weight_kernel,
        name="conv_weight_grads",
        in_specs=[SMEM_SPEC, HBM_SPEC, HBM_SPEC, VMEM_SPEC],
        out_shape=jax.ShapeDtypeStruct((80, LANES), bf16),
        scratch_shapes=[
            pltpu.VMEM(xpad.shape, f32),
            pltpu.VMEM(gpad.shape, f32),
            pltpu.VMEM((2, BODY, DIM), f32),
            pltpu.VMEM((27, 8, DIM), f32),
            pltpu.VMEM((3, 32, LANES), f32),
            pltpu.VMEM((80, LANES), f32),
            pltpu.SemaphoreType.DMA((len(FRAME_GROUPS),)),
            pltpu.SemaphoreType.DMA((len(FRAME_GROUPS),)),
        ],
        compiler_params=params(18),
    )(frames, in_hbm(xpad), in_hbm(gpad), gvec)


def token_piece_kernel(piece, frames_ref, convp, gsource, back, *refs):
    if piece > 0:
        refs = refs[1:]
    gtok, passed, masked, slots, sums, comp, rows, sem = refs
    frames = frames_ref[0]
    passed[0] = frames
    copies = fetch_frames(gsource, slots, sem, 4 * piece, 4)
    for copy in copies:
        copy.start()
    rows[...] = jnp.zeros(rows.shape, f32)
    copies[0].wait()

    def each(member, carry):
        @pl.when(member == 1)
        def _():
            copies[1].wait()

        frame = 4 * piece + member
        there = frame < frames
        before = there & (frame > 0)
        after = frame + 1 < frames
        mask_weights(convp, masked, after, there, before)
        at = (member + jnp.where(before, 0, 1), member + 1, member + jnp.where(after, 2, 1))
        mix_frame(slots, at, masked, sums, comp, -1)
        place = pl.ds(pl.multiple_of(192 * member, 16), 208)
        rows[place, :] += dot(back[member], comp[...].astype(bf16))
        return carry

    lax.fori_loop(0, 4, each, 0)
    gtok[...] = rows[...].astype(bf16)


def token_piece(piece, frames, convp, gpad, back, gtok):
    count = gpad.shape[0]
    operands = [frames, convp, in_hbm(gpad), back] + ([] if piece == 0 else [gtok])
    return pl.pallas_call(
        functools.partial(token_piece_kernel, piece),
        name=f"token_piece{piece}",
        grid=(1,),
        in_specs=[SMEM_SPEC, VMEM_SPEC, HBM_SPEC, VMEM_SPEC] + [ANY_SPEC] * (piece > 0),
        out_specs=[pl.BlockSpec((PIECE, DIM), lambda i: (piece, 0)), SMEM_SPEC],
        out_shape=[
            jax.ShapeDtypeStruct((count * FRAME, DIM), bf16),
            jax.ShapeDtypeStruct((1,), jnp.int32),
        ],
        input_output_aliases={4: 0} if piece else {},
        scratch_shapes=[
            pltpu.VMEM((32, DIM), f32),
            pltpu.VMEM((6, PAD_ROWS, DIM), f32),
            pltpu.VMEM((3, BODY, DIM), f32),
            pltpu.VMEM((BODY, DIM), f32),
            pltpu.VMEM((PIECE, DIM), f32),
            pltpu.SemaphoreType.DMA((2,)),
        ],
        compiler_params=params(10),
    )(*operands)


def put_half(flat, index, value, side, step=1, count=1):
    row, wanted = divmod(index, 2)
    place = pl.ds(row, count, stride=step) if step > 1 else pl.ds(row, count)
    lane = lane_of(value.shape)
    if wanted == 0:
        flat[place, :] += jnp.where(lane < 64, low_half(value, side), 0.0)
    else:
        flat[place, :] += jnp.where(lane >= 64, high_half(value, side), 0.0)


def put_vector(flat, index, value):
    width = value.shape[1]
    for j in range(width // 64):
        low = (j // 2) * LANES
        part = value[:, low : min(low + LANES, width)]
        if part.shape[1] < LANES:
            part = jnp.concatenate([part, jnp.zeros((1, 64), f32)], axis=1)
        put_half(flat, index + j, part, j % 2)


PACK_BASE = 2432


def pack_main_kernel(gproj, gfc1, gfc2, gvec, gfc1b, out, flat):
    flat[...] = jnp.zeros(flat.shape, f32)
    for parity in range(2):
        for j in range(5):
            value = gproj[j // 2, pl.ds(parity, DIM // 2, stride=2), :]
            put_half(flat, AT_PROJ + parity * 5 + j, value, j % 2, 5, DIM // 2)
            value = gfc2[j // 2, pl.ds(parity, FFN // 2, stride=2), :]
            put_half(flat, AT_FC2 + parity * 5 + j, value, j % 2, 5, FFN // 2)
    for j in range(20):
        value = gfc1[:, (j // 2) * LANES : (j // 2 + 1) * LANES]
        put_half(flat, AT_FC1 + j, value, j % 2, 10, DIM)
    for row in range(3):
        put_vector(flat, AT_VEC + 5 * row, gvec[row : row + 1, :])
    put_vector(flat, AT_FC2B, gvec[3:4, :])
    put_vector(flat, AT_FC1B, gfc1b[...])
    out[...] = flat[...].astype(bf16)


def pack_main(gproj, gfc1, gfc2, gvec, gfc1b, rows):
    return pl.pallas_call(
        pack_main_kernel,
        name="pack_main",
        out_shape=jax.ShapeDtypeStruct((rows, LANES), bf16),
        scratch_shapes=[pltpu.VMEM((rows, LANES), f32)],
        compiler_params=params(14),
    )(gproj, gfc1, gfc2, gvec, gfc1b)


QKV_ROWS = 2480


def pack_qkv_kernel(gqkv, gbias, out, end, flat):
    flat[...] = jnp.zeros(flat.shape, f32)
    for parity in range(2):
        for j in range(15):
            kind, head = divmod(j, HEADS)
            value = gqkv[kind * PAIRS + head // 2, pl.ds(parity, DIM // 2, stride=2), :]
            put_half(flat, AT_QKV + parity * 15 + j, value, head % 2, 15, DIM // 2)
    for j in range(10):
        start = (0 if j < HEADS else 2 * PAIR_COLUMNS) + j % HEADS // 2 * LANES
        put_half(flat, AT_QV + j, gbias[:, start : start + LANES], j % HEADS % 2)
    out[...] = flat[:PACK_BASE, :].astype(bf16)
    end[...] = flat[PACK_BASE:, :].astype(bf16)


def pack_qkv(gqkv, gbias):
    return pl.pallas_call(
        pack_qkv_kernel,
        name="pack_qkv",
        out_shape=[
            jax.ShapeDtypeStruct((PACK_BASE, LANES), bf16),
            jax.ShapeDtypeStruct((QKV_ROWS - PACK_BASE, LANES), bf16),
        ],
        scratch_shapes=[pltpu.VMEM((QKV_ROWS, LANES), f32)],
        compiler_params=params(10),
    )(gqkv, gbias)


AXES = ("wide", "narrow")


def exchange(value, bit):
    count = lax.axis_size(AXES)
    return lax.ppermute(value, AXES, [(i, i ^ (1 << bit)) for i in range(count)])


def my_bit(bit):
    return (lax.axis_index(AXES) >> bit) & 1


def tie(*values):
    return lax.optimization_barrier(values)


def split(value, bit):
    value = value.reshape(value.shape[0] // 2, 2, -1, LANES)
    mine = my_bit(bit)
    keep = lax.dynamic_index_in_dim(value, mine, 1, keepdims=False)
    return keep, lax.dynamic_index_in_dim(value, 1 - mine, 1, keepdims=False)


def on_device(master, momentum, average, tokens, clip_ids, borders, cotangent):
    wide_count, narrow_count = lax.axis_size("wide"), lax.axis_size("narrow")
    count = wide_count * narrow_count
    bits = count.bit_length() - 1
    own_rows = master.shape[0]
    filled = jnp.sum((clip_ids >= 0).astype(jnp.int32))
    frames = jnp.where(filled > 6 * FRAME, 12, jnp.where(filled > 3 * FRAME, 6, 3)).reshape(1)
    me = lax.axis_index(AXES)
    quarter = me >> (bits - 2)
    blocks = master.astype(bf16)[None]
    other = exchange(blocks, bits - 2)
    other, frames = tie(other, frames)
    blocks = jnp.concatenate([blocks, other], axis=0)
    blocks, frames = tie(blocks, frames)
    other = exchange(blocks, bits - 1)
    xpad, spread, back, frames = prepare(frames, tokens.T)
    other, frames = tie(other, frames)
    blocks = jnp.concatenate([blocks, other], axis=0)
    first = lax.dynamic_index_in_dim(blocks, quarter, 0)
    rest = [lax.dynamic_index_in_dim(blocks, quarter ^ index, 0) for index in (1, 2, 3)]
    rest = jnp.concatenate(rest, axis=0)[None]
    low_bits = list(range(bits - 3, -1, -1))
    for step, bit in enumerate(low_bits):
        if step == 0:
            first, frames = tie(first, frames)
        other = exchange(first, bit)
        if step == 0:
            cotangent, frames = turn(frames, cotangent.T)
            other, frames = tie(other, frames)
        first = jnp.concatenate([first, other], axis=0)
        if step == 0:
            first, rest, frames = tie(first, rest, frames)
            rest = jnp.concatenate([rest, exchange(rest, bit)], axis=0)
    order = [0] * (count // 4)
    for step, bit in enumerate(low_bits):
        order = [place | (((index >> bit) & 1) << step) for index, place in enumerate(order)]
    mine = sum((((me >> bit) & 1) << step) for step, bit in enumerate(low_bits))
    order = jnp.array(order, jnp.int32) ^ mine
    head = lax.dynamic_index_in_dim(first, mine, 0, keepdims=False)
    head = jnp.concatenate([head, jnp.zeros((4, LANES), bf16)], axis=0)[:80] if own_rows < 80 else head[:80]
    mixed, convp = None, None
    for step, bit in enumerate(low_bits[1:]):
        if step < 2:
            rest, frames = tie(rest, frames)
        other = exchange(rest, bit)
        if step == 0:
            mixed, convp, frames = conv_piece(0, 8, frames, head, xpad, back, None)
        elif step == 1:
            mixed, convp, frames = conv_piece(8, 4, frames, head, xpad, back, mixed)
        other, frames = tie(other, frames)
        rest = jnp.concatenate([rest, other], axis=0)
    wqkv, wproj, fc1, fc2, bqkv, vecs, fc1b = unpack(order, first, rest)
    normed, q, k, v, size = project(frames, mixed, convp, wqkv, bqkv)
    o, q_back = attend(q, k, v, size)
    output, gmid, do, gproj, gfc1, gfc2, gvec, gfc1b = feed_forward(
        frames, o, mixed, cotangent, wproj, fc1, fc2, vecs, fc1b
    )
    main = pack_main(gproj, gfc1, gfc2, gvec, gfc1b, count * own_rows)
    main = main.reshape(wide_count, narrow_count, own_rows, LANES)
    main = lax.psum_scatter(main, "wide", scatter_dimension=0, tiled=True)[0]
    q_back, do, k, v = (in_hbm(value) for value in (q_back, do, k, v))
    dq, dk, dv = attend_back(q_back, do, k, v)
    gpad, gqkv, gbias, gvec_one = project_back(dq, dk, dv, normed, mixed, gmid, wqkv, convp, spread)
    qkv, qkv_end = pack_qkv(gqkv, gbias)
    qkv = qkv.reshape(count // 4, own_rows, LANES)
    narrow_bits = narrow_count.bit_length() - 1
    keep, give = split(qkv, 0)
    gvec_one, give = tie(gvec_one, give)
    arriving = exchange(give, 0)
    conv = conv_weight_grads(frames, xpad, gpad, gvec_one)
    late = jnp.concatenate([conv, qkv_end], axis=0)
    main, late = tie(main, late)
    for bit in range(1, narrow_bits):
        keep, give = split(keep + arriving, bit)
        arriving = exchange(give, bit)
    gtok = None
    for step, bit in enumerate([*range(bits - 2), bits - 1, bits - 2]):
        if bit < narrow_bits:
            stays, give = split(main, bit)
        elif bit < bits - 2:
            stays, give = split(qkv, bit)
        else:
            stays, give = qkv, qkv
        sent = give.shape[0] * own_rows
        packet = jnp.concatenate([give.reshape(sent, LANES), late], axis=0)
        packet, frames = tie(packet, frames)
        other = exchange(packet, bit)
        if step == 0:
            output, frames = turn(frames, output)
        elif step < 4:
            gtok, frames = token_piece(step - 1, frames, convp, gpad, back, gtok)
        elif step == 4:
            gtok, frames = turn(frames, gtok)
        other, frames = tie(other, frames)
        if bit == narrow_bits - 1:
            other, arriving = tie(other, arriving)
            qkv = keep + arriving
        summed = stays + other[:sent].reshape(stays.shape)
        late = late + other[sent:]
        if bit < narrow_bits:
            main = summed
        else:
            qkv = summed
    main, qkv = main[0], qkv[0]
    early = jnp.where(me < count // 4, qkv.astype(f32), main.astype(f32))
    conv, qkv_end = late[:80].astype(f32), late[80:].astype(f32)
    if own_rows < 80:
        conv = conv[:own_rows]
    conv = jnp.pad(conv, ((0, own_rows - conv.shape[0]), (0, 0)))
    qkv_end = jnp.pad(qkv_end, ((0, own_rows - qkv_end.shape[0]), (0, 0)))
    owned = early + jnp.where(me == 0, conv, jnp.where(me == count // 4, qkv_end, 0.0))
    rate = RATE_FACTOR / math.sqrt(tokens.shape[0] * count)
    decayed = owned + DECAY_RATE * master
    new_momentum = MOMENTUM * momentum + decayed
    new_master = master - rate * (decayed + MOMENTUM * new_momentum)
    new_average = AVERAGE_KEEP * average + (1.0 - AVERAGE_KEEP) * new_master
    return (output.T, gtok.T, owned, new_master, new_momentum, new_average, new_master.astype(bf16))


def solution(mesh):
    rows = P(("wide", "narrow"), None)
    return jax.shard_map(
        on_device,
        mesh=mesh,
        in_specs=(rows, rows, rows, rows, P(("wide", "narrow")), P(("wide", "narrow")), rows),
        out_specs=(rows,) * 7,
        check_vma=False,
    )
```
